32 devices in a mesh: dp: 4 (over y, core), seq: 8 (over z, x).
Axes of the slice: x: 2, y: 2, z: 4, core: 2. Of those that a mesh axis runs over, the one named last changes fastest.
Arguments:
- inputs: bfloat16 [4096, 768], P(('dp', 'seq')), may hold values from -6 to 6
- norm_gain: float32 [768], replicated, may hold values from 0.5 to 1.5
- in_proj: bfloat16 [768, 3352], P(('dp', 'seq')), may hold values from -0.21875 to 0.21875
- conv_weight: float32 [1792, 4], replicated, may hold values from -0.5 to 0.5
- conv_bias: float32 [1792], replicated, may hold values from -0.5 to 0.5
- dt_bias: float32 [24], replicated, may hold values from -10 to -3
- a_log: float32 [24], replicated, may hold values from -1 to 1.5
- skip_gain: float32 [24], replicated, may hold values from 0.5 to 1.5
- gated_gain: float32 [1536], replicated, may hold values from 0.5 to 1.5
- out_proj: bfloat16 [768, 1536], P(('dp', 'seq')), may hold values from -0.15625 to 0.15625
- cotangent: bfloat16 [4096, 768], P(('dp', 'seq')), may hold values from -6 to 6
Outputs:
- layer_out: bfloat16 [4096, 768], P(('dp', 'seq'))
- input_grad: float32 [4096, 768], P(('dp', 'seq'))
- in_proj_grad: float32 [768, 3352], P(('dp', 'seq'))
- out_proj_grad: float32 [768, 1536], P(('dp', 'seq'))
- norm_gain_grad: float32 [768], replicated
- conv_weight_grad: float32 [1792, 4], replicated
- conv_bias_grad: float32 [1792], replicated
- dt_bias_grad: float32 [24], replicated
- a_log_grad: float32 [24], replicated
- skip_grad: float32 [24], replicated
- gated_gain_grad: float32 [1536], replicated
The draws below stay inside these ranges and needn't reach their ends.
All inputs are finite; a program needn't handle non-finite values.
Results may differ from the reference program's by a relative error of at most 0.015.
Values may be sent and summed in bfloat16 or wider, within the bound.
A program may use at most 192 MiB of HBM per device.

```python
import jax
import jax.numpy as jnp
from jax import lax

D = 768
HEADS = 24
HEAD_DIM = 64
STATE = 128
CONV = 4
SPAN = 256
TOK_DEV = 128
DI = 1536
XBC = 1792
PROJ = 3352
LENGTH = 1024
TOKENS = 4096
N_DP = 4
N_SEQ = 8


def raised(array, key, source, target, shards_of, factor):
    owner, partner = [(jnp.arange(array.shape[dim]) // (array.shape[dim] // shards_of)).reshape([-1 if axis == dim else 1 for axis in range(array.ndim)]) for dim in (source, target)]
    chosen = jax.random.permutation(key, shards_of)[partner]
    strong = (owner == chosen) | (owner == (partner + shards_of // 2) % shards_of)
    return jnp.where(strong, factor * array, array)


def block_scale(stream_key, dims, cuts, smallest, top_value):
    level, own = 1.0, jax.random.fold_in(stream_key, 6)
    for axis_at, blocks in cuts:
        steps = jnp.exp(jax.random.uniform(jax.random.fold_in(own, axis_at), (blocks,), jnp.float32, smallest / len(cuts), top_value / len(cuts)))
        level = level * jnp.repeat(steps, dims[axis_at] // blocks).reshape([-1 if axis == axis_at else 1 for axis in range(len(dims))])
    return level


def bell_draw(key, dims, width, most, split=(), dtype=jnp.bfloat16):
    array = width * jax.random.normal(key, dims, jnp.float32)
    if split:
        array = array * block_scale(key, dims, split, -0.22, 0.18)
    return jnp.clip(array, -most, most).astype(dtype)


def gaussian_with(rng, shape, scale, bound, shards, heavy, held_as=jnp.bfloat16):
    entries = scale * jax.random.normal(rng, shape, jnp.float32)
    if shards:
        entries = entries * block_scale(rng, shape, shards, -0.22, 0.18)
    return jnp.clip(raised(entries, jax.random.fold_in(rng, 3), *heavy), -bound, bound).astype(held_as)


def setup_inputs(seed: int = 0) -> dict:
    splits = jax.random.split(jax.random.key(seed), 12)
    return {
        "inputs": bell_draw(splits[0], (TOKENS, D), 1.0, 6.0, ((0, 32),)),
        "norm_gain": jnp.clip(1.0 + 0.1 * jax.random.normal(splits[1], (D,), jnp.float32), 0.5, 1.5),
        "in_proj": bell_draw(splits[2], (D, PROJ), D ** -0.5, 0.21875, ((0, 32),)),
        "conv_weight": jnp.clip(jax.random.uniform(splits[3], (XBC, CONV), jnp.float32, -0.5, 0.5), -0.5, 0.5),
        "conv_bias": jnp.clip(jax.random.uniform(splits[4], (XBC,), jnp.float32, -0.5, 0.5), -0.5, 0.5),
        "dt_bias": jnp.clip(jax.random.uniform(splits[5], (HEADS,), jnp.float32, -10.0, -3.0), -10.0, -3.0),
        "a_log": jnp.clip(jax.random.uniform(splits[6], (HEADS,), jnp.float32, -1.0, 1.5), -1.0, 1.5),
        "skip_gain": jnp.clip(jax.random.uniform(splits[7], (HEADS,), jnp.float32, 0.5, 1.5), 0.5, 1.5),
        "gated_gain": jnp.clip(1.0 + 0.1 * jax.random.normal(splits[8], (DI,), jnp.float32), 0.5, 1.5),
        "out_proj": bell_draw(splits[9], (D, DI), DI ** -0.5, 0.15625, ((0, 32),)),
        "cotangent": gaussian_with(splits[10], (TOKENS, D), 1.0, 6.0, ((0, 32),), (0, 1, 32, 2.75)),
    }


EPS = 1e-05
HIGH = lax.Precision.HIGHEST

def pre_norm(residual_in, norm_gain):
    scale_rms = lax.rsqrt(lax.optimization_barrier(jnp.mean(residual_in * residual_in, axis=-1, keepdims=True)) + EPS)
    return residual_in * scale_rms * norm_gain

def conv_silu(padded, conv_weight, conv_bias, row_count):
    total = jnp.zeros((row_count, padded.shape[1]), jnp.float32) + conv_bias[None, :]
    for offset in range(conv_weight.shape[1]):
        total = total + conv_weight[:, offset][None, :] * padded[offset:offset + row_count]
    return jax.nn.silu(total)

def ssd_block(heads_x, b_block, c_block, step_block, decay_block, carried):
    cumulative = jnp.cumsum(decay_block, axis=0)
    by_head = cumulative.T
    spread = by_head[:, :, None] - by_head[:, None, :]
    places = jnp.arange(decay_block.shape[0])
    lower = places[:, None] >= places[None, :]
    weights_mat = jnp.exp(jnp.where(lower[None], spread, -jnp.inf))
    intersection = jnp.dot(c_block, b_block.T, precision=HIGH)
    scaled_x = heads_x * step_block[:, :, None]
    scores = weights_mat * intersection[None]
    output = jnp.einsum('hts,shp->thp', scores, scaled_x, precision=HIGH)
    output = output + jnp.einsum('tn,hpn->thp', c_block, carried, precision=HIGH) * jnp.exp(cumulative)[:, :, None]
    tail = jnp.exp(cumulative[-1][None, :] - cumulative)
    fresh = jnp.einsum('shp,sn->hpn', scaled_x * tail[:, :, None], b_block, precision=HIGH)
    return (output, fresh + jnp.exp(cumulative[-1])[:, None, None] * carried)

def ssd_scan(xs, b_mat, c_mat, step, log_decay, block_rows):
    row_count = xs.shape[0]
    count = row_count // block_rows
    pieces = (xs.reshape(count, block_rows, HEADS, HEAD_DIM), b_mat.reshape(count, block_rows, STATE), c_mat.reshape(count, block_rows, STATE), step.reshape(count, block_rows, HEADS), log_decay.reshape(count, block_rows, HEADS))
    start_state = jnp.zeros((HEADS, HEAD_DIM, STATE), jnp.float32)

    def advance(carried, piece):
        output, carried = ssd_block(piece[0], piece[1], piece[2], piece[3], piece[4], carried)
        return (carried, output)
    final, outputs = lax.scan(advance, start_state, pieces)
    return (outputs.reshape(row_count, HEADS * HEAD_DIM), final)

def mid_local(xbc, dt_raw, edge, conv_weight, conv_bias, dt_bias, a_log, block_rows):
    row_count = xbc.shape[0]
    activated = conv_silu(jnp.concatenate([edge, xbc], axis=0), conv_weight, conv_bias, row_count)
    xs = activated[:, :DI]
    b_mat = activated[:, DI:DI + STATE]
    c_mat = activated[:, DI + STATE:]
    step = jax.nn.softplus(dt_raw + dt_bias)
    log_decay = step * -jnp.exp(a_log)
    ssd_out, final = ssd_scan(xs, b_mat, c_mat, step, log_decay, block_rows)
    return (ssd_out, xs, c_mat, jnp.cumsum(log_decay, axis=0), final)

def post_gate(ssd_out, xs, gate_part, skip_gain, gated_gain):
    row_count = xs.shape[0]
    skipped = (xs.reshape(row_count, HEADS, HEAD_DIM) * skip_gain[None, :, None]).reshape(row_count, DI)
    mixed_in = (ssd_out + skipped) * jax.nn.silu(gate_part)
    scale_rms = lax.rsqrt(lax.optimization_barrier(jnp.mean(mixed_in * mixed_in, axis=-1, keepdims=True)) + EPS)
    return mixed_in * scale_rms * gated_gain

def mixer(projected, conv_weight, conv_bias, dt_bias, a_log, skip_gain, gated_gain):
    gate_part = projected[:, :DI]
    xbc = projected[:, DI:DI + XBC]
    dt_raw = projected[:, DI + XBC:]
    edge = jnp.zeros((CONV - 1, XBC), jnp.float32)
    block_rows = SPAN if TOK_DEV % SPAN == 0 else TOK_DEV
    ssd_out, xs, c_mat, cumulative, final = mid_local(xbc, dt_raw, edge, conv_weight, conv_bias, dt_bias, a_log, block_rows)
    return post_gate(ssd_out, xs, gate_part, skip_gain, gated_gain)

def rounded(value):
    return lax.optimization_barrier(value.astype(jnp.bfloat16)).astype(jnp.float32)

def block_grads(normed, projected_cot, cot_rows, gated):
    pieces = (normed.reshape(N_SEQ, TOK_DEV, D), projected_cot.reshape(N_SEQ, TOK_DEV, PROJ), cot_rows.reshape(N_SEQ, TOK_DEV, D), gated.reshape(N_SEQ, TOK_DEV, DI))

    def add_block(totals, piece):
        in_term = jnp.dot(piece[0].T, piece[1], preferred_element_type=jnp.float32)
        out_term = jnp.dot(piece[2].T, piece[3], preferred_element_type=jnp.float32)
        return ((totals[0] + rounded(in_term), totals[1] + rounded(out_term)), None)
    start = (jnp.zeros((D, PROJ), jnp.float32), jnp.zeros((D, DI), jnp.float32))
    totals, unused = lax.scan(add_block, start, pieces)
    return totals

def reference(inputs, norm_gain, in_proj, conv_weight, conv_bias, dt_bias, a_log, skip_gain, gated_gain, out_proj, cotangent):

    def one_sequence(totals, pieces):
        tokens, cot_rows = pieces
        residual_in = tokens.astype(jnp.float32)
        normed_full, norm_back = jax.vjp(pre_norm, residual_in, norm_gain)
        normed = normed_full.astype(jnp.bfloat16)
        projected = jnp.dot(normed, in_proj, preferred_element_type=jnp.float32)
        gated_full, mixer_back = jax.vjp(mixer, projected, conv_weight, conv_bias, dt_bias, a_log, skip_gain, gated_gain)
        gated = gated_full.astype(jnp.bfloat16)
        mixed = jnp.dot(gated, out_proj.T, preferred_element_type=jnp.float32)
        layer_out = (residual_in + mixed).astype(jnp.bfloat16)
        gated_cot = jnp.dot(cot_rows, out_proj, preferred_element_type=jnp.float32)
        grads = mixer_back(gated_cot)
        projected_cot = grads[0].astype(jnp.bfloat16)
        in_grad, out_grad = block_grads(normed, projected_cot, cot_rows, gated)
        normed_cot = jnp.dot(projected_cot, in_proj.T, preferred_element_type=jnp.float32)
        input_part, gain_grad = norm_back(normed_cot)
        input_grad = cot_rows.astype(jnp.float32) + input_part
        updates = (in_grad, out_grad, gain_grad) + tuple(grads[1:])
        totals = tuple((earlier + later for earlier, later in zip(totals, updates)))
        return (totals, (layer_out, input_grad))
    start = (jnp.zeros((D, PROJ), jnp.float32), jnp.zeros((D, DI), jnp.float32), jnp.zeros((D,), jnp.float32), jnp.zeros((XBC, CONV), jnp.float32), jnp.zeros((XBC,), jnp.float32), jnp.zeros((HEADS,), jnp.float32), jnp.zeros((HEADS,), jnp.float32), jnp.zeros((HEADS,), jnp.float32), jnp.zeros((DI,), jnp.float32))
    sequences = (inputs.reshape(N_DP, LENGTH, D), cotangent.reshape(N_DP, LENGTH, D))
    totals, stacked = lax.scan(one_sequence, start, sequences)
    return (stacked[0].reshape(TOKENS, D), stacked[1].reshape(TOKENS, D), totals[0], totals[1], totals[2], totals[3], totals[4], totals[5], totals[6], totals[7], totals[8])
```

```python
from functools import partial

import jax
import jax.numpy as jnp
from jax import lax
from jax.experimental import pallas as pl
from jax.experimental.pallas import tpu as pltpu
from jax.sharding import PartitionSpec as P

HEADS = 24
HEAD_DIM = 64
STATE = 128
CONV = 4
DI = 1536
XBC = 1792
PROJ = DI + XBC + HEADS
LANES = 128
WIDE = -(-PROJ // LANES) * LANES


EPS = 1e-05
HIGH = lax.Precision.HIGHEST
MESH = pl.DeviceIdType.MESH
VMEM_BYTES = 60 * 1024 * 1024


def bits_of(count):
    return count.bit_length() - 1


def bit_at(place, bit):
    return (place // 2**bit) % 2


def places():
    return lax.axis_index("dp"), lax.axis_index("seq")


def partner(bit, seq_bits):
    dp_at, seq_at = places()
    if bit < seq_bits:
        return dp_at, seq_at + (1 - 2 * bit_at(seq_at, bit)) * 2**bit
    up = bit - seq_bits
    return dp_at + (1 - 2 * bit_at(dp_at, up)) * 2**up, seq_at


def greet(bits, seq_bits):
    barrier = pltpu.get_barrier_semaphore()
    for bit in range(bits):
        pl.semaphore_signal(barrier, inc=1, device_id=partner(bit, seq_bits), device_id_type=MESH)
    pl.semaphore_wait(barrier, bits)


def gather_orders(seq_bits, dp_bits):
    x_count = seq_bits // 2
    x_bits = list(range(x_count))
    z_bits = list(range(x_count, seq_bits))[::-1]
    core = [seq_bits]
    y_bits = [seq_bits + 1 + i for i in range(dp_bits - 1)]
    return (
        z_bits + x_bits + y_bits + core,
        z_bits + y_bits + x_bits + core,
        z_bits[:1] + x_bits + y_bits + z_bits[1:] + core,
        z_bits[:1] + y_bits + x_bits + z_bits[1:] + core,
    )


SHARES = (0.3, 0.3, 0.2, 0.2)


def split_lanes(width, shares):
    tiles = width // LANES
    edges = [round(tiles * sum(shares[:i])) * LANES for i in range(len(shares) + 1)]
    return [(low, high - low) for low, high in zip(edges, edges[1:])]


def gather_kernel(seq_bits, streams, bits, *refs):
    array_count = 1 + max(stream[0] for stream in streams)
    shards, outs = refs[:array_count], refs[array_count : 2 * array_count]
    send_sem, recv_sem, own_sem = refs[2 * array_count :]
    dp_at, seq_at = places()
    place = dp_at * 2**seq_bits + seq_at
    own = [
        pltpu.make_async_copy(shard, out.at[place], own_sem.at[i])
        for i, (shard, out) in enumerate(zip(shards, outs))
    ]
    for copy in own:
        copy.start()
    greet(bits, seq_bits)
    for copy in own:
        copy.wait()

    def landed(stream, stage, sem):
        which, low, width, _ = streams[stream]
        view = outs[which].at[pl.ds(0, 2**stage), :, pl.ds(low, width)]
        pltpu.make_async_copy(view, view, sem.at[stream, stage]).wait()

    for stage in range(bits + 1):
        for stream, (which, low, width, order) in enumerate(streams):
            if stage > 0:
                landed(stream, stage - 1, recv_sem)
            if stage == bits:
                continue
            free = order[:stage]
            run = 0
            while run in free:
                run += 1
            base = place
            for bit in free:
                base = base - bit_at(place, bit) * 2**bit
            upper = [bit for bit in free if bit > run]
            for combo in range(2 ** len(upper)):
                start = base + sum(2**bit for i, bit in enumerate(upper) if combo >> i & 1)
                view = outs[which].at[pl.ds(start, 2**run), :, pl.ds(low, width)]
                pltpu.make_async_remote_copy(
                    src_ref=view,
                    dst_ref=view,
                    send_sem=send_sem.at[stream, stage],
                    recv_sem=recv_sem.at[stream, stage],
                    device_id=partner(order[stage], seq_bits),
                    device_id_type=MESH,
                ).start()
    for stage in range(bits):
        for stream in range(len(streams)):
            landed(stream, stage, send_sem)


def gather_all(shards, collective_id):
    seq_bits, dp_bits = bits_of(lax.axis_size("seq")), bits_of(lax.axis_size("dp"))
    bits = seq_bits + dp_bits
    orders = gather_orders(seq_bits, dp_bits)
    streams = [
        (which, low, width, order)
        for which, shard in enumerate(shards)
        for (low, width), order in zip(split_lanes(shard.shape[1], SHARES), orders)
    ]
    return pl.pallas_call(
        partial(gather_kernel, seq_bits, streams, bits),
        out_shape=[jax.ShapeDtypeStruct((2**bits, *a.shape), a.dtype) for a in shards],
        in_specs=[pl.BlockSpec(memory_space=pltpu.VMEM)] * len(shards),
        out_specs=[pl.BlockSpec(memory_space=pl.ANY)] * len(shards),
        scratch_shapes=[
            pltpu.SemaphoreType.DMA((len(streams), bits)),
            pltpu.SemaphoreType.DMA((len(streams), bits)),
            pltpu.SemaphoreType.DMA((len(shards),)),
        ],
        compiler_params=pltpu.CompilerParams(
            collective_id=collective_id, has_side_effects=True, vmem_limit_bytes=VMEM_BYTES
        ),
        name="gather_rows",
    )(*shards)


def sum_kernel(seq_bits, streams, bits, array_count, *refs):
    terms, vector = refs[:array_count], refs[array_count]
    outs, vector_out = refs[array_count + 1 : 2 * array_count + 1], refs[2 * array_count + 1]
    held = refs[2 * array_count + 2 : 2 * array_count + 2 + len(streams) * bits]
    rest = refs[2 * array_count + 2 + len(streams) * bits :]
    vector_in, vector_sum, send_sem, recv_sem, vector_send, vector_recv = rest
    dp_at, seq_at = places()
    place = dp_at * 2**seq_bits + seq_at
    greet(bits, seq_bits)

    def source(stream, stage):
        which, low, width, _ = streams[stream]
        if stage == 0:
            return terms[which], pl.ds(low, width)
        return held[stream * bits + stage - 1], pl.ds(0, width)

    def position(stream, stage):
        order = streams[stream][3]
        remaining = sorted(order[stage:])
        return remaining.index(order[stage]), bit_at(place, order[stage])

    def landed(stream, stage, sem):
        view = held[stream * bits + stage]
        pltpu.make_async_copy(view, view, sem.at[stream, stage]).wait()

    def vector_copy(stage):
        return pltpu.make_async_remote_copy(
            src_ref=vector if stage == 0 else vector_sum.at[stage - 1],
            dst_ref=vector_in.at[stage],
            send_sem=vector_send.at[stage],
            recv_sem=vector_recv.at[stage],
            device_id=partner(stage, seq_bits),
            device_id_type=MESH,
        )

    for stage in range(bits + 1):
        if stage > 0:
            vector_copy(stage - 1).wait_recv()
            before = vector[...] if stage == 1 else vector_sum[stage - 2]
            total = before + vector_in[stage - 1]
            if stage < bits:
                vector_sum[stage - 1] = total
            else:
                vector_out[...] = total
        if stage < bits:
            vector_copy(stage).start()
        for stream, (which, low, width, order) in enumerate(streams):
            if stage > 0:
                landed(stream, stage - 1, recv_sem)
                spot, mine = position(stream, stage - 1)
                kept, lanes = source(stream, stage - 1)
                came = held[stream * bits + stage - 1]
                if stage == bits:
                    outs[which][:, pl.ds(low, width)] = kept[mine, :, lanes].astype(
                        jnp.float32
                    ) + came[0].astype(jnp.float32)
                    continue

                def add_one(block, carry, spot=spot, mine=mine, kept=kept, lanes=lanes, came=came):
                    from_block = (block // 2**spot) * 2 ** (spot + 1) + mine * 2**spot
                    from_block = from_block + block % 2**spot
                    added = kept[from_block, :, lanes].astype(jnp.float32) + came[block].astype(
                        jnp.float32
                    )
                    came[block] = added.astype(came.dtype)
                    return carry

                lax.fori_loop(0, 2 ** (bits - stage), add_one, 0)
            spot, mine = position(stream, stage)
            sent, lanes = source(stream, stage)
            for high in range(2 ** (bits - stage - 1 - spot)):
                start = high * 2 ** (spot + 1) + (1 - mine) * 2**spot
                pltpu.make_async_remote_copy(
                    src_ref=sent.at[pl.ds(start, 2**spot), :, lanes],
                    dst_ref=held[stream * bits + stage].at[pl.ds(high * 2**spot, 2**spot)],
                    send_sem=send_sem.at[stream, stage],
                    recv_sem=recv_sem.at[stream, stage],
                    device_id=partner(order[stage], seq_bits),
                    device_id_type=MESH,
                ).start()
    for stage in range(bits):
        vector_copy(stage).wait_send()
        for stream in range(len(streams)):
            landed(stream, stage, send_sem)


def sum_to_owners(terms, vector, collective_id):
    seq_bits, dp_bits = bits_of(lax.axis_size("seq")), bits_of(lax.axis_size("dp"))
    bits = seq_bits + dp_bits
    orders = [order[::-1] for order in gather_orders(seq_bits, dp_bits)]
    terms = [term.reshape(2**bits, -1, term.shape[1]) for term in terms]
    streams = [
        (which, low, width, order)
        for which, term in enumerate(terms)
        for (low, width), order in zip(split_lanes(term.shape[2], SHARES), orders)
    ]
    rows = terms[0].shape[1]
    in_vmem = pl.BlockSpec(memory_space=pltpu.VMEM)
    held = [
        pltpu.VMEM((2 ** (bits - 1 - stage), rows, width), jnp.bfloat16)
        for _, _, width, _ in streams
        for stage in range(bits)
    ]
    return pl.pallas_call(
        partial(sum_kernel, seq_bits, streams, bits, len(terms)),
        out_shape=[jax.ShapeDtypeStruct(a.shape[1:], jnp.float32) for a in terms]
        + [jax.ShapeDtypeStruct(vector.shape, vector.dtype)],
        in_specs=[in_vmem] * (len(terms) + 1),
        out_specs=[in_vmem] * (len(terms) + 1),
        scratch_shapes=held
        + [
            pltpu.VMEM((bits, *vector.shape), jnp.float32),
            pltpu.VMEM((bits, *vector.shape), jnp.float32),
            pltpu.SemaphoreType.DMA((len(streams), bits)),
            pltpu.SemaphoreType.DMA((len(streams), bits)),
            pltpu.SemaphoreType.DMA((bits,)),
            pltpu.SemaphoreType.DMA((bits,)),
        ],
        compiler_params=pltpu.CompilerParams(
            collective_id=collective_id, has_side_effects=True, vmem_limit_bytes=VMEM_BYTES
        ),
        name="sum_rows",
    )(*terms, vector)


GROUP = 4
GROUP_LANES = GROUP * HEAD_DIM


def inner_product(left, right, dims):
    return lax.dot_general(
        left, right, (dims, ((), ())), precision=HIGH, preferred_element_type=jnp.float32
    )


def group_lanes(group):
    return pl.ds(pl.multiple_of(group * GROUP_LANES, GROUP_LANES), GROUP_LANES)


def head_weights(cumulative, head):
    row = cumulative[pl.ds(head, 1), :]
    count = row.shape[1]
    spread = jnp.broadcast_to(row, (count, count))
    later = lax.broadcasted_iota(jnp.int32, (count, count), 0)
    earlier = lax.broadcasted_iota(jnp.int32, (count, count), 1)
    return jnp.exp(jnp.where(later >= earlier, spread.T - spread, -jnp.inf))


def inside_work(first, last, scaled_x, b_mat, c_mat, cumulative, output, crossed):
    if first == 0:
        crossed[...] = inner_product(c_mat[...], b_mat[...], ((1,), (1,)))

    def one(group, carry):
        values = scaled_x[:, group_lanes(group)]
        parts = []
        for i in range(GROUP):
            scores = head_weights(cumulative, group * GROUP + i) * crossed[...]
            head = values[:, i * HEAD_DIM : (i + 1) * HEAD_DIM]
            parts.append(inner_product(scores, head, ((1,), (0,))))
        output[:, group_lanes(group)] = jnp.concatenate(parts, axis=1)
        return carry

    lax.fori_loop(first, last, one, 0)


def inside_back(
    first,
    last,
    output_cot,
    scaled_x,
    b_mat,
    c_mat,
    cumulative,
    scaled_cot,
    b_cot,
    c_cot,
    cumulative_cot,
    crossed,
    crossed_cot,
):
    if first == 0:
        crossed[...] = inner_product(c_mat[...], b_mat[...], ((1,), (1,)))
        crossed_cot[...] = jnp.zeros_like(crossed_cot)

    def one(group, carry):
        values = scaled_x[:, group_lanes(group)]
        cots = output_cot[:, group_lanes(group)]
        parts = []
        total = crossed_cot[...]
        for i in range(GROUP):
            weights = head_weights(cumulative, group * GROUP + i)
            scores = weights * crossed[...]
            head = values[:, i * HEAD_DIM : (i + 1) * HEAD_DIM]
            cot = cots[:, i * HEAD_DIM : (i + 1) * HEAD_DIM]
            weighted = weights * inner_product(cot, head, ((1,), (1,)))
            total = total + weighted
            parts.append(inner_product(scores, cot, ((0,), (0,))))
            moved = weighted * crossed[...]
            cumulative_cot[pl.ds(group * GROUP + i, 1), :] = jnp.sum(
                moved.T, axis=0, keepdims=True
            ) - jnp.sum(moved, axis=0, keepdims=True)
        crossed_cot[...] = total
        scaled_cot[:, group_lanes(group)] = jnp.concatenate(parts, axis=1)
        return carry

    lax.fori_loop(first, last, one, 0)
    if last == HEADS // GROUP:
        b_cot[...] = inner_product(crossed_cot[...], c_mat[...], ((0,), (0,)))
        c_cot[...] = inner_product(crossed_cot[...], b_mat[...], ((1,), (0,)))


def scan_kernel(count, reverse, work, inputs, outputs, *refs):
    state, decay = refs[:2]
    given = refs[2 : 2 + inputs]
    out = refs[2 + inputs]
    made = refs[3 + inputs : 3 + inputs + outputs]
    came, came_decay, ready = refs[3 + inputs + outputs : 6 + inputs + outputs]
    sems = refs[6 + inputs + outputs : 12 + inputs + outputs]
    held = refs[12 + inputs + outputs :]
    out_send, out_recv, decay_send, decay_recv, back_send, back_recv = sems
    dp_at, seq_at = places()
    barrier = pltpu.get_barrier_semaphore()
    peers = [(seq_at + hop) % count for hop in range(1, count)]
    for peer in peers:
        pl.semaphore_signal(barrier, inc=1, device_id=(dp_at, peer), device_id_type=MESH)
    pl.semaphore_wait(barrier, count - 1)

    def copy(hop, which):
        target = (seq_at + hop) % count
        source, landing, send_sem, recv_sem = (
            (state.at[target], came.at[seq_at], out_send, out_recv),
            (decay, came_decay.at[seq_at], decay_send, decay_recv),
            (ready.at[target], out.at[seq_at], back_send, back_recv),
        )[which]
        return pltpu.make_async_remote_copy(
            src_ref=source,
            dst_ref=landing,
            send_sem=send_sem.at[hop],
            recv_sem=recv_sem.at[hop],
            device_id=(dp_at, target),
            device_id_type=MESH,
        )

    for hop in range(1, count):
        copy(hop, 0).start()
        copy(hop, 1).start()
    came[seq_at] = state[seq_at]
    came_decay[seq_at] = decay[...]
    groups = HEADS // GROUP
    work(0, groups // 2, *given, *made, *held)
    for hop in range(1, count):
        copy(hop, 0).wait_recv()
        copy(hop, 1).wait_recv()
    total = jnp.zeros(state.shape[1:], jnp.float32)
    for place in range(count)[:: -1 if reverse else 1]:
        ready[place] = total.astype(ready.dtype)
        total = came_decay[place] * total + came[place].astype(jnp.float32)
    for hop in range(1, count):
        copy(hop, 2).start()
    out[seq_at] = ready[seq_at]
    work(groups // 2, groups, *given, *made, *held)
    for hop in range(1, count):
        copy(hop, 2).wait_recv()
    for hop in range(1, count):
        for which in range(3):
            copy(hop, which).wait_send()


def scan_states(state, decay, work, given, made, held, reverse, collective_id):
    count = lax.axis_size("seq")
    state = state.astype(jnp.bfloat16).reshape(count, STATE // count, DI)
    in_vmem = pl.BlockSpec(memory_space=pltpu.VMEM)
    got = pl.pallas_call(
        partial(scan_kernel, count, reverse, work, len(given), len(made)),
        out_shape=[jax.ShapeDtypeStruct(state.shape, state.dtype)]
        + [jax.ShapeDtypeStruct(shape, jnp.float32) for shape in made],
        in_specs=[in_vmem] * (2 + len(given)),
        out_specs=[in_vmem] * (1 + len(made)),
        scratch_shapes=[
            pltpu.VMEM(state.shape, state.dtype),
            pltpu.VMEM((count, 1, DI), jnp.float32),
            pltpu.VMEM(state.shape, state.dtype),
        ]
        + [pltpu.SemaphoreType.DMA((count,))] * 6
        + [pltpu.VMEM(shape, jnp.float32) for shape in held],
        compiler_params=pltpu.CompilerParams(
            collective_id=collective_id, has_side_effects=True, vmem_limit_bytes=VMEM_BYTES
        ),
        name="scan_back" if reverse else "scan_states",
    )(state, decay[None, :], *given)
    return got[0].reshape(STATE, DI).astype(jnp.float32), *got[1:]


def passed_along(value, axis, steps):
    count = lax.axis_size(axis)
    first, last = (max(0, -steps), min(count, count - steps))
    return lax.ppermute(value, axis, [(source, source + steps) for source in range(first, last)])


def pre_norm(residual_in, norm_gain):
    scale_rms = lax.rsqrt(jnp.mean(residual_in * residual_in, axis=-1, keepdims=True) + EPS)
    return residual_in * scale_rms * norm_gain


def conv_silu(padded, conv_weight, conv_bias, row_count):
    total = jnp.zeros((row_count, padded.shape[1]), jnp.float32) + conv_bias[None, :]
    for offset in range(conv_weight.shape[1]):
        total = total + conv_weight[:, offset][None, :] * padded[offset : offset + row_count]
    return jax.nn.silu(total)


def head_lanes():
    lanes = jnp.arange(DI, dtype=jnp.int32) // HEAD_DIM
    return (jnp.arange(HEADS, dtype=jnp.int32)[:, None] == lanes[None, :]).astype(jnp.float32)


def spread_heads(by_head):
    return jnp.dot(by_head, head_lanes(), precision=HIGH)


def sum_heads(by_lane):
    return jnp.dot(by_lane, head_lanes().T, precision=HIGH)


def before_states(xbc, dt_raw, edge, conv_weight, conv_bias, dt_bias, a_log):
    row_count = xbc.shape[0]
    activated = conv_silu(jnp.concatenate([edge, xbc], axis=0), conv_weight, conv_bias, row_count)
    xs = activated[:, :DI]
    b_mat = activated[:, DI : DI + STATE]
    c_mat = activated[:, DI + STATE :]
    step = jax.nn.softplus(dt_raw + dt_bias)
    log_decay = step * -jnp.exp(a_log)
    at = jnp.arange(row_count)
    lower = (at[:, None] >= at[None, :]).astype(jnp.float32)
    cumulative = jnp.dot(lower, log_decay, precision=HIGH)
    scaled_x = xs * spread_heads(step)
    tail = jnp.exp(cumulative[-1][None, :] - cumulative)
    fresh = jnp.dot(b_mat.T, scaled_x * spread_heads(tail), precision=HIGH)
    return (xs, scaled_x, b_mat, c_mat, cumulative, fresh)


def post_gate(ssd_out, xs, gate_part, skip_gain, gated_gain):
    skipped = xs * spread_heads(skip_gain[None, :])
    mixed_in = (ssd_out + skipped) * jax.nn.silu(gate_part)
    scale_rms = lax.rsqrt(jnp.mean(mixed_in * mixed_in, axis=-1, keepdims=True) + EPS)
    return mixed_in * scale_rms * gated_gain


def contract_rows(left, right):
    return lax.dot_general(
        left, right, (((0,), (0,)), ((), ())), preferred_element_type=jnp.float32
    )


def contract_cols(left, right):
    return lax.dot_general(
        left, right, (((1,), (1,)), ((), ())), preferred_element_type=jnp.float32
    )


def body(
    inputs,
    norm_gain,
    in_proj,
    conv_weight,
    conv_bias,
    dt_bias,
    a_log,
    skip_gain,
    gated_gain,
    out_proj,
    cotangent,
):
    row_count = inputs.shape[0]
    residual_in = inputs.astype(jnp.float32)
    normed_full, norm_back = jax.vjp(pre_norm, residual_in, norm_gain)
    normed = normed_full.astype(jnp.bfloat16)
    in_whole, out_whole = gather_all(
        [jnp.pad(in_proj, ((0, 0), (0, WIDE - PROJ))), out_proj], collective_id=1
    )
    in_whole = in_whole.reshape(-1, WIDE)
    out_whole = out_whole.reshape(-1, DI)
    projected = jnp.dot(normed, in_whole, preferred_element_type=jnp.float32)
    gate_part = projected[:, :DI]
    xbc = projected[:, DI : DI + XBC]
    dt_raw = projected[:, DI + XBC : PROJ]
    edge = passed_along(xbc[row_count - (CONV - 1) :], "seq", 1)
    primal, mid_back = jax.vjp(
        before_states, xbc, dt_raw, edge, conv_weight, conv_bias, dt_bias, a_log
    )
    xs, scaled_x, b_mat, c_mat, cumulative, s_local = primal
    by_head = cumulative.T
    decay = jnp.exp(cumulative[-1])
    wide_decay = spread_heads(decay[None, :])[0]
    square = (row_count, row_count)
    state_in, local_out = scan_states(
        s_local,
        wide_decay,
        inside_work,
        [scaled_x, b_mat, c_mat, by_head],
        [xs.shape],
        [square],
        False,
        collective_id=2,
    )
    weighted = spread_heads(jnp.exp(cumulative))
    carried_part = jnp.dot(c_mat, state_in, precision=HIGH) * weighted
    ssd_out = local_out + carried_part
    gated_full, post_back = jax.vjp(post_gate, ssd_out, xs, gate_part, skip_gain, gated_gain)
    gated = gated_full.astype(jnp.bfloat16)
    mixed = contract_cols(gated, out_whole)
    layer_out = (residual_in + mixed).astype(jnp.bfloat16)
    gated_cot = jnp.dot(cotangent, out_whole, preferred_element_type=jnp.float32)
    ssd_cot, xs_cot, gate_cot, skip_grad, gated_gain_grad = post_back(gated_cot)
    scaled_cot = ssd_cot * weighted
    local_grad = jnp.dot(c_mat.T, scaled_cot, precision=HIGH)
    later_grad, scaled_x_cot, b_cot, inner_c_cot, by_head_cot = scan_states(
        local_grad,
        wide_decay,
        inside_back,
        [ssd_cot, scaled_x, b_mat, c_mat, by_head],
        [xs.shape, b_mat.shape, c_mat.shape, by_head.shape],
        [square, square],
        True,
        collective_id=3,
    )
    c_cot = lax.dot_general(scaled_cot, state_in, (((1,), (1,)), ((), ())), precision=HIGH)
    cum_cot = sum_heads(ssd_cot * carried_part)
    last_cot = sum_heads(jnp.sum(later_grad * state_in, axis=0, keepdims=True))[0] * decay
    is_last = (jnp.arange(row_count) == row_count - 1)[:, None]
    cum_cot = cum_cot + jnp.where(is_last, last_cot[None, :], 0.0)
    mid_grads = mid_back(
        (xs_cot, scaled_x_cot, b_cot, c_cot + inner_c_cot, cum_cot + by_head_cot.T, later_grad)
    )
    xbc_cot, dt_cot, edge_cot, conv_weight_grad, conv_bias_grad, dt_bias_grad, a_log_grad = (
        mid_grads
    )
    edge_back = passed_along(edge_cot, "seq", -1)
    xbc_cot = xbc_cot + jnp.pad(edge_back, ((row_count - (CONV - 1), 0), (0, 0)))
    projected_cot = jnp.concatenate(
        [gate_cot, xbc_cot, dt_cot, jnp.zeros((row_count, WIDE - PROJ), jnp.float32)], axis=1
    ).astype(jnp.bfloat16)
    in_term = contract_rows(normed, projected_cot).astype(jnp.bfloat16)
    out_term = contract_rows(cotangent, gated).astype(jnp.bfloat16)
    normed_cot = contract_cols(projected_cot, in_whole)
    input_part, norm_gain_grad = norm_back(normed_cot)
    input_grad = cotangent.astype(jnp.float32) + input_part
    small = (
        norm_gain_grad,
        conv_weight_grad.T,
        conv_bias_grad,
        gated_gain_grad,
        dt_bias_grad,
        a_log_grad,
        skip_grad,
    )
    flat = jnp.concatenate([a.reshape(-1) for a in small])
    tile = 8 * LANES
    flat = jnp.pad(flat, (0, -flat.shape[0] % tile))
    in_proj_grad, out_proj_grad, summed = sum_to_owners(
        [in_term, out_term], flat.reshape(-1, LANES), collective_id=4
    )
    summed = summed.reshape(-1)
    parts, at = [], 0
    for a in small:
        parts.append(summed[at : at + a.size].reshape(a.shape))
        at += a.size
    return (
        layer_out,
        input_grad,
        in_proj_grad[:, :PROJ],
        out_proj_grad,
        parts[0],
        parts[1].T,
        parts[2],
        parts[4],
        parts[5],
        parts[6],
        parts[3],
    )


QUAD = 4
CHUNK = 128
TAIL = 16
QCH = DI // QUAD
QHEADS = HEADS // QUAD
PAIRS = QCH // LANES
BC = 2 * STATE
QXBC = QCH + BC
SLAB = QXBC + LANES
GRAD_ROWS = 16


def flip(value, bit):
    return value + (1 - 2 * bit_at(value, bit)) * 2**bit


def flip_quad(value, mask):
    for bit in range(2):
        if mask >> bit & 1:
            value = flip(value, bit)
    return value


def dot_nn(left, right):
    return lax.dot_general(
        left, right, (((1,), (0,)), ((), ())), preferred_element_type=jnp.float32
    )


def dot_nt(left, right):
    return lax.dot_general(
        left, right, (((1,), (1,)), ((), ())), preferred_element_type=jnp.float32
    )


def dot_tn(left, right):
    return lax.dot_general(
        left, right, (((0,), (0,)), ((), ())), preferred_element_type=jnp.float32
    )


def in_parts(value, count):
    parts = []
    for _ in range(count):
        part = value.astype(jnp.bfloat16)
        parts.append(part)
        value = value - part.astype(jnp.float32)
    return parts


def lane_tile(i):
    return pl.ds(i * LANES, LANES)


def chunk_rows(c, offset=0, count=CHUNK):
    return pl.ds(pl.multiple_of(c * CHUNK + offset, 8), count)


def column_sum(value):
    return jnp.sum(value, axis=0, keepdims=True)


def block_kernel(
    x_ref,
    cot_ref,
    early_ref,
    late_ref,
    par_ref,
    out_ref,
    grad_ref,
    early_grad_ref,
    late_grad_ref,
    small_ref,
    xq,
    cq,
    xtail,
    early_slots,
    late_slots,
    early_w,
    late_w,
    xn,
    proj,
    act,
    act_slope,
    step_s,
    step_slope,
    log_s,
    cum_s,
    sx_s,
    fresh_s,
    state_out,
    state_come,
    state_s,
    weights_s,
    scores_s,
    ssd_s,
    gate_s,
    gc_s,
    m_s,
    sums_s,
    gated_s,
    gate_cot_s,
    y_s,
    z_s,
    back_s,
    later_s,
    cross_s,
    sx_cot_s,
    pre_cot_s,
    early_cot_s,
    late_term,
    early_term,
    mixed_s,
    mixed_come,
    normed_cot_s,
    normed_out,
    normed_come,
    tail_out,
    tail_come,
    small_s,
    small_come,
    small_quad,
    *rest,
):
    stream_held = [rest[4 * i : 4 * i + 4] for i in range(3)]
    send_sem, recv_sem = rest[12:]
    f32, bf16 = jnp.float32, jnp.bfloat16
    dp_at, seq_at = places()
    q, g = seq_at % QUAD, seq_at // QUAD
    core, y_at = dp_at % 2, dp_at // 2
    place = dp_at * 8 + seq_at
    used = [0]
    sent = []

    barrier = pltpu.get_barrier_semaphore()
    peers = [(dp_at, (seq_at + hop) % 8) for hop in range(1, 8)]
    peers += [(flip(dp_at, 0), seq_at), (flip(dp_at, 1), seq_at)]
    for peer in peers:
        pl.semaphore_signal(barrier, inc=1, device_id=peer, device_id_type=MESH)

    def remote(source, landing, target, own=True):
        at = used[0]
        used[0] += 1
        copy = pltpu.make_async_remote_copy(
            src_ref=source,
            dst_ref=landing,
            send_sem=send_sem.at[at],
            recv_sem=recv_sem.at[at],
            device_id=target,
            device_id_type=MESH,
        )
        if own:
            copy.start()
            sent.append(copy)
        return copy

    def in_quad(mask):
        return dp_at, flip_quad(seq_at, mask)

    far = (dp_at, flip(seq_at, 2))
    beside = (flip(dp_at, 1), seq_at)
    twin = (flip(dp_at, 0), seq_at)

    def arrived(copies):
        for copy in copies:
            copy.wait_recv()

    lane = lax.broadcasted_iota(jnp.int32, (1, LANES), 1)
    first_half = lane < HEAD_DIM
    half0 = jnp.where(first_half, 1.0, 0.0)
    half1 = 1.0 - half0
    half0b, half1b = half0.astype(bf16), half1.astype(bf16)
    row_at = lax.broadcasted_iota(jnp.int32, (CHUNK, CHUNK), 0)
    lane_at = lax.broadcasted_iota(jnp.int32, (CHUNK, CHUNK), 1)
    causal = row_at >= lane_at
    lower = jnp.where(causal, 1.0, 0.0).astype(bf16)
    upper = jnp.where(row_at <= lane_at, 1.0, 0.0).astype(bf16)
    lower3 = jnp.concatenate([lower] * 3, axis=1)
    upper3 = jnp.concatenate([upper] * 3, axis=1)

    def spread(by_head, i):
        return jnp.where(first_half, by_head[:, 2 * i : 2 * i + 1], by_head[:, 2 * i + 1 : 2 * i + 2])

    def head_sum(value, i):
        owner = 2 * i + row_at // HEAD_DIM
        pick = jnp.where(owner == lane_at, 1.0, 0.0).astype(bf16)
        return dot_nn(
            jnp.concatenate(in_parts(value, 2), axis=1), jnp.concatenate([pick] * 2, axis=0)
        )

    def par(row, lanes):
        return par_ref[q, pl.ds(row, 1), lanes]

    def stacked(value):
        return jnp.concatenate([value * half0b, value * half1b], axis=0)

    pl.semaphore_wait(barrier, len(peers))

    token_copies = [remote(x_ref, xq.at[q], in_quad(mask)) for mask in (1, 2, 3)]

    def scatter(shard, slots):
        return [
            remote(shard.at[flip_quad(q, mask)], slots.at[place], in_quad(mask))
            for mask in (1, 2, 3)
        ]

    early_0 = scatter(early_ref, early_slots)
    late_0 = scatter(late_ref, late_slots)
    cot_copies = [remote(cot_ref, cq.at[q], in_quad(mask)) for mask in (1, 2, 3)]
    tail_sends = [
        remote(x_ref.at[pl.ds(CHUNK - TAIL, TAIL)], xtail, (dp_at, QUAD + i), own=False)
        for i in range(QUAD)
    ]
    at_end = seq_at == QUAD - 1

    @pl.when(at_end)
    def _():
        for copy in tail_sends:
            copy.start()

    early_slots[place] = early_ref[q]
    late_slots[place] = late_ref[q]
    xq[q] = x_ref[...]
    cq[q] = cot_ref[...]

    def cross_far(slots):
        return [
            remote(
                slots.at[pl.ds(dp_at * 8 + g * 4, 4), :, lane_part],
                slots.at[pl.ds(dp_at * 8 + g * 4, 4), :, lane_part],
                far,
            )
            for lane_part in (pl.ds(0, SLAB // 2), pl.ds(SLAB // 2, SLAB // 2))
        ]

    def cross_beside(slots, copies):
        made = []
        for part, copy in enumerate(copies):
            copy.wait_recv()
            view = slots.at[pl.ds(dp_at * 8, 8), :, pl.ds(part * (SLAB // 2), SLAB // 2)]
            made.append(remote(view, view, beside))
        return made

    def cross_twin(slots, copies):
        made = []
        for part, copy in enumerate(copies):
            copy.wait_recv()
            for up in range(2):
                view = slots.at[
                    pl.ds((2 * up + core) * 8, 8), :, pl.ds(part * (SLAB // 2), SLAB // 2)
                ]
                made.append(remote(view, view, twin))
        return made

    def flatten(slots, flat):
        def one(pair, carry):
            value = slots[pl.ds(2 * pair, 2)].astype(f32).reshape(48, SLAB)
            flat[pl.ds(pl.multiple_of(pair * 48, 16), 48), :] = value.astype(bf16)
            return carry

        lax.fori_loop(0, 16, one, 0)

    arrived(early_0)
    early_1 = cross_far(early_slots)
    arrived(late_0)
    late_1 = cross_far(late_slots)
    early_2 = cross_beside(early_slots, early_1)

    arrived(token_copies)

    for i in range(QUAD):

        @pl.when((g == 1) & (q == i))
        def _():
            tail_sends[i].wait_recv()

    @pl.when(g == 0)
    def _():
        xtail[...] = jnp.zeros_like(xtail)

    gain = par(9, slice(None))

    def scaled_rows(value):
        value = value.astype(f32)
        return value * lax.rsqrt(jnp.mean(value * value, axis=-1, keepdims=True) + EPS)

    xn[pl.ds(0, TAIL), :] = (scaled_rows(xtail[...]) * gain).astype(bf16)

    def norm_block(c, carry):
        xn[pl.ds(pl.multiple_of(c * CHUNK + TAIL, 16), CHUNK), :] = (
            scaled_rows(xq[c]) * gain
        ).astype(bf16)
        return carry

    lax.fori_loop(0, QUAD, norm_block, 0)
    early_3 = cross_twin(early_slots, early_2)
    late_2 = cross_beside(late_slots, late_1)
    small_s[...] = jnp.zeros_like(small_s)
    pre_cot_s[pl.ds(0, TAIL), :] = jnp.zeros((TAIL, QXBC), f32)
    pre_cot_s[pl.ds(TAIL + QUAD * CHUNK, 8), :] = jnp.zeros((8, QXBC), f32)
    arrived(early_3)
    flatten(early_slots, early_w)

    for n in range(3):
        cols = pl.ds(n * 256, 256)
        proj[:, cols] = dot_nn(xn[...], early_w[:, cols])

    rate = -jnp.exp(par(8, lane_tile(0)))
    head_lane = lane < QHEADS

    def forward_states(c, carry):
        rows = chunk_rows(c)
        for i in range(QXBC // LANES):
            lanes = lane_tile(i)
            window = proj[chunk_rows(c, 8, CHUNK + 8), lanes]
            total = par(4, lanes)
            for k in range(CONV):
                total = total + par(k, lanes) * pltpu.roll(window, CHUNK + 3 - k, 0)[:CHUNK]
            sig = lax.logistic(total)
            act[rows, lanes] = total * sig
            act_slope[rows, lanes] = sig * (1.0 + total * (1.0 - sig))
        raw = proj[chunk_rows(c, TAIL), pl.ds(QXBC, LANES)] + par(7, lane_tile(0))
        step = jnp.maximum(raw, 0.0) + jnp.log1p(jnp.exp(-jnp.abs(raw)))
        step = jnp.where(head_lane, step, 0.0)
        log_decay = step * rate
        cum = dot_nn(lower3, jnp.concatenate(in_parts(log_decay, 3), axis=0))
        step_s[rows, :] = step
        step_slope[rows, :] = lax.logistic(raw)
        log_s[rows, :] = log_decay
        cum_s[rows, :] = cum
        tail = jnp.exp(cum[CHUNK - 1 :] - cum)
        b_mat = act[rows, pl.ds(QCH, STATE)].astype(bf16)
        for i in range(PAIRS):
            lanes = lane_tile(i)
            sx = act[rows, lanes] * spread(step, i)
            sx_s[rows, lanes] = sx.astype(bf16)
            fresh_s[c, i] = dot_tn(b_mat, (sx * spread(tail, i)).astype(bf16))
        return carry

    lax.fori_loop(0, QUAD, forward_states, 0)

    def chunk_decay(c, i):
        last = cum_s[chunk_rows(c, CHUNK - 8, 8), :][7:]
        return spread(jnp.exp(last), i)

    for i in range(PAIRS):
        total = fresh_s[0, i]
        for c in range(1, QUAD):
            total = chunk_decay(c, i) * total + fresh_s[c, i]
        state_out[i] = total.astype(bf16)
    state_copy = remote(state_out, state_come, far)
    late_3 = cross_twin(late_slots, late_2)

    def forward_local(c, carry):
        rows = chunk_rows(c)
        b_mat = act[rows, pl.ds(QCH, STATE)].astype(bf16)
        c_mat = act[rows, pl.ds(QCH + STATE, STATE)].astype(bf16)
        crossed = dot_nt(c_mat, b_mat)
        cum = cum_s[rows, :]
        cum_t = cum.T
        for i in range(PAIRS):
            lanes = lane_tile(i)
            pair = []
            for head in (2 * i, 2 * i + 1):
                gap = cum[:, head : head + 1] - cum_t[head : head + 1, :]
                pair.append(jnp.exp(jnp.where(causal, gap, -1e30)))
            weights_s[c, i] = jnp.concatenate(pair, axis=1).astype(bf16)
            scores = jnp.concatenate([w * crossed for w in pair], axis=1).astype(bf16)
            scores_s[c, i] = scores
            ssd_s[rows, lanes] = dot_nn(scores, stacked(sx_s[rows, lanes]))
        return carry

    lax.fori_loop(0, QUAD, forward_local, 0)
    arrived(late_3)
    flatten(late_slots, late_w)
    gate_w = pl.ds(0, QCH)
    out_w = pl.ds(QCH, QCH)
    gate_s[...] = dot_nn(xn[pl.ds(TAIL, QUAD * CHUNK), :], late_w[:, gate_w])
    arrived(cot_copies)

    def cot_block(c, carry):
        gc_s[chunk_rows(c), :] = dot_nn(cq[c], late_w[:, out_w])
        return carry

    lax.fori_loop(0, QUAD, cot_block, 0)
    state_copy.wait_recv()
    for i in range(PAIRS):
        total = jnp.where(g == 1, state_come[i].astype(f32), 0.0)
        for c in range(QUAD):
            state_s[c, i] = total.astype(bf16)
            if c < QUAD - 1:
                total = chunk_decay(c, i) * total + fresh_s[c, i]

    def forward_gate(c, carry):
        rows = chunk_rows(c)
        c_mat = act[rows, pl.ds(QCH + STATE, STATE)].astype(bf16)
        grown = jnp.exp(cum_s[rows, :])
        square, crossed = 0.0, 0.0
        for i in range(PAIRS):
            lanes = lane_tile(i)
            ssd = ssd_s[rows, lanes] + dot_nn(c_mat, state_s[c, i]) * spread(grown, i)
            ssd_s[rows, lanes] = ssd
            gate = gate_s[rows, lanes]
            m = (ssd + act[rows, lanes] * par(6, lanes)) * gate * lax.logistic(gate)
            m_s[rows, lanes] = m
            square = square + m * m
            crossed = crossed + gc_s[rows, lanes] * par(5, lanes) * m
        square = jnp.sum(square, axis=1, keepdims=True)
        crossed = jnp.sum(crossed, axis=1, keepdims=True)
        both = jnp.where(lane == 0, square, jnp.where(lane == 1, crossed, 0.0))
        sums_s[q, :, pl.ds(pl.multiple_of(c * CHUNK, CHUNK), CHUNK)] = (
            both.T[:8]
        )
        return carry

    lax.fori_loop(0, QUAD, forward_gate, 0)
    arrived([remote(sums_s.at[q], sums_s.at[q], in_quad(mask)) for mask in (1, 2, 3)])

    def backward_states(c, carry):
        rows = chunk_rows(c)
        cols = pl.ds(pl.multiple_of(c * CHUNK, CHUNK), CHUNK)
        sums = sums_s[0, :, cols] + sums_s[1, :, cols] + sums_s[2, :, cols] + sums_s[3, :, cols]
        sums = jnp.concatenate([sums] * (CHUNK // 8), axis=0).T
        scale = lax.rsqrt(sums[:, 0:1] * (1.0 / DI) + EPS)
        pull = scale * scale * scale * (sums[:, 1:2] * (1.0 / DI))
        c_mat = act[rows, pl.ds(QCH + STATE, STATE)].astype(bf16)
        grown = jnp.exp(cum_s[rows, :])
        for i in range(PAIRS):
            lanes = lane_tile(i)
            m, gc, gate = m_s[rows, lanes], gc_s[rows, lanes], gate_s[rows, lanes]
            xs = act[rows, lanes]
            mr = m * scale
            gated_s[rows, lanes] = (mr * par(5, lanes)).astype(bf16)
            small_s[5:6, lanes] += column_sum(gc * mr)
            m_cot = scale * (gc * par(5, lanes)) - m * pull
            sig = lax.logistic(gate)
            mixed = ssd_s[rows, lanes] + xs * par(6, lanes)
            gate_cot_s[rows, lanes] = (
                m_cot * mixed * (sig * (1.0 + gate * (1.0 - sig)))
            ).astype(bf16)
            y = m_cot * gate * sig
            y_s[rows, lanes] = y
            small_s[6:7, lanes] += column_sum(y * xs)
            z = (y * spread(grown, i)).astype(bf16)
            z_s[rows, lanes] = z
            back_s[c, i] = dot_tn(c_mat, z)
        return carry

    lax.fori_loop(0, QUAD, backward_states, 0)
    state_copy.wait_send()
    sent[:] = [copy for copy in sent if copy is not state_copy]
    for i in range(PAIRS):
        total = back_s[QUAD - 1, i]
        for c in range(QUAD - 2, -1, -1):
            total = chunk_decay(c, i) * total + back_s[c, i]
        state_out[i] = total.astype(bf16)
    later_copy = remote(state_out, later_s.at[QUAD], far)

    def term_rows(term, half, value, lanes):
        term[pl.ds(half * 16, 16), :, lanes] = value.reshape(16, 24, value.shape[1]).astype(bf16)

    def late_half(half, carry):
        cols = pl.ds(pl.multiple_of(half * QCH, QCH), QCH)
        term_rows(
            late_term,
            half,
            dot_tn(xn[pl.ds(TAIL, QUAD * CHUNK), cols], gate_cot_s[...]),
            gate_w,
        )
        total = dot_tn(cq[0, :, cols], gated_s[pl.ds(0, CHUNK), :])
        for c in range(1, QUAD):
            total = total + dot_tn(cq[c, :, cols], gated_s[pl.ds(c * CHUNK, CHUNK), :])
        term_rows(late_term, half, total, out_w)
        return carry

    lax.fori_loop(0, 2, late_half, 0)

    streams = [(late_term, pl.ds(0, SLAB))] + [
        (early_term, pl.ds(i * (SLAB // 2), SLAB // 2)) for i in range(2)
    ]

    def reduce_twin(stream):
        term, lanes = streams[stream]
        return [
            remote(
                term.at[pl.ds((2 * up + 1 - core) * 8, 8), :, lanes],
                stream_held[stream][0].at[pl.ds(8 * up, 8)],
                twin,
            )
            for up in range(2)
        ]

    def reduce_beside(stream, copies):
        arrived(copies)
        term, lanes = streams[stream]
        held = stream_held[stream][0]

        def add(slot, carry):
            mine = (2 * (slot // 8) + core) * 8 + slot % 8
            held[slot] = (term[mine, :, lanes].astype(f32) + held[slot].astype(f32)).astype(bf16)
            return carry

        lax.fori_loop(0, 16, add, 0)
        return [remote(held.at[pl.ds((1 - y_at) * 8, 8)], stream_held[stream][1], beside)]

    def reduce_far(stream, copies):
        arrived(copies)
        before, held = stream_held[stream][:2]

        def add(slot, carry):
            held[slot] = (
                before[y_at * 8 + slot].astype(f32) + held[slot].astype(f32)
            ).astype(bf16)
            return carry

        lax.fori_loop(0, 8, add, 0)
        return [remote(held.at[pl.ds((1 - g) * 4, 4)], stream_held[stream][2], far)]

    def reduce_quad(stream, copies):
        arrived(copies)
        before, held, result = stream_held[stream][1:]

        def add(slot, carry):
            held[slot] = (before[g * 4 + slot].astype(f32) + held[slot].astype(f32)).astype(bf16)
            return carry

        lax.fori_loop(0, 4, add, 0)
        made = [
            remote(held.at[flip_quad(q, mask)], result.at[q], in_quad(mask)) for mask in (1, 2, 3)
        ]
        result[q] = held[q]
        return made

    late_r0 = reduce_twin(0)

    def mixed_block(c, carry):
        mixed_s[c] = dot_nt(gated_s[chunk_rows(c), :], late_w[:, out_w]).astype(bf16)
        return carry

    lax.fori_loop(0, QUAD, mixed_block, 0)
    mixed_copies = [
        remote(mixed_s.at[flip_quad(q, mask)], mixed_come.at[mask - 1], in_quad(mask))
        for mask in (1, 2, 3)
    ]

    def backward_local(c, carry):
        rows = chunk_rows(c)
        total = jnp.zeros((CHUNK, CHUNK), f32)
        for i in range(PAIRS):
            lanes = lane_tile(i)
            y = y_s[rows, lanes].astype(bf16)
            moved = weights_s[c, i].astype(f32) * dot_nt(y, stacked(sx_s[rows, lanes]))
            total = total + moved[:, :CHUNK] + moved[:, CHUNK:]
            both = dot_tn(scores_s[c, i], y)
            sx_cot_s[rows, lanes] = both[:CHUNK] * half0 + both[CHUNK:] * half1
        cross_s[c] = total.astype(bf16)
        return carry

    late_r1 = reduce_beside(0, late_r0)
    lax.fori_loop(0, QUAD, backward_local, 0)
    later_copy.wait_recv()
    for i in range(PAIRS):
        total = jnp.where(g == 0, later_s[QUAD, i].astype(f32), 0.0)
        for c in range(QUAD - 1, -1, -1):
            later_s[c, i] = total.astype(bf16)
            if c > 0:
                total = chunk_decay(c, i) * total + back_s[c, i]

    def backward_mix(c, carry):
        rows = chunk_rows(c)
        shifted = chunk_rows(c, TAIL)
        b_mat = act[rows, pl.ds(QCH, STATE)].astype(bf16)
        c_mat = act[rows, pl.ds(QCH + STATE, STATE)].astype(bf16)
        cum, step = cum_s[rows, :], step_s[rows, :]
        tail = jnp.exp(cum[CHUNK - 1 :] - cum)
        decay = jnp.exp(cum[CHUNK - 1 :])
        cross = cross_s[c]
        b_cot = dot_tn(cross, c_mat)
        c_cot = dot_nn(cross, b_mat)
        cum_cot = jnp.zeros((CHUNK, LANES), f32)
        step_cot = jnp.zeros((CHUNK, LANES), f32)
        last_cot = jnp.zeros((8, LANES), f32)
        for i in range(PAIRS):
            lanes = lane_tile(i)
            xs, y = act[rows, lanes], y_s[rows, lanes]
            later, state = later_s[c, i], state_s[c, i]
            wide_step, wide_tail = spread(step, i), spread(tail, i)
            tailed = (xs * wide_step * wide_tail).astype(bf16)
            from_later = dot_nn(b_mat, later) * wide_tail
            b_cot = b_cot + dot_nt(tailed, later)
            c_cot = c_cot + dot_nt(z_s[rows, lanes], state)
            sx = sx_s[rows, lanes].astype(f32)
            sx_cot = sx_cot_s[rows, lanes] + from_later
            cum_cot = cum_cot + head_sum(
                y.astype(bf16).astype(f32) * ssd_s[rows, lanes] - sx * sx_cot, i
            )
            step_cot = step_cot + head_sum(sx_cot * xs, i)
            last = column_sum(sx * from_later) + column_sum(
                later.astype(f32) * state.astype(f32)
            ) * spread(decay, i)
            last_cot = last_cot + head_sum(jnp.broadcast_to(last, (8, LANES)), i)
            pre_cot_s[shifted, lanes] = (
                sx_cot * wide_step + y * par(6, lanes)
            ) * act_slope[rows, lanes]
        pre_cot_s[shifted, pl.ds(QCH, STATE)] = b_cot * act_slope[rows, pl.ds(QCH, STATE)]
        pre_cot_s[shifted, pl.ds(QCH + STATE, STATE)] = (
            c_cot * act_slope[rows, pl.ds(QCH + STATE, STATE)]
        )
        log_cot = dot_nn(upper3, jnp.concatenate(in_parts(cum_cot, 3), axis=0)) + last_cot[:1]
        dt_cot = (step_cot + log_cot * rate) * step_slope[rows, :]
        small_s[8:9, lane_tile(0)] += column_sum(log_cot * log_s[rows, :])
        small_s[7:8, lane_tile(0)] += column_sum(dt_cot)
        early_cot_s[pl.ds(pl.multiple_of(c * CHUNK + TAIL, 16), CHUNK), pl.ds(QXBC, LANES)] = (
            dt_cot.astype(bf16)
        )
        return carry

    lax.fori_loop(0, QUAD, backward_mix, 0)
    late_r2 = reduce_far(0, late_r1)
    early_cot_s[pl.ds(0, TAIL), pl.ds(QXBC, LANES)] = jnp.zeros((TAIL, LANES), bf16)

    for i in range(QXBC // LANES):
        lanes = lane_tile(i)
        edge = pre_cot_s[pl.ds(0, 24), lanes]
        total = par(CONV - 1, lanes) * edge[:TAIL]
        for k in range(CONV - 1):
            total = total + par(k, lanes) * pltpu.roll(edge, 24 - (3 - k), 0)[:TAIL]
        early_cot_s[pl.ds(0, TAIL), lanes] = total.astype(bf16)

    def backward_conv(c, carry):
        shifted = pl.ds(pl.multiple_of(c * CHUNK + TAIL, 16), CHUNK)
        for i in range(QXBC // LANES):
            lanes = lane_tile(i)
            cots = pre_cot_s[chunk_rows(c, TAIL, CHUNK + 8), lanes]
            window = proj[chunk_rows(c, 8, CHUNK + 8), lanes]
            cot = cots[:CHUNK]
            total = par(CONV - 1, lanes) * cot
            for k in range(CONV - 1):
                total = total + par(k, lanes) * pltpu.roll(cots, CHUNK + 8 - (3 - k), 0)[:CHUNK]
            early_cot_s[shifted, lanes] = total.astype(bf16)
            for k in range(CONV):
                small_s[k : k + 1, lanes] += column_sum(
                    cot * pltpu.roll(window, CHUNK + 3 - k, 0)[:CHUNK]
                )
            small_s[4:5, lanes] += column_sum(cot)
        return carry

    lax.fori_loop(0, QUAD, backward_conv, 0)

    early_r0 = []
    for part in range(2):
        lanes = pl.ds(part * (SLAB // 2), SLAB // 2)

        def early_half(half, carry, lanes=lanes):
            cols = pl.ds(pl.multiple_of(half * QCH, QCH), QCH)
            term_rows(early_term, half, dot_tn(xn[:, cols], early_cot_s[:, lanes]), lanes)
            return carry

        lax.fori_loop(0, 2, early_half, 0)
        early_r0.append(reduce_twin(1 + part))

    early_r1 = [reduce_beside(1 + part, early_r0[part]) for part in range(2)]
    late_r3 = reduce_quad(0, late_r2)

    tail_value = dot_nt(early_cot_s[pl.ds(0, TAIL), :], early_w[...])
    tail_out[...] = tail_value
    tail_index = used[0]
    used[0] += QUAD

    def tail_copy(i):
        return pltpu.make_async_remote_copy(
            src_ref=tail_out,
            dst_ref=tail_come.at[i],
            send_sem=send_sem.at[tail_index + i],
            recv_sem=recv_sem.at[tail_index + i],
            device_id=(dp_at, QUAD - 1),
            device_id_type=MESH,
        )

    for i in range(QUAD):

        @pl.when((g == 1) & (q == i))
        def _():
            tail_copy(i).start()

    small_s[9:10, :] += column_sum(tail_value * scaled_rows(xtail[...]))

    def normed_block(c, carry):
        rows = pl.ds(pl.multiple_of(c * CHUNK + TAIL, 16), CHUNK)
        value = dot_nt(early_cot_s[rows, :], early_w[...]) + dot_nt(
            gate_cot_s[chunk_rows(c), :], late_w[:, gate_w]
        )
        normed_cot_s[c] = value
        normed_out[c] = value.astype(bf16)
        small_s[9:10, :] += column_sum(value * scaled_rows(xq[c]))
        return carry

    lax.fori_loop(0, QUAD, normed_block, 0)
    normed_copies = [
        remote(normed_out.at[flip_quad(q, mask)], normed_come.at[mask - 1], in_quad(mask))
        for mask in (1, 2, 3)
    ]
    small_copy = remote(small_s, small_come.at[0], twin)
    early_r2 = []
    early_r2.append(reduce_far(1, early_r1[0]))
    small_copy.wait_recv()
    small_come[3] = small_s[...] + small_come[0]
    small_copy = remote(small_come.at[3], small_come.at[1], beside)
    early_r2.append(reduce_far(2, early_r1[1]))

    arrived(mixed_copies)
    total = x_ref[...].astype(f32) + mixed_s[q].astype(f32)
    for mask in range(3):
        total = total + mixed_come[mask].astype(f32)
    out_ref[...] = total.astype(bf16)

    small_copy.wait_recv()
    small_come[4] = small_come[3] + small_come[1]
    small_copy = remote(small_come.at[4], small_come.at[2], far)
    early_r3 = [reduce_quad(1, early_r2[0])]
    small_copy.wait_recv()
    small_quad[q] = small_come[4] + small_come[2]
    small_copies = [remote(small_quad.at[q], small_quad.at[q], in_quad(mask)) for mask in (1, 2, 3)]
    early_r3.append(reduce_quad(2, early_r2[1]))

    arrived(normed_copies)
    value = normed_cot_s[q]
    for mask in range(3):
        value = value + normed_come[mask].astype(f32)
    normed_cot_s[q] = value

    @pl.when(at_end)
    def _():
        for i in range(QUAD):
            tail_copy(i).wait_recv()
        rows = pl.ds(CHUNK - TAIL, TAIL)
        normed_cot_s[q, rows, :] += tail_come[0] + tail_come[1] + tail_come[2] + tail_come[3]

    cot = normed_cot_s[q] * gain
    rows = x_ref[...].astype(f32)
    scale = lax.rsqrt(jnp.mean(rows * rows, axis=-1, keepdims=True) + EPS)
    pull = scale * scale * scale * jnp.mean(cot * rows, axis=-1, keepdims=True)
    grad_ref[...] = cot_ref[...].astype(f32) + scale * cot - rows * pull

    arrived(late_r3)
    late_grad_ref[...] = stream_held[0][3][...].astype(f32)
    arrived(early_r3[0])
    early_grad_ref[:, :, pl.ds(0, SLAB // 2)] = stream_held[1][3][...].astype(f32)
    arrived(early_r3[1])
    early_grad_ref[:, :, pl.ds(SLAB // 2, SLAB // 2)] = stream_held[2][3][...].astype(f32)
    arrived(small_copies)
    small_ref[...] = small_quad[...]

    for copy in sent:
        copy.wait_send()

    @pl.when(at_end)
    def _():
        for copy in tail_sends:
            copy.wait_send()

    for i in range(QUAD):

        @pl.when((g == 1) & (q == i))
        def _():
            tail_copy(i).wait_send()


def quad_columns(value, width):
    value = value.reshape(value.shape[0], QUAD, -1)
    return jnp.pad(value, ((0, 0), (0, 0), (0, width - value.shape[2])))


def quad_body(
    inputs,
    norm_gain,
    in_proj,
    conv_weight,
    conv_bias,
    dt_bias,
    a_log,
    skip_gain,
    gated_gain,
    out_proj,
    cotangent,
):
    f32, bf16 = jnp.float32, jnp.bfloat16
    rows = in_proj.shape[0]
    shared = in_proj[:, DI + DI : DI + XBC]
    early = jnp.concatenate(
        [
            quad_columns(in_proj[:, DI : DI + DI], QCH),
            jnp.broadcast_to(shared[:, None], (rows, QUAD, BC)),
            quad_columns(in_proj[:, DI + XBC :], LANES),
        ],
        axis=2,
    ).transpose(1, 0, 2)
    late = jnp.concatenate(
        [quad_columns(in_proj[:, :DI], QCH), quad_columns(out_proj, QCH)], axis=2
    ).transpose(1, 0, 2)
    channels = jnp.concatenate([conv_weight.T, conv_bias[None]], axis=0)
    channels = jnp.concatenate(
        [
            quad_columns(channels[:, :DI], QCH),
            jnp.broadcast_to(channels[:, None, DI:], (CONV + 1, QUAD, BC)),
            jnp.zeros((CONV + 1, QUAD, SLAB - QXBC), f32),
        ],
        axis=2,
    )
    params = jnp.concatenate(
        [
            channels,
            quad_columns(gated_gain[None], SLAB),
            quad_columns(jnp.repeat(skip_gain, HEAD_DIM)[None], SLAB),
            quad_columns(dt_bias[None], SLAB),
            quad_columns(a_log[None], SLAB),
            jnp.broadcast_to(norm_gain[None, None], (1, QUAD, SLAB)),
            jnp.zeros((GRAD_ROWS - 10, QUAD, SLAB), f32),
        ],
        axis=0,
    ).transpose(1, 0, 2)
    tokens = QUAD * CHUNK
    slots = lax.axis_size("dp") * lax.axis_size("seq")
    width = inputs.shape[1]
    vmem = pltpu.VMEM
    half = SLAB // 2
    held = [
        vmem((count, rows, w), bf16) for w in (SLAB, half, half) for count in (16, 8, 4, 4)
    ]
    scratch = [
        vmem((QUAD, CHUNK, width), bf16),
        vmem((QUAD, CHUNK, width), bf16),
        vmem((TAIL, width), bf16),
        vmem((slots, rows, SLAB), bf16),
        vmem((slots, rows, SLAB), bf16),
        vmem((width, SLAB), bf16),
        vmem((width, SLAB), bf16),
        vmem((TAIL + tokens, width), bf16),
        vmem((TAIL + tokens, SLAB), f32),
        vmem((tokens, QXBC), f32),
        vmem((tokens, QXBC), f32),
        vmem((tokens, LANES), f32),
        vmem((tokens, LANES), f32),
        vmem((tokens, LANES), f32),
        vmem((tokens, LANES), f32),
        vmem((tokens, QCH), bf16),
        vmem((QUAD, PAIRS, STATE, LANES), f32),
        vmem((PAIRS, STATE, LANES), bf16),
        vmem((PAIRS, STATE, LANES), bf16),
        vmem((QUAD, PAIRS, STATE, LANES), bf16),
        vmem((QUAD, PAIRS, CHUNK, 2 * CHUNK), bf16),
        vmem((QUAD, PAIRS, CHUNK, 2 * CHUNK), bf16),
        vmem((tokens, QCH), f32),
        vmem((tokens, QCH), f32),
        vmem((tokens, QCH), f32),
        vmem((tokens, QCH), f32),
        vmem((QUAD, 8, tokens), f32),
        vmem((tokens, QCH), bf16),
        vmem((tokens, QCH), bf16),
        vmem((tokens, QCH), f32),
        vmem((tokens, QCH), bf16),
        vmem((QUAD, PAIRS, STATE, LANES), f32),
        vmem((QUAD + 1, PAIRS, STATE, LANES), bf16),
        vmem((QUAD, CHUNK, CHUNK), bf16),
        vmem((tokens, QCH), f32),
        vmem((TAIL + tokens + 8, QXBC), f32),
        vmem((TAIL + tokens, SLAB), bf16),
        vmem((slots, rows, SLAB), bf16),
        vmem((slots, rows, SLAB), bf16),
        vmem((QUAD, CHUNK, width), bf16),
        vmem((3, CHUNK, width), bf16),
        vmem((QUAD, CHUNK, width), f32),
        vmem((QUAD, CHUNK, width), bf16),
        vmem((3, CHUNK, width), bf16),
        vmem((TAIL, width), f32),
        vmem((QUAD, TAIL, width), f32),
        vmem((GRAD_ROWS, SLAB), f32),
        vmem((5, GRAD_ROWS, SLAB), f32),
        vmem((QUAD, GRAD_ROWS, SLAB), f32),
        *held,
        pltpu.SemaphoreType.DMA((96,)),
        pltpu.SemaphoreType.DMA((96,)),
    ]
    in_vmem = pl.BlockSpec(memory_space=pltpu.VMEM)
    layer_out, input_grad, early_grad, late_grad, small = pl.pallas_call(
        block_kernel,
        out_shape=[
            jax.ShapeDtypeStruct(inputs.shape, bf16),
            jax.ShapeDtypeStruct(inputs.shape, f32),
            jax.ShapeDtypeStruct((QUAD, rows, SLAB), f32),
            jax.ShapeDtypeStruct((QUAD, rows, SLAB), f32),
            jax.ShapeDtypeStruct((QUAD, GRAD_ROWS, SLAB), f32),
        ],
        in_specs=[in_vmem] * 5,
        out_specs=[in_vmem] * 5,
        scratch_shapes=scratch,
        compiler_params=pltpu.CompilerParams(
            collective_id=1, has_side_effects=True, vmem_limit_bytes=VMEM_BYTES
        ),
        name="residual_block",
    )(inputs, cotangent, early, late, params)

    def whole(value):
        return value.transpose(1, 0, 2).reshape(value.shape[1], -1)

    in_proj_grad = jnp.concatenate(
        [
            whole(late_grad[:, :, :QCH]),
            whole(early_grad[:, :, :QCH]),
            jnp.sum(early_grad[:, :, QCH:QXBC], axis=0),
            whole(early_grad[:, :, QXBC : QXBC + QHEADS]),
        ],
        axis=1,
    )
    out_proj_grad = whole(late_grad[:, :, QCH:])
    conv = jnp.concatenate(
        [
            whole(small[:, : CONV + 1, :QCH]),
            jnp.sum(small[:, : CONV + 1, QCH:QXBC], axis=0),
        ],
        axis=1,
    )
    return (
        layer_out,
        input_grad,
        in_proj_grad,
        out_proj_grad,
        jnp.sum(small[:, 9], axis=0),
        conv[:CONV].T,
        conv[CONV],
        small[:, 7, :QHEADS].reshape(-1),
        small[:, 8, :QHEADS].reshape(-1),
        jnp.sum(small[:, 6, :QCH].reshape(HEADS, HEAD_DIM), axis=1),
        small[:, 5, :QCH].reshape(-1),
    )


def fits_quads(mesh):
    return mesh.shape["dp"] == 4 and mesh.shape["seq"] == 2 * QUAD


def solution(mesh):
    placed = (
        P(("dp", "seq"), None),
        P(),
        P(("dp", "seq"), None),
        P(),
        P(),
        P(),
        P(),
        P(),
        P(),
        P(("dp", "seq"), None),
        P(("dp", "seq"), None),
    )
    return jax.shard_map(
        quad_body if fits_quads(mesh) else body,
        mesh=mesh,
        in_specs=placed,
        out_specs=(
            P(("dp", "seq"), None),
            P(("dp", "seq"), None),
            P(("dp", "seq"), None),
            P(("dp", "seq"), None),
            P(),
            P(),
            P(),
            P(),
            P(),
            P(),
            P(),
        ),
        check_vma=False,
    )
```

```python
from functools import partial

import jax
import jax.numpy as jnp
from jax import lax
from jax.experimental import pallas as pl
from jax.experimental.pallas import tpu as pltpu
from jax.sharding import PartitionSpec as P

HEADS = 24
HEAD_DIM = 64
STATE = 128
CONV = 4
DI = 1536
XBC = 1792
PROJ = DI + XBC + HEADS
LANES = 128
WIDE = -(-PROJ // LANES) * LANES


EPS = 1e-05
HIGH = lax.Precision.HIGHEST
MESH = pl.DeviceIdType.MESH
VMEM_BYTES = 60 * 1024 * 1024


def bits_of(count):
    return count.bit_length() - 1


def bit_at(place, bit):
    return (place // 2**bit) % 2


def places():
    return lax.axis_index("dp"), lax.axis_index("seq")


def partner(bit, seq_bits):
    dp_at, seq_at = places()
    if bit < seq_bits:
        return dp_at, seq_at + (1 - 2 * bit_at(seq_at, bit)) * 2**bit
    up = bit - seq_bits
    return dp_at + (1 - 2 * bit_at(dp_at, up)) * 2**up, seq_at


def greet(bits, seq_bits):
    barrier = pltpu.get_barrier_semaphore()
    for bit in range(bits):
        pl.semaphore_signal(barrier, inc=1, device_id=partner(bit, seq_bits), device_id_type=MESH)
    pl.semaphore_wait(barrier, bits)


def gather_orders(seq_bits, dp_bits):
    x_count = seq_bits // 2
    x_bits = list(range(x_count))
    z_bits = list(range(x_count, seq_bits))[::-1]
    core = [seq_bits]
    y_bits = [seq_bits + 1 + i for i in range(dp_bits - 1)]
    return (
        z_bits + x_bits + y_bits + core,
        z_bits + y_bits + x_bits + core,
        z_bits[:1] + x_bits + y_bits + z_bits[1:] + core,
        z_bits[:1] + y_bits + x_bits + z_bits[1:] + core,
    )


SHARES = (0.3, 0.3, 0.2, 0.2)


def split_lanes(width, shares):
    tiles = width // LANES
    edges = [round(tiles * sum(shares[:i])) * LANES for i in range(len(shares) + 1)]
    return [(low, high - low) for low, high in zip(edges, edges[1:])]


def gather_kernel(seq_bits, streams, bits, *refs):
    array_count = 1 + max(stream[0] for stream in streams)
    shards, outs = refs[:array_count], refs[array_count : 2 * array_count]
    send_sem, recv_sem, own_sem = refs[2 * array_count :]
    dp_at, seq_at = places()
    place = dp_at * 2**seq_bits + seq_at
    own = [
        pltpu.make_async_copy(shard, out.at[place], own_sem.at[i])
        for i, (shard, out) in enumerate(zip(shards, outs))
    ]
    for copy in own:
        copy.start()
    greet(bits, seq_bits)
    for copy in own:
        copy.wait()

    def landed(stream, stage, sem):
        which, low, width, _ = streams[stream]
        view = outs[which].at[pl.ds(0, 2**stage), :, pl.ds(low, width)]
        pltpu.make_async_copy(view, view, sem.at[stream, stage]).wait()

    for stage in range(bits + 1):
        for stream, (which, low, width, order) in enumerate(streams):
            if stage > 0:
                landed(stream, stage - 1, recv_sem)
            if stage == bits:
                continue
            free = order[:stage]
            run = 0
            while run in free:
                run += 1
            base = place
            for bit in free:
                base = base - bit_at(place, bit) * 2**bit
            upper = [bit for bit in free if bit > run]
            for combo in range(2 ** len(upper)):
                start = base + sum(2**bit for i, bit in enumerate(upper) if combo >> i & 1)
                view = outs[which].at[pl.ds(start, 2**run), :, pl.ds(low, width)]
                pltpu.make_async_remote_copy(
                    src_ref=view,
                    dst_ref=view,
                    send_sem=send_sem.at[stream, stage],
                    recv_sem=recv_sem.at[stream, stage],
                    device_id=partner(order[stage], seq_bits),
                    device_id_type=MESH,
                ).start()
    for stage in range(bits):
        for stream in range(len(streams)):
            landed(stream, stage, send_sem)


def gather_all(shards, collective_id):
    seq_bits, dp_bits = bits_of(lax.axis_size("seq")), bits_of(lax.axis_size("dp"))
    bits = seq_bits + dp_bits
    orders = gather_orders(seq_bits, dp_bits)
    streams = [
        (which, low, width, order)
        for which, shard in enumerate(shards)
        for (low, width), order in zip(split_lanes(shard.shape[1], SHARES), orders)
    ]
    return pl.pallas_call(
        partial(gather_kernel, seq_bits, streams, bits),
        out_shape=[jax.ShapeDtypeStruct((2**bits, *a.shape), a.dtype) for a in shards],
        in_specs=[pl.BlockSpec(memory_space=pltpu.VMEM)] * len(shards),
        out_specs=[pl.BlockSpec(memory_space=pl.ANY)] * len(shards),
        scratch_shapes=[
            pltpu.SemaphoreType.DMA((len(streams), bits)),
            pltpu.SemaphoreType.DMA((len(streams), bits)),
            pltpu.SemaphoreType.DMA((len(shards),)),
        ],
        compiler_params=pltpu.CompilerParams(
            collective_id=collective_id, has_side_effects=True, vmem_limit_bytes=VMEM_BYTES
        ),
        name="gather_rows",
    )(*shards)


def sum_kernel(seq_bits, streams, bits, array_count, *refs):
    terms, vector = refs[:array_count], refs[array_count]
    outs, vector_out = refs[array_count + 1 : 2 * array_count + 1], refs[2 * array_count + 1]
    held = refs[2 * array_count + 2 : 2 * array_count + 2 + len(streams) * bits]
    rest = refs[2 * array_count + 2 + len(streams) * bits :]
    vector_in, vector_sum, send_sem, recv_sem, vector_send, vector_recv = rest
    dp_at, seq_at = places()
    place = dp_at * 2**seq_bits + seq_at
    greet(bits, seq_bits)

    def source(stream, stage):
        which, low, width, _ = streams[stream]
        if stage == 0:
            return terms[which], pl.ds(low, width)
        return held[stream * bits + stage - 1], pl.ds(0, width)

    def position(stream, stage):
        order = streams[stream][3]
        remaining = sorted(order[stage:])
        return remaining.index(order[stage]), bit_at(place, order[stage])

    def landed(stream, stage, sem):
        view = held[stream * bits + stage]
        pltpu.make_async_copy(view, view, sem.at[stream, stage]).wait()

    def vector_copy(stage):
        return pltpu.make_async_remote_copy(
            src_ref=vector if stage == 0 else vector_sum.at[stage - 1],
            dst_ref=vector_in.at[stage],
            send_sem=vector_send.at[stage],
            recv_sem=vector_recv.at[stage],
            device_id=partner(stage, seq_bits),
            device_id_type=MESH,
        )

    for stage in range(bits + 1):
        if stage > 0:
            vector_copy(stage - 1).wait_recv()
            before = vector[...] if stage == 1 else vector_sum[stage - 2]
            total = before + vector_in[stage - 1]
            if stage < bits:
                vector_sum[stage - 1] = total
            else:
                vector_out[...] = total
        if stage < bits:
            vector_copy(stage).start()
        for stream, (which, low, width, order) in enumerate(streams):
            if stage > 0:
                landed(stream, stage - 1, recv_sem)
                spot, mine = position(stream, stage - 1)
                kept, lanes = source(stream, stage - 1)
                came = held[stream * bits + stage - 1]
                if stage == bits:
                    outs[which][:, pl.ds(low, width)] = kept[mine, :, lanes].astype(
                        jnp.float32
                    ) + came[0].astype(jnp.float32)
                    continue

                def add_one(block, carry, spot=spot, mine=mine, kept=kept, lanes=lanes, came=came):
                    from_block = (block // 2**spot) * 2 ** (spot + 1) + mine * 2**spot
                    from_block = from_block + block % 2**spot
                    added = kept[from_block, :, lanes].astype(jnp.float32) + came[block].astype(
                        jnp.float32
                    )
                    came[block] = added.astype(came.dtype)
                    return carry

                lax.fori_loop(0, 2 ** (bits - stage), add_one, 0)
            spot, mine = position(stream, stage)
            sent, lanes = source(stream, stage)
            for high in range(2 ** (bits - stage - 1 - spot)):
                start = high * 2 ** (spot + 1) + (1 - mine) * 2**spot
                pltpu.make_async_remote_copy(
                    src_ref=sent.at[pl.ds(start, 2**spot), :, lanes],
                    dst_ref=held[stream * bits + stage].at[pl.ds(high * 2**spot, 2**spot)],
                    send_sem=send_sem.at[stream, stage],
                    recv_sem=recv_sem.at[stream, stage],
                    device_id=partner(order[stage], seq_bits),
                    device_id_type=MESH,
                ).start()
    for stage in range(bits):
        vector_copy(stage).wait_send()
        for stream in range(len(streams)):
            landed(stream, stage, send_sem)


def sum_to_owners(terms, vector, collective_id):
    seq_bits, dp_bits = bits_of(lax.axis_size("seq")), bits_of(lax.axis_size("dp"))
    bits = seq_bits + dp_bits
    orders = [order[::-1] for order in gather_orders(seq_bits, dp_bits)]
    terms = [term.reshape(2**bits, -1, term.shape[1]) for term in terms]
    streams = [
        (which, low, width, order)
        for which, term in enumerate(terms)
        for (low, width), order in zip(split_lanes(term.shape[2], SHARES), orders)
    ]
    rows = terms[0].shape[1]
    in_vmem = pl.BlockSpec(memory_space=pltpu.VMEM)
    held = [
        pltpu.VMEM((2 ** (bits - 1 - stage), rows, width), jnp.bfloat16)
        for _, _, width, _ in streams
        for stage in range(bits)
    ]
    return pl.pallas_call(
        partial(sum_kernel, seq_bits, streams, bits, len(terms)),
        out_shape=[jax.ShapeDtypeStruct(a.shape[1:], jnp.float32) for a in terms]
        + [jax.ShapeDtypeStruct(vector.shape, vector.dtype)],
        in_specs=[in_vmem] * (len(terms) + 1),
        out_specs=[in_vmem] * (len(terms) + 1),
        scratch_shapes=held
        + [
            pltpu.VMEM((bits, *vector.shape), jnp.float32),
            pltpu.VMEM((bits, *vector.shape), jnp.float32),
            pltpu.SemaphoreType.DMA((len(streams), bits)),
            pltpu.SemaphoreType.DMA((len(streams), bits)),
            pltpu.SemaphoreType.DMA((bits,)),
            pltpu.SemaphoreType.DMA((bits,)),
        ],
        compiler_params=pltpu.CompilerParams(
            collective_id=collective_id, has_side_effects=True, vmem_limit_bytes=VMEM_BYTES
        ),
        name="sum_rows",
    )(*terms, vector)


GROUP = 4
GROUP_LANES = GROUP * HEAD_DIM


def inner_product(left, right, dims):
    return lax.dot_general(
        left, right, (dims, ((), ())), precision=HIGH, preferred_element_type=jnp.float32
    )


def group_lanes(group):
    return pl.ds(pl.multiple_of(group * GROUP_LANES, GROUP_LANES), GROUP_LANES)


def head_weights(cumulative, head):
    row = cumulative[pl.ds(head, 1), :]
    count = row.shape[1]
    spread = jnp.broadcast_to(row, (count, count))
    later = lax.broadcasted_iota(jnp.int32, (count, count), 0)
    earlier = lax.broadcasted_iota(jnp.int32, (count, count), 1)
    return jnp.exp(jnp.where(later >= earlier, spread.T - spread, -jnp.inf))


def inside_work(first, last, scaled_x, b_mat, c_mat, cumulative, output, crossed):
    if first == 0:
        crossed[...] = inner_product(c_mat[...], b_mat[...], ((1,), (1,)))

    def one(group, carry):
        values = scaled_x[:, group_lanes(group)]
        parts = []
        for i in range(GROUP):
            scores = head_weights(cumulative, group * GROUP + i) * crossed[...]
            head = values[:, i * HEAD_DIM : (i + 1) * HEAD_DIM]
            parts.append(inner_product(scores, head, ((1,), (0,))))
        output[:, group_lanes(group)] = jnp.concatenate(parts, axis=1)
        return carry

    lax.fori_loop(first, last, one, 0)


def inside_back(
    first,
    last,
    output_cot,
    scaled_x,
    b_mat,
    c_mat,
    cumulative,
    scaled_cot,
    b_cot,
    c_cot,
    cumulative_cot,
    crossed,
    crossed_cot,
):
    if first == 0:
        crossed[...] = inner_product(c_mat[...], b_mat[...], ((1,), (1,)))
        crossed_cot[...] = jnp.zeros_like(crossed_cot)

    def one(group, carry):
        values = scaled_x[:, group_lanes(group)]
        cots = output_cot[:, group_lanes(group)]
        parts = []
        total = crossed_cot[...]
        for i in range(GROUP):
            weights = head_weights(cumulative, group * GROUP + i)
            scores = weights * crossed[...]
            head = values[:, i * HEAD_DIM : (i + 1) * HEAD_DIM]
            cot = cots[:, i * HEAD_DIM : (i + 1) * HEAD_DIM]
            weighted = weights * inner_product(cot, head, ((1,), (1,)))
            total = total + weighted
            parts.append(inner_product(scores, cot, ((0,), (0,))))
            moved = weighted * crossed[...]
            cumulative_cot[pl.ds(group * GROUP + i, 1), :] = jnp.sum(
                moved.T, axis=0, keepdims=True
            ) - jnp.sum(moved, axis=0, keepdims=True)
        crossed_cot[...] = total
        scaled_cot[:, group_lanes(group)] = jnp.concatenate(parts, axis=1)
        return carry

    lax.fori_loop(first, last, one, 0)
    if last == HEADS // GROUP:
        b_cot[...] = inner_product(crossed_cot[...], c_mat[...], ((0,), (0,)))
        c_cot[...] = inner_product(crossed_cot[...], b_mat[...], ((1,), (0,)))


def scan_kernel(count, reverse, work, inputs, outputs, *refs):
    state, decay = refs[:2]
    given = refs[2 : 2 + inputs]
    out = refs[2 + inputs]
    made = refs[3 + inputs : 3 + inputs + outputs]
    came, came_decay, ready = refs[3 + inputs + outputs : 6 + inputs + outputs]
    sems = refs[6 + inputs + outputs : 12 + inputs + outputs]
    held = refs[12 + inputs + outputs :]
    out_send, out_recv, decay_send, decay_recv, back_send, back_recv = sems
    dp_at, seq_at = places()
    barrier = pltpu.get_barrier_semaphore()
    peers = [(seq_at + hop) % count for hop in range(1, count)]
    for peer in peers:
        pl.semaphore_signal(barrier, inc=1, device_id=(dp_at, peer), device_id_type=MESH)
    pl.semaphore_wait(barrier, count - 1)

    def copy(hop, which):
        target = (seq_at + hop) % count
        source, landing, send_sem, recv_sem = (
            (state.at[target], came.at[seq_at], out_send, out_recv),
            (decay, came_decay.at[seq_at], decay_send, decay_recv),
            (ready.at[target], out.at[seq_at], back_send, back_recv),
        )[which]
        return pltpu.make_async_remote_copy(
            src_ref=source,
            dst_ref=landing,
            send_sem=send_sem.at[hop],
            recv_sem=recv_sem.at[hop],
            device_id=(dp_at, target),
            device_id_type=MESH,
        )

    for hop in range(1, count):
        copy(hop, 0).start()
        copy(hop, 1).start()
    came[seq_at] = state[seq_at]
    came_decay[seq_at] = decay[...]
    groups = HEADS // GROUP
    work(0, groups // 2, *given, *made, *held)
    for hop in range(1, count):
        copy(hop, 0).wait_recv()
        copy(hop, 1).wait_recv()
    total = jnp.zeros(state.shape[1:], jnp.float32)
    for place in range(count)[:: -1 if reverse else 1]:
        ready[place] = total.astype(ready.dtype)
        total = came_decay[place] * total + came[place].astype(jnp.float32)
    for hop in range(1, count):
        copy(hop, 2).start()
    out[seq_at] = ready[seq_at]
    work(groups // 2, groups, *given, *made, *held)
    for hop in range(1, count):
        copy(hop, 2).wait_recv()
    for hop in range(1, count):
        for which in range(3):
            copy(hop, which).wait_send()


def scan_states(state, decay, work, given, made, held, reverse, collective_id):
    count = lax.axis_size("seq")
    state = state.astype(jnp.bfloat16).reshape(count, STATE // count, DI)
    in_vmem = pl.BlockSpec(memory_space=pltpu.VMEM)
    got = pl.pallas_call(
        partial(scan_kernel, count, reverse, work, len(given), len(made)),
        out_shape=[jax.ShapeDtypeStruct(state.shape, state.dtype)]
        + [jax.ShapeDtypeStruct(shape, jnp.float32) for shape in made],
        in_specs=[in_vmem] * (2 + len(given)),
        out_specs=[in_vmem] * (1 + len(made)),
        scratch_shapes=[
            pltpu.VMEM(state.shape, state.dtype),
            pltpu.VMEM((count, 1, DI), jnp.float32),
            pltpu.VMEM(state.shape, state.dtype),
        ]
        + [pltpu.SemaphoreType.DMA((count,))] * 6
        + [pltpu.VMEM(shape, jnp.float32) for shape in held],
        compiler_params=pltpu.CompilerParams(
            collective_id=collective_id, has_side_effects=True, vmem_limit_bytes=VMEM_BYTES
        ),
        name="scan_back" if reverse else "scan_states",
    )(state, decay[None, :], *given)
    return got[0].reshape(STATE, DI).astype(jnp.float32), *got[1:]


def passed_along(value, axis, steps):
    count = lax.axis_size(axis)
    first, last = (max(0, -steps), min(count, count - steps))
    return lax.ppermute(value, axis, [(source, source + steps) for source in range(first, last)])


def pre_norm(residual_in, norm_gain):
    scale_rms = lax.rsqrt(jnp.mean(residual_in * residual_in, axis=-1, keepdims=True) + EPS)
    return residual_in * scale_rms * norm_gain


def conv_silu(padded, conv_weight, conv_bias, row_count):
    total = jnp.zeros((row_count, padded.shape[1]), jnp.float32) + conv_bias[None, :]
    for offset in range(conv_weight.shape[1]):
        total = total + conv_weight[:, offset][None, :] * padded[offset : offset + row_count]
    return jax.nn.silu(total)


def head_lanes():
    lanes = jnp.arange(DI, dtype=jnp.int32) // HEAD_DIM
    return (jnp.arange(HEADS, dtype=jnp.int32)[:, None] == lanes[None, :]).astype(jnp.float32)


def spread_heads(by_head):
    return jnp.dot(by_head, head_lanes(), precision=HIGH)


def sum_heads(by_lane):
    return jnp.dot(by_lane, head_lanes().T, precision=HIGH)


def before_states(xbc, dt_raw, edge, conv_weight, conv_bias, dt_bias, a_log):
    row_count = xbc.shape[0]
    activated = conv_silu(jnp.concatenate([edge, xbc], axis=0), conv_weight, conv_bias, row_count)
    xs = activated[:, :DI]
    b_mat = activated[:, DI : DI + STATE]
    c_mat = activated[:, DI + STATE :]
    step = jax.nn.softplus(dt_raw + dt_bias)
    log_decay = step * -jnp.exp(a_log)
    at = jnp.arange(row_count)
    lower = (at[:, None] >= at[None, :]).astype(jnp.float32)
    cumulative = jnp.dot(lower, log_decay, precision=HIGH)
    scaled_x = xs * spread_heads(step)
    tail = jnp.exp(cumulative[-1][None, :] - cumulative)
    fresh = jnp.dot(b_mat.T, scaled_x * spread_heads(tail), precision=HIGH)
    return (xs, scaled_x, b_mat, c_mat, cumulative, fresh)


def post_gate(ssd_out, xs, gate_part, skip_gain, gated_gain):
    skipped = xs * spread_heads(skip_gain[None, :])
    mixed_in = (ssd_out + skipped) * jax.nn.silu(gate_part)
    scale_rms = lax.rsqrt(jnp.mean(mixed_in * mixed_in, axis=-1, keepdims=True) + EPS)
    return mixed_in * scale_rms * gated_gain


def contract_rows(left, right):
    return lax.dot_general(
        left, right, (((0,), (0,)), ((), ())), preferred_element_type=jnp.float32
    )


def contract_cols(left, right):
    return lax.dot_general(
        left, right, (((1,), (1,)), ((), ())), preferred_element_type=jnp.float32
    )


def body(
    inputs,
    norm_gain,
    in_proj,
    conv_weight,
    conv_bias,
    dt_bias,
    a_log,
    skip_gain,
    gated_gain,
    out_proj,
    cotangent,
):
    row_count = inputs.shape[0]
    residual_in = inputs.astype(jnp.float32)
    normed_full, norm_back = jax.vjp(pre_norm, residual_in, norm_gain)
    normed = normed_full.astype(jnp.bfloat16)
    in_whole, out_whole = gather_all(
        [jnp.pad(in_proj, ((0, 0), (0, WIDE - PROJ))), out_proj], collective_id=1
    )
    in_whole = in_whole.reshape(-1, WIDE)
    out_whole = out_whole.reshape(-1, DI)
    projected = jnp.dot(normed, in_whole, preferred_element_type=jnp.float32)
    gate_part = projected[:, :DI]
    xbc = projected[:, DI : DI + XBC]
    dt_raw = projected[:, DI + XBC : PROJ]
    edge = passed_along(xbc[row_count - (CONV - 1) :], "seq", 1)
    primal, mid_back = jax.vjp(
        before_states, xbc, dt_raw, edge, conv_weight, conv_bias, dt_bias, a_log
    )
    xs, scaled_x, b_mat, c_mat, cumulative, s_local = primal
    by_head = cumulative.T
    decay = jnp.exp(cumulative[-1])
    wide_decay = spread_heads(decay[None, :])[0]
    square = (row_count, row_count)
    state_in, local_out = scan_states(
        s_local,
        wide_decay,
        inside_work,
        [scaled_x, b_mat, c_mat, by_head],
        [xs.shape],
        [square],
        False,
        collective_id=2,
    )
    weighted = spread_heads(jnp.exp(cumulative))
    carried_part = jnp.dot(c_mat, state_in, precision=HIGH) * weighted
    ssd_out = local_out + carried_part
    gated_full, post_back = jax.vjp(post_gate, ssd_out, xs, gate_part, skip_gain, gated_gain)
    gated = gated_full.astype(jnp.bfloat16)
    mixed = contract_cols(gated, out_whole)
    layer_out = (residual_in + mixed).astype(jnp.bfloat16)
    gated_cot = jnp.dot(cotangent, out_whole, preferred_element_type=jnp.float32)
    ssd_cot, xs_cot, gate_cot, skip_grad, gated_gain_grad = post_back(gated_cot)
    scaled_cot = ssd_cot * weighted
    local_grad = jnp.dot(c_mat.T, scaled_cot, precision=HIGH)
    later_grad, scaled_x_cot, b_cot, inner_c_cot, by_head_cot = scan_states(
        local_grad,
        wide_decay,
        inside_back,
        [ssd_cot, scaled_x, b_mat, c_mat, by_head],
        [xs.shape, b_mat.shape, c_mat.shape, by_head.shape],
        [square, square],
        True,
        collective_id=3,
    )
    c_cot = lax.dot_general(scaled_cot, state_in, (((1,), (1,)), ((), ())), precision=HIGH)
    cum_cot = sum_heads(ssd_cot * carried_part)
    last_cot = sum_heads(jnp.sum(later_grad * state_in, axis=0, keepdims=True))[0] * decay
    is_last = (jnp.arange(row_count) == row_count - 1)[:, None]
    cum_cot = cum_cot + jnp.where(is_last, last_cot[None, :], 0.0)
    mid_grads = mid_back(
        (xs_cot, scaled_x_cot, b_cot, c_cot + inner_c_cot, cum_cot + by_head_cot.T, later_grad)
    )
    xbc_cot, dt_cot, edge_cot, conv_weight_grad, conv_bias_grad, dt_bias_grad, a_log_grad = (
        mid_grads
    )
    edge_back = passed_along(edge_cot, "seq", -1)
    xbc_cot = xbc_cot + jnp.pad(edge_back, ((row_count - (CONV - 1), 0), (0, 0)))
    projected_cot = jnp.concatenate(
        [gate_cot, xbc_cot, dt_cot, jnp.zeros((row_count, WIDE - PROJ), jnp.float32)], axis=1
    ).astype(jnp.bfloat16)
    in_term = contract_rows(normed, projected_cot).astype(jnp.bfloat16)
    out_term = contract_rows(cotangent, gated).astype(jnp.bfloat16)
    normed_cot = contract_cols(projected_cot, in_whole)
    input_part, norm_gain_grad = norm_back(normed_cot)
    input_grad = cotangent.astype(jnp.float32) + input_part
    small = (
        norm_gain_grad,
        conv_weight_grad.T,
        conv_bias_grad,
        gated_gain_grad,
        dt_bias_grad,
        a_log_grad,
        skip_grad,
    )
    flat = jnp.concatenate([a.reshape(-1) for a in small])
    tile = 8 * LANES
    flat = jnp.pad(flat, (0, -flat.shape[0] % tile))
    in_proj_grad, out_proj_grad, summed = sum_to_owners(
        [in_term, out_term], flat.reshape(-1, LANES), collective_id=4
    )
    summed = summed.reshape(-1)
    parts, at = [], 0
    for a in small:
        parts.append(summed[at : at + a.size].reshape(a.shape))
        at += a.size
    return (
        layer_out,
        input_grad,
        in_proj_grad[:, :PROJ],
        out_proj_grad,
        parts[0],
        parts[1].T,
        parts[2],
        parts[4],
        parts[5],
        parts[6],
        parts[3],
    )


QUAD = 4
CHUNK = 128
TAIL = 16
QCH = DI // QUAD
QHEADS = HEADS // QUAD
PAIRS = QCH // LANES
BC = 2 * STATE
QXBC = QCH + BC
SLAB = QXBC + LANES
GRAD_ROWS = 16


def flip(value, bit):
    return value + (1 - 2 * bit_at(value, bit)) * 2**bit


def flip_quad(value, mask):
    for bit in range(2):
        if mask >> bit & 1:
            value = flip(value, bit)
    return value


def dot_nn(left, right):
    return lax.dot_general(
        left, right, (((1,), (0,)), ((), ())), preferred_element_type=jnp.float32
    )


def dot_nt(left, right):
    return lax.dot_general(
        left, right, (((1,), (1,)), ((), ())), preferred_element_type=jnp.float32
    )


def dot_tn(left, right):
    return lax.dot_general(
        left, right, (((0,), (0,)), ((), ())), preferred_element_type=jnp.float32
    )


def in_parts(value, count):
    parts = []
    for _ in range(count):
        part = value.astype(jnp.bfloat16)
        parts.append(part)
        value = value - part.astype(jnp.float32)
    return parts


def lane_tile(i):
    return pl.ds(i * LANES, LANES)


def chunk_rows(c, offset=0, count=CHUNK):
    return pl.ds(pl.multiple_of(c * CHUNK + offset, 8), count)


def column_sum(value):
    return jnp.sum(value, axis=0, keepdims=True)


def block_kernel(
    x_ref,
    gain_ref,
    in_ref,
    taps_ref,
    bias_ref,
    dt_bias_ref,
    a_log_ref,
    skip_ref,
    gated_gain_ref,
    proj_ref,
    cot_ref,
    out_ref,
    grad_ref,
    in_grad_ref,
    proj_grad_ref,
    gain_grad_ref,
    taps_grad_ref,
    bias_grad_ref,
    dt_bias_grad_ref,
    a_log_grad_ref,
    skip_grad_ref,
    gated_gain_grad_ref,
    early_ref,
    late_ref,
    xq,
    cq,
    xtail,
    early_slots,
    late_slots,
    early_w,
    late_w,
    xn,
    proj,
    act,
    act_slope,
    step_s,
    step_slope,
    log_s,
    cum_s,
    sx_s,
    fresh_s,
    state_out,
    state_come,
    state_s,
    weights_s,
    scores_s,
    ssd_s,
    gate_s,
    gc_s,
    m_s,
    sums_s,
    gated_s,
    gate_cot_s,
    y_s,
    z_s,
    back_s,
    later_s,
    cross_s,
    sx_cot_s,
    pre_cot_s,
    early_cot_s,
    late_term,
    early_term,
    mixed_s,
    mixed_come,
    normed_cot_s,
    normed_out,
    normed_come,
    tail_out,
    tail_come,
    small_s,
    small_come,
    small_quad,
    *rest,
):
    stream_held = [rest[4 * i : 4 * i + 4] for i in range(3)]
    send_sem, recv_sem = rest[12:]
    f32, bf16 = jnp.float32, jnp.bfloat16
    dp_at, seq_at = places()
    q, g = seq_at % QUAD, seq_at // QUAD
    core, y_at = dp_at % 2, dp_at // 2
    place = dp_at * 8 + seq_at
    used = [0]
    sent = []

    barrier = pltpu.get_barrier_semaphore()
    peers = [(dp_at, (seq_at + hop) % 8) for hop in range(1, 8)]
    peers += [(flip(dp_at, 0), seq_at), (flip(dp_at, 1), seq_at)]
    for peer in peers:
        pl.semaphore_signal(barrier, inc=1, device_id=peer, device_id_type=MESH)

    def remote(source, landing, target, own=True):
        at = used[0]
        used[0] += 1
        copy = pltpu.make_async_remote_copy(
            src_ref=source,
            dst_ref=landing,
            send_sem=send_sem.at[at],
            recv_sem=recv_sem.at[at],
            device_id=target,
            device_id_type=MESH,
        )
        if own:
            copy.start()
            sent.append(copy)
        return copy

    def in_quad(mask):
        return dp_at, flip_quad(seq_at, mask)

    far = (dp_at, flip(seq_at, 2))
    beside = (flip(dp_at, 1), seq_at)
    twin = (flip(dp_at, 0), seq_at)

    def arrived(copies):
        for copy in copies:
            copy.wait_recv()

    lane = lax.broadcasted_iota(jnp.int32, (1, LANES), 1)
    first_half = lane < HEAD_DIM
    half0 = jnp.where(first_half, 1.0, 0.0)
    half1 = 1.0 - half0
    half0b, half1b = half0.astype(bf16), half1.astype(bf16)
    row_at = lax.broadcasted_iota(jnp.int32, (CHUNK, CHUNK), 0)
    lane_at = lax.broadcasted_iota(jnp.int32, (CHUNK, CHUNK), 1)
    causal = row_at >= lane_at
    lower = jnp.where(causal, 1.0, 0.0).astype(bf16)
    upper = jnp.where(row_at <= lane_at, 1.0, 0.0).astype(bf16)
    lower3 = jnp.concatenate([lower] * 3, axis=1)
    upper3 = jnp.concatenate([upper] * 3, axis=1)

    def spread(by_head, i):
        return jnp.where(first_half, by_head[:, 2 * i : 2 * i + 1], by_head[:, 2 * i + 1 : 2 * i + 2])

    def head_sum(value, i):
        owner = 2 * i + row_at // HEAD_DIM
        pick = jnp.where(owner == lane_at, 1.0, 0.0).astype(bf16)
        return dot_nn(
            jnp.concatenate(in_parts(value, 2), axis=1), jnp.concatenate([pick] * 2, axis=0)
        )

    def flat_row(ref, low, count):
        return ref[pl.ds(low, count)].reshape(1, count)

    def own_channels(i):
        return pl.ds(pl.multiple_of(q * QCH + i * LANES, LANES), LANES)

    def conv_channels(i):
        return own_channels(i) if i < PAIRS else pl.ds(DI + (i - PAIRS) * LANES, LANES)

    def tap(k, i):
        return taps_ref[pl.ds(k, 1), conv_channels(i)]

    def gated_gain(i):
        return gated_gain_ref[own_channels(i)].reshape(1, LANES)

    def own_heads(ref):
        head_at = lax.broadcasted_iota(jnp.int32, (HEADS, LANES), 0)
        to = lax.broadcasted_iota(jnp.int32, (HEADS, LANES), 1)
        pick = jnp.where((head_at == to + q * QHEADS) & (to < QHEADS), 1.0, 0.0)
        value = jnp.broadcast_to(ref[...].reshape(1, HEADS), (8, HEADS))
        return inner_product(value, pick, ((1,), (0,)))[:1]

    def stacked(value):
        return jnp.concatenate([value * half0b, value * half1b], axis=0)

    for j in range(QUAD):
        own = pl.ds(j * QCH, QCH)
        early_ref[j, :, pl.ds(0, QCH)] = in_ref[:, pl.ds(DI + j * QCH, QCH)]
        early_ref[j, :, pl.ds(QCH, BC)] = in_ref[:, pl.ds(2 * DI, BC)]
        head_at = lax.broadcasted_iota(jnp.int32, (HEADS, LANES), 0)
        to = lax.broadcasted_iota(jnp.int32, (HEADS, LANES), 1)
        pick = jnp.where((head_at == to + j * QHEADS) & (to < QHEADS), 1.0, 0.0)
        early_ref[j, :, pl.ds(QXBC, LANES)] = dot_nn(
            in_ref[:, pl.ds(DI + XBC, HEADS)], pick.astype(bf16)
        ).astype(bf16)
        late_ref[j, :, pl.ds(0, QCH)] = in_ref[:, own]
        late_ref[j, :, pl.ds(QCH, QCH)] = proj_ref[:, own]

    pl.semaphore_wait(barrier, len(peers))

    def scatter(shard, slots):
        return [
            remote(shard.at[flip_quad(q, mask)], slots.at[place], in_quad(mask))
            for mask in (1, 2, 3)
        ]

    early_0 = scatter(early_ref, early_slots)
    token_copies = [remote(x_ref, xq.at[q], in_quad(mask)) for mask in (1, 2, 3)]
    tail_sends = [
        remote(x_ref.at[pl.ds(CHUNK - TAIL, TAIL)], xtail, (dp_at, QUAD + i), own=False)
        for i in range(QUAD)
    ]
    at_end = seq_at == QUAD - 1

    @pl.when(at_end)
    def _():
        for copy in tail_sends:
            copy.start()

    early_slots[place] = early_ref[q]
    late_slots[place] = late_ref[q]
    xq[q] = x_ref[...]
    cq[q] = cot_ref[...]

    def cross_far(slots):
        return [
            remote(
                slots.at[pl.ds(dp_at * 8 + g * 4, 4), :, lane_part],
                slots.at[pl.ds(dp_at * 8 + g * 4, 4), :, lane_part],
                far,
            )
            for lane_part in (pl.ds(0, SLAB // 2), pl.ds(SLAB // 2, SLAB // 2))
        ]

    def cross_beside(slots, copies):
        made = []
        for part, copy in enumerate(copies):
            copy.wait_recv()
            view = slots.at[pl.ds(dp_at * 8, 8), :, pl.ds(part * (SLAB // 2), SLAB // 2)]
            made.append(remote(view, view, beside))
        return made

    def cross_twin(slots, copies):
        made = []
        for part, copy in enumerate(copies):
            copy.wait_recv()
            for up in range(2):
                view = slots.at[
                    pl.ds((2 * up + core) * 8, 8), :, pl.ds(part * (SLAB // 2), SLAB // 2)
                ]
                made.append(remote(view, view, twin))
        return made

    def flatten(slots, flat):
        def one(pair, carry):
            value = slots[pl.ds(2 * pair, 2)].astype(f32).reshape(48, SLAB)
            flat[pl.ds(pl.multiple_of(pair * 48, 16), 48), :] = value.astype(bf16)
            return carry

        lax.fori_loop(0, 16, one, 0)

    arrived(early_0)
    early_1 = cross_far(early_slots)
    late_0 = scatter(late_ref, late_slots)
    early_2 = cross_beside(early_slots, early_1)
    arrived(late_0)
    late_1 = cross_far(late_slots)
    cot_copies = [remote(cot_ref, cq.at[q], in_quad(mask)) for mask in (1, 2, 3)]

    arrived(token_copies)

    for i in range(QUAD):

        @pl.when((g == 1) & (q == i))
        def _():
            tail_sends[i].wait_recv()

    @pl.when(g == 0)
    def _():
        xtail[...] = jnp.zeros_like(xtail)

    gain = flat_row(gain_ref, 0, x_ref.shape[1])

    def scaled_rows(value):
        value = value.astype(f32)
        return value * lax.rsqrt(jnp.mean(value * value, axis=-1, keepdims=True) + EPS)

    xn[pl.ds(0, TAIL), :] = (scaled_rows(xtail[...]) * gain).astype(bf16)

    def norm_block(c, carry):
        xn[pl.ds(pl.multiple_of(c * CHUNK + TAIL, 16), CHUNK), :] = (
            scaled_rows(xq[c]) * gain
        ).astype(bf16)
        return carry

    lax.fori_loop(0, QUAD, norm_block, 0)
    early_3 = cross_twin(early_slots, early_2)
    late_2 = cross_beside(late_slots, late_1)
    small_s[...] = jnp.zeros_like(small_s)
    pre_cot_s[pl.ds(0, TAIL), :] = jnp.zeros((TAIL, QXBC), f32)
    pre_cot_s[pl.ds(TAIL + QUAD * CHUNK, 8), :] = jnp.zeros((8, QXBC), f32)
    arrived(early_3)
    flatten(early_slots, early_w)

    for n in range(3):
        cols = pl.ds(n * 256, 256)
        proj[:, cols] = dot_nn(xn[...], early_w[:, cols])

    rate = -jnp.exp(own_heads(a_log_ref))
    dt_bias = own_heads(dt_bias_ref)
    skips = own_heads(skip_ref)
    skip_wide = [spread(skips, i) for i in range(PAIRS)]
    head_lane = lane < QHEADS

    def forward_states(c, carry):
        rows = chunk_rows(c)
        for i in range(QXBC // LANES):
            lanes = lane_tile(i)
            window = proj[chunk_rows(c, 8, CHUNK + 8), lanes]
            total = bias_ref[conv_channels(i)].reshape(1, LANES)
            for k in range(CONV):
                total = total + tap(k, i) * pltpu.roll(window, CHUNK + 3 - k, 0)[:CHUNK]
            sig = lax.logistic(total)
            act[rows, lanes] = total * sig
            act_slope[rows, lanes] = sig * (1.0 + total * (1.0 - sig))
        raw = proj[chunk_rows(c, TAIL), pl.ds(QXBC, LANES)] + dt_bias
        step = jnp.maximum(raw, 0.0) + jnp.log1p(jnp.exp(-jnp.abs(raw)))
        step = jnp.where(head_lane, step, 0.0)
        log_decay = step * rate
        cum = dot_nn(lower3, jnp.concatenate(in_parts(log_decay, 3), axis=0))
        step_s[rows, :] = step
        step_slope[rows, :] = lax.logistic(raw)
        log_s[rows, :] = log_decay
        cum_s[rows, :] = cum
        tail = jnp.exp(cum[CHUNK - 1 :] - cum)
        b_mat = act[rows, pl.ds(QCH, STATE)].astype(bf16)
        for i in range(PAIRS):
            lanes = lane_tile(i)
            sx = act[rows, lanes] * spread(step, i)
            sx_s[rows, lanes] = sx.astype(bf16)
            fresh_s[c, i] = dot_tn(b_mat, (sx * spread(tail, i)).astype(bf16))
        return carry

    lax.fori_loop(0, QUAD, forward_states, 0)

    def chunk_decay(c, i):
        last = cum_s[chunk_rows(c, CHUNK - 8, 8), :][7:]
        return spread(jnp.exp(last), i)

    for i in range(PAIRS):
        total = fresh_s[0, i]
        for c in range(1, QUAD):
            total = chunk_decay(c, i) * total + fresh_s[c, i]
        state_out[i] = total.astype(bf16)
    state_copy = remote(state_out, state_come, far)
    late_3 = cross_twin(late_slots, late_2)

    def forward_local(c, carry):
        rows = chunk_rows(c)
        b_mat = act[rows, pl.ds(QCH, STATE)].astype(bf16)
        c_mat = act[rows, pl.ds(QCH + STATE, STATE)].astype(bf16)
        crossed = dot_nt(c_mat, b_mat)
        cum = cum_s[rows, :]
        cum_t = cum.T
        for i in range(PAIRS):
            lanes = lane_tile(i)
            pair = []
            for head in (2 * i, 2 * i + 1):
                gap = cum[:, head : head + 1] - cum_t[head : head + 1, :]
                pair.append(jnp.exp(jnp.where(causal, gap, -1e30)))
            weights_s[c, i] = jnp.concatenate(pair, axis=1).astype(bf16)
            scores = jnp.concatenate([w * crossed for w in pair], axis=1).astype(bf16)
            scores_s[c, i] = scores
            ssd_s[rows, lanes] = dot_nn(scores, stacked(sx_s[rows, lanes]))
        return carry

    lax.fori_loop(0, QUAD, forward_local, 0)
    arrived(late_3)
    flatten(late_slots, late_w)
    gate_w = pl.ds(0, QCH)
    out_w = pl.ds(QCH, QCH)
    gate_s[...] = dot_nn(xn[pl.ds(TAIL, QUAD * CHUNK), :], late_w[:, gate_w])
    arrived(cot_copies)

    def cot_block(c, carry):
        gc_s[chunk_rows(c), :] = dot_nn(cq[c], late_w[:, out_w])
        return carry

    lax.fori_loop(0, QUAD, cot_block, 0)
    state_copy.wait_recv()
    for i in range(PAIRS):
        total = jnp.where(g == 1, state_come[i].astype(f32), 0.0)
        for c in range(QUAD):
            state_s[c, i] = total.astype(bf16)
            if c < QUAD - 1:
                total = chunk_decay(c, i) * total + fresh_s[c, i]

    def forward_gate(c, carry):
        rows = chunk_rows(c)
        c_mat = act[rows, pl.ds(QCH + STATE, STATE)].astype(bf16)
        grown = jnp.exp(cum_s[rows, :])
        square, crossed = 0.0, 0.0
        for i in range(PAIRS):
            lanes = lane_tile(i)
            ssd = ssd_s[rows, lanes] + dot_nn(c_mat, state_s[c, i]) * spread(grown, i)
            ssd_s[rows, lanes] = ssd
            gate = gate_s[rows, lanes]
            m = (ssd + act[rows, lanes] * skip_wide[i]) * gate * lax.logistic(gate)
            m_s[rows, lanes] = m
            square = square + m * m
            crossed = crossed + gc_s[rows, lanes] * gated_gain(i) * m
        square = jnp.sum(square, axis=1, keepdims=True)
        crossed = jnp.sum(crossed, axis=1, keepdims=True)
        both = jnp.where(lane == 0, square, jnp.where(lane == 1, crossed, 0.0))
        sums_s[q, :, pl.ds(pl.multiple_of(c * CHUNK, CHUNK), CHUNK)] = (
            both.T[:8]
        )
        return carry

    lax.fori_loop(0, QUAD, forward_gate, 0)
    arrived([remote(sums_s.at[q], sums_s.at[q], in_quad(mask)) for mask in (1, 2, 3)])

    def backward_states(c, carry):
        rows = chunk_rows(c)
        cols = pl.ds(pl.multiple_of(c * CHUNK, CHUNK), CHUNK)
        sums = sums_s[0, :, cols] + sums_s[1, :, cols] + sums_s[2, :, cols] + sums_s[3, :, cols]
        sums = jnp.concatenate([sums] * (CHUNK // 8), axis=0).T
        scale = lax.rsqrt(sums[:, 0:1] * (1.0 / DI) + EPS)
        pull = scale * scale * scale * (sums[:, 1:2] * (1.0 / DI))
        c_mat = act[rows, pl.ds(QCH + STATE, STATE)].astype(bf16)
        grown = jnp.exp(cum_s[rows, :])
        for i in range(PAIRS):
            lanes = lane_tile(i)
            m, gc, gate = m_s[rows, lanes], gc_s[rows, lanes], gate_s[rows, lanes]
            xs = act[rows, lanes]
            mr = m * scale
            gated_s[rows, lanes] = (mr * gated_gain(i)).astype(bf16)
            small_s[5:6, lanes] += column_sum(gc * mr)
            m_cot = scale * (gc * gated_gain(i)) - m * pull
            sig = lax.logistic(gate)
            mixed = ssd_s[rows, lanes] + xs * skip_wide[i]
            gate_cot_s[rows, lanes] = (
                m_cot * mixed * (sig * (1.0 + gate * (1.0 - sig)))
            ).astype(bf16)
            y = m_cot * gate * sig
            y_s[rows, lanes] = y
            small_s[6:7, lanes] += column_sum(y * xs)
            z = (y * spread(grown, i)).astype(bf16)
            z_s[rows, lanes] = z
            back_s[c, i] = dot_tn(c_mat, z)
        return carry

    lax.fori_loop(0, QUAD, backward_states, 0)
    state_copy.wait_send()
    sent[:] = [copy for copy in sent if copy is not state_copy]
    for i in range(PAIRS):
        total = back_s[QUAD - 1, i]
        for c in range(QUAD - 2, -1, -1):
            total = chunk_decay(c, i) * total + back_s[c, i]
        state_out[i] = total.astype(bf16)
    later_copy = remote(state_out, later_s.at[QUAD], far)

    def term_rows(term, half, value, lanes):
        term[pl.ds(half * 16, 16), :, lanes] = value.reshape(16, 24, value.shape[1]).astype(bf16)

    def late_half(half, carry):
        cols = pl.ds(pl.multiple_of(half * QCH, QCH), QCH)
        term_rows(
            late_term,
            half,
            dot_tn(xn[pl.ds(TAIL, QUAD * CHUNK), cols], gate_cot_s[...]),
            gate_w,
        )
        total = dot_tn(cq[0, :, cols], gated_s[pl.ds(0, CHUNK), :])
        for c in range(1, QUAD):
            total = total + dot_tn(cq[c, :, cols], gated_s[pl.ds(c * CHUNK, CHUNK), :])
        term_rows(late_term, half, total, out_w)
        return carry

    lax.fori_loop(0, 2, late_half, 0)

    streams = [(late_term, pl.ds(0, SLAB))] + [
        (early_term, pl.ds(i * (SLAB // 2), SLAB // 2)) for i in range(2)
    ]

    def reduce_twin(stream):
        term, lanes = streams[stream]
        return [
            remote(
                term.at[pl.ds((2 * up + 1 - core) * 8, 8), :, lanes],
                stream_held[stream][0].at[pl.ds(8 * up, 8)],
                twin,
            )
            for up in range(2)
        ]

    def reduce_beside(stream, copies):
        arrived(copies)
        term, lanes = streams[stream]
        held = stream_held[stream][0]

        def add(slot, carry):
            mine = (2 * (slot // 8) + core) * 8 + slot % 8
            held[slot] = (term[mine, :, lanes].astype(f32) + held[slot].astype(f32)).astype(bf16)
            return carry

        lax.fori_loop(0, 16, add, 0)
        return [remote(held.at[pl.ds((1 - y_at) * 8, 8)], stream_held[stream][1], beside)]

    def reduce_far(stream, copies):
        arrived(copies)
        before, held = stream_held[stream][:2]

        def add(slot, carry):
            held[slot] = (
                before[y_at * 8 + slot].astype(f32) + held[slot].astype(f32)
            ).astype(bf16)
            return carry

        lax.fori_loop(0, 8, add, 0)
        return [remote(held.at[pl.ds((1 - g) * 4, 4)], stream_held[stream][2], far)]

    def reduce_quad(stream, copies):
        arrived(copies)
        before, held, result = stream_held[stream][1:]

        def add(slot, carry):
            held[slot] = (before[g * 4 + slot].astype(f32) + held[slot].astype(f32)).astype(bf16)
            return carry

        lax.fori_loop(0, 4, add, 0)
        made = [
            remote(held.at[flip_quad(q, mask)], result.at[q], in_quad(mask)) for mask in (1, 2, 3)
        ]
        result[q] = held[q]
        return made

    late_r0 = reduce_twin(0)

    def mixed_block(c, carry):
        mixed_s[c] = dot_nt(gated_s[chunk_rows(c), :], late_w[:, out_w]).astype(bf16)
        return carry

    lax.fori_loop(0, QUAD, mixed_block, 0)
    mixed_copies = [
        remote(mixed_s.at[flip_quad(q, mask)], mixed_come.at[mask - 1], in_quad(mask))
        for mask in (1, 2, 3)
    ]

    def backward_local(c, carry):
        rows = chunk_rows(c)
        total = jnp.zeros((CHUNK, CHUNK), f32)
        for i in range(PAIRS):
            lanes = lane_tile(i)
            y = y_s[rows, lanes].astype(bf16)
            moved = weights_s[c, i].astype(f32) * dot_nt(y, stacked(sx_s[rows, lanes]))
            total = total + moved[:, :CHUNK] + moved[:, CHUNK:]
            both = dot_tn(scores_s[c, i], y)
            sx_cot_s[rows, lanes] = both[:CHUNK] * half0 + both[CHUNK:] * half1
        cross_s[c] = total.astype(bf16)
        return carry

    late_r1 = reduce_beside(0, late_r0)
    lax.fori_loop(0, QUAD, backward_local, 0)
    later_copy.wait_recv()
    for i in range(PAIRS):
        total = jnp.where(g == 0, later_s[QUAD, i].astype(f32), 0.0)
        for c in range(QUAD - 1, -1, -1):
            later_s[c, i] = total.astype(bf16)
            if c > 0:
                total = chunk_decay(c, i) * total + back_s[c, i]

    def backward_mix(c, carry):
        rows = chunk_rows(c)
        shifted = chunk_rows(c, TAIL)
        b_mat = act[rows, pl.ds(QCH, STATE)].astype(bf16)
        c_mat = act[rows, pl.ds(QCH + STATE, STATE)].astype(bf16)
        cum, step = cum_s[rows, :], step_s[rows, :]
        tail = jnp.exp(cum[CHUNK - 1 :] - cum)
        decay = jnp.exp(cum[CHUNK - 1 :])
        cross = cross_s[c]
        b_cot = dot_tn(cross, c_mat)
        c_cot = dot_nn(cross, b_mat)
        cum_cot = jnp.zeros((CHUNK, LANES), f32)
        step_cot = jnp.zeros((CHUNK, LANES), f32)
        last_cot = jnp.zeros((8, LANES), f32)
        for i in range(PAIRS):
            lanes = lane_tile(i)
            xs, y = act[rows, lanes], y_s[rows, lanes]
            later, state = later_s[c, i], state_s[c, i]
            wide_step, wide_tail = spread(step, i), spread(tail, i)
            tailed = (xs * wide_step * wide_tail).astype(bf16)
            from_later = dot_nn(b_mat, later) * wide_tail
            b_cot = b_cot + dot_nt(tailed, later)
            c_cot = c_cot + dot_nt(z_s[rows, lanes], state)
            sx = sx_s[rows, lanes].astype(f32)
            sx_cot = sx_cot_s[rows, lanes] + from_later
            cum_cot = cum_cot + head_sum(
                y.astype(bf16).astype(f32) * ssd_s[rows, lanes] - sx * sx_cot, i
            )
            step_cot = step_cot + head_sum(sx_cot * xs, i)
            last = column_sum(sx * from_later) + column_sum(
                later.astype(f32) * state.astype(f32)
            ) * spread(decay, i)
            last_cot = last_cot + head_sum(jnp.broadcast_to(last, (8, LANES)), i)
            pre_cot_s[shifted, lanes] = (
                sx_cot * wide_step + y * skip_wide[i]
            ) * act_slope[rows, lanes]
        pre_cot_s[shifted, pl.ds(QCH, STATE)] = b_cot * act_slope[rows, pl.ds(QCH, STATE)]
        pre_cot_s[shifted, pl.ds(QCH + STATE, STATE)] = (
            c_cot * act_slope[rows, pl.ds(QCH + STATE, STATE)]
        )
        log_cot = dot_nn(upper3, jnp.concatenate(in_parts(cum_cot, 3), axis=0)) + last_cot[:1]
        dt_cot = (step_cot + log_cot * rate) * step_slope[rows, :]
        small_s[8:9, lane_tile(0)] += column_sum(log_cot * log_s[rows, :])
        small_s[7:8, lane_tile(0)] += column_sum(dt_cot)
        early_cot_s[pl.ds(pl.multiple_of(c * CHUNK + TAIL, 16), CHUNK), pl.ds(QXBC, LANES)] = (
            dt_cot.astype(bf16)
        )
        return carry

    lax.fori_loop(0, QUAD, backward_mix, 0)
    late_r2 = reduce_far(0, late_r1)
    early_cot_s[pl.ds(0, TAIL), pl.ds(QXBC, LANES)] = jnp.zeros((TAIL, LANES), bf16)

    for i in range(QXBC // LANES):
        lanes = lane_tile(i)
        edge = pre_cot_s[pl.ds(0, 24), lanes]
        total = tap(CONV - 1, i) * edge[:TAIL]
        for k in range(CONV - 1):
            total = total + tap(k, i) * pltpu.roll(edge, 24 - (3 - k), 0)[:TAIL]
        early_cot_s[pl.ds(0, TAIL), lanes] = total.astype(bf16)

    def backward_conv(c, carry):
        shifted = pl.ds(pl.multiple_of(c * CHUNK + TAIL, 16), CHUNK)
        for i in range(QXBC // LANES):
            lanes = lane_tile(i)
            cots = pre_cot_s[chunk_rows(c, TAIL, CHUNK + 8), lanes]
            window = proj[chunk_rows(c, 8, CHUNK + 8), lanes]
            cot = cots[:CHUNK]
            total = tap(CONV - 1, i) * cot
            for k in range(CONV - 1):
                total = total + tap(k, i) * pltpu.roll(cots, CHUNK + 8 - (3 - k), 0)[:CHUNK]
            early_cot_s[shifted, lanes] = total.astype(bf16)
            for k in range(CONV):
                small_s[k : k + 1, lanes] += column_sum(
                    cot * pltpu.roll(window, CHUNK + 3 - k, 0)[:CHUNK]
                )
            small_s[4:5, lanes] += column_sum(cot)
        return carry

    lax.fori_loop(0, QUAD, backward_conv, 0)

    heads = jnp.zeros((8, LANES), f32)
    for i in range(PAIRS):
        heads = heads + head_sum(jnp.broadcast_to(small_s[6:7, lane_tile(i)], (8, LANES)), i)
    small_s[6:7, lane_tile(0)] = heads[:1]

    early_r0 = []
    for part in range(2):
        lanes = pl.ds(part * (SLAB // 2), SLAB // 2)

        def early_half(half, carry, lanes=lanes):
            cols = pl.ds(pl.multiple_of(half * QCH, QCH), QCH)
            term_rows(early_term, half, dot_tn(xn[:, cols], early_cot_s[:, lanes]), lanes)
            return carry

        lax.fori_loop(0, 2, early_half, 0)
        early_r0.append(reduce_twin(1 + part))

    early_r1 = [reduce_beside(1 + part, early_r0[part]) for part in range(2)]
    late_r3 = reduce_quad(0, late_r2)

    tail_value = dot_nt(early_cot_s[pl.ds(0, TAIL), :], early_w[...])
    tail_out[...] = tail_value
    tail_index = used[0]
    used[0] += QUAD

    def tail_copy(i):
        return pltpu.make_async_remote_copy(
            src_ref=tail_out,
            dst_ref=tail_come.at[i],
            send_sem=send_sem.at[tail_index + i],
            recv_sem=recv_sem.at[tail_index + i],
            device_id=(dp_at, QUAD - 1),
            device_id_type=MESH,
        )

    for i in range(QUAD):

        @pl.when((g == 1) & (q == i))
        def _():
            tail_copy(i).start()

    small_s[9:10, :] += column_sum(tail_value * scaled_rows(xtail[...]))

    def normed_block(c, carry):
        rows = pl.ds(pl.multiple_of(c * CHUNK + TAIL, 16), CHUNK)
        value = dot_nt(early_cot_s[rows, :], early_w[...]) + dot_nt(
            gate_cot_s[chunk_rows(c), :], late_w[:, gate_w]
        )
        normed_cot_s[c] = value
        normed_out[c] = value.astype(bf16)
        small_s[9:10, :] += column_sum(value * scaled_rows(xq[c]))
        return carry

    lax.fori_loop(0, QUAD, normed_block, 0)
    normed_copies = [
        remote(normed_out.at[flip_quad(q, mask)], normed_come.at[mask - 1], in_quad(mask))
        for mask in (1, 2, 3)
    ]
    small_copy = remote(small_s, small_come.at[0], twin)
    early_r2 = []
    early_r2.append(reduce_far(1, early_r1[0]))
    small_copy.wait_recv()
    small_come[3] = small_s[...] + small_come[0]
    small_copy = remote(small_come.at[3], small_come.at[1], beside)
    early_r2.append(reduce_far(2, early_r1[1]))

    arrived(mixed_copies)
    total = x_ref[...].astype(f32) + mixed_s[q].astype(f32)
    for mask in range(3):
        total = total + mixed_come[mask].astype(f32)
    out_ref[...] = total.astype(bf16)

    small_copy.wait_recv()
    small_come[4] = small_come[3] + small_come[1]
    small_copy = remote(small_come.at[4], small_come.at[2], far)
    early_r3 = [reduce_quad(1, early_r2[0])]
    small_copy.wait_recv()
    small_quad[q] = small_come[4] + small_come[2]
    small_copies = [remote(small_quad.at[q], small_quad.at[q], in_quad(mask)) for mask in (1, 2, 3)]
    early_r3.append(reduce_quad(2, early_r2[1]))

    arrived(normed_copies)
    value = normed_cot_s[q]
    for mask in range(3):
        value = value + normed_come[mask].astype(f32)
    normed_cot_s[q] = value

    @pl.when(at_end)
    def _():
        for i in range(QUAD):
            tail_copy(i).wait_recv()
        rows = pl.ds(CHUNK - TAIL, TAIL)
        normed_cot_s[q, rows, :] += tail_come[0] + tail_come[1] + tail_come[2] + tail_come[3]

    cot = normed_cot_s[q] * gain
    rows = x_ref[...].astype(f32)
    scale = lax.rsqrt(jnp.mean(rows * rows, axis=-1, keepdims=True) + EPS)
    pull = scale * scale * scale * jnp.mean(cot * rows, axis=-1, keepdims=True)
    grad_ref[...] = cot_ref[...].astype(f32) + scale * cot - rows * pull

    arrived(small_copies)
    for j in range(QUAD):
        own = pl.ds(j * QCH, QCH)
        taps_grad_ref[:, own] = small_quad[j, 0:CONV, pl.ds(0, QCH)]
        bias_grad_ref[own] = small_quad[j, CONV : CONV + 1, pl.ds(0, QCH)].reshape(QCH)
        gated_gain_grad_ref[own] = small_quad[j, 5:6, pl.ds(0, QCH)].reshape(QCH)
    quads = small_quad[0] + small_quad[1] + small_quad[2] + small_quad[3]
    taps_grad_ref[:, pl.ds(DI, BC)] = quads[:CONV, QCH:QXBC]
    bias_grad_ref[pl.ds(DI, BC)] = quads[CONV : CONV + 1, QCH:QXBC].reshape(BC)
    gain_grad_ref[...] = quads[9:10].reshape(quads.shape[1])

    def in_head_order(parts):
        total = parts[0]
        for j in range(1, QUAD):
            total = total + pltpu.roll(parts[j], j * QHEADS, 1)
        return total[:, :HEADS]

    by_head = in_head_order([small_quad[j, :, lane_tile(0)] for j in range(QUAD)])
    skip_grad_ref[...] = by_head[6:7].reshape(HEADS)
    dt_bias_grad_ref[...] = by_head[7:8].reshape(HEADS)
    a_log_grad_ref[...] = by_head[8:9].reshape(HEADS)

    arrived(late_r3)
    for j in range(QUAD):
        own = pl.ds(j * QCH, QCH)
        in_grad_ref[:, own] = stream_held[0][3][j, :, pl.ds(0, QCH)].astype(f32)
        proj_grad_ref[:, own] = stream_held[0][3][j, :, pl.ds(QCH, QCH)].astype(f32)
    arrived(early_r3[0])
    arrived(early_r3[1])
    half = SLAB // 2

    def early_result(j, low):
        return stream_held[1 + low // half][3][j, :, pl.ds(low % half, LANES)].astype(f32)

    for j in range(QUAD):
        for i in range(PAIRS):
            in_grad_ref[:, pl.ds(DI + j * QCH + i * LANES, LANES)] = early_result(j, i * LANES)
    for i in range(BC // LANES):
        total = early_result(0, QCH + i * LANES)
        for j in range(1, QUAD):
            total = total + early_result(j, QCH + i * LANES)
        in_grad_ref[:, pl.ds(2 * DI + i * LANES, LANES)] = total
    in_grad_ref[:, pl.ds(DI + XBC, HEADS)] = in_head_order(
        [early_result(j, QXBC) for j in range(QUAD)]
    )

    for copy in sent:
        copy.wait_send()

    @pl.when(at_end)
    def _():
        for copy in tail_sends:
            copy.wait_send()

    for i in range(QUAD):

        @pl.when((g == 1) & (q == i))
        def _():
            tail_copy(i).wait_send()


def quad_body(
    inputs,
    norm_gain,
    in_proj,
    conv_weight,
    conv_bias,
    dt_bias,
    a_log,
    skip_gain,
    gated_gain,
    out_proj,
    cotangent,
):
    f32, bf16 = jnp.float32, jnp.bfloat16
    rows = in_proj.shape[0]
    tokens = QUAD * CHUNK
    slots = lax.axis_size("dp") * lax.axis_size("seq")
    width = inputs.shape[1]
    vmem = pltpu.VMEM
    half = SLAB // 2
    held = [
        vmem((count, rows, w), bf16) for w in (SLAB, half, half) for count in (16, 8, 4, 4)
    ]
    scratch = [
        vmem((QUAD, rows, SLAB), bf16),
        vmem((QUAD, rows, SLAB), bf16),
        vmem((QUAD, CHUNK, width), bf16),
        vmem((QUAD, CHUNK, width), bf16),
        vmem((TAIL, width), bf16),
        vmem((slots, rows, SLAB), bf16),
        vmem((slots, rows, SLAB), bf16),
        vmem((width, SLAB), bf16),
        vmem((width, SLAB), bf16),
        vmem((TAIL + tokens, width), bf16),
        vmem((TAIL + tokens, SLAB), f32),
        vmem((tokens, QXBC), f32),
        vmem((tokens, QXBC), f32),
        vmem((tokens, LANES), f32),
        vmem((tokens, LANES), f32),
        vmem((tokens, LANES), f32),
        vmem((tokens, LANES), f32),
        vmem((tokens, QCH), bf16),
        vmem((QUAD, PAIRS, STATE, LANES), f32),
        vmem((PAIRS, STATE, LANES), bf16),
        vmem((PAIRS, STATE, LANES), bf16),
        vmem((QUAD, PAIRS, STATE, LANES), bf16),
        vmem((QUAD, PAIRS, CHUNK, 2 * CHUNK), bf16),
        vmem((QUAD, PAIRS, CHUNK, 2 * CHUNK), bf16),
        vmem((tokens, QCH), f32),
        vmem((tokens, QCH), f32),
        vmem((tokens, QCH), f32),
        vmem((tokens, QCH), f32),
        vmem((QUAD, 8, tokens), f32),
        vmem((tokens, QCH), bf16),
        vmem((tokens, QCH), bf16),
        vmem((tokens, QCH), f32),
        vmem((tokens, QCH), bf16),
        vmem((QUAD, PAIRS, STATE, LANES), f32),
        vmem((QUAD + 1, PAIRS, STATE, LANES), bf16),
        vmem((QUAD, CHUNK, CHUNK), bf16),
        vmem((tokens, QCH), f32),
        vmem((TAIL + tokens + 8, QXBC), f32),
        vmem((TAIL + tokens, SLAB), bf16),
        vmem((slots, rows, SLAB), bf16),
        vmem((slots, rows, SLAB), bf16),
        vmem((QUAD, CHUNK, width), bf16),
        vmem((3, CHUNK, width), bf16),
        vmem((QUAD, CHUNK, width), f32),
        vmem((QUAD, CHUNK, width), bf16),
        vmem((3, CHUNK, width), bf16),
        vmem((TAIL, width), f32),
        vmem((QUAD, TAIL, width), f32),
        vmem((GRAD_ROWS, SLAB), f32),
        vmem((5, GRAD_ROWS, SLAB), f32),
        vmem((QUAD, GRAD_ROWS, SLAB), f32),
        *held,
        pltpu.SemaphoreType.DMA((96,)),
        pltpu.SemaphoreType.DMA((96,)),
    ]
    in_vmem = pl.BlockSpec(memory_space=pltpu.VMEM)
    shapes = [inputs.shape, inputs.shape, in_proj.shape, out_proj.shape]
    shapes += [(width,), (CONV, XBC), (XBC,), (HEADS,), (HEADS,), (HEADS,), (DI,)]
    got = pl.pallas_call(
        block_kernel,
        out_shape=[
            jax.ShapeDtypeStruct(shape, f32 if at else bf16) for at, shape in enumerate(shapes)
        ],
        in_specs=[in_vmem] * 11,
        out_specs=[in_vmem] * 11,
        scratch_shapes=scratch,
        compiler_params=pltpu.CompilerParams(
            collective_id=1, has_side_effects=True, vmem_limit_bytes=VMEM_BYTES
        ),
        name="residual_block",
    )(
        inputs,
        norm_gain,
        in_proj,
        conv_weight.T,
        conv_bias,
        dt_bias,
        a_log,
        skip_gain,
        gated_gain,
        out_proj,
        cotangent,
    )
    got = pl.pallas_call(
        copy_out_kernel,
        out_shape=[jax.ShapeDtypeStruct(value.shape, value.dtype) for value in got],
        in_specs=[in_vmem] * 11,
        out_specs=[pl.BlockSpec(memory_space=pl.ANY)] * 11,
        scratch_shapes=[pltpu.SemaphoreType.DMA((11,))],
        name="copy_out",
    )(*got)
    return (*got[:5], got[5].T, *got[6:])


def copy_out_kernel(*refs):
    count = len(refs) // 2
    sems = refs[2 * count]
    copies = [
        pltpu.make_async_copy(refs[i], refs[count + i], sems.at[i]) for i in range(count)
    ]
    for copy in copies:
        copy.start()
    for copy in copies:
        copy.wait()


def fits_quads(mesh):
    return mesh.shape["dp"] == 4 and mesh.shape["seq"] == 2 * QUAD


def solution(mesh):
    placed = (
        P(("dp", "seq"), None),
        P(),
        P(("dp", "seq"), None),
        P(),
        P(),
        P(),
        P(),
        P(),
        P(),
        P(("dp", "seq"), None),
        P(("dp", "seq"), None),
    )
    return jax.shard_map(
        quad_body if fits_quads(mesh) else body,
        mesh=mesh,
        in_specs=placed,
        out_specs=(
            P(("dp", "seq"), None),
            P(("dp", "seq"), None),
            P(("dp", "seq"), None),
            P(("dp", "seq"), None),
            P(),
            P(),
            P(),
            P(),
            P(),
            P(),
            P(),
        ),
        check_vma=False,
    )
```

```python
from functools import partial

import jax
import jax.numpy as jnp
from jax import lax
from jax.experimental import pallas as pl
from jax.experimental.pallas import tpu as pltpu
from jax.sharding import PartitionSpec as P

HEADS = 24
HEAD_DIM = 64
STATE = 128
CONV = 4
DI = 1536
XBC = 1792
PROJ = DI + XBC + HEADS
LANES = 128
WIDE = -(-PROJ // LANES) * LANES


EPS = 1e-05
HIGH = lax.Precision.HIGHEST
MESH = pl.DeviceIdType.MESH
VMEM_BYTES = 60 * 1024 * 1024


def bits_of(count):
    return count.bit_length() - 1


def bit_at(place, bit):
    return (place // 2**bit) % 2


def places():
    return lax.axis_index("dp"), lax.axis_index("seq")


def partner(bit, seq_bits):
    dp_at, seq_at = places()
    if bit < seq_bits:
        return dp_at, seq_at + (1 - 2 * bit_at(seq_at, bit)) * 2**bit
    up = bit - seq_bits
    return dp_at + (1 - 2 * bit_at(dp_at, up)) * 2**up, seq_at


def greet(bits, seq_bits):
    barrier = pltpu.get_barrier_semaphore()
    for bit in range(bits):
        pl.semaphore_signal(barrier, inc=1, device_id=partner(bit, seq_bits), device_id_type=MESH)
    pl.semaphore_wait(barrier, bits)


def gather_orders(seq_bits, dp_bits):
    x_count = seq_bits // 2
    x_bits = list(range(x_count))
    z_bits = list(range(x_count, seq_bits))[::-1]
    core = [seq_bits]
    y_bits = [seq_bits + 1 + i for i in range(dp_bits - 1)]
    return (
        z_bits + x_bits + y_bits + core,
        z_bits + y_bits + x_bits + core,
        z_bits[:1] + x_bits + y_bits + z_bits[1:] + core,
        z_bits[:1] + y_bits + x_bits + z_bits[1:] + core,
    )


SHARES = (0.3, 0.3, 0.2, 0.2)


def split_lanes(width, shares):
    tiles = width // LANES
    edges = [round(tiles * sum(shares[:i])) * LANES for i in range(len(shares) + 1)]
    return [(low, high - low) for low, high in zip(edges, edges[1:])]


def gather_kernel(seq_bits, streams, bits, *refs):
    array_count = 1 + max(stream[0] for stream in streams)
    shards, outs = refs[:array_count], refs[array_count : 2 * array_count]
    send_sem, recv_sem, own_sem = refs[2 * array_count :]
    dp_at, seq_at = places()
    place = dp_at * 2**seq_bits + seq_at
    own = [
        pltpu.make_async_copy(shard, out.at[place], own_sem.at[i])
        for i, (shard, out) in enumerate(zip(shards, outs))
    ]
    for copy in own:
        copy.start()
    greet(bits, seq_bits)
    for copy in own:
        copy.wait()

    def landed(stream, stage, sem):
        which, low, width, _ = streams[stream]
        view = outs[which].at[pl.ds(0, 2**stage), :, pl.ds(low, width)]
        pltpu.make_async_copy(view, view, sem.at[stream, stage]).wait()

    for stage in range(bits + 1):
        for stream, (which, low, width, order) in enumerate(streams):
            if stage > 0:
                landed(stream, stage - 1, recv_sem)
            if stage == bits:
                continue
            free = order[:stage]
            run = 0
            while run in free:
                run += 1
            base = place
            for bit in free:
                base = base - bit_at(place, bit) * 2**bit
            upper = [bit for bit in free if bit > run]
            for combo in range(2 ** len(upper)):
                start = base + sum(2**bit for i, bit in enumerate(upper) if combo >> i & 1)
                view = outs[which].at[pl.ds(start, 2**run), :, pl.ds(low, width)]
                pltpu.make_async_remote_copy(
                    src_ref=view,
                    dst_ref=view,
                    send_sem=send_sem.at[stream, stage],
                    recv_sem=recv_sem.at[stream, stage],
                    device_id=partner(order[stage], seq_bits),
                    device_id_type=MESH,
                ).start()
    for stage in range(bits):
        for stream in range(len(streams)):
            landed(stream, stage, send_sem)


def gather_all(shards, collective_id):
    seq_bits, dp_bits = bits_of(lax.axis_size("seq")), bits_of(lax.axis_size("dp"))
    bits = seq_bits + dp_bits
    orders = gather_orders(seq_bits, dp_bits)
    streams = [
        (which, low, width, order)
        for which, shard in enumerate(shards)
        for (low, width), order in zip(split_lanes(shard.shape[1], SHARES), orders)
    ]
    return pl.pallas_call(
        partial(gather_kernel, seq_bits, streams, bits),
        out_shape=[jax.ShapeDtypeStruct((2**bits, *a.shape), a.dtype) for a in shards],
        in_specs=[pl.BlockSpec(memory_space=pltpu.VMEM)] * len(shards),
        out_specs=[pl.BlockSpec(memory_space=pl.ANY)] * len(shards),
        scratch_shapes=[
            pltpu.SemaphoreType.DMA((len(streams), bits)),
            pltpu.SemaphoreType.DMA((len(streams), bits)),
            pltpu.SemaphoreType.DMA((len(shards),)),
        ],
        compiler_params=pltpu.CompilerParams(
            collective_id=collective_id, has_side_effects=True, vmem_limit_bytes=VMEM_BYTES
        ),
        name="gather_rows",
    )(*shards)


def sum_kernel(seq_bits, streams, bits, array_count, *refs):
    terms, vector = refs[:array_count], refs[array_count]
    outs, vector_out = refs[array_count + 1 : 2 * array_count + 1], refs[2 * array_count + 1]
    held = refs[2 * array_count + 2 : 2 * array_count + 2 + len(streams) * bits]
    rest = refs[2 * array_count + 2 + len(streams) * bits :]
    vector_in, vector_sum, send_sem, recv_sem, vector_send, vector_recv = rest
    dp_at, seq_at = places()
    place = dp_at * 2**seq_bits + seq_at
    greet(bits, seq_bits)

    def source(stream, stage):
        which, low, width, _ = streams[stream]
        if stage == 0:
            return terms[which], pl.ds(low, width)
        return held[stream * bits + stage - 1], pl.ds(0, width)

    def position(stream, stage):
        order = streams[stream][3]
        remaining = sorted(order[stage:])
        return remaining.index(order[stage]), bit_at(place, order[stage])

    def landed(stream, stage, sem):
        view = held[stream * bits + stage]
        pltpu.make_async_copy(view, view, sem.at[stream, stage]).wait()

    def vector_copy(stage):
        return pltpu.make_async_remote_copy(
            src_ref=vector if stage == 0 else vector_sum.at[stage - 1],
            dst_ref=vector_in.at[stage],
            send_sem=vector_send.at[stage],
            recv_sem=vector_recv.at[stage],
            device_id=partner(stage, seq_bits),
            device_id_type=MESH,
        )

    for stage in range(bits + 1):
        if stage > 0:
            vector_copy(stage - 1).wait_recv()
            before = vector[...] if stage == 1 else vector_sum[stage - 2]
            total = before + vector_in[stage - 1]
            if stage < bits:
                vector_sum[stage - 1] = total
            else:
                vector_out[...] = total
        if stage < bits:
            vector_copy(stage).start()
        for stream, (which, low, width, order) in enumerate(streams):
            if stage > 0:
                landed(stream, stage - 1, recv_sem)
                spot, mine = position(stream, stage - 1)
                kept, lanes = source(stream, stage - 1)
                came = held[stream * bits + stage - 1]
                if stage == bits:
                    outs[which][:, pl.ds(low, width)] = kept[mine, :, lanes].astype(
                        jnp.float32
                    ) + came[0].astype(jnp.float32)
                    continue

                def add_one(block, carry, spot=spot, mine=mine, kept=kept, lanes=lanes, came=came):
                    from_block = (block // 2**spot) * 2 ** (spot + 1) + mine * 2**spot
                    from_block = from_block + block % 2**spot
                    added = kept[from_block, :, lanes].astype(jnp.float32) + came[block].astype(
                        jnp.float32
                    )
                    came[block] = added.astype(came.dtype)
                    return carry

                lax.fori_loop(0, 2 ** (bits - stage), add_one, 0)
            spot, mine = position(stream, stage)
            sent, lanes = source(stream, stage)
            for high in range(2 ** (bits - stage - 1 - spot)):
                start = high * 2 ** (spot + 1) + (1 - mine) * 2**spot
                pltpu.make_async_remote_copy(
                    src_ref=sent.at[pl.ds(start, 2**spot), :, lanes],
                    dst_ref=held[stream * bits + stage].at[pl.ds(high * 2**spot, 2**spot)],
                    send_sem=send_sem.at[stream, stage],
                    recv_sem=recv_sem.at[stream, stage],
                    device_id=partner(order[stage], seq_bits),
                    device_id_type=MESH,
                ).start()
    for stage in range(bits):
        vector_copy(stage).wait_send()
        for stream in range(len(streams)):
            landed(stream, stage, send_sem)


def sum_to_owners(terms, vector, collective_id):
    seq_bits, dp_bits = bits_of(lax.axis_size("seq")), bits_of(lax.axis_size("dp"))
    bits = seq_bits + dp_bits
    orders = [order[::-1] for order in gather_orders(seq_bits, dp_bits)]
    terms = [term.reshape(2**bits, -1, term.shape[1]) for term in terms]
    streams = [
        (which, low, width, order)
        for which, term in enumerate(terms)
        for (low, width), order in zip(split_lanes(term.shape[2], SHARES), orders)
    ]
    rows = terms[0].shape[1]
    in_vmem = pl.BlockSpec(memory_space=pltpu.VMEM)
    held = [
        pltpu.VMEM((2 ** (bits - 1 - stage), rows, width), jnp.bfloat16)
        for _, _, width, _ in streams
        for stage in range(bits)
    ]
    return pl.pallas_call(
        partial(sum_kernel, seq_bits, streams, bits, len(terms)),
        out_shape=[jax.ShapeDtypeStruct(a.shape[1:], jnp.float32) for a in terms]
        + [jax.ShapeDtypeStruct(vector.shape, vector.dtype)],
        in_specs=[in_vmem] * (len(terms) + 1),
        out_specs=[in_vmem] * (len(terms) + 1),
        scratch_shapes=held
        + [
            pltpu.VMEM((bits, *vector.shape), jnp.float32),
            pltpu.VMEM((bits, *vector.shape), jnp.float32),
            pltpu.SemaphoreType.DMA((len(streams), bits)),
            pltpu.SemaphoreType.DMA((len(streams), bits)),
            pltpu.SemaphoreType.DMA((bits,)),
            pltpu.SemaphoreType.DMA((bits,)),
        ],
        compiler_params=pltpu.CompilerParams(
            collective_id=collective_id, has_side_effects=True, vmem_limit_bytes=VMEM_BYTES
        ),
        name="sum_rows",
    )(*terms, vector)


GROUP = 4
GROUP_LANES = GROUP * HEAD_DIM


def inner_product(left, right, dims):
    return lax.dot_general(
        left, right, (dims, ((), ())), precision=HIGH, preferred_element_type=jnp.float32
    )


def group_lanes(group):
    return pl.ds(pl.multiple_of(group * GROUP_LANES, GROUP_LANES), GROUP_LANES)


def head_weights(cumulative, head):
    row = cumulative[pl.ds(head, 1), :]
    count = row.shape[1]
    spread = jnp.broadcast_to(row, (count, count))
    later = lax.broadcasted_iota(jnp.int32, (count, count), 0)
    earlier = lax.broadcasted_iota(jnp.int32, (count, count), 1)
    return jnp.exp(jnp.where(later >= earlier, spread.T - spread, -jnp.inf))


def inside_work(first, last, scaled_x, b_mat, c_mat, cumulative, output, crossed):
    if first == 0:
        crossed[...] = inner_product(c_mat[...], b_mat[...], ((1,), (1,)))

    def one(group, carry):
        values = scaled_x[:, group_lanes(group)]
        parts = []
        for i in range(GROUP):
            scores = head_weights(cumulative, group * GROUP + i) * crossed[...]
            head = values[:, i * HEAD_DIM : (i + 1) * HEAD_DIM]
            parts.append(inner_product(scores, head, ((1,), (0,))))
        output[:, group_lanes(group)] = jnp.concatenate(parts, axis=1)
        return carry

    lax.fori_loop(first, last, one, 0)


def inside_back(
    first,
    last,
    output_cot,
    scaled_x,
    b_mat,
    c_mat,
    cumulative,
    scaled_cot,
    b_cot,
    c_cot,
    cumulative_cot,
    crossed,
    crossed_cot,
):
    if first == 0:
        crossed[...] = inner_product(c_mat[...], b_mat[...], ((1,), (1,)))
        crossed_cot[...] = jnp.zeros_like(crossed_cot)

    def one(group, carry):
        values = scaled_x[:, group_lanes(group)]
        cots = output_cot[:, group_lanes(group)]
        parts = []
        total = crossed_cot[...]
        for i in range(GROUP):
            weights = head_weights(cumulative, group * GROUP + i)
            scores = weights * crossed[...]
            head = values[:, i * HEAD_DIM : (i + 1) * HEAD_DIM]
            cot = cots[:, i * HEAD_DIM : (i + 1) * HEAD_DIM]
            weighted = weights * inner_product(cot, head, ((1,), (1,)))
            total = total + weighted
            parts.append(inner_product(scores, cot, ((0,), (0,))))
            moved = weighted * crossed[...]
            cumulative_cot[pl.ds(group * GROUP + i, 1), :] = jnp.sum(
                moved.T, axis=0, keepdims=True
            ) - jnp.sum(moved, axis=0, keepdims=True)
        crossed_cot[...] = total
        scaled_cot[:, group_lanes(group)] = jnp.concatenate(parts, axis=1)
        return carry

    lax.fori_loop(first, last, one, 0)
    if last == HEADS // GROUP:
        b_cot[...] = inner_product(crossed_cot[...], c_mat[...], ((0,), (0,)))
        c_cot[...] = inner_product(crossed_cot[...], b_mat[...], ((1,), (0,)))


def scan_kernel(count, reverse, work, inputs, outputs, *refs):
    state, decay = refs[:2]
    given = refs[2 : 2 + inputs]
    out = refs[2 + inputs]
    made = refs[3 + inputs : 3 + inputs + outputs]
    came, came_decay, ready = refs[3 + inputs + outputs : 6 + inputs + outputs]
    sems = refs[6 + inputs + outputs : 12 + inputs + outputs]
    held = refs[12 + inputs + outputs :]
    out_send, out_recv, decay_send, decay_recv, back_send, back_recv = sems
    dp_at, seq_at = places()
    barrier = pltpu.get_barrier_semaphore()
    peers = [(seq_at + hop) % count for hop in range(1, count)]
    for peer in peers:
        pl.semaphore_signal(barrier, inc=1, device_id=(dp_at, peer), device_id_type=MESH)
    pl.semaphore_wait(barrier, count - 1)

    def copy(hop, which):
        target = (seq_at + hop) % count
        source, landing, send_sem, recv_sem = (
            (state.at[target], came.at[seq_at], out_send, out_recv),
            (decay, came_decay.at[seq_at], decay_send, decay_recv),
            (ready.at[target], out.at[seq_at], back_send, back_recv),
        )[which]
        return pltpu.make_async_remote_copy(
            src_ref=source,
            dst_ref=landing,
            send_sem=send_sem.at[hop],
            recv_sem=recv_sem.at[hop],
            device_id=(dp_at, target),
            device_id_type=MESH,
        )

    for hop in range(1, count):
        copy(hop, 0).start()
        copy(hop, 1).start()
    came[seq_at] = state[seq_at]
    came_decay[seq_at] = decay[...]
    groups = HEADS // GROUP
    work(0, groups // 2, *given, *made, *held)
    for hop in range(1, count):
        copy(hop, 0).wait_recv()
        copy(hop, 1).wait_recv()
    total = jnp.zeros(state.shape[1:], jnp.float32)
    for place in range(count)[:: -1 if reverse else 1]:
        ready[place] = total.astype(ready.dtype)
        total = came_decay[place] * total + came[place].astype(jnp.float32)
    for hop in range(1, count):
        copy(hop, 2).start()
    out[seq_at] = ready[seq_at]
    work(groups // 2, groups, *given, *made, *held)
    for hop in range(1, count):
        copy(hop, 2).wait_recv()
    for hop in range(1, count):
        for which in range(3):
            copy(hop, which).wait_send()


def scan_states(state, decay, work, given, made, held, reverse, collective_id):
    count = lax.axis_size("seq")
    state = state.astype(jnp.bfloat16).reshape(count, STATE // count, DI)
    in_vmem = pl.BlockSpec(memory_space=pltpu.VMEM)
    got = pl.pallas_call(
        partial(scan_kernel, count, reverse, work, len(given), len(made)),
        out_shape=[jax.ShapeDtypeStruct(state.shape, state.dtype)]
        + [jax.ShapeDtypeStruct(shape, jnp.float32) for shape in made],
        in_specs=[in_vmem] * (2 + len(given)),
        out_specs=[in_vmem] * (1 + len(made)),
        scratch_shapes=[
            pltpu.VMEM(state.shape, state.dtype),
            pltpu.VMEM((count, 1, DI), jnp.float32),
            pltpu.VMEM(state.shape, state.dtype),
        ]
        + [pltpu.SemaphoreType.DMA((count,))] * 6
        + [pltpu.VMEM(shape, jnp.float32) for shape in held],
        compiler_params=pltpu.CompilerParams(
            collective_id=collective_id, has_side_effects=True, vmem_limit_bytes=VMEM_BYTES
        ),
        name="scan_back" if reverse else "scan_states",
    )(state, decay[None, :], *given)
    return got[0].reshape(STATE, DI).astype(jnp.float32), *got[1:]


def passed_along(value, axis, steps):
    count = lax.axis_size(axis)
    first, last = (max(0, -steps), min(count, count - steps))
    return lax.ppermute(value, axis, [(source, source + steps) for source in range(first, last)])


def pre_norm(residual_in, norm_gain):
    scale_rms = lax.rsqrt(jnp.mean(residual_in * residual_in, axis=-1, keepdims=True) + EPS)
    return residual_in * scale_rms * norm_gain


def conv_silu(padded, conv_weight, conv_bias, row_count):
    total = jnp.zeros((row_count, padded.shape[1]), jnp.float32) + conv_bias[None, :]
    for offset in range(conv_weight.shape[1]):
        total = total + conv_weight[:, offset][None, :] * padded[offset : offset + row_count]
    return jax.nn.silu(total)


def head_lanes():
    lanes = jnp.arange(DI, dtype=jnp.int32) // HEAD_DIM
    return (jnp.arange(HEADS, dtype=jnp.int32)[:, None] == lanes[None, :]).astype(jnp.float32)


def spread_heads(by_head):
    return jnp.dot(by_head, head_lanes(), precision=HIGH)


def sum_heads(by_lane):
    return jnp.dot(by_lane, head_lanes().T, precision=HIGH)


def before_states(xbc, dt_raw, edge, conv_weight, conv_bias, dt_bias, a_log):
    row_count = xbc.shape[0]
    activated = conv_silu(jnp.concatenate([edge, xbc], axis=0), conv_weight, conv_bias, row_count)
    xs = activated[:, :DI]
    b_mat = activated[:, DI : DI + STATE]
    c_mat = activated[:, DI + STATE :]
    step = jax.nn.softplus(dt_raw + dt_bias)
    log_decay = step * -jnp.exp(a_log)
    at = jnp.arange(row_count)
    lower = (at[:, None] >= at[None, :]).astype(jnp.float32)
    cumulative = jnp.dot(lower, log_decay, precision=HIGH)
    scaled_x = xs * spread_heads(step)
    tail = jnp.exp(cumulative[-1][None, :] - cumulative)
    fresh = jnp.dot(b_mat.T, scaled_x * spread_heads(tail), precision=HIGH)
    return (xs, scaled_x, b_mat, c_mat, cumulative, fresh)


def post_gate(ssd_out, xs, gate_part, skip_gain, gated_gain):
    skipped = xs * spread_heads(skip_gain[None, :])
    mixed_in = (ssd_out + skipped) * jax.nn.silu(gate_part)
    scale_rms = lax.rsqrt(jnp.mean(mixed_in * mixed_in, axis=-1, keepdims=True) + EPS)
    return mixed_in * scale_rms * gated_gain


def contract_rows(left, right):
    return lax.dot_general(
        left, right, (((0,), (0,)), ((), ())), preferred_element_type=jnp.float32
    )


def contract_cols(left, right):
    return lax.dot_general(
        left, right, (((1,), (1,)), ((), ())), preferred_element_type=jnp.float32
    )


def body(
    inputs,
    norm_gain,
    in_proj,
    conv_weight,
    conv_bias,
    dt_bias,
    a_log,
    skip_gain,
    gated_gain,
    out_proj,
    cotangent,
):
    row_count = inputs.shape[0]
    residual_in = inputs.astype(jnp.float32)
    normed_full, norm_back = jax.vjp(pre_norm, residual_in, norm_gain)
    normed = normed_full.astype(jnp.bfloat16)
    in_whole, out_whole = gather_all(
        [jnp.pad(in_proj, ((0, 0), (0, WIDE - PROJ))), out_proj], collective_id=1
    )
    in_whole = in_whole.reshape(-1, WIDE)
    out_whole = out_whole.reshape(-1, DI)
    projected = jnp.dot(normed, in_whole, preferred_element_type=jnp.float32)
    gate_part = projected[:, :DI]
    xbc = projected[:, DI : DI + XBC]
    dt_raw = projected[:, DI + XBC : PROJ]
    edge = passed_along(xbc[row_count - (CONV - 1) :], "seq", 1)
    primal, mid_back = jax.vjp(
        before_states, xbc, dt_raw, edge, conv_weight, conv_bias, dt_bias, a_log
    )
    xs, scaled_x, b_mat, c_mat, cumulative, s_local = primal
    by_head = cumulative.T
    decay = jnp.exp(cumulative[-1])
    wide_decay = spread_heads(decay[None, :])[0]
    square = (row_count, row_count)
    state_in, local_out = scan_states(
        s_local,
        wide_decay,
        inside_work,
        [scaled_x, b_mat, c_mat, by_head],
        [xs.shape],
        [square],
        False,
        collective_id=2,
    )
    weighted = spread_heads(jnp.exp(cumulative))
    carried_part = jnp.dot(c_mat, state_in, precision=HIGH) * weighted
    ssd_out = local_out + carried_part
    gated_full, post_back = jax.vjp(post_gate, ssd_out, xs, gate_part, skip_gain, gated_gain)
    gated = gated_full.astype(jnp.bfloat16)
    mixed = contract_cols(gated, out_whole)
    layer_out = (residual_in + mixed).astype(jnp.bfloat16)
    gated_cot = jnp.dot(cotangent, out_whole, preferred_element_type=jnp.float32)
    ssd_cot, xs_cot, gate_cot, skip_grad, gated_gain_grad = post_back(gated_cot)
    scaled_cot = ssd_cot * weighted
    local_grad = jnp.dot(c_mat.T, scaled_cot, precision=HIGH)
    later_grad, scaled_x_cot, b_cot, inner_c_cot, by_head_cot = scan_states(
        local_grad,
        wide_decay,
        inside_back,
        [ssd_cot, scaled_x, b_mat, c_mat, by_head],
        [xs.shape, b_mat.shape, c_mat.shape, by_head.shape],
        [square, square],
        True,
        collective_id=3,
    )
    c_cot = lax.dot_general(scaled_cot, state_in, (((1,), (1,)), ((), ())), precision=HIGH)
    cum_cot = sum_heads(ssd_cot * carried_part)
    last_cot = sum_heads(jnp.sum(later_grad * state_in, axis=0, keepdims=True))[0] * decay
    is_last = (jnp.arange(row_count) == row_count - 1)[:, None]
    cum_cot = cum_cot + jnp.where(is_last, last_cot[None, :], 0.0)
    mid_grads = mid_back(
        (xs_cot, scaled_x_cot, b_cot, c_cot + inner_c_cot, cum_cot + by_head_cot.T, later_grad)
    )
    xbc_cot, dt_cot, edge_cot, conv_weight_grad, conv_bias_grad, dt_bias_grad, a_log_grad = (
        mid_grads
    )
    edge_back = passed_along(edge_cot, "seq", -1)
    xbc_cot = xbc_cot + jnp.pad(edge_back, ((row_count - (CONV - 1), 0), (0, 0)))
    projected_cot = jnp.concatenate(
        [gate_cot, xbc_cot, dt_cot, jnp.zeros((row_count, WIDE - PROJ), jnp.float32)], axis=1
    ).astype(jnp.bfloat16)
    in_term = contract_rows(normed, projected_cot).astype(jnp.bfloat16)
    out_term = contract_rows(cotangent, gated).astype(jnp.bfloat16)
    normed_cot = contract_cols(projected_cot, in_whole)
    input_part, norm_gain_grad = norm_back(normed_cot)
    input_grad = cotangent.astype(jnp.float32) + input_part
    small = (
        norm_gain_grad,
        conv_weight_grad.T,
        conv_bias_grad,
        gated_gain_grad,
        dt_bias_grad,
        a_log_grad,
        skip_grad,
    )
    flat = jnp.concatenate([a.reshape(-1) for a in small])
    tile = 8 * LANES
    flat = jnp.pad(flat, (0, -flat.shape[0] % tile))
    in_proj_grad, out_proj_grad, summed = sum_to_owners(
        [in_term, out_term], flat.reshape(-1, LANES), collective_id=4
    )
    summed = summed.reshape(-1)
    parts, at = [], 0
    for a in small:
        parts.append(summed[at : at + a.size].reshape(a.shape))
        at += a.size
    return (
        layer_out,
        input_grad,
        in_proj_grad[:, :PROJ],
        out_proj_grad,
        parts[0],
        parts[1].T,
        parts[2],
        parts[4],
        parts[5],
        parts[6],
        parts[3],
    )


QUAD = 4
CHUNK = 128
TAIL = 16
QCH = DI // QUAD
QHEADS = HEADS // QUAD
PAIRS = QCH // LANES
BC = 2 * STATE
QXBC = QCH + BC
SLAB = QXBC + LANES
PARTS = 3
PART = SLAB // PARTS
GRAD_ROWS = 8


def flip(value, bit):
    return value + (1 - 2 * bit_at(value, bit)) * 2**bit


def flip_quad(value, mask):
    for bit in range(2):
        if mask >> bit & 1:
            value = flip(value, bit)
    return value


def dot_nn(left, right):
    return lax.dot_general(
        left, right, (((1,), (0,)), ((), ())), preferred_element_type=jnp.float32
    )


def dot_nt(left, right):
    return lax.dot_general(
        left, right, (((1,), (1,)), ((), ())), preferred_element_type=jnp.float32
    )


def dot_tn(left, right):
    return lax.dot_general(
        left, right, (((0,), (0,)), ((), ())), preferred_element_type=jnp.float32
    )


def in_parts(value, count):
    parts = []
    for _ in range(count):
        part = value.astype(jnp.bfloat16)
        parts.append(part)
        value = value - part.astype(jnp.float32)
    return parts


def lane_tile(i):
    return pl.ds(i * LANES, LANES)


def chunk_rows(c, offset=0, count=CHUNK):
    return pl.ds(pl.multiple_of(c * CHUNK + offset, 8), count)


def column_sum(value):
    return jnp.sum(value, axis=0, keepdims=True)


def block_kernel(
    x_ref,
    gain_ref,
    in_ref,
    taps_ref,
    bias_ref,
    dt_bias_ref,
    a_log_ref,
    skip_ref,
    gated_gain_ref,
    proj_ref,
    cot_ref,
    out_ref,
    grad_ref,
    in_grad_ref,
    proj_grad_ref,
    gain_grad_ref,
    taps_grad_ref,
    bias_grad_ref,
    dt_bias_grad_ref,
    a_log_grad_ref,
    skip_grad_ref,
    gated_gain_grad_ref,
    early_ref,
    late_ref,
    xq,
    cq,
    xtail,
    early_slots,
    late_slots,
    early_w,
    late_w,
    xn,
    proj,
    act,
    act_slope,
    step_s,
    step_slope,
    log_s,
    cum_s,
    sx_s,
    fresh_s,
    state_out,
    state_come,
    state_s,
    weights_s,
    scores_s,
    ssd_s,
    gate_s,
    gc_s,
    m_s,
    sums_s,
    gated_s,
    gate_cot_s,
    y_s,
    z_s,
    back_s,
    later_s,
    cross_s,
    sx_cot_s,
    pre_cot_s,
    early_cot_s,
    late_term,
    early_term,
    mixed_s,
    mixed_come,
    normed_t,
    cot_t,
    normed_cot_s,
    normed_out,
    normed_come,
    tail_out,
    tail_come,
    small_s,
    skip_s,
    small_come,
    small_quad,
    *rest,
):
    stream_held = [rest[4 * i : 4 * i + 4] for i in range(1 + PARTS)]
    send_sem, recv_sem = rest[4 + 4 * PARTS :]
    f32, bf16 = jnp.float32, jnp.bfloat16
    dp_at, seq_at = places()
    q, g = seq_at % QUAD, seq_at // QUAD
    core, y_at = dp_at % 2, dp_at // 2
    place = dp_at * 8 + seq_at
    used = [0]
    sent = []

    barrier = pltpu.get_barrier_semaphore()
    peers = [(dp_at, (seq_at + hop) % 8) for hop in range(1, 8)]
    peers += [(flip(dp_at, 0), seq_at), (flip(dp_at, 1), seq_at)]
    peers += [(flip(dp_at, 1), flip(seq_at, 2))]
    for peer in peers:
        pl.semaphore_signal(barrier, inc=1, device_id=peer, device_id_type=MESH)

    def remote(source, landing, target, own=True):
        at = used[0]
        used[0] += 1
        copy = pltpu.make_async_remote_copy(
            src_ref=source,
            dst_ref=landing,
            send_sem=send_sem.at[at],
            recv_sem=recv_sem.at[at],
            device_id=target,
            device_id_type=MESH,
        )
        if own:
            copy.start()
            sent.append(copy)
        return copy

    def in_quad(mask):
        return dp_at, flip_quad(seq_at, mask)

    far = (dp_at, flip(seq_at, 2))
    beside = (flip(dp_at, 1), seq_at)
    twin = (flip(dp_at, 0), seq_at)

    def arrived(copies):
        for copy in copies:
            copy.wait_recv()

    lane = lax.broadcasted_iota(jnp.int32, (1, LANES), 1)
    first_half = lane < HEAD_DIM
    half0 = jnp.where(first_half, 1.0, 0.0)
    half1 = 1.0 - half0
    half0b, half1b = half0.astype(bf16), half1.astype(bf16)
    row_at = lax.broadcasted_iota(jnp.int32, (CHUNK, CHUNK), 0)
    lane_at = lax.broadcasted_iota(jnp.int32, (CHUNK, CHUNK), 1)
    causal = row_at >= lane_at
    lower = jnp.where(causal, 1.0, 0.0).astype(bf16)
    upper = jnp.where(row_at <= lane_at, 1.0, 0.0).astype(bf16)
    lower3 = jnp.concatenate([lower] * 3, axis=1)
    upper3 = jnp.concatenate([upper] * 3, axis=1)

    def spread(by_head, i):
        return jnp.where(first_half, by_head[:, 2 * i : 2 * i + 1], by_head[:, 2 * i + 1 : 2 * i + 2])

    def head_sum(value, i):
        owner = 2 * i + row_at // HEAD_DIM
        pick = jnp.where(owner == lane_at, 1.0, 0.0).astype(bf16)
        return dot_nn(
            jnp.concatenate(in_parts(value, 2), axis=1), jnp.concatenate([pick] * 2, axis=0)
        )

    def flat_row(ref, low, count):
        return ref[pl.ds(low, count)].reshape(1, count)

    def own_channels(i):
        return pl.ds(pl.multiple_of(q * QCH + i * LANES, LANES), LANES)

    def conv_channels(i):
        return own_channels(i) if i < PAIRS else pl.ds(DI + (i - PAIRS) * LANES, LANES)

    def tap(k, i):
        return taps_ref[pl.ds(k, 1), conv_channels(i)]

    def gated_gain(i):
        return gated_gain_ref[own_channels(i)].reshape(1, LANES)

    def own_heads(ref):
        head_at = lax.broadcasted_iota(jnp.int32, (HEADS, LANES), 0)
        to = lax.broadcasted_iota(jnp.int32, (HEADS, LANES), 1)
        pick = jnp.where((head_at == to + q * QHEADS) & (to < QHEADS), 1.0, 0.0)
        value = jnp.broadcast_to(ref[...].reshape(1, HEADS), (8, HEADS))
        return inner_product(value, pick, ((1,), (0,)))[:1]

    def stacked(value):
        return jnp.concatenate([value * half0b, value * half1b], axis=0)

    for j in range(QUAD):
        own = pl.ds(j * QCH, QCH)
        early_ref[j, :, pl.ds(0, QCH)] = in_ref[:, pl.ds(DI + j * QCH, QCH)]
        early_ref[j, :, pl.ds(QCH, BC)] = in_ref[:, pl.ds(2 * DI, BC)]
        head_at = lax.broadcasted_iota(jnp.int32, (HEADS, LANES), 0)
        to = lax.broadcasted_iota(jnp.int32, (HEADS, LANES), 1)
        pick = jnp.where((head_at == to + j * QHEADS) & (to < QHEADS), 1.0, 0.0)
        early_ref[j, :, pl.ds(QXBC, LANES)] = dot_nn(
            in_ref[:, pl.ds(DI + XBC, HEADS)], pick.astype(bf16)
        ).astype(bf16)
        late_ref[j, :, pl.ds(0, QCH)] = in_ref[:, own]
        late_ref[j, :, pl.ds(QCH, QCH)] = proj_ref[:, own]

    pl.semaphore_wait(barrier, len(peers))

    def scatter(shard, slots):
        return [
            remote(shard.at[flip_quad(q, mask)], slots.at[place], in_quad(mask))
            for mask in (1, 2, 3)
        ]

    early_0 = scatter(early_ref, early_slots)
    token_copies = [remote(x_ref, xq.at[q], in_quad(mask)) for mask in (1, 2, 3)]
    tail_sends = [
        remote(x_ref.at[pl.ds(CHUNK - TAIL, TAIL)], xtail, (dp_at, QUAD + i), own=False)
        for i in range(QUAD)
    ]
    at_end = seq_at == QUAD - 1

    @pl.when(at_end)
    def _():
        for copy in tail_sends:
            copy.start()

    early_slots[place] = early_ref[q]
    late_slots[place] = late_ref[q]
    xq[q] = x_ref[...]
    cq[q] = cot_ref[...]

    def cross_far(slots):
        return [
            remote(
                slots.at[pl.ds(dp_at * 8 + g * 4, 4), :, lane_part],
                slots.at[pl.ds(dp_at * 8 + g * 4, 4), :, lane_part],
                far,
            )
            for lane_part in [pl.ds(part * PART, PART) for part in range(PARTS)]
        ]

    def cross_beside(slots, copies):
        made = []
        for part, copy in enumerate(copies):
            copy.wait_recv()
            view = slots.at[pl.ds(dp_at * 8, 8), :, pl.ds(part * PART, PART)]
            made.append(remote(view, view, beside))
        return made

    def cross_twin(slots, copies):
        made = []
        for part, copy in enumerate(copies):
            copy.wait_recv()
            for up in range(2):
                view = slots.at[pl.ds((2 * up + core) * 8, 8), :, pl.ds(part * PART, PART)]
                made.append(remote(view, view, twin))
        return made

    def flatten(slots, flat):
        def one(pair, carry):
            value = slots[pl.ds(2 * pair, 2)].astype(f32).reshape(48, SLAB)
            flat[pl.ds(pl.multiple_of(pair * 48, 16), 48), :] = value.astype(bf16)
            return carry

        lax.fori_loop(0, 16, one, 0)

    arrived(early_0)
    early_1 = cross_far(early_slots)
    late_0 = scatter(late_ref, late_slots)
    early_2 = cross_beside(early_slots, early_1)
    arrived(late_0)
    late_1 = cross_far(late_slots)
    cot_copies = [remote(cot_ref, cq.at[q], in_quad(mask)) for mask in (1, 2, 3)]

    arrived(token_copies)

    for i in range(QUAD):

        @pl.when((g == 1) & (q == i))
        def _():
            tail_sends[i].wait_recv()

    @pl.when(g == 0)
    def _():
        xtail[...] = jnp.zeros_like(xtail)

    gain = flat_row(gain_ref, 0, x_ref.shape[1])

    def scaled_rows(value):
        value = value.astype(f32)
        return value * lax.rsqrt(jnp.mean(value * value, axis=-1, keepdims=True) + EPS)

    xn[pl.ds(0, TAIL), :] = (scaled_rows(xtail[...]) * gain).astype(bf16)

    def norm_block(c, carry):
        value = scaled_rows(xq[c]) * gain
        xn[pl.ds(pl.multiple_of(c * CHUNK + TAIL, 16), CHUNK), :] = value.astype(bf16)
        normed_t[:, pl.ds(pl.multiple_of(c * CHUNK, CHUNK), CHUNK)] = value.T.astype(bf16)
        return carry

    lax.fori_loop(0, QUAD, norm_block, 0)
    early_3 = cross_twin(early_slots, early_2)
    late_2 = cross_beside(late_slots, late_1)
    small_s[...] = jnp.zeros_like(small_s)
    skip_s[...] = jnp.zeros_like(skip_s)
    pre_cot_s[pl.ds(0, TAIL), :] = jnp.zeros((TAIL, QXBC), f32)
    pre_cot_s[pl.ds(TAIL + QUAD * CHUNK, 8), :] = jnp.zeros((8, QXBC), f32)
    arrived(early_3)
    flatten(early_slots, early_w)

    for n in range(3):
        cols = pl.ds(n * 256, 256)
        proj[:, cols] = dot_nn(xn[...], early_w[:, cols])

    rate = -jnp.exp(own_heads(a_log_ref))
    dt_bias = own_heads(dt_bias_ref)
    skips = own_heads(skip_ref)
    skip_wide = [spread(skips, i) for i in range(PAIRS)]
    head_lane = lane < QHEADS

    def forward_states(c, carry):
        rows = chunk_rows(c)
        for i in range(QXBC // LANES):
            lanes = lane_tile(i)
            window = proj[chunk_rows(c, 8, CHUNK + 8), lanes]
            total = bias_ref[conv_channels(i)].reshape(1, LANES)
            for k in range(CONV):
                total = total + tap(k, i) * pltpu.roll(window, CHUNK + 3 - k, 0)[:CHUNK]
            sig = lax.logistic(total)
            act[rows, lanes] = total * sig
            act_slope[rows, lanes] = sig * (1.0 + total * (1.0 - sig))
        raw = proj[chunk_rows(c, TAIL), pl.ds(QXBC, LANES)] + dt_bias
        step = jnp.maximum(raw, 0.0) + jnp.log1p(jnp.exp(-jnp.abs(raw)))
        step = jnp.where(head_lane, step, 0.0)
        log_decay = step * rate
        cum = dot_nn(lower3, jnp.concatenate(in_parts(log_decay, 3), axis=0))
        step_s[rows, :] = step
        step_slope[rows, :] = lax.logistic(raw)
        log_s[rows, :] = log_decay
        cum_s[rows, :] = cum
        tail = jnp.exp(cum[CHUNK - 1 :] - cum)
        b_mat = act[rows, pl.ds(QCH, STATE)].astype(bf16)
        for i in range(PAIRS):
            lanes = lane_tile(i)
            sx = act[rows, lanes] * spread(step, i)
            sx_s[rows, lanes] = sx.astype(bf16)
            fresh_s[c, i] = dot_tn(b_mat, (sx * spread(tail, i)).astype(bf16))
        return carry

    lax.fori_loop(0, QUAD, forward_states, 0)

    def chunk_decay(c, i):
        last = cum_s[chunk_rows(c, CHUNK - 8, 8), :][7:]
        return spread(jnp.exp(last), i)

    for i in range(PAIRS):
        total = fresh_s[0, i]
        for c in range(1, QUAD):
            total = chunk_decay(c, i) * total + fresh_s[c, i]
        state_out[i] = total.astype(bf16)
    state_copy = remote(state_out, state_come, far)
    late_3 = cross_twin(late_slots, late_2)

    def forward_local(c, carry):
        rows = chunk_rows(c)
        b_mat = act[rows, pl.ds(QCH, STATE)].astype(bf16)
        c_mat = act[rows, pl.ds(QCH + STATE, STATE)].astype(bf16)
        crossed = dot_nt(c_mat, b_mat)
        cum = cum_s[rows, :]
        cum_t = cum.T
        for i in range(PAIRS):
            lanes = lane_tile(i)
            pair = []
            for head in (2 * i, 2 * i + 1):
                gap = cum[:, head : head + 1] - cum_t[head : head + 1, :]
                pair.append(jnp.exp(jnp.where(causal, gap, -1e30)))
            weights_s[c, i] = jnp.concatenate(pair, axis=1).astype(bf16)
            scores = jnp.concatenate([w * crossed for w in pair], axis=1).astype(bf16)
            scores_s[c, i] = scores
            ssd_s[rows, lanes] = dot_nn(scores, stacked(sx_s[rows, lanes]))
        return carry

    lax.fori_loop(0, QUAD, forward_local, 0)
    arrived(late_3)
    flatten(late_slots, late_w)
    gate_w = pl.ds(0, QCH)
    out_w = pl.ds(QCH, QCH)
    gate_s[...] = dot_nn(xn[pl.ds(TAIL, QUAD * CHUNK), :], late_w[:, gate_w])
    arrived(cot_copies)

    def cot_block(c, carry):
        gc_s[chunk_rows(c), :] = dot_nn(cq[c], late_w[:, out_w])
        return carry

    lax.fori_loop(0, QUAD, cot_block, 0)
    state_copy.wait_recv()
    for i in range(PAIRS):
        total = jnp.where(g == 1, state_come[i].astype(f32), 0.0)
        for c in range(QUAD):
            state_s[c, i] = total.astype(bf16)
            if c < QUAD - 1:
                total = chunk_decay(c, i) * total + fresh_s[c, i]

    def forward_gate(c, carry):
        rows = chunk_rows(c)
        c_mat = act[rows, pl.ds(QCH + STATE, STATE)].astype(bf16)
        grown = jnp.exp(cum_s[rows, :])
        square, crossed = 0.0, 0.0
        for i in range(PAIRS):
            lanes = lane_tile(i)
            ssd = ssd_s[rows, lanes] + dot_nn(c_mat, state_s[c, i]) * spread(grown, i)
            ssd_s[rows, lanes] = ssd
            gate = gate_s[rows, lanes]
            m = (ssd + act[rows, lanes] * skip_wide[i]) * gate * lax.logistic(gate)
            m_s[rows, lanes] = m
            square = square + m * m
            crossed = crossed + gc_s[rows, lanes] * gated_gain(i) * m
        square = jnp.sum(square, axis=1, keepdims=True)
        crossed = jnp.sum(crossed, axis=1, keepdims=True)
        both = jnp.where(lane == 0, square, jnp.where(lane == 1, crossed, 0.0))
        sums_s[q, :, pl.ds(pl.multiple_of(c * CHUNK, CHUNK), CHUNK)] = (
            both.T[:8]
        )
        return carry

    lax.fori_loop(0, QUAD, forward_gate, 0)
    sums_copies = [remote(sums_s.at[q], sums_s.at[q], in_quad(mask)) for mask in (1, 2, 3)]

    def turn_cot(c, carry):
        cot_t[:, pl.ds(pl.multiple_of(c * CHUNK, CHUNK), CHUNK)] = (
            cq[c].astype(f32).T.astype(bf16)
        )
        return carry

    lax.fori_loop(0, QUAD, turn_cot, 0)
    arrived(sums_copies)

    def backward_states(c, carry):
        rows = chunk_rows(c)
        cols = pl.ds(pl.multiple_of(c * CHUNK, CHUNK), CHUNK)
        sums = sums_s[0, :, cols] + sums_s[1, :, cols] + sums_s[2, :, cols] + sums_s[3, :, cols]
        sums = jnp.concatenate([sums] * (CHUNK // 8), axis=0).T
        scale = lax.rsqrt(sums[:, 0:1] * (1.0 / DI) + EPS)
        pull = scale * scale * scale * (sums[:, 1:2] * (1.0 / DI))
        c_mat = act[rows, pl.ds(QCH + STATE, STATE)].astype(bf16)
        grown = jnp.exp(cum_s[rows, :])
        for i in range(PAIRS):
            lanes = lane_tile(i)
            m, gc, gate = m_s[rows, lanes], gc_s[rows, lanes], gate_s[rows, lanes]
            xs = act[rows, lanes]
            mr = m * scale
            gated_s[rows, lanes] = (mr * gated_gain(i)).astype(bf16)
            small_s[5:6, lanes] += column_sum(gc * mr)
            m_cot = scale * (gc * gated_gain(i)) - m * pull
            sig = lax.logistic(gate)
            mixed = ssd_s[rows, lanes] + xs * skip_wide[i]
            gate_cot_s[rows, lanes] = (
                m_cot * mixed * (sig * (1.0 + gate * (1.0 - sig)))
            ).astype(bf16)
            y = m_cot * gate * sig
            y_s[rows, lanes] = y
            skip_s[0:1, lanes] += column_sum(y * xs)
            z = (y * spread(grown, i)).astype(bf16)
            z_s[rows, lanes] = z
            back_s[c, i] = dot_tn(c_mat, z)
        return carry

    lax.fori_loop(0, QUAD, backward_states, 0)
    state_copy.wait_send()
    sent[:] = [copy for copy in sent if copy is not state_copy]
    for i in range(PAIRS):
        total = back_s[QUAD - 1, i]
        for c in range(QUAD - 2, -1, -1):
            total = chunk_decay(c, i) * total + back_s[c, i]
        state_out[i] = total.astype(bf16)
    later_copy = remote(state_out, later_s.at[QUAD], far)

    def term_rows(term, half, value, lanes):
        term[pl.ds(half * 16, 16), :, lanes] = value.reshape(16, 24, value.shape[1]).astype(bf16)

    def late_half(half, carry):
        own = pl.ds(pl.multiple_of(half * QCH, QCH), QCH)
        term_rows(late_term, half, dot_nn(normed_t[own, :], gate_cot_s[...]), gate_w)
        term_rows(late_term, half, dot_nn(cot_t[own, :], gated_s[...]), out_w)
        return carry

    lax.fori_loop(0, 2, late_half, 0)

    streams = [(late_term, pl.ds(0, SLAB))] + [
        (early_term, pl.ds(i * PART, PART)) for i in range(PARTS)
    ]

    def reduce_twin(stream):
        term, lanes = streams[stream]
        return [
            remote(
                term.at[pl.ds((2 * up + 1 - core) * 8, 8), :, lanes],
                stream_held[stream][0].at[pl.ds(8 * up, 8)],
                twin,
            )
            for up in range(2)
        ]

    def reduce_beside(stream, copies):
        arrived(copies)
        term, lanes = streams[stream]
        held = stream_held[stream][0]

        def add(slot, carry):
            mine = (2 * (slot // 8) + core) * 8 + slot % 8
            held[slot] = (term[mine, :, lanes].astype(f32) + held[slot].astype(f32)).astype(bf16)
            return carry

        lax.fori_loop(0, 16, add, 0)
        return [remote(held.at[pl.ds((1 - y_at) * 8, 8)], stream_held[stream][1], beside)]

    def reduce_far(stream, copies):
        arrived(copies)
        before, held = stream_held[stream][:2]

        def add(slot, carry):
            held[slot] = (
                before[y_at * 8 + slot].astype(f32) + held[slot].astype(f32)
            ).astype(bf16)
            return carry

        lax.fori_loop(0, 8, add, 0)
        return [remote(held.at[pl.ds((1 - g) * 4, 4)], stream_held[stream][2], far)]

    def reduce_quad(stream, copies):
        arrived(copies)
        before, held, result = stream_held[stream][1:]

        def add(slot, carry):
            held[slot] = (before[g * 4 + slot].astype(f32) + held[slot].astype(f32)).astype(bf16)
            return carry

        lax.fori_loop(0, 4, add, 0)
        made = [
            remote(held.at[flip_quad(q, mask)], result.at[q], in_quad(mask)) for mask in (1, 2, 3)
        ]
        result[q] = held[q]
        return made

    late_r0 = reduce_twin(0)

    def mixed_block(c, carry):
        mixed_s[c] = dot_nt(gated_s[chunk_rows(c), :], late_w[:, out_w]).astype(bf16)
        return carry

    lax.fori_loop(0, QUAD, mixed_block, 0)
    mixed_copies = [
        remote(mixed_s.at[flip_quad(q, mask)], mixed_come.at[mask - 1], in_quad(mask))
        for mask in (1, 2, 3)
    ]

    def backward_local(c, carry):
        rows = chunk_rows(c)
        total = jnp.zeros((CHUNK, CHUNK), f32)
        for i in range(PAIRS):
            lanes = lane_tile(i)
            y = y_s[rows, lanes].astype(bf16)
            moved = weights_s[c, i].astype(f32) * dot_nt(y, stacked(sx_s[rows, lanes]))
            total = total + moved[:, :CHUNK] + moved[:, CHUNK:]
            both = dot_tn(scores_s[c, i], y)
            sx_cot_s[rows, lanes] = both[:CHUNK] * half0 + both[CHUNK:] * half1
        cross_s[c] = total.astype(bf16)
        return carry

    lax.fori_loop(0, QUAD, backward_local, 0)
    late_r1 = reduce_beside(0, late_r0)
    later_copy.wait_recv()
    for i in range(PAIRS):
        total = jnp.where(g == 0, later_s[QUAD, i].astype(f32), 0.0)
        for c in range(QUAD - 1, -1, -1):
            later_s[c, i] = total.astype(bf16)
            if c > 0:
                total = chunk_decay(c, i) * total + back_s[c, i]

    def backward_mix(c, carry):
        rows = chunk_rows(c)
        shifted = chunk_rows(c, TAIL)
        b_mat = act[rows, pl.ds(QCH, STATE)].astype(bf16)
        c_mat = act[rows, pl.ds(QCH + STATE, STATE)].astype(bf16)
        cum, step = cum_s[rows, :], step_s[rows, :]
        tail = jnp.exp(cum[CHUNK - 1 :] - cum)
        decay = jnp.exp(cum[CHUNK - 1 :])
        cross = cross_s[c]
        b_cot = dot_tn(cross, c_mat)
        c_cot = dot_nn(cross, b_mat)
        cum_cot = jnp.zeros((CHUNK, LANES), f32)
        step_cot = jnp.zeros((CHUNK, LANES), f32)
        last_cot = jnp.zeros((8, LANES), f32)
        for i in range(PAIRS):
            lanes = lane_tile(i)
            xs, y = act[rows, lanes], y_s[rows, lanes]
            later, state = later_s[c, i], state_s[c, i]
            wide_step, wide_tail = spread(step, i), spread(tail, i)
            tailed = (xs * wide_step * wide_tail).astype(bf16)
            from_later = dot_nn(b_mat, later) * wide_tail
            b_cot = b_cot + dot_nt(tailed, later)
            c_cot = c_cot + dot_nt(z_s[rows, lanes], state)
            sx = sx_s[rows, lanes].astype(f32)
            sx_cot = sx_cot_s[rows, lanes] + from_later
            cum_cot = cum_cot + head_sum(
                y.astype(bf16).astype(f32) * ssd_s[rows, lanes] - sx * sx_cot, i
            )
            step_cot = step_cot + head_sum(sx_cot * xs, i)
            last = column_sum(sx * from_later) + column_sum(
                later.astype(f32) * state.astype(f32)
            ) * spread(decay, i)
            last_cot = last_cot + head_sum(jnp.broadcast_to(last, (8, LANES)), i)
            pre_cot_s[shifted, lanes] = (
                sx_cot * wide_step + y * skip_wide[i]
            ) * act_slope[rows, lanes]
        pre_cot_s[shifted, pl.ds(QCH, STATE)] = b_cot * act_slope[rows, pl.ds(QCH, STATE)]
        pre_cot_s[shifted, pl.ds(QCH + STATE, STATE)] = (
            c_cot * act_slope[rows, pl.ds(QCH + STATE, STATE)]
        )
        log_cot = dot_nn(upper3, jnp.concatenate(in_parts(cum_cot, 3), axis=0)) + last_cot[:1]
        dt_cot = (step_cot + log_cot * rate) * step_slope[rows, :]
        small_s[7:8, lane_tile(1)] += column_sum(log_cot * log_s[rows, :])
        small_s[5:6, lane_tile(4)] += column_sum(dt_cot)
        early_cot_s[pl.ds(pl.multiple_of(c * CHUNK + TAIL, 16), CHUNK), pl.ds(QXBC, LANES)] = (
            dt_cot.astype(bf16)
        )
        return carry

    lax.fori_loop(0, QUAD, backward_mix, 0)
    late_r2 = reduce_far(0, late_r1)
    early_cot_s[pl.ds(0, TAIL), pl.ds(QXBC, LANES)] = jnp.zeros((TAIL, LANES), bf16)

    for i in range(QXBC // LANES):
        lanes = lane_tile(i)
        edge = pre_cot_s[pl.ds(0, 24), lanes]
        total = tap(CONV - 1, i) * edge[:TAIL]
        for k in range(CONV - 1):
            total = total + tap(k, i) * pltpu.roll(edge, 24 - (3 - k), 0)[:TAIL]
        early_cot_s[pl.ds(0, TAIL), lanes] = total.astype(bf16)

    def backward_conv(c, carry):
        shifted = pl.ds(pl.multiple_of(c * CHUNK + TAIL, 16), CHUNK)
        for i in range(QXBC // LANES):
            lanes = lane_tile(i)
            cots = pre_cot_s[chunk_rows(c, TAIL, CHUNK + 8), lanes]
            window = proj[chunk_rows(c, 8, CHUNK + 8), lanes]
            cot = cots[:CHUNK]
            total = tap(CONV - 1, i) * cot
            for k in range(CONV - 1):
                total = total + tap(k, i) * pltpu.roll(cots, CHUNK + 8 - (3 - k), 0)[:CHUNK]
            early_cot_s[shifted, lanes] = total.astype(bf16)
            for k in range(CONV):
                small_s[k : k + 1, lanes] += column_sum(
                    cot * pltpu.roll(window, CHUNK + 3 - k, 0)[:CHUNK]
                )
            small_s[4:5, lanes] += column_sum(cot)
        return carry

    lax.fori_loop(0, QUAD, backward_conv, 0)

    heads = jnp.zeros((8, LANES), f32)
    for i in range(PAIRS):
        heads = heads + head_sum(jnp.broadcast_to(skip_s[0:1, lane_tile(i)], (8, LANES)), i)
    small_s[5:6, lane_tile(3)] = heads[:1]

    tail_value = dot_nt(early_cot_s[pl.ds(0, TAIL), :], early_w[...])
    tail_out[...] = tail_value
    tail_index = used[0]
    used[0] += QUAD

    def tail_copy(i):
        return pltpu.make_async_remote_copy(
            src_ref=tail_out,
            dst_ref=tail_come.at[i],
            send_sem=send_sem.at[tail_index + i],
            recv_sem=recv_sem.at[tail_index + i],
            device_id=(dp_at, QUAD - 1),
            device_id_type=MESH,
        )

    for i in range(QUAD):

        @pl.when((g == 1) & (q == i))
        def _():
            tail_copy(i).start()

    def add_gain(value, rows):
        total = column_sum(value * scaled_rows(rows))
        small_s[6:7, :] += total[:, :QXBC]
        small_s[7:8, lane_tile(0)] += total[:, QXBC:]

    add_gain(tail_value, xtail[...])

    def normed_block(c, carry):
        rows = pl.ds(pl.multiple_of(c * CHUNK + TAIL, 16), CHUNK)
        value = dot_nt(early_cot_s[rows, :], early_w[...]) + dot_nt(
            gate_cot_s[chunk_rows(c), :], late_w[:, gate_w]
        )
        normed_cot_s[c] = value
        normed_out[c] = value.astype(bf16)
        add_gain(value, xq[c])
        return carry

    lax.fori_loop(0, QUAD, normed_block, 0)
    normed_copies = [
        remote(normed_out.at[flip_quad(q, mask)], normed_come.at[mask - 1], in_quad(mask))
        for mask in (1, 2, 3)
    ]
    small_copy = remote(small_s, small_come.at[0], twin)
    early_r0 = []
    for part in range(PARTS):
        lanes = pl.ds(part * PART, PART)

        def early_half(half, carry, lanes=lanes):
            own = pl.ds(pl.multiple_of(half * QCH, QCH), QCH)
            value = dot_nn(normed_t[own, :], early_cot_s[pl.ds(TAIL, QUAD * CHUNK), lanes])
            value = value + dot_tn(xn[pl.ds(0, TAIL), own], early_cot_s[pl.ds(0, TAIL), lanes])
            term_rows(early_term, half, value, lanes)
            return carry

        lax.fori_loop(0, 2, early_half, 0)
        early_r0.append(reduce_twin(1 + part))

    early_r1 = [reduce_beside(1 + part, early_r0[part]) for part in range(PARTS)]

    early_r2 = [reduce_far(1, early_r1[0])]
    small_copy.wait_recv()
    small_come[4] = small_s[...] + small_come[0]
    across = (flip(dp_at, 1), flip(seq_at, 2))
    small_copies = [
        remote(small_come.at[4], small_come.at[1 + i], target)
        for i, target in enumerate((beside, far, across))
    ]
    early_r2.append(reduce_far(2, early_r1[1]))
    late_r3 = reduce_quad(0, late_r2)
    early_r2.append(reduce_far(3, early_r1[2]))
    arrived(small_copies)
    small_quad[q] = small_come[4] + small_come[1] + (small_come[2] + small_come[3])
    small_copies = [remote(small_quad.at[q], small_quad.at[q], in_quad(mask)) for mask in (1, 2, 3)]

    arrived(mixed_copies)
    total = x_ref[...].astype(f32) + mixed_s[q].astype(f32)
    for mask in range(3):
        total = total + mixed_come[mask].astype(f32)
    out_ref[...] = total.astype(bf16)
    early_r3 = [reduce_quad(1 + part, early_r2[part]) for part in range(PARTS)]

    arrived(normed_copies)
    value = normed_cot_s[q]
    for mask in range(3):
        value = value + normed_come[mask].astype(f32)
    normed_cot_s[q] = value

    @pl.when(at_end)
    def _():
        for i in range(QUAD):
            tail_copy(i).wait_recv()
        rows = pl.ds(CHUNK - TAIL, TAIL)
        normed_cot_s[q, rows, :] += tail_come[0] + tail_come[1] + tail_come[2] + tail_come[3]

    cot = normed_cot_s[q] * gain
    rows = x_ref[...].astype(f32)
    scale = lax.rsqrt(jnp.mean(rows * rows, axis=-1, keepdims=True) + EPS)
    pull = scale * scale * scale * jnp.mean(cot * rows, axis=-1, keepdims=True)
    grad_ref[...] = cot_ref[...].astype(f32) + scale * cot - rows * pull

    arrived(small_copies)
    for j in range(QUAD):
        own = pl.ds(j * QCH, QCH)
        taps_grad_ref[:, own] = small_quad[j, 0:CONV, pl.ds(0, QCH)]
        bias_grad_ref[own] = small_quad[j, CONV : CONV + 1, pl.ds(0, QCH)].reshape(QCH)
        gated_gain_grad_ref[own] = small_quad[j, 5:6, pl.ds(0, QCH)].reshape(QCH)
    quads = small_quad[0] + small_quad[1] + small_quad[2] + small_quad[3]
    taps_grad_ref[:, pl.ds(DI, BC)] = quads[:CONV, QCH:QXBC]
    bias_grad_ref[pl.ds(DI, BC)] = quads[CONV : CONV + 1, QCH:QXBC].reshape(BC)
    gain_grad_ref[pl.ds(0, QXBC)] = quads[6:7].reshape(QXBC)
    gain_grad_ref[pl.ds(QXBC, LANES)] = quads[7:8, :LANES].reshape(LANES)

    def in_head_order(parts):
        total = parts[0]
        for j in range(1, QUAD):
            total = total + pltpu.roll(parts[j], j * QHEADS, 1)
        return total[:, :HEADS]

    def small_heads(row, i):
        parts = [small_quad[j, :, lane_tile(i)] for j in range(QUAD)]
        return in_head_order(parts)[row : row + 1].reshape(HEADS)

    skip_grad_ref[...] = small_heads(5, 3)
    dt_bias_grad_ref[...] = small_heads(5, 4)
    a_log_grad_ref[...] = small_heads(7, 1)

    arrived(late_r3)
    for j in range(QUAD):
        own = pl.ds(j * QCH, QCH)
        in_grad_ref[:, own] = stream_held[0][3][j, :, pl.ds(0, QCH)].astype(f32)
        proj_grad_ref[:, own] = stream_held[0][3][j, :, pl.ds(QCH, QCH)].astype(f32)
    for part in range(PARTS):
        arrived(early_r3[part])

    def early_result(j, low):
        return stream_held[1 + low // PART][3][j, :, pl.ds(low % PART, LANES)].astype(f32)

    for j in range(QUAD):
        for i in range(PAIRS):
            in_grad_ref[:, pl.ds(DI + j * QCH + i * LANES, LANES)] = early_result(j, i * LANES)
    for i in range(BC // LANES):
        total = early_result(0, QCH + i * LANES)
        for j in range(1, QUAD):
            total = total + early_result(j, QCH + i * LANES)
        in_grad_ref[:, pl.ds(2 * DI + i * LANES, LANES)] = total
    in_grad_ref[:, pl.ds(DI + XBC, HEADS)] = in_head_order(
        [early_result(j, QXBC) for j in range(QUAD)]
    )

    for copy in sent:
        copy.wait_send()

    @pl.when(at_end)
    def _():
        for copy in tail_sends:
            copy.wait_send()

    for i in range(QUAD):

        @pl.when((g == 1) & (q == i))
        def _():
            tail_copy(i).wait_send()


def quad_body(
    inputs,
    norm_gain,
    in_proj,
    conv_weight,
    conv_bias,
    dt_bias,
    a_log,
    skip_gain,
    gated_gain,
    out_proj,
    cotangent,
):
    f32, bf16 = jnp.float32, jnp.bfloat16
    rows = in_proj.shape[0]
    tokens = QUAD * CHUNK
    slots = lax.axis_size("dp") * lax.axis_size("seq")
    width = inputs.shape[1]
    vmem = pltpu.VMEM
    held = [
        vmem((count, rows, w), bf16) for w in (SLAB, *[PART] * PARTS) for count in (16, 8, 4, 4)
    ]
    scratch = [
        vmem((QUAD, rows, SLAB), bf16),
        vmem((QUAD, rows, SLAB), bf16),
        vmem((QUAD, CHUNK, width), bf16),
        vmem((QUAD, CHUNK, width), bf16),
        vmem((TAIL, width), bf16),
        vmem((slots, rows, SLAB), bf16),
        vmem((slots, rows, SLAB), bf16),
        vmem((width, SLAB), bf16),
        vmem((width, SLAB), bf16),
        vmem((TAIL + tokens, width), bf16),
        vmem((TAIL + tokens, SLAB), f32),
        vmem((tokens, QXBC), f32),
        vmem((tokens, QXBC), f32),
        vmem((tokens, LANES), f32),
        vmem((tokens, LANES), f32),
        vmem((tokens, LANES), f32),
        vmem((tokens, LANES), f32),
        vmem((tokens, QCH), bf16),
        vmem((QUAD, PAIRS, STATE, LANES), f32),
        vmem((PAIRS, STATE, LANES), bf16),
        vmem((PAIRS, STATE, LANES), bf16),
        vmem((QUAD, PAIRS, STATE, LANES), bf16),
        vmem((QUAD, PAIRS, CHUNK, 2 * CHUNK), bf16),
        vmem((QUAD, PAIRS, CHUNK, 2 * CHUNK), bf16),
        vmem((tokens, QCH), f32),
        vmem((tokens, QCH), f32),
        vmem((tokens, QCH), f32),
        vmem((tokens, QCH), f32),
        vmem((QUAD, 8, tokens), f32),
        vmem((tokens, QCH), bf16),
        vmem((tokens, QCH), bf16),
        vmem((tokens, QCH), f32),
        vmem((tokens, QCH), bf16),
        vmem((QUAD, PAIRS, STATE, LANES), f32),
        vmem((QUAD + 1, PAIRS, STATE, LANES), bf16),
        vmem((QUAD, CHUNK, CHUNK), bf16),
        vmem((tokens, QCH), f32),
        vmem((TAIL + tokens + 8, QXBC), f32),
        vmem((TAIL + tokens, SLAB), bf16),
        vmem((slots, rows, SLAB), bf16),
        vmem((slots, rows, SLAB), bf16),
        vmem((QUAD, CHUNK, width), bf16),
        vmem((3, CHUNK, width), bf16),
        vmem((width, tokens), bf16),
        vmem((width, tokens), bf16),
        vmem((QUAD, CHUNK, width), f32),
        vmem((QUAD, CHUNK, width), bf16),
        vmem((3, CHUNK, width), bf16),
        vmem((TAIL, width), f32),
        vmem((QUAD, TAIL, width), f32),
        vmem((GRAD_ROWS, QXBC), f32),
        vmem((8, QCH), f32),
        vmem((5, GRAD_ROWS, QXBC), f32),
        vmem((QUAD, GRAD_ROWS, QXBC), f32),
        *held,
        pltpu.SemaphoreType.DMA((112,)),
        pltpu.SemaphoreType.DMA((112,)),
    ]
    in_vmem = pl.BlockSpec(memory_space=pltpu.VMEM)
    shapes = [inputs.shape, inputs.shape, in_proj.shape, out_proj.shape]
    shapes += [(width,), (CONV, XBC), (XBC,), (HEADS,), (HEADS,), (HEADS,), (DI,)]
    got = pl.pallas_call(
        block_kernel,
        out_shape=[
            jax.ShapeDtypeStruct(shape, f32 if at else bf16) for at, shape in enumerate(shapes)
        ],
        in_specs=[in_vmem] * 11,
        out_specs=[in_vmem] * 11,
        scratch_shapes=scratch,
        compiler_params=pltpu.CompilerParams(
            collective_id=1, has_side_effects=True, vmem_limit_bytes=VMEM_BYTES
        ),
        name="residual_block",
    )(
        inputs,
        norm_gain,
        in_proj,
        conv_weight.T,
        conv_bias,
        dt_bias,
        a_log,
        skip_gain,
        gated_gain,
        out_proj,
        cotangent,
    )
    got = pl.pallas_call(
        copy_out_kernel,
        out_shape=[jax.ShapeDtypeStruct(value.shape, value.dtype) for value in got],
        in_specs=[in_vmem] * 11,
        out_specs=[pl.BlockSpec(memory_space=pl.ANY)] * 11,
        scratch_shapes=[pltpu.SemaphoreType.DMA((11,))],
        name="copy_out",
    )(*got)
    return (*got[:5], got[5].T, *got[6:])


def copy_out_kernel(*refs):
    count = len(refs) // 2
    sems = refs[2 * count]
    copies = [
        pltpu.make_async_copy(refs[i], refs[count + i], sems.at[i]) for i in range(count)
    ]
    for copy in copies:
        copy.start()
    for copy in copies:
        copy.wait()


def fits_quads(mesh):
    return mesh.shape["dp"] == 4 and mesh.shape["seq"] == 2 * QUAD


def solution(mesh):
    placed = (
        P(("dp", "seq"), None),
        P(),
        P(("dp", "seq"), None),
        P(),
        P(),
        P(),
        P(),
        P(),
        P(),
        P(("dp", "seq"), None),
        P(("dp", "seq"), None),
    )
    return jax.shard_map(
        quad_body if fits_quads(mesh) else body,
        mesh=mesh,
        in_specs=placed,
        out_specs=(
            P(("dp", "seq"), None),
            P(("dp", "seq"), None),
            P(("dp", "seq"), None),
            P(("dp", "seq"), None),
            P(),
            P(),
            P(),
            P(),
            P(),
            P(),
            P(),
        ),
        check_vma=False,
    )
```

```python
from functools import partial

import jax
import jax.numpy as jnp
from jax import lax
from jax.experimental import pallas as pl
from jax.experimental.pallas import tpu as pltpu
from jax.sharding import PartitionSpec as P

HEADS = 24
HEAD_DIM = 64
STATE = 128
CONV = 4
DI = 1536
XBC = 1792
PROJ = DI + XBC + HEADS
LANES = 128
WIDE = -(-PROJ // LANES) * LANES


EPS = 1e-05
HIGH = lax.Precision.HIGHEST
MESH = pl.DeviceIdType.MESH
VMEM_BYTES = 60 * 1024 * 1024


def bits_of(count):
    return count.bit_length() - 1


def bit_at(place, bit):
    return (place // 2**bit) % 2


def places():
    return lax.axis_index("dp"), lax.axis_index("seq")


def partner(bit, seq_bits):
    dp_at, seq_at = places()
    if bit < seq_bits:
        return dp_at, seq_at + (1 - 2 * bit_at(seq_at, bit)) * 2**bit
    up = bit - seq_bits
    return dp_at + (1 - 2 * bit_at(dp_at, up)) * 2**up, seq_at


def greet(bits, seq_bits):
    barrier = pltpu.get_barrier_semaphore()
    for bit in range(bits):
        pl.semaphore_signal(barrier, inc=1, device_id=partner(bit, seq_bits), device_id_type=MESH)
    pl.semaphore_wait(barrier, bits)


def gather_orders(seq_bits, dp_bits):
    x_count = seq_bits // 2
    x_bits = list(range(x_count))
    z_bits = list(range(x_count, seq_bits))[::-1]
    core = [seq_bits]
    y_bits = [seq_bits + 1 + i for i in range(dp_bits - 1)]
    return (
        z_bits + x_bits + y_bits + core,
        z_bits + y_bits + x_bits + core,
        z_bits[:1] + x_bits + y_bits + z_bits[1:] + core,
        z_bits[:1] + y_bits + x_bits + z_bits[1:] + core,
    )


SHARES = (0.3, 0.3, 0.2, 0.2)


def split_lanes(width, shares):
    tiles = width // LANES
    edges = [round(tiles * sum(shares[:i])) * LANES for i in range(len(shares) + 1)]
    return [(low, high - low) for low, high in zip(edges, edges[1:])]


def gather_kernel(seq_bits, streams, bits, *refs):
    array_count = 1 + max(stream[0] for stream in streams)
    shards, outs = refs[:array_count], refs[array_count : 2 * array_count]
    send_sem, recv_sem, own_sem = refs[2 * array_count :]
    dp_at, seq_at = places()
    place = dp_at * 2**seq_bits + seq_at
    own = [
        pltpu.make_async_copy(shard, out.at[place], own_sem.at[i])
        for i, (shard, out) in enumerate(zip(shards, outs))
    ]
    for copy in own:
        copy.start()
    greet(bits, seq_bits)
    for copy in own:
        copy.wait()

    def landed(stream, stage, sem):
        which, low, width, _ = streams[stream]
        view = outs[which].at[pl.ds(0, 2**stage), :, pl.ds(low, width)]
        pltpu.make_async_copy(view, view, sem.at[stream, stage]).wait()

    for stage in range(bits + 1):
        for stream, (which, low, width, order) in enumerate(streams):
            if stage > 0:
                landed(stream, stage - 1, recv_sem)
            if stage == bits:
                continue
            free = order[:stage]
            run = 0
            while run in free:
                run += 1
            base = place
            for bit in free:
                base = base - bit_at(place, bit) * 2**bit
            upper = [bit for bit in free if bit > run]
            for combo in range(2 ** len(upper)):
                start = base + sum(2**bit for i, bit in enumerate(upper) if combo >> i & 1)
                view = outs[which].at[pl.ds(start, 2**run), :, pl.ds(low, width)]
                pltpu.make_async_remote_copy(
                    src_ref=view,
                    dst_ref=view,
                    send_sem=send_sem.at[stream, stage],
                    recv_sem=recv_sem.at[stream, stage],
                    device_id=partner(order[stage], seq_bits),
                    device_id_type=MESH,
                ).start()
    for stage in range(bits):
        for stream in range(len(streams)):
            landed(stream, stage, send_sem)


def gather_all(shards, collective_id):
    seq_bits, dp_bits = bits_of(lax.axis_size("seq")), bits_of(lax.axis_size("dp"))
    bits = seq_bits + dp_bits
    orders = gather_orders(seq_bits, dp_bits)
    streams = [
        (which, low, width, order)
        for which, shard in enumerate(shards)
        for (low, width), order in zip(split_lanes(shard.shape[1], SHARES), orders)
    ]
    return pl.pallas_call(
        partial(gather_kernel, seq_bits, streams, bits),
        out_shape=[jax.ShapeDtypeStruct((2**bits, *a.shape), a.dtype) for a in shards],
        in_specs=[pl.BlockSpec(memory_space=pltpu.VMEM)] * len(shards),
        out_specs=[pl.BlockSpec(memory_space=pl.ANY)] * len(shards),
        scratch_shapes=[
            pltpu.SemaphoreType.DMA((len(streams), bits)),
            pltpu.SemaphoreType.DMA((len(streams), bits)),
            pltpu.SemaphoreType.DMA((len(shards),)),
        ],
        compiler_params=pltpu.CompilerParams(
            collective_id=collective_id, has_side_effects=True, vmem_limit_bytes=VMEM_BYTES
        ),
        name="gather_rows",
    )(*shards)


def sum_kernel(seq_bits, streams, bits, array_count, *refs):
    terms, vector = refs[:array_count], refs[array_count]
    outs, vector_out = refs[array_count + 1 : 2 * array_count + 1], refs[2 * array_count + 1]
    held = refs[2 * array_count + 2 : 2 * array_count + 2 + len(streams) * bits]
    rest = refs[2 * array_count + 2 + len(streams) * bits :]
    vector_in, vector_sum, send_sem, recv_sem, vector_send, vector_recv = rest
    dp_at, seq_at = places()
    place = dp_at * 2**seq_bits + seq_at
    greet(bits, seq_bits)

    def source(stream, stage):
        which, low, width, _ = streams[stream]
        if stage == 0:
            return terms[which], pl.ds(low, width)
        return held[stream * bits + stage - 1], pl.ds(0, width)

    def position(stream, stage):
        order = streams[stream][3]
        remaining = sorted(order[stage:])
        return remaining.index(order[stage]), bit_at(place, order[stage])

    def landed(stream, stage, sem):
        view = held[stream * bits + stage]
        pltpu.make_async_copy(view, view, sem.at[stream, stage]).wait()

    def vector_copy(stage):
        return pltpu.make_async_remote_copy(
            src_ref=vector if stage == 0 else vector_sum.at[stage - 1],
            dst_ref=vector_in.at[stage],
            send_sem=vector_send.at[stage],
            recv_sem=vector_recv.at[stage],
            device_id=partner(stage, seq_bits),
            device_id_type=MESH,
        )

    for stage in range(bits + 1):
        if stage > 0:
            vector_copy(stage - 1).wait_recv()
            before = vector[...] if stage == 1 else vector_sum[stage - 2]
            total = before + vector_in[stage - 1]
            if stage < bits:
                vector_sum[stage - 1] = total
            else:
                vector_out[...] = total
        if stage < bits:
            vector_copy(stage).start()
        for stream, (which, low, width, order) in enumerate(streams):
            if stage > 0:
                landed(stream, stage - 1, recv_sem)
                spot, mine = position(stream, stage - 1)
                kept, lanes = source(stream, stage - 1)
                came = held[stream * bits + stage - 1]
                if stage == bits:
                    outs[which][:, pl.ds(low, width)] = kept[mine, :, lanes].astype(
                        jnp.float32
                    ) + came[0].astype(jnp.float32)
                    continue

                def add_one(block, carry, spot=spot, mine=mine, kept=kept, lanes=lanes, came=came):
                    from_block = (block // 2**spot) * 2 ** (spot + 1) + mine * 2**spot
                    from_block = from_block + block % 2**spot
                    added = kept[from_block, :, lanes].astype(jnp.float32) + came[block].astype(
                        jnp.float32
                    )
                    came[block] = added.astype(came.dtype)
                    return carry

                lax.fori_loop(0, 2 ** (bits - stage), add_one, 0)
            spot, mine = position(stream, stage)
            sent, lanes = source(stream, stage)
            for high in range(2 ** (bits - stage - 1 - spot)):
                start = high * 2 ** (spot + 1) + (1 - mine) * 2**spot
                pltpu.make_async_remote_copy(
                    src_ref=sent.at[pl.ds(start, 2**spot), :, lanes],
                    dst_ref=held[stream * bits + stage].at[pl.ds(high * 2**spot, 2**spot)],
                    send_sem=send_sem.at[stream, stage],
                    recv_sem=recv_sem.at[stream, stage],
                    device_id=partner(order[stage], seq_bits),
                    device_id_type=MESH,
                ).start()
    for stage in range(bits):
        vector_copy(stage).wait_send()
        for stream in range(len(streams)):
            landed(stream, stage, send_sem)


def sum_to_owners(terms, vector, collective_id):
    seq_bits, dp_bits = bits_of(lax.axis_size("seq")), bits_of(lax.axis_size("dp"))
    bits = seq_bits + dp_bits
    orders = [order[::-1] for order in gather_orders(seq_bits, dp_bits)]
    terms = [term.reshape(2**bits, -1, term.shape[1]) for term in terms]
    streams = [
        (which, low, width, order)
        for which, term in enumerate(terms)
        for (low, width), order in zip(split_lanes(term.shape[2], SHARES), orders)
    ]
    rows = terms[0].shape[1]
    in_vmem = pl.BlockSpec(memory_space=pltpu.VMEM)
    held = [
        pltpu.VMEM((2 ** (bits - 1 - stage), rows, width), jnp.bfloat16)
        for _, _, width, _ in streams
        for stage in range(bits)
    ]
    return pl.pallas_call(
        partial(sum_kernel, seq_bits, streams, bits, len(terms)),
        out_shape=[jax.ShapeDtypeStruct(a.shape[1:], jnp.float32) for a in terms]
        + [jax.ShapeDtypeStruct(vector.shape, vector.dtype)],
        in_specs=[in_vmem] * (len(terms) + 1),
        out_specs=[in_vmem] * (len(terms) + 1),
        scratch_shapes=held
        + [
            pltpu.VMEM((bits, *vector.shape), jnp.float32),
            pltpu.VMEM((bits, *vector.shape), jnp.float32),
            pltpu.SemaphoreType.DMA((len(streams), bits)),
            pltpu.SemaphoreType.DMA((len(streams), bits)),
            pltpu.SemaphoreType.DMA((bits,)),
            pltpu.SemaphoreType.DMA((bits,)),
        ],
        compiler_params=pltpu.CompilerParams(
            collective_id=collective_id, has_side_effects=True, vmem_limit_bytes=VMEM_BYTES
        ),
        name="sum_rows",
    )(*terms, vector)


GROUP = 4
GROUP_LANES = GROUP * HEAD_DIM


def inner_product(left, right, dims):
    return lax.dot_general(
        left, right, (dims, ((), ())), precision=HIGH, preferred_element_type=jnp.float32
    )


def group_lanes(group):
    return pl.ds(pl.multiple_of(group * GROUP_LANES, GROUP_LANES), GROUP_LANES)


def head_weights(cumulative, head):
    row = cumulative[pl.ds(head, 1), :]
    count = row.shape[1]
    spread = jnp.broadcast_to(row, (count, count))
    later = lax.broadcasted_iota(jnp.int32, (count, count), 0)
    earlier = lax.broadcasted_iota(jnp.int32, (count, count), 1)
    return jnp.exp(jnp.where(later >= earlier, spread.T - spread, -jnp.inf))


def inside_work(first, last, scaled_x, b_mat, c_mat, cumulative, output, crossed):
    if first == 0:
        crossed[...] = inner_product(c_mat[...], b_mat[...], ((1,), (1,)))

    def one(group, carry):
        values = scaled_x[:, group_lanes(group)]
        parts = []
        for i in range(GROUP):
            scores = head_weights(cumulative, group * GROUP + i) * crossed[...]
            head = values[:, i * HEAD_DIM : (i + 1) * HEAD_DIM]
            parts.append(inner_product(scores, head, ((1,), (0,))))
        output[:, group_lanes(group)] = jnp.concatenate(parts, axis=1)
        return carry

    lax.fori_loop(first, last, one, 0)


def inside_back(
    first,
    last,
    output_cot,
    scaled_x,
    b_mat,
    c_mat,
    cumulative,
    scaled_cot,
    b_cot,
    c_cot,
    cumulative_cot,
    crossed,
    crossed_cot,
):
    if first == 0:
        crossed[...] = inner_product(c_mat[...], b_mat[...], ((1,), (1,)))
        crossed_cot[...] = jnp.zeros_like(crossed_cot)

    def one(group, carry):
        values = scaled_x[:, group_lanes(group)]
        cots = output_cot[:, group_lanes(group)]
        parts = []
        total = crossed_cot[...]
        for i in range(GROUP):
            weights = head_weights(cumulative, group * GROUP + i)
            scores = weights * crossed[...]
            head = values[:, i * HEAD_DIM : (i + 1) * HEAD_DIM]
            cot = cots[:, i * HEAD_DIM : (i + 1) * HEAD_DIM]
            weighted = weights * inner_product(cot, head, ((1,), (1,)))
            total = total + weighted
            parts.append(inner_product(scores, cot, ((0,), (0,))))
            moved = weighted * crossed[...]
            cumulative_cot[pl.ds(group * GROUP + i, 1), :] = jnp.sum(
                moved.T, axis=0, keepdims=True
            ) - jnp.sum(moved, axis=0, keepdims=True)
        crossed_cot[...] = total
        scaled_cot[:, group_lanes(group)] = jnp.concatenate(parts, axis=1)
        return carry

    lax.fori_loop(first, last, one, 0)
    if last == HEADS // GROUP:
        b_cot[...] = inner_product(crossed_cot[...], c_mat[...], ((0,), (0,)))
        c_cot[...] = inner_product(crossed_cot[...], b_mat[...], ((1,), (0,)))


def scan_kernel(count, reverse, work, inputs, outputs, *refs):
    state, decay = refs[:2]
    given = refs[2 : 2 + inputs]
    out = refs[2 + inputs]
    made = refs[3 + inputs : 3 + inputs + outputs]
    came, came_decay, ready = refs[3 + inputs + outputs : 6 + inputs + outputs]
    sems = refs[6 + inputs + outputs : 12 + inputs + outputs]
    held = refs[12 + inputs + outputs :]
    out_send, out_recv, decay_send, decay_recv, back_send, back_recv = sems
    dp_at, seq_at = places()
    barrier = pltpu.get_barrier_semaphore()
    peers = [(seq_at + hop) % count for hop in range(1, count)]
    for peer in peers:
        pl.semaphore_signal(barrier, inc=1, device_id=(dp_at, peer), device_id_type=MESH)
    pl.semaphore_wait(barrier, count - 1)

    def copy(hop, which):
        target = (seq_at + hop) % count
        source, landing, send_sem, recv_sem = (
            (state.at[target], came.at[seq_at], out_send, out_recv),
            (decay, came_decay.at[seq_at], decay_send, decay_recv),
            (ready.at[target], out.at[seq_at], back_send, back_recv),
        )[which]
        return pltpu.make_async_remote_copy(
            src_ref=source,
            dst_ref=landing,
            send_sem=send_sem.at[hop],
            recv_sem=recv_sem.at[hop],
            device_id=(dp_at, target),
            device_id_type=MESH,
        )

    for hop in range(1, count):
        copy(hop, 0).start()
        copy(hop, 1).start()
    came[seq_at] = state[seq_at]
    came_decay[seq_at] = decay[...]
    groups = HEADS // GROUP
    work(0, groups // 2, *given, *made, *held)
    for hop in range(1, count):
        copy(hop, 0).wait_recv()
        copy(hop, 1).wait_recv()
    total = jnp.zeros(state.shape[1:], jnp.float32)
    for place in range(count)[:: -1 if reverse else 1]:
        ready[place] = total.astype(ready.dtype)
        total = came_decay[place] * total + came[place].astype(jnp.float32)
    for hop in range(1, count):
        copy(hop, 2).start()
    out[seq_at] = ready[seq_at]
    work(groups // 2, groups, *given, *made, *held)
    for hop in range(1, count):
        copy(hop, 2).wait_recv()
    for hop in range(1, count):
        for which in range(3):
            copy(hop, which).wait_send()


def scan_states(state, decay, work, given, made, held, reverse, collective_id):
    count = lax.axis_size("seq")
    state = state.astype(jnp.bfloat16).reshape(count, STATE // count, DI)
    in_vmem = pl.BlockSpec(memory_space=pltpu.VMEM)
    got = pl.pallas_call(
        partial(scan_kernel, count, reverse, work, len(given), len(made)),
        out_shape=[jax.ShapeDtypeStruct(state.shape, state.dtype)]
        + [jax.ShapeDtypeStruct(shape, jnp.float32) for shape in made],
        in_specs=[in_vmem] * (2 + len(given)),
        out_specs=[in_vmem] * (1 + len(made)),
        scratch_shapes=[
            pltpu.VMEM(state.shape, state.dtype),
            pltpu.VMEM((count, 1, DI), jnp.float32),
            pltpu.VMEM(state.shape, state.dtype),
        ]
        + [pltpu.SemaphoreType.DMA((count,))] * 6
        + [pltpu.VMEM(shape, jnp.float32) for shape in held],
        compiler_params=pltpu.CompilerParams(
            collective_id=collective_id, has_side_effects=True, vmem_limit_bytes=VMEM_BYTES
        ),
        name="scan_back" if reverse else "scan_states",
    )(state, decay[None, :], *given)
    return got[0].reshape(STATE, DI).astype(jnp.float32), *got[1:]


def passed_along(value, axis, steps):
    count = lax.axis_size(axis)
    first, last = (max(0, -steps), min(count, count - steps))
    return lax.ppermute(value, axis, [(source, source + steps) for source in range(first, last)])


def pre_norm(residual_in, norm_gain):
    scale_rms = lax.rsqrt(jnp.mean(residual_in * residual_in, axis=-1, keepdims=True) + EPS)
    return residual_in * scale_rms * norm_gain


def conv_silu(padded, conv_weight, conv_bias, row_count):
    total = jnp.zeros((row_count, padded.shape[1]), jnp.float32) + conv_bias[None, :]
    for offset in range(conv_weight.shape[1]):
        total = total + conv_weight[:, offset][None, :] * padded[offset : offset + row_count]
    return jax.nn.silu(total)


def head_lanes():
    lanes = jnp.arange(DI, dtype=jnp.int32) // HEAD_DIM
    return (jnp.arange(HEADS, dtype=jnp.int32)[:, None] == lanes[None, :]).astype(jnp.float32)


def spread_heads(by_head):
    return jnp.dot(by_head, head_lanes(), precision=HIGH)


def sum_heads(by_lane):
    return jnp.dot(by_lane, head_lanes().T, precision=HIGH)


def before_states(xbc, dt_raw, edge, conv_weight, conv_bias, dt_bias, a_log):
    row_count = xbc.shape[0]
    activated = conv_silu(jnp.concatenate([edge, xbc], axis=0), conv_weight, conv_bias, row_count)
    xs = activated[:, :DI]
    b_mat = activated[:, DI : DI + STATE]
    c_mat = activated[:, DI + STATE :]
    step = jax.nn.softplus(dt_raw + dt_bias)
    log_decay = step * -jnp.exp(a_log)
    at = jnp.arange(row_count)
    lower = (at[:, None] >= at[None, :]).astype(jnp.float32)
    cumulative = jnp.dot(lower, log_decay, precision=HIGH)
    scaled_x = xs * spread_heads(step)
    tail = jnp.exp(cumulative[-1][None, :] - cumulative)
    fresh = jnp.dot(b_mat.T, scaled_x * spread_heads(tail), precision=HIGH)
    return (xs, scaled_x, b_mat, c_mat, cumulative, fresh)


def post_gate(ssd_out, xs, gate_part, skip_gain, gated_gain):
    skipped = xs * spread_heads(skip_gain[None, :])
    mixed_in = (ssd_out + skipped) * jax.nn.silu(gate_part)
    scale_rms = lax.rsqrt(jnp.mean(mixed_in * mixed_in, axis=-1, keepdims=True) + EPS)
    return mixed_in * scale_rms * gated_gain


def contract_rows(left, right):
    return lax.dot_general(
        left, right, (((0,), (0,)), ((), ())), preferred_element_type=jnp.float32
    )


def contract_cols(left, right):
    return lax.dot_general(
        left, right, (((1,), (1,)), ((), ())), preferred_element_type=jnp.float32
    )


def body(
    inputs,
    norm_gain,
    in_proj,
    conv_weight,
    conv_bias,
    dt_bias,
    a_log,
    skip_gain,
    gated_gain,
    out_proj,
    cotangent,
):
    row_count = inputs.shape[0]
    residual_in = inputs.astype(jnp.float32)
    normed_full, norm_back = jax.vjp(pre_norm, residual_in, norm_gain)
    normed = normed_full.astype(jnp.bfloat16)
    in_whole, out_whole = gather_all(
        [jnp.pad(in_proj, ((0, 0), (0, WIDE - PROJ))), out_proj], collective_id=1
    )
    in_whole = in_whole.reshape(-1, WIDE)
    out_whole = out_whole.reshape(-1, DI)
    projected = jnp.dot(normed, in_whole, preferred_element_type=jnp.float32)
    gate_part = projected[:, :DI]
    xbc = projected[:, DI : DI + XBC]
    dt_raw = projected[:, DI + XBC : PROJ]
    edge = passed_along(xbc[row_count - (CONV - 1) :], "seq", 1)
    primal, mid_back = jax.vjp(
        before_states, xbc, dt_raw, edge, conv_weight, conv_bias, dt_bias, a_log
    )
    xs, scaled_x, b_mat, c_mat, cumulative, s_local = primal
    by_head = cumulative.T
    decay = jnp.exp(cumulative[-1])
    wide_decay = spread_heads(decay[None, :])[0]
    square = (row_count, row_count)
    state_in, local_out = scan_states(
        s_local,
        wide_decay,
        inside_work,
        [scaled_x, b_mat, c_mat, by_head],
        [xs.shape],
        [square],
        False,
        collective_id=2,
    )
    weighted = spread_heads(jnp.exp(cumulative))
    carried_part = jnp.dot(c_mat, state_in, precision=HIGH) * weighted
    ssd_out = local_out + carried_part
    gated_full, post_back = jax.vjp(post_gate, ssd_out, xs, gate_part, skip_gain, gated_gain)
    gated = gated_full.astype(jnp.bfloat16)
    mixed = contract_cols(gated, out_whole)
    layer_out = (residual_in + mixed).astype(jnp.bfloat16)
    gated_cot = jnp.dot(cotangent, out_whole, preferred_element_type=jnp.float32)
    ssd_cot, xs_cot, gate_cot, skip_grad, gated_gain_grad = post_back(gated_cot)
    scaled_cot = ssd_cot * weighted
    local_grad = jnp.dot(c_mat.T, scaled_cot, precision=HIGH)
    later_grad, scaled_x_cot, b_cot, inner_c_cot, by_head_cot = scan_states(
        local_grad,
        wide_decay,
        inside_back,
        [ssd_cot, scaled_x, b_mat, c_mat, by_head],
        [xs.shape, b_mat.shape, c_mat.shape, by_head.shape],
        [square, square],
        True,
        collective_id=3,
    )
    c_cot = lax.dot_general(scaled_cot, state_in, (((1,), (1,)), ((), ())), precision=HIGH)
    cum_cot = sum_heads(ssd_cot * carried_part)
    last_cot = sum_heads(jnp.sum(later_grad * state_in, axis=0, keepdims=True))[0] * decay
    is_last = (jnp.arange(row_count) == row_count - 1)[:, None]
    cum_cot = cum_cot + jnp.where(is_last, last_cot[None, :], 0.0)
    mid_grads = mid_back(
        (xs_cot, scaled_x_cot, b_cot, c_cot + inner_c_cot, cum_cot + by_head_cot.T, later_grad)
    )
    xbc_cot, dt_cot, edge_cot, conv_weight_grad, conv_bias_grad, dt_bias_grad, a_log_grad = (
        mid_grads
    )
    edge_back = passed_along(edge_cot, "seq", -1)
    xbc_cot = xbc_cot + jnp.pad(edge_back, ((row_count - (CONV - 1), 0), (0, 0)))
    projected_cot = jnp.concatenate(
        [gate_cot, xbc_cot, dt_cot, jnp.zeros((row_count, WIDE - PROJ), jnp.float32)], axis=1
    ).astype(jnp.bfloat16)
    in_term = contract_rows(normed, projected_cot).astype(jnp.bfloat16)
    out_term = contract_rows(cotangent, gated).astype(jnp.bfloat16)
    normed_cot = contract_cols(projected_cot, in_whole)
    input_part, norm_gain_grad = norm_back(normed_cot)
    input_grad = cotangent.astype(jnp.float32) + input_part
    small = (
        norm_gain_grad,
        conv_weight_grad.T,
        conv_bias_grad,
        gated_gain_grad,
        dt_bias_grad,
        a_log_grad,
        skip_grad,
    )
    flat = jnp.concatenate([a.reshape(-1) for a in small])
    tile = 8 * LANES
    flat = jnp.pad(flat, (0, -flat.shape[0] % tile))
    in_proj_grad, out_proj_grad, summed = sum_to_owners(
        [in_term, out_term], flat.reshape(-1, LANES), collective_id=4
    )
    summed = summed.reshape(-1)
    parts, at = [], 0
    for a in small:
        parts.append(summed[at : at + a.size].reshape(a.shape))
        at += a.size
    return (
        layer_out,
        input_grad,
        in_proj_grad[:, :PROJ],
        out_proj_grad,
        parts[0],
        parts[1].T,
        parts[2],
        parts[4],
        parts[5],
        parts[6],
        parts[3],
    )


QUAD = 4
CHUNK = 128
TAIL = 16
QCH = DI // QUAD
QHEADS = HEADS // QUAD
PAIRS = QCH // LANES
BC = 2 * STATE
QXBC = QCH + BC
SLAB = QXBC + LANES
PARTS = 3
PART = SLAB // PARTS
GRAD_ROWS = 8
SEMS = 98


def flip(value, bit):
    return value + (1 - 2 * bit_at(value, bit)) * 2**bit


def flip_quad(value, mask):
    for bit in range(2):
        if mask >> bit & 1:
            value = flip(value, bit)
    return value


def dot_nn(left, right):
    return lax.dot_general(
        left, right, (((1,), (0,)), ((), ())), preferred_element_type=jnp.float32
    )


def dot_nt(left, right):
    return lax.dot_general(
        left, right, (((1,), (1,)), ((), ())), preferred_element_type=jnp.float32
    )


def dot_tn(left, right):
    return lax.dot_general(
        left, right, (((0,), (0,)), ((), ())), preferred_element_type=jnp.float32
    )


def in_parts(value, count):
    parts = []
    for _ in range(count):
        part = value.astype(jnp.bfloat16)
        parts.append(part)
        value = value - part.astype(jnp.float32)
    return parts


def lane_tile(i):
    return pl.ds(i * LANES, LANES)


def chunk_rows(c, offset=0, count=CHUNK):
    return pl.ds(pl.multiple_of(c * CHUNK + offset, 8), count)


def column_sum(value):
    return jnp.sum(value, axis=0, keepdims=True)


def block_kernel(
    x_ref,
    gain_ref,
    in_ref,
    taps_ref,
    bias_ref,
    dt_bias_ref,
    a_log_ref,
    skip_ref,
    gated_gain_ref,
    proj_ref,
    cot_ref,
    out_ref,
    grad_ref,
    in_grad_ref,
    proj_grad_ref,
    gain_grad_ref,
    taps_grad_ref,
    bias_grad_ref,
    dt_bias_grad_ref,
    a_log_grad_ref,
    skip_grad_ref,
    gated_gain_grad_ref,
    early_ref,
    late_ref,
    xq,
    cq,
    xtail,
    early_slots,
    late_slots,
    early_w,
    late_w,
    xn,
    proj,
    act,
    act_slope,
    step_s,
    step_slope,
    log_s,
    cum_s,
    sx_s,
    fresh_s,
    state_out,
    state_come,
    state_s,
    weights_s,
    scores_s,
    ssd_s,
    gate_s,
    gc_s,
    m_s,
    sums_s,
    gated_s,
    gate_cot_s,
    y_s,
    z_s,
    back_s,
    later_s,
    cross_s,
    sx_cot_s,
    pre_cot_s,
    early_cot_s,
    late_term,
    early_term,
    mixed_s,
    mixed_come,
    normed_t,
    cot_t,
    early_wt,
    late_wt,
    normed_cot_s,
    normed_out,
    normed_come,
    tail_out,
    tail_come,
    small_s,
    skip_s,
    small_come,
    small_quad,
    *rest,
):
    stream_held = [rest[4 * i : 4 * i + 4] for i in range(1 + PARTS)]
    send_sem, recv_sem = rest[4 + 4 * PARTS :]
    f32, bf16 = jnp.float32, jnp.bfloat16
    dp_at, seq_at = places()
    q, g = seq_at % QUAD, seq_at // QUAD
    core, y_at = dp_at % 2, dp_at // 2
    place = dp_at * 8 + seq_at
    used = [0]
    sent = []

    barrier = pltpu.get_barrier_semaphore()
    peers = [(dp_at, (seq_at + hop) % 8) for hop in range(1, 8)]
    peers += [(flip(dp_at, 0), seq_at), (flip(dp_at, 1), seq_at)]
    peers += [(flip(dp_at, 1), flip(seq_at, 2))]
    for peer in peers:
        pl.semaphore_signal(barrier, inc=1, device_id=peer, device_id_type=MESH)

    def remote(source, landing, target, own=True):
        at = used[0]
        used[0] += 1
        copy = pltpu.make_async_remote_copy(
            src_ref=source,
            dst_ref=landing,
            send_sem=send_sem.at[at],
            recv_sem=recv_sem.at[at],
            device_id=target,
            device_id_type=MESH,
        )
        if own:
            copy.start()
            sent.append(copy)
        return copy

    half_lanes = [pl.ds(h * SLAB // 2, SLAB // 2) for h in range(2)]

    def share_block(own_block, slots):
        over_z = [
            remote(own_block.at[:, lanes], slots.at[q, :, lanes], in_quad(2))
            for lanes in half_lanes
        ]
        return over_z, remote(own_block, slots.at[q], in_quad(1))

    def pass_block(slots, over_z):
        made = []
        for copy, lanes in zip(over_z, half_lanes):
            copy.wait_recv()
            view = slots.at[flip_quad(q, 2), :, lanes]
            made.append(remote(view, view, in_quad(1)))
        return made

    def send_sums(blocks, landing):
        over_x = [
            remote(blocks.at[flip_quad(q, 3), :, lanes], landing.at[0, :, lanes], in_quad(1))
            for lanes in half_lanes
        ]
        return over_x, remote(blocks.at[flip_quad(q, 1)], landing.at[1], in_quad(1))

    def pass_sums(mine, blocks, landing, over_x):
        made = []
        other = flip_quad(q, 2)
        for copy, lanes in zip(over_x, half_lanes):
            copy.wait_recv()
            blocks[other, :, lanes] = (
                mine[other, :, lanes].astype(f32) + landing[0, :, lanes].astype(f32)
            ).astype(bf16)
            made.append(
                remote(blocks.at[other, :, lanes], landing.at[2, :, lanes], in_quad(2))
            )
        return made

    def in_quad(mask):
        return dp_at, flip_quad(seq_at, mask)

    far = (dp_at, flip(seq_at, 2))
    beside = (flip(dp_at, 1), seq_at)
    twin = (flip(dp_at, 0), seq_at)

    def arrived(copies):
        for copy in copies:
            copy.wait_recv()

    lane = lax.broadcasted_iota(jnp.int32, (1, LANES), 1)
    first_half = lane < HEAD_DIM
    half0 = jnp.where(first_half, 1.0, 0.0)
    half1 = 1.0 - half0
    half0b, half1b = half0.astype(bf16), half1.astype(bf16)
    row_at = lax.broadcasted_iota(jnp.int32, (CHUNK, CHUNK), 0)
    lane_at = lax.broadcasted_iota(jnp.int32, (CHUNK, CHUNK), 1)
    causal = row_at >= lane_at
    lower = jnp.where(causal, 1.0, 0.0).astype(bf16)
    upper = jnp.where(row_at <= lane_at, 1.0, 0.0).astype(bf16)
    lower3 = jnp.concatenate([lower] * 3, axis=1)
    upper3 = jnp.concatenate([upper] * 3, axis=1)

    def spread(by_head, i):
        return jnp.where(first_half, by_head[:, 2 * i : 2 * i + 1], by_head[:, 2 * i + 1 : 2 * i + 2])

    head_picks = []
    for i in range(PAIRS):
        pick = jnp.where(2 * i + row_at // HEAD_DIM == lane_at, 1.0, 0.0).astype(bf16)
        head_picks.append(jnp.concatenate([pick] * 2, axis=0))

    def head_sum(value, i):
        return dot_nn(jnp.concatenate(in_parts(value, 2), axis=1), head_picks[i])

    def flat_row(ref, low, count):
        return ref[pl.ds(low, count)].reshape(1, count)

    def own_channels(i):
        return pl.ds(pl.multiple_of(q * QCH + i * LANES, LANES), LANES)

    def conv_channels(i):
        return own_channels(i) if i < PAIRS else pl.ds(DI + (i - PAIRS) * LANES, LANES)

    def tap(k, i):
        return taps_ref[pl.ds(k, 1), conv_channels(i)]

    def gated_gain(i):
        return gated_gain_ref[own_channels(i)].reshape(1, LANES)

    def own_heads(ref):
        head_at = lax.broadcasted_iota(jnp.int32, (HEADS, LANES), 0)
        to = lax.broadcasted_iota(jnp.int32, (HEADS, LANES), 1)
        pick = jnp.where((head_at == to + q * QHEADS) & (to < QHEADS), 1.0, 0.0)
        value = jnp.broadcast_to(ref[...].reshape(1, HEADS), (8, HEADS))
        return inner_product(value, pick, ((1,), (0,)))[:1]

    def stacked(value):
        return jnp.concatenate([value * half0b, value * half1b], axis=0)

    for j in range(QUAD):
        own = pl.ds(j * QCH, QCH)
        early_ref[j, :, pl.ds(0, QCH)] = in_ref[:, pl.ds(DI + j * QCH, QCH)]
        early_ref[j, :, pl.ds(QCH, BC)] = in_ref[:, pl.ds(2 * DI, BC)]
        head_at = lax.broadcasted_iota(jnp.int32, (HEADS, LANES), 0)
        to = lax.broadcasted_iota(jnp.int32, (HEADS, LANES), 1)
        pick = jnp.where((head_at == to + j * QHEADS) & (to < QHEADS), 1.0, 0.0)
        early_ref[j, :, pl.ds(QXBC, LANES)] = dot_nn(
            in_ref[:, pl.ds(DI + XBC, HEADS)], pick.astype(bf16)
        ).astype(bf16)
        late_ref[j, :, pl.ds(0, QCH)] = in_ref[:, own]
        late_ref[j, :, pl.ds(QCH, QCH)] = proj_ref[:, own]

    pl.semaphore_wait(barrier, len(peers))

    def scatter(shard, slots):
        return [
            remote(shard.at[flip_quad(q, mask)], slots.at[place], in_quad(mask))
            for mask in (1, 2, 3)
        ]

    early_0 = scatter(early_ref, early_slots)
    token_z, token_x = share_block(x_ref, xq)
    tail_sends = [
        remote(x_ref.at[pl.ds(CHUNK - TAIL, TAIL)], xtail, (dp_at, QUAD + i), own=False)
        for i in range(QUAD)
    ]
    at_end = seq_at == QUAD - 1

    @pl.when(at_end)
    def _():
        for copy in tail_sends:
            copy.start()

    early_slots[place] = early_ref[q]
    late_slots[place] = late_ref[q]
    xq[q] = x_ref[...]
    cq[q] = cot_ref[...]

    def cross_far(slots):
        return [
            remote(
                slots.at[pl.ds(dp_at * 8 + g * 4, 4), :, lane_part],
                slots.at[pl.ds(dp_at * 8 + g * 4, 4), :, lane_part],
                far,
            )
            for lane_part in [pl.ds(part * PART, PART) for part in range(PARTS)]
        ]

    def cross_beside(slots, copies):
        made = []
        for part, copy in enumerate(copies):
            copy.wait_recv()
            view = slots.at[pl.ds(dp_at * 8, 8), :, pl.ds(part * PART, PART)]
            made.append(remote(view, view, beside))
        return made

    def cross_twin(slots, copies):
        made = []
        for part, copy in enumerate(copies):
            copy.wait_recv()
            for up in range(2):
                view = slots.at[pl.ds((2 * up + core) * 8, 8), :, pl.ds(part * PART, PART)]
                made.append(remote(view, view, twin))
        return made

    def flatten(slots, flat):
        def one(pair, carry):
            value = slots[pl.ds(2 * pair, 2)].astype(f32).reshape(48, SLAB)
            flat[pl.ds(pl.multiple_of(pair * 48, 16), 48), :] = value.astype(bf16)
            return carry

        lax.fori_loop(0, 16, one, 0)

    arrived(early_0)
    early_1 = cross_far(early_slots)
    token_pass = pass_block(xq, token_z)
    late_0 = scatter(late_ref, late_slots)
    early_2 = cross_beside(early_slots, early_1)
    arrived(late_0)
    late_1 = cross_far(late_slots)
    cot_z, cot_x = share_block(cot_ref, cq)

    arrived([token_x, *token_pass])

    for i in range(QUAD):

        @pl.when((g == 1) & (q == i))
        def _():
            tail_sends[i].wait_recv()

    @pl.when(g == 0)
    def _():
        xtail[...] = jnp.zeros_like(xtail)

    gain = flat_row(gain_ref, 0, x_ref.shape[1])

    def scaled_rows(value):
        value = value.astype(f32)
        return value * lax.rsqrt(jnp.mean(value * value, axis=-1, keepdims=True) + EPS)

    tail_rows = scaled_rows(xtail[...]) * gain
    xn[pl.ds(0, TAIL), :] = tail_rows.astype(bf16)
    normed_t[:, pl.ds(QUAD * CHUNK, LANES)] = jnp.concatenate(
        [tail_rows, jnp.zeros((LANES - TAIL, tail_rows.shape[1]), f32)], axis=0
    ).T.astype(bf16)
    early_cot_s[pl.ds(QUAD * CHUNK, LANES), :] = jnp.zeros((LANES, SLAB), bf16)

    def norm_block(c, carry):
        value = scaled_rows(xq[c]) * gain
        xn[pl.ds(pl.multiple_of(c * CHUNK + TAIL, 16), CHUNK), :] = value.astype(bf16)
        normed_t[:, pl.ds(pl.multiple_of(c * CHUNK, CHUNK), CHUNK)] = value.T.astype(bf16)
        return carry

    lax.fori_loop(0, QUAD, norm_block, 0)
    early_3 = cross_twin(early_slots, early_2)
    cot_pass = pass_block(cq, cot_z)
    late_2 = cross_beside(late_slots, late_1)
    small_s[...] = jnp.zeros_like(small_s)
    skip_s[...] = jnp.zeros_like(skip_s)
    pre_cot_s[pl.ds(0, TAIL), :] = jnp.zeros((TAIL, QXBC), f32)
    pre_cot_s[pl.ds(TAIL + QUAD * CHUNK, 8), :] = jnp.zeros((8, QXBC), f32)
    arrived(early_3)
    flatten(early_slots, early_w)

    for n in range(3):
        cols = pl.ds(n * 256, 256)
        proj[:, cols] = dot_nn(xn[...], early_w[:, cols])

    rate = -jnp.exp(own_heads(a_log_ref))
    dt_bias = own_heads(dt_bias_ref)
    skips = own_heads(skip_ref)
    skip_wide = [spread(skips, i) for i in range(PAIRS)]
    head_lane = lane < QHEADS

    def forward_states(c, carry):
        rows = chunk_rows(c)
        for i in range(QXBC // LANES):
            lanes = lane_tile(i)
            window = proj[chunk_rows(c, 8, CHUNK + 8), lanes]
            total = bias_ref[conv_channels(i)].reshape(1, LANES)
            for k in range(CONV):
                total = total + tap(k, i) * pltpu.roll(window, CHUNK + 3 - k, 0)[:CHUNK]
            sig = lax.logistic(total)
            act[rows, lanes] = total * sig
            act_slope[rows, lanes] = sig * (1.0 + total * (1.0 - sig))
        raw = proj[chunk_rows(c, TAIL), pl.ds(QXBC, LANES)] + dt_bias
        step = jnp.maximum(raw, 0.0) + jnp.log1p(jnp.exp(-jnp.abs(raw)))
        step = jnp.where(head_lane, step, 0.0)
        log_decay = step * rate
        cum = dot_nn(lower3, jnp.concatenate(in_parts(log_decay, 3), axis=0))
        step_s[rows, :] = step
        step_slope[rows, :] = lax.logistic(raw)
        log_s[rows, :] = log_decay
        cum_s[rows, :] = cum
        tail = jnp.exp(cum[CHUNK - 1 :] - cum)
        b_mat = act[rows, pl.ds(QCH, STATE)].astype(bf16)
        for i in range(PAIRS):
            lanes = lane_tile(i)
            sx = act[rows, lanes] * spread(step, i)
            sx_s[rows, lanes] = sx.astype(bf16)
            fresh_s[c, i] = dot_tn(b_mat, (sx * spread(tail, i)).astype(bf16))
        return carry

    lax.fori_loop(0, QUAD, forward_states, 0)

    def chunk_decay(c, i):
        last = cum_s[chunk_rows(c, CHUNK - 8, 8), :][7:]
        return spread(jnp.exp(last), i)

    for i in range(PAIRS):
        total = fresh_s[0, i]
        for c in range(1, QUAD):
            total = chunk_decay(c, i) * total + fresh_s[c, i]
        state_out[i] = total.astype(bf16)
    state_copy = remote(state_out, state_come, far)
    late_3 = cross_twin(late_slots, late_2)

    def forward_local(c, carry):
        rows = chunk_rows(c)
        b_mat = act[rows, pl.ds(QCH, STATE)].astype(bf16)
        c_mat = act[rows, pl.ds(QCH + STATE, STATE)].astype(bf16)
        crossed = dot_nt(c_mat, b_mat)
        cum = cum_s[rows, :]
        cum_t = cum.T
        for i in range(PAIRS):
            lanes = lane_tile(i)
            pair = []
            for head in (2 * i, 2 * i + 1):
                gap = cum[:, head : head + 1] - cum_t[head : head + 1, :]
                pair.append(jnp.exp(jnp.where(causal, gap, -1e30)))
            weights_s[c, i] = jnp.concatenate(pair, axis=1).astype(bf16)
            scores = jnp.concatenate([w * crossed for w in pair], axis=1).astype(bf16)
            scores_s[c, i] = scores
            ssd_s[rows, lanes] = dot_nn(scores, stacked(sx_s[rows, lanes]))
        return carry

    lax.fori_loop(0, QUAD, forward_local, 0)
    arrived(late_3)
    flatten(late_slots, late_w)
    gate_w = pl.ds(0, QCH)
    out_w = pl.ds(QCH, QCH)
    gate_s[...] = dot_nn(xn[pl.ds(TAIL, QUAD * CHUNK), :], late_w[:, gate_w])
    arrived([cot_x, *cot_pass])

    def cot_block(c, carry):
        gc_s[chunk_rows(c), :] = dot_nn(cq[c], late_w[:, out_w])
        return carry

    lax.fori_loop(0, QUAD, cot_block, 0)
    state_copy.wait_recv()
    for i in range(PAIRS):
        total = jnp.where(g == 1, state_come[i].astype(f32), 0.0)
        for c in range(QUAD):
            state_s[c, i] = total.astype(bf16)
            if c < QUAD - 1:
                total = chunk_decay(c, i) * total + fresh_s[c, i]

    def forward_gate(c, carry):
        rows = chunk_rows(c)
        c_mat = act[rows, pl.ds(QCH + STATE, STATE)].astype(bf16)
        grown = jnp.exp(cum_s[rows, :])
        square, crossed = 0.0, 0.0
        for i in range(PAIRS):
            lanes = lane_tile(i)
            ssd = ssd_s[rows, lanes] + dot_nn(c_mat, state_s[c, i]) * spread(grown, i)
            ssd_s[rows, lanes] = ssd
            gate = gate_s[rows, lanes]
            m = (ssd + act[rows, lanes] * skip_wide[i]) * gate * lax.logistic(gate)
            m_s[rows, lanes] = m
            square = square + m * m
            crossed = crossed + gc_s[rows, lanes] * gated_gain(i) * m
        square = jnp.sum(square, axis=1, keepdims=True)
        crossed = jnp.sum(crossed, axis=1, keepdims=True)
        both = jnp.where(lane == 0, square, jnp.where(lane == 1, crossed, 0.0))
        sums_s[q, :, pl.ds(pl.multiple_of(c * CHUNK, CHUNK), CHUNK)] = (
            both.T[:8]
        )
        return carry

    lax.fori_loop(0, QUAD, forward_gate, 0)
    sums_copies = [remote(sums_s.at[q], sums_s.at[q], in_quad(mask)) for mask in (1, 2, 3)]

    def turn_cot(c, carry):
        cot_t[:, pl.ds(pl.multiple_of(c * CHUNK, CHUNK), CHUNK)] = (
            cq[c].astype(f32).T.astype(bf16)
        )
        return carry

    lax.fori_loop(0, QUAD, turn_cot, 0)

    def turn_weights(c, carry):
        own = pl.ds(pl.multiple_of(c * CHUNK, CHUNK), CHUNK)
        late_wt[:, own] = late_w[own, :].astype(f32).T.astype(bf16)
        early_wt[:, own] = early_w[own, :].astype(f32).T.astype(bf16)
        return carry

    lax.fori_loop(0, x_ref.shape[1] // CHUNK, turn_weights, 0)
    arrived(sums_copies)

    def backward_states(c, carry):
        rows = chunk_rows(c)
        cols = pl.ds(pl.multiple_of(c * CHUNK, CHUNK), CHUNK)
        sums = sums_s[0, :, cols] + sums_s[1, :, cols] + sums_s[2, :, cols] + sums_s[3, :, cols]
        sums = jnp.concatenate([sums] * (CHUNK // 8), axis=0).T
        scale = lax.rsqrt(sums[:, 0:1] * (1.0 / DI) + EPS)
        pull = scale * scale * scale * (sums[:, 1:2] * (1.0 / DI))
        c_mat = act[rows, pl.ds(QCH + STATE, STATE)].astype(bf16)
        grown = jnp.exp(cum_s[rows, :])
        for i in range(PAIRS):
            lanes = lane_tile(i)
            m, gc, gate = m_s[rows, lanes], gc_s[rows, lanes], gate_s[rows, lanes]
            xs = act[rows, lanes]
            mr = m * scale
            gated_s[rows, lanes] = (mr * gated_gain(i)).astype(bf16)
            small_s[5:6, lanes] += column_sum(gc * mr)
            m_cot = scale * (gc * gated_gain(i)) - m * pull
            sig = lax.logistic(gate)
            mixed = ssd_s[rows, lanes] + xs * skip_wide[i]
            gate_cot_s[rows, lanes] = (
                m_cot * mixed * (sig * (1.0 + gate * (1.0 - sig)))
            ).astype(bf16)
            y = m_cot * gate * sig
            y_s[rows, lanes] = y
            skip_s[0:1, lanes] += column_sum(y * xs)
            z = (y * spread(grown, i)).astype(bf16)
            z_s[rows, lanes] = z
            back_s[c, i] = dot_tn(c_mat, z)
        return carry

    lax.fori_loop(0, QUAD, backward_states, 0)
    state_copy.wait_send()
    sent[:] = [copy for copy in sent if copy is not state_copy]
    for i in range(PAIRS):
        total = back_s[QUAD - 1, i]
        for c in range(QUAD - 2, -1, -1):
            total = chunk_decay(c, i) * total + back_s[c, i]
        state_out[i] = total.astype(bf16)
    later_copy = remote(state_out, later_s.at[QUAD], far)

    def term_rows(term, half, value, lanes):
        term[pl.ds(half * 16, 16), :, lanes] = value.reshape(16, 24, value.shape[1]).astype(bf16)

    def late_half(half, carry):
        own = pl.ds(pl.multiple_of(half * QCH, QCH), QCH)
        term_rows(late_term, half, dot_nn(normed_t[own, pl.ds(0, QUAD * CHUNK)], gate_cot_s[...]), gate_w)
        term_rows(late_term, half, dot_nn(cot_t[own, :], gated_s[...]), out_w)
        return carry

    lax.fori_loop(0, 2, late_half, 0)

    streams = [(late_term, pl.ds(0, SLAB))] + [
        (early_term, pl.ds(i * PART, PART)) for i in range(PARTS)
    ]

    def reduce_twin(stream):
        term, lanes = streams[stream]
        return [
            remote(
                term.at[pl.ds((2 * up + 1 - core) * 8, 8), :, lanes],
                stream_held[stream][0].at[pl.ds(8 * up, 8)],
                twin,
            )
            for up in range(2)
        ]

    def reduce_beside(stream, copies):
        arrived(copies)
        term, lanes = streams[stream]
        held = stream_held[stream][0]

        def add(slot, carry):
            mine = (2 * (slot // 8) + core) * 8 + slot % 8
            held[slot] = (term[mine, :, lanes].astype(f32) + held[slot].astype(f32)).astype(bf16)
            return carry

        lax.fori_loop(0, 16, add, 0)
        return [remote(held.at[pl.ds((1 - y_at) * 8, 8)], stream_held[stream][1], beside)]

    def reduce_far(stream, copies):
        arrived(copies)
        before, held = stream_held[stream][:2]

        def add(slot, carry):
            held[slot] = (
                before[y_at * 8 + slot].astype(f32) + held[slot].astype(f32)
            ).astype(bf16)
            return carry

        lax.fori_loop(0, 8, add, 0)
        return [remote(held.at[pl.ds((1 - g) * 4, 4)], stream_held[stream][2], far)]

    def reduce_quad(stream, copies):
        arrived(copies)
        before, held, result = stream_held[stream][1:]

        def add(slot, carry):
            held[slot] = (before[g * 4 + slot].astype(f32) + held[slot].astype(f32)).astype(bf16)
            return carry

        lax.fori_loop(0, 4, add, 0)
        made = [
            remote(held.at[flip_quad(q, mask)], result.at[q], in_quad(mask)) for mask in (1, 2, 3)
        ]
        result[q] = held[q]
        return made

    late_r0 = reduce_twin(0)

    for n in range(3):
        cols = pl.ds(n * 256, 256)
        value = dot_nn(gated_s[...], late_wt[out_w, cols]).astype(bf16)
        for c in range(QUAD):
            mixed_s[c, :, cols] = value[c * CHUNK : (c + 1) * CHUNK]

    mixed_x, mixed_own = send_sums(mixed_s, mixed_come)

    def backward_local(c, carry):
        rows = chunk_rows(c)
        total = jnp.zeros((CHUNK, CHUNK), f32)
        for i in range(PAIRS):
            lanes = lane_tile(i)
            y = y_s[rows, lanes].astype(bf16)
            moved = weights_s[c, i].astype(f32) * dot_nt(y, stacked(sx_s[rows, lanes]))
            total = total + moved[:, :CHUNK] + moved[:, CHUNK:]
            both = dot_tn(scores_s[c, i], y)
            sx_cot_s[rows, lanes] = both[:CHUNK] * half0 + both[CHUNK:] * half1
        cross_s[c] = total.astype(bf16)
        return carry

    lax.fori_loop(0, QUAD, backward_local, 0)
    late_r1 = reduce_beside(0, late_r0)
    mixed_z = pass_sums(mixed_s, mixed_s, mixed_come, mixed_x)
    later_copy.wait_recv()
    for i in range(PAIRS):
        total = jnp.where(g == 0, later_s[QUAD, i].astype(f32), 0.0)
        for c in range(QUAD - 1, -1, -1):
            later_s[c, i] = total.astype(bf16)
            if c > 0:
                total = chunk_decay(c, i) * total + back_s[c, i]

    def backward_mix(c, carry):
        rows = chunk_rows(c)
        shifted = chunk_rows(c, TAIL)
        b_mat = act[rows, pl.ds(QCH, STATE)].astype(bf16)
        c_mat = act[rows, pl.ds(QCH + STATE, STATE)].astype(bf16)
        cum, step = cum_s[rows, :], step_s[rows, :]
        tail = jnp.exp(cum[CHUNK - 1 :] - cum)
        decay = jnp.exp(cum[CHUNK - 1 :])
        cross = cross_s[c]
        b_cot = dot_tn(cross, c_mat)
        c_cot = dot_nn(cross, b_mat)
        by_head = jnp.zeros((2 * CHUNK + 8, LANES), f32)
        for i in range(PAIRS):
            lanes = lane_tile(i)
            xs, y = act[rows, lanes], y_s[rows, lanes]
            later, state = later_s[c, i], state_s[c, i]
            wide_step, wide_tail = spread(step, i), spread(tail, i)
            tailed = (xs * wide_step * wide_tail).astype(bf16)
            from_later = dot_nn(b_mat, later) * wide_tail
            b_cot = b_cot + dot_nt(tailed, later)
            c_cot = c_cot + dot_nt(z_s[rows, lanes], state)
            sx = sx_s[rows, lanes].astype(f32)
            sx_cot = sx_cot_s[rows, lanes] + from_later
            last = column_sum(sx * from_later) + column_sum(
                later.astype(f32) * state.astype(f32)
            ) * spread(decay, i)
            by_head = by_head + head_sum(
                jnp.concatenate(
                    [
                        y.astype(bf16).astype(f32) * ssd_s[rows, lanes] - sx * sx_cot,
                        sx_cot * xs,
                        jnp.broadcast_to(last, (8, LANES)),
                    ],
                    axis=0,
                ),
                i,
            )
            pre_cot_s[shifted, lanes] = (
                sx_cot * wide_step + y * skip_wide[i]
            ) * act_slope[rows, lanes]
        pre_cot_s[shifted, pl.ds(QCH, STATE)] = b_cot * act_slope[rows, pl.ds(QCH, STATE)]
        pre_cot_s[shifted, pl.ds(QCH + STATE, STATE)] = (
            c_cot * act_slope[rows, pl.ds(QCH + STATE, STATE)]
        )
        cum_cot, step_cot = by_head[:CHUNK], by_head[CHUNK : 2 * CHUNK]
        last_cot = by_head[2 * CHUNK : 2 * CHUNK + 1]
        log_cot = dot_nn(upper3, jnp.concatenate(in_parts(cum_cot, 3), axis=0)) + last_cot
        dt_cot = (step_cot + log_cot * rate) * step_slope[rows, :]
        small_s[7:8, lane_tile(1)] += column_sum(log_cot * log_s[rows, :])
        small_s[5:6, lane_tile(4)] += column_sum(dt_cot)
        early_cot_s[rows, pl.ds(QXBC, LANES)] = dt_cot.astype(bf16)
        return carry

    lax.fori_loop(0, QUAD, backward_mix, 0)
    late_r2 = reduce_far(0, late_r1)

    for i in range(QXBC // LANES):
        lanes = lane_tile(i)
        edge = pre_cot_s[pl.ds(0, 24), lanes]
        total = tap(CONV - 1, i) * edge[:TAIL]
        for k in range(CONV - 1):
            total = total + tap(k, i) * pltpu.roll(edge, 24 - (3 - k), 0)[:TAIL]
        early_cot_s[pl.ds(QUAD * CHUNK, TAIL), lanes] = total.astype(bf16)

    def backward_conv(c, carry):
        for i in range(QXBC // LANES):
            lanes = lane_tile(i)
            cots = pre_cot_s[chunk_rows(c, TAIL, CHUNK + 8), lanes]
            window = proj[chunk_rows(c, 8, CHUNK + 8), lanes]
            cot = cots[:CHUNK]
            total = tap(CONV - 1, i) * cot
            for k in range(CONV - 1):
                total = total + tap(k, i) * pltpu.roll(cots, CHUNK + 8 - (3 - k), 0)[:CHUNK]
            early_cot_s[chunk_rows(c), lanes] = total.astype(bf16)
            for k in range(CONV):
                small_s[k : k + 1, lanes] += column_sum(
                    cot * pltpu.roll(window, CHUNK + 3 - k, 0)[:CHUNK]
                )
            small_s[4:5, lanes] += column_sum(cot)
        return carry

    lax.fori_loop(0, QUAD, backward_conv, 0)

    heads = jnp.zeros((8, LANES), f32)
    for i in range(PAIRS):
        heads = heads + head_sum(jnp.broadcast_to(skip_s[0:1, lane_tile(i)], (8, LANES)), i)
    small_s[5:6, lane_tile(3)] = heads[:1]

    tail_value = dot_nn(early_cot_s[pl.ds(QUAD * CHUNK, TAIL), :], early_wt[...])
    tail_out[...] = tail_value
    tail_index = used[0]
    used[0] += QUAD

    def tail_copy(i):
        return pltpu.make_async_remote_copy(
            src_ref=tail_out,
            dst_ref=tail_come.at[i],
            send_sem=send_sem.at[tail_index + i],
            recv_sem=recv_sem.at[tail_index + i],
            device_id=(dp_at, QUAD - 1),
            device_id_type=MESH,
        )

    for i in range(QUAD):

        @pl.when((g == 1) & (q == i))
        def _():
            tail_copy(i).start()

    def add_gain(value, rows):
        total = column_sum(value * scaled_rows(rows))
        small_s[6:7, :] += total[:, :QXBC]
        small_s[7:8, lane_tile(0)] += total[:, QXBC:]

    add_gain(tail_value, xtail[...])

    for n in range(3):
        cols = pl.ds(n * 256, 256)
        value = dot_nn(early_cot_s[pl.ds(0, QUAD * CHUNK), :], early_wt[:, cols])
        value = value + dot_nn(gate_cot_s[...], late_wt[gate_w, cols])
        for c in range(QUAD):
            part = value[c * CHUNK : (c + 1) * CHUNK]
            normed_cot_s[c, :, cols] = part
            normed_out[c, :, cols] = part.astype(bf16)

    normed_x, normed_own = send_sums(normed_out, normed_come)
    for c in range(QUAD):
        add_gain(normed_cot_s[c], xq[c])
    small_copy = remote(small_s, small_come.at[0], twin)
    early_r0 = []
    for part in range(PARTS):
        lanes = pl.ds(part * PART, PART)

        def early_half(half, carry, lanes=lanes):
            own = pl.ds(pl.multiple_of(half * QCH, QCH), QCH)
            value = dot_nn(normed_t[own, :], early_cot_s[:, lanes])
            term_rows(early_term, half, value, lanes)
            return carry

        lax.fori_loop(0, 2, early_half, 0)
        early_r0.append(reduce_twin(1 + part))

    early_r1 = [reduce_beside(1 + part, early_r0[part]) for part in range(PARTS)]
    normed_z = pass_sums(normed_cot_s, normed_out, normed_come, normed_x)

    early_r2 = [reduce_far(1, early_r1[0])]
    small_copy.wait_recv()
    small_come[4] = small_s[...] + small_come[0]
    across = (flip(dp_at, 1), flip(seq_at, 2))
    small_copies = [
        remote(small_come.at[4], small_come.at[1 + i], target)
        for i, target in enumerate((beside, far, across))
    ]
    early_r2.append(reduce_far(2, early_r1[1]))
    late_r3 = reduce_quad(0, late_r2)
    early_r2.append(reduce_far(3, early_r1[2]))
    arrived(small_copies)
    small_quad[q] = small_come[4] + small_come[1] + (small_come[2] + small_come[3])
    small_copies = [remote(small_quad.at[q], small_quad.at[q], in_quad(mask)) for mask in (1, 2, 3)]

    arrived([mixed_own, *mixed_z])
    total = x_ref[...].astype(f32) + mixed_s[q].astype(f32)
    total = total + mixed_come[1].astype(f32) + mixed_come[2].astype(f32)
    out_ref[...] = total.astype(bf16)
    early_r3 = [reduce_quad(1 + part, early_r2[part]) for part in range(PARTS)]

    arrived([normed_own, *normed_z])
    value = normed_cot_s[q] + normed_come[1].astype(f32) + normed_come[2].astype(f32)
    normed_cot_s[q] = value

    @pl.when(at_end)
    def _():
        for i in range(QUAD):
            tail_copy(i).wait_recv()
        rows = pl.ds(CHUNK - TAIL, TAIL)
        normed_cot_s[q, rows, :] += tail_come[0] + tail_come[1] + tail_come[2] + tail_come[3]

    cot = normed_cot_s[q] * gain
    rows = x_ref[...].astype(f32)
    scale = lax.rsqrt(jnp.mean(rows * rows, axis=-1, keepdims=True) + EPS)
    pull = scale * scale * scale * jnp.mean(cot * rows, axis=-1, keepdims=True)
    grad_ref[...] = cot_ref[...].astype(f32) + scale * cot - rows * pull

    arrived(small_copies)
    for j in range(QUAD):
        own = pl.ds(j * QCH, QCH)
        taps_grad_ref[:, own] = small_quad[j, 0:CONV, pl.ds(0, QCH)]
        bias_grad_ref[own] = small_quad[j, CONV : CONV + 1, pl.ds(0, QCH)].reshape(QCH)
        gated_gain_grad_ref[own] = small_quad[j, 5:6, pl.ds(0, QCH)].reshape(QCH)
    quads = small_quad[0] + small_quad[1] + small_quad[2] + small_quad[3]
    taps_grad_ref[:, pl.ds(DI, BC)] = quads[:CONV, QCH:QXBC]
    bias_grad_ref[pl.ds(DI, BC)] = quads[CONV : CONV + 1, QCH:QXBC].reshape(BC)
    gain_grad_ref[pl.ds(0, QXBC)] = quads[6:7].reshape(QXBC)
    gain_grad_ref[pl.ds(QXBC, LANES)] = quads[7:8, :LANES].reshape(LANES)

    def in_head_order(parts):
        total = parts[0]
        for j in range(1, QUAD):
            total = total + pltpu.roll(parts[j], j * QHEADS, 1)
        return total[:, :HEADS]

    def small_heads(row, i):
        parts = [small_quad[j, :, lane_tile(i)] for j in range(QUAD)]
        return in_head_order(parts)[row : row + 1].reshape(HEADS)

    skip_grad_ref[...] = small_heads(5, 3)
    dt_bias_grad_ref[...] = small_heads(5, 4)
    a_log_grad_ref[...] = small_heads(7, 1)

    arrived(late_r3)
    for j in range(QUAD):
        own = pl.ds(j * QCH, QCH)
        in_grad_ref[:, own] = stream_held[0][3][j, :, pl.ds(0, QCH)].astype(f32)
        proj_grad_ref[:, own] = stream_held[0][3][j, :, pl.ds(QCH, QCH)].astype(f32)
    for part in range(PARTS):
        arrived(early_r3[part])

    def early_result(j, low):
        return stream_held[1 + low // PART][3][j, :, pl.ds(low % PART, LANES)].astype(f32)

    for j in range(QUAD):
        for i in range(PAIRS):
            in_grad_ref[:, pl.ds(DI + j * QCH + i * LANES, LANES)] = early_result(j, i * LANES)
    for i in range(BC // LANES):
        total = early_result(0, QCH + i * LANES)
        for j in range(1, QUAD):
            total = total + early_result(j, QCH + i * LANES)
        in_grad_ref[:, pl.ds(2 * DI + i * LANES, LANES)] = total
    in_grad_ref[:, pl.ds(DI + XBC, HEADS)] = in_head_order(
        [early_result(j, QXBC) for j in range(QUAD)]
    )

    assert used[0] == SEMS
    for copy in sent:
        copy.wait_send()

    @pl.when(at_end)
    def _():
        for copy in tail_sends:
            copy.wait_send()

    for i in range(QUAD):

        @pl.when((g == 1) & (q == i))
        def _():
            tail_copy(i).wait_send()


def quad_body(
    inputs,
    norm_gain,
    in_proj,
    conv_weight,
    conv_bias,
    dt_bias,
    a_log,
    skip_gain,
    gated_gain,
    out_proj,
    cotangent,
):
    f32, bf16 = jnp.float32, jnp.bfloat16
    rows = in_proj.shape[0]
    tokens = QUAD * CHUNK
    slots = lax.axis_size("dp") * lax.axis_size("seq")
    width = inputs.shape[1]
    vmem = pltpu.VMEM
    held = [
        vmem((count, rows, w), bf16) for w in (SLAB, *[PART] * PARTS) for count in (16, 8, 4, 4)
    ]
    scratch = [
        vmem((QUAD, rows, SLAB), bf16),
        vmem((QUAD, rows, SLAB), bf16),
        vmem((QUAD, CHUNK, width), bf16),
        vmem((QUAD, CHUNK, width), bf16),
        vmem((TAIL, width), bf16),
        vmem((slots, rows, SLAB), bf16),
        vmem((slots, rows, SLAB), bf16),
        vmem((width, SLAB), bf16),
        vmem((width, SLAB), bf16),
        vmem((TAIL + tokens, width), bf16),
        vmem((TAIL + tokens, SLAB), f32),
        vmem((tokens, QXBC), f32),
        vmem((tokens, QXBC), f32),
        vmem((tokens, LANES), f32),
        vmem((tokens, LANES), f32),
        vmem((tokens, LANES), f32),
        vmem((tokens, LANES), f32),
        vmem((tokens, QCH), bf16),
        vmem((QUAD, PAIRS, STATE, LANES), f32),
        vmem((PAIRS, STATE, LANES), bf16),
        vmem((PAIRS, STATE, LANES), bf16),
        vmem((QUAD, PAIRS, STATE, LANES), bf16),
        vmem((QUAD, PAIRS, CHUNK, 2 * CHUNK), bf16),
        vmem((QUAD, PAIRS, CHUNK, 2 * CHUNK), bf16),
        vmem((tokens, QCH), f32),
        vmem((tokens, QCH), f32),
        vmem((tokens, QCH), f32),
        vmem((tokens, QCH), f32),
        vmem((QUAD, 8, tokens), f32),
        vmem((tokens, QCH), bf16),
        vmem((tokens, QCH), bf16),
        vmem((tokens, QCH), f32),
        vmem((tokens, QCH), bf16),
        vmem((QUAD, PAIRS, STATE, LANES), f32),
        vmem((QUAD + 1, PAIRS, STATE, LANES), bf16),
        vmem((QUAD, CHUNK, CHUNK), bf16),
        vmem((tokens, QCH), f32),
        vmem((TAIL + tokens + 8, QXBC), f32),
        vmem((tokens + LANES, SLAB), bf16),
        vmem((slots, rows, SLAB), bf16),
        vmem((slots, rows, SLAB), bf16),
        vmem((QUAD, CHUNK, width), bf16),
        vmem((3, CHUNK, width), bf16),
        vmem((width, tokens + LANES), bf16),
        vmem((width, tokens), bf16),
        vmem((SLAB, width), bf16),
        vmem((SLAB, width), bf16),
        vmem((QUAD, CHUNK, width), f32),
        vmem((QUAD, CHUNK, width), bf16),
        vmem((3, CHUNK, width), bf16),
        vmem((TAIL, width), f32),
        vmem((QUAD, TAIL, width), f32),
        vmem((GRAD_ROWS, QXBC), f32),
        vmem((8, QCH), f32),
        vmem((5, GRAD_ROWS, QXBC), f32),
        vmem((QUAD, GRAD_ROWS, QXBC), f32),
        *held,
        pltpu.SemaphoreType.DMA((SEMS,)),
        pltpu.SemaphoreType.DMA((SEMS,)),
    ]
    in_vmem = pl.BlockSpec(memory_space=pltpu.VMEM)
    shapes = [inputs.shape, inputs.shape, in_proj.shape, out_proj.shape]
    shapes += [(width,), (CONV, XBC), (XBC,), (HEADS,), (HEADS,), (HEADS,), (DI,)]
    got = pl.pallas_call(
        block_kernel,
        out_shape=[
            jax.ShapeDtypeStruct(shape, f32 if at else bf16) for at, shape in enumerate(shapes)
        ],
        in_specs=[in_vmem] * 11,
        out_specs=[in_vmem] * 11,
        scratch_shapes=scratch,
        compiler_params=pltpu.CompilerParams(
            collective_id=1, has_side_effects=True, vmem_limit_bytes=VMEM_BYTES
        ),
        name="residual_block",
    )(
        inputs,
        norm_gain,
        in_proj,
        conv_weight.T,
        conv_bias,
        dt_bias,
        a_log,
        skip_gain,
        gated_gain,
        out_proj,
        cotangent,
    )
    got = pl.pallas_call(
        copy_out_kernel,
        out_shape=[jax.ShapeDtypeStruct(value.shape, value.dtype) for value in got],
        in_specs=[in_vmem] * 11,
        out_specs=[pl.BlockSpec(memory_space=pl.ANY)] * 11,
        scratch_shapes=[pltpu.SemaphoreType.DMA((11,))],
        name="copy_out",
    )(*got)
    return (*got[:5], got[5].T, *got[6:])


def copy_out_kernel(*refs):
    count = len(refs) // 2
    sems = refs[2 * count]
    copies = [
        pltpu.make_async_copy(refs[i], refs[count + i], sems.at[i]) for i in range(count)
    ]
    for copy in copies:
        copy.start()
    for copy in copies:
        copy.wait()


def fits_quads(mesh):
    return mesh.shape["dp"] == 4 and mesh.shape["seq"] == 2 * QUAD


def solution(mesh):
    placed = (
        P(("dp", "seq"), None),
        P(),
        P(("dp", "seq"), None),
        P(),
        P(),
        P(),
        P(),
        P(),
        P(),
        P(("dp", "seq"), None),
        P(("dp", "seq"), None),
    )
    return jax.shard_map(
        quad_body if fits_quads(mesh) else body,
        mesh=mesh,
        in_specs=placed,
        out_specs=(
            P(("dp", "seq"), None),
            P(("dp", "seq"), None),
            P(("dp", "seq"), None),
            P(("dp", "seq"), None),
            P(),
            P(),
            P(),
            P(),
            P(),
            P(),
            P(),
        ),
        check_vma=False,
    )
```

```python
from functools import partial

import jax
import jax.numpy as jnp
from jax import lax
from jax.experimental import pallas as pl
from jax.experimental.pallas import tpu as pltpu
from jax.sharding import PartitionSpec as P

HEADS = 24
HEAD_DIM = 64
STATE = 128
CONV = 4
DI = 1536
XBC = 1792
PROJ = DI + XBC + HEADS
LANES = 128
WIDE = -(-PROJ // LANES) * LANES


EPS = 1e-05
HIGH = lax.Precision.HIGHEST
MESH = pl.DeviceIdType.MESH
VMEM_BYTES = 60 * 1024 * 1024


def bits_of(count):
    return count.bit_length() - 1


def bit_at(place, bit):
    return (place // 2**bit) % 2


def places():
    return lax.axis_index("dp"), lax.axis_index("seq")


def partner(bit, seq_bits):
    dp_at, seq_at = places()
    if bit < seq_bits:
        return dp_at, seq_at + (1 - 2 * bit_at(seq_at, bit)) * 2**bit
    up = bit - seq_bits
    return dp_at + (1 - 2 * bit_at(dp_at, up)) * 2**up, seq_at


def greet(bits, seq_bits):
    barrier = pltpu.get_barrier_semaphore()
    for bit in range(bits):
        pl.semaphore_signal(barrier, inc=1, device_id=partner(bit, seq_bits), device_id_type=MESH)
    pl.semaphore_wait(barrier, bits)


def gather_orders(seq_bits, dp_bits):
    x_count = seq_bits // 2
    x_bits = list(range(x_count))
    z_bits = list(range(x_count, seq_bits))[::-1]
    core = [seq_bits]
    y_bits = [seq_bits + 1 + i for i in range(dp_bits - 1)]
    return (
        z_bits + x_bits + y_bits + core,
        z_bits + y_bits + x_bits + core,
        z_bits[:1] + x_bits + y_bits + z_bits[1:] + core,
        z_bits[:1] + y_bits + x_bits + z_bits[1:] + core,
    )


SHARES = (0.3, 0.3, 0.2, 0.2)


def split_lanes(width, shares):
    tiles = width // LANES
    edges = [round(tiles * sum(shares[:i])) * LANES for i in range(len(shares) + 1)]
    return [(low, high - low) for low, high in zip(edges, edges[1:])]


def gather_kernel(seq_bits, streams, bits, *refs):
    array_count = 1 + max(stream[0] for stream in streams)
    shards, outs = refs[:array_count], refs[array_count : 2 * array_count]
    send_sem, recv_sem, own_sem = refs[2 * array_count :]
    dp_at, seq_at = places()
    place = dp_at * 2**seq_bits + seq_at
    own = [
        pltpu.make_async_copy(shard, out.at[place], own_sem.at[i])
        for i, (shard, out) in enumerate(zip(shards, outs))
    ]
    for copy in own:
        copy.start()
    greet(bits, seq_bits)
    for copy in own:
        copy.wait()

    def landed(stream, stage, sem):
        which, low, width, _ = streams[stream]
        view = outs[which].at[pl.ds(0, 2**stage), :, pl.ds(low, width)]
        pltpu.make_async_copy(view, view, sem.at[stream, stage]).wait()

    for stage in range(bits + 1):
        for stream, (which, low, width, order) in enumerate(streams):
            if stage > 0:
                landed(stream, stage - 1, recv_sem)
            if stage == bits:
                continue
            free = order[:stage]
            run = 0
            while run in free:
                run += 1
            base = place
            for bit in free:
                base = base - bit_at(place, bit) * 2**bit
            upper = [bit for bit in free if bit > run]
            for combo in range(2 ** len(upper)):
                start = base + sum(2**bit for i, bit in enumerate(upper) if combo >> i & 1)
                view = outs[which].at[pl.ds(start, 2**run), :, pl.ds(low, width)]
                pltpu.make_async_remote_copy(
                    src_ref=view,
                    dst_ref=view,
                    send_sem=send_sem.at[stream, stage],
                    recv_sem=recv_sem.at[stream, stage],
                    device_id=partner(order[stage], seq_bits),
                    device_id_type=MESH,
                ).start()
    for stage in range(bits):
        for stream in range(len(streams)):
            landed(stream, stage, send_sem)


def gather_all(shards, collective_id):
    seq_bits, dp_bits = bits_of(lax.axis_size("seq")), bits_of(lax.axis_size("dp"))
    bits = seq_bits + dp_bits
    orders = gather_orders(seq_bits, dp_bits)
    streams = [
        (which, low, width, order)
        for which, shard in enumerate(shards)
        for (low, width), order in zip(split_lanes(shard.shape[1], SHARES), orders)
    ]
    return pl.pallas_call(
        partial(gather_kernel, seq_bits, streams, bits),
        out_shape=[jax.ShapeDtypeStruct((2**bits, *a.shape), a.dtype) for a in shards],
        in_specs=[pl.BlockSpec(memory_space=pltpu.VMEM)] * len(shards),
        out_specs=[pl.BlockSpec(memory_space=pl.ANY)] * len(shards),
        scratch_shapes=[
            pltpu.SemaphoreType.DMA((len(streams), bits)),
            pltpu.SemaphoreType.DMA((len(streams), bits)),
            pltpu.SemaphoreType.DMA((len(shards),)),
        ],
        compiler_params=pltpu.CompilerParams(
            collective_id=collective_id, has_side_effects=True, vmem_limit_bytes=VMEM_BYTES
        ),
        name="gather_rows",
    )(*shards)


def sum_kernel(seq_bits, streams, bits, array_count, *refs):
    terms, vector = refs[:array_count], refs[array_count]
    outs, vector_out = refs[array_count + 1 : 2 * array_count + 1], refs[2 * array_count + 1]
    held = refs[2 * array_count + 2 : 2 * array_count + 2 + len(streams) * bits]
    rest = refs[2 * array_count + 2 + len(streams) * bits :]
    vector_in, vector_sum, send_sem, recv_sem, vector_send, vector_recv = rest
    dp_at, seq_at = places()
    place = dp_at * 2**seq_bits + seq_at
    greet(bits, seq_bits)

    def source(stream, stage):
        which, low, width, _ = streams[stream]
        if stage == 0:
            return terms[which], pl.ds(low, width)
        return held[stream * bits + stage - 1], pl.ds(0, width)

    def position(stream, stage):
        order = streams[stream][3]
        remaining = sorted(order[stage:])
        return remaining.index(order[stage]), bit_at(place, order[stage])

    def landed(stream, stage, sem):
        view = held[stream * bits + stage]
        pltpu.make_async_copy(view, view, sem.at[stream, stage]).wait()

    def vector_copy(stage):
        return pltpu.make_async_remote_copy(
            src_ref=vector if stage == 0 else vector_sum.at[stage - 1],
            dst_ref=vector_in.at[stage],
            send_sem=vector_send.at[stage],
            recv_sem=vector_recv.at[stage],
            device_id=partner(stage, seq_bits),
            device_id_type=MESH,
        )

    for stage in range(bits + 1):
        if stage > 0:
            vector_copy(stage - 1).wait_recv()
            before = vector[...] if stage == 1 else vector_sum[stage - 2]
            total = before + vector_in[stage - 1]
            if stage < bits:
                vector_sum[stage - 1] = total
            else:
                vector_out[...] = total
        if stage < bits:
            vector_copy(stage).start()
        for stream, (which, low, width, order) in enumerate(streams):
            if stage > 0:
                landed(stream, stage - 1, recv_sem)
                spot, mine = position(stream, stage - 1)
                kept, lanes = source(stream, stage - 1)
                came = held[stream * bits + stage - 1]
                if stage == bits:
                    outs[which][:, pl.ds(low, width)] = kept[mine, :, lanes].astype(
                        jnp.float32
                    ) + came[0].astype(jnp.float32)
                    continue

                def add_one(block, carry, spot=spot, mine=mine, kept=kept, lanes=lanes, came=came):
                    from_block = (block // 2**spot) * 2 ** (spot + 1) + mine * 2**spot
                    from_block = from_block + block % 2**spot
                    added = kept[from_block, :, lanes].astype(jnp.float32) + came[block].astype(
                        jnp.float32
                    )
                    came[block] = added.astype(came.dtype)
                    return carry

                lax.fori_loop(0, 2 ** (bits - stage), add_one, 0)
            spot, mine = position(stream, stage)
            sent, lanes = source(stream, stage)
            for high in range(2 ** (bits - stage - 1 - spot)):
                start = high * 2 ** (spot + 1) + (1 - mine) * 2**spot
                pltpu.make_async_remote_copy(
                    src_ref=sent.at[pl.ds(start, 2**spot), :, lanes],
                    dst_ref=held[stream * bits + stage].at[pl.ds(high * 2**spot, 2**spot)],
                    send_sem=send_sem.at[stream, stage],
                    recv_sem=recv_sem.at[stream, stage],
                    device_id=partner(order[stage], seq_bits),
                    device_id_type=MESH,
                ).start()
    for stage in range(bits):
        vector_copy(stage).wait_send()
        for stream in range(len(streams)):
            landed(stream, stage, send_sem)


def sum_to_owners(terms, vector, collective_id):
    seq_bits, dp_bits = bits_of(lax.axis_size("seq")), bits_of(lax.axis_size("dp"))
    bits = seq_bits + dp_bits
    orders = [order[::-1] for order in gather_orders(seq_bits, dp_bits)]
    terms = [term.reshape(2**bits, -1, term.shape[1]) for term in terms]
    streams = [
        (which, low, width, order)
        for which, term in enumerate(terms)
        for (low, width), order in zip(split_lanes(term.shape[2], SHARES), orders)
    ]
    rows = terms[0].shape[1]
    in_vmem = pl.BlockSpec(memory_space=pltpu.VMEM)
    held = [
        pltpu.VMEM((2 ** (bits - 1 - stage), rows, width), jnp.bfloat16)
        for _, _, width, _ in streams
        for stage in range(bits)
    ]
    return pl.pallas_call(
        partial(sum_kernel, seq_bits, streams, bits, len(terms)),
        out_shape=[jax.ShapeDtypeStruct(a.shape[1:], jnp.float32) for a in terms]
        + [jax.ShapeDtypeStruct(vector.shape, vector.dtype)],
        in_specs=[in_vmem] * (len(terms) + 1),
        out_specs=[in_vmem] * (len(terms) + 1),
        scratch_shapes=held
        + [
            pltpu.VMEM((bits, *vector.shape), jnp.float32),
            pltpu.VMEM((bits, *vector.shape), jnp.float32),
            pltpu.SemaphoreType.DMA((len(streams), bits)),
            pltpu.SemaphoreType.DMA((len(streams), bits)),
            pltpu.SemaphoreType.DMA((bits,)),
            pltpu.SemaphoreType.DMA((bits,)),
        ],
        compiler_params=pltpu.CompilerParams(
            collective_id=collective_id, has_side_effects=True, vmem_limit_bytes=VMEM_BYTES
        ),
        name="sum_rows",
    )(*terms, vector)


GROUP = 4
GROUP_LANES = GROUP * HEAD_DIM


def inner_product(left, right, dims):
    return lax.dot_general(
        left, right, (dims, ((), ())), precision=HIGH, preferred_element_type=jnp.float32
    )


def group_lanes(group):
    return pl.ds(pl.multiple_of(group * GROUP_LANES, GROUP_LANES), GROUP_LANES)


def head_weights(cumulative, head):
    row = cumulative[pl.ds(head, 1), :]
    count = row.shape[1]
    spread = jnp.broadcast_to(row, (count, count))
    later = lax.broadcasted_iota(jnp.int32, (count, count), 0)
    earlier = lax.broadcasted_iota(jnp.int32, (count, count), 1)
    return jnp.exp(jnp.where(later >= earlier, spread.T - spread, -jnp.inf))


def inside_work(first, last, scaled_x, b_mat, c_mat, cumulative, output, crossed):
    if first == 0:
        crossed[...] = inner_product(c_mat[...], b_mat[...], ((1,), (1,)))

    def one(group, carry):
        values = scaled_x[:, group_lanes(group)]
        parts = []
        for i in range(GROUP):
            scores = head_weights(cumulative, group * GROUP + i) * crossed[...]
            head = values[:, i * HEAD_DIM : (i + 1) * HEAD_DIM]
            parts.append(inner_product(scores, head, ((1,), (0,))))
        output[:, group_lanes(group)] = jnp.concatenate(parts, axis=1)
        return carry

    lax.fori_loop(first, last, one, 0)


def inside_back(
    first,
    last,
    output_cot,
    scaled_x,
    b_mat,
    c_mat,
    cumulative,
    scaled_cot,
    b_cot,
    c_cot,
    cumulative_cot,
    crossed,
    crossed_cot,
):
    if first == 0:
        crossed[...] = inner_product(c_mat[...], b_mat[...], ((1,), (1,)))
        crossed_cot[...] = jnp.zeros_like(crossed_cot)

    def one(group, carry):
        values = scaled_x[:, group_lanes(group)]
        cots = output_cot[:, group_lanes(group)]
        parts = []
        total = crossed_cot[...]
        for i in range(GROUP):
            weights = head_weights(cumulative, group * GROUP + i)
            scores = weights * crossed[...]
            head = values[:, i * HEAD_DIM : (i + 1) * HEAD_DIM]
            cot = cots[:, i * HEAD_DIM : (i + 1) * HEAD_DIM]
            weighted = weights * inner_product(cot, head, ((1,), (1,)))
            total = total + weighted
            parts.append(inner_product(scores, cot, ((0,), (0,))))
            moved = weighted * crossed[...]
            cumulative_cot[pl.ds(group * GROUP + i, 1), :] = jnp.sum(
                moved.T, axis=0, keepdims=True
            ) - jnp.sum(moved, axis=0, keepdims=True)
        crossed_cot[...] = total
        scaled_cot[:, group_lanes(group)] = jnp.concatenate(parts, axis=1)
        return carry

    lax.fori_loop(first, last, one, 0)
    if last == HEADS // GROUP:
        b_cot[...] = inner_product(crossed_cot[...], c_mat[...], ((0,), (0,)))
        c_cot[...] = inner_product(crossed_cot[...], b_mat[...], ((1,), (0,)))


def scan_kernel(count, reverse, work, inputs, outputs, *refs):
    state, decay = refs[:2]
    given = refs[2 : 2 + inputs]
    out = refs[2 + inputs]
    made = refs[3 + inputs : 3 + inputs + outputs]
    came, came_decay, ready = refs[3 + inputs + outputs : 6 + inputs + outputs]
    sems = refs[6 + inputs + outputs : 12 + inputs + outputs]
    held = refs[12 + inputs + outputs :]
    out_send, out_recv, decay_send, decay_recv, back_send, back_recv = sems
    dp_at, seq_at = places()
    barrier = pltpu.get_barrier_semaphore()
    peers = [(seq_at + hop) % count for hop in range(1, count)]
    for peer in peers:
        pl.semaphore_signal(barrier, inc=1, device_id=(dp_at, peer), device_id_type=MESH)
    pl.semaphore_wait(barrier, count - 1)

    def copy(hop, which):
        target = (seq_at + hop) % count
        source, landing, send_sem, recv_sem = (
            (state.at[target], came.at[seq_at], out_send, out_recv),
            (decay, came_decay.at[seq_at], decay_send, decay_recv),
            (ready.at[target], out.at[seq_at], back_send, back_recv),
        )[which]
        return pltpu.make_async_remote_copy(
            src_ref=source,
            dst_ref=landing,
            send_sem=send_sem.at[hop],
            recv_sem=recv_sem.at[hop],
            device_id=(dp_at, target),
            device_id_type=MESH,
        )

    for hop in range(1, count):
        copy(hop, 0).start()
        copy(hop, 1).start()
    came[seq_at] = state[seq_at]
    came_decay[seq_at] = decay[...]
    groups = HEADS // GROUP
    work(0, groups // 2, *given, *made, *held)
    for hop in range(1, count):
        copy(hop, 0).wait_recv()
        copy(hop, 1).wait_recv()
    total = jnp.zeros(state.shape[1:], jnp.float32)
    for place in range(count)[:: -1 if reverse else 1]:
        ready[place] = total.astype(ready.dtype)
        total = came_decay[place] * total + came[place].astype(jnp.float32)
    for hop in range(1, count):
        copy(hop, 2).start()
    out[seq_at] = ready[seq_at]
    work(groups // 2, groups, *given, *made, *held)
    for hop in range(1, count):
        copy(hop, 2).wait_recv()
    for hop in range(1, count):
        for which in range(3):
            copy(hop, which).wait_send()


def scan_states(state, decay, work, given, made, held, reverse, collective_id):
    count = lax.axis_size("seq")
    state = state.astype(jnp.bfloat16).reshape(count, STATE // count, DI)
    in_vmem = pl.BlockSpec(memory_space=pltpu.VMEM)
    got = pl.pallas_call(
        partial(scan_kernel, count, reverse, work, len(given), len(made)),
        out_shape=[jax.ShapeDtypeStruct(state.shape, state.dtype)]
        + [jax.ShapeDtypeStruct(shape, jnp.float32) for shape in made],
        in_specs=[in_vmem] * (2 + len(given)),
        out_specs=[in_vmem] * (1 + len(made)),
        scratch_shapes=[
            pltpu.VMEM(state.shape, state.dtype),
            pltpu.VMEM((count, 1, DI), jnp.float32),
            pltpu.VMEM(state.shape, state.dtype),
        ]
        + [pltpu.SemaphoreType.DMA((count,))] * 6
        + [pltpu.VMEM(shape, jnp.float32) for shape in held],
        compiler_params=pltpu.CompilerParams(
            collective_id=collective_id, has_side_effects=True, vmem_limit_bytes=VMEM_BYTES
        ),
        name="scan_back" if reverse else "scan_states",
    )(state, decay[None, :], *given)
    return got[0].reshape(STATE, DI).astype(jnp.float32), *got[1:]


def passed_along(value, axis, steps):
    count = lax.axis_size(axis)
    first, last = (max(0, -steps), min(count, count - steps))
    return lax.ppermute(value, axis, [(source, source + steps) for source in range(first, last)])


def pre_norm(residual_in, norm_gain):
    scale_rms = lax.rsqrt(jnp.mean(residual_in * residual_in, axis=-1, keepdims=True) + EPS)
    return residual_in * scale_rms * norm_gain


def conv_silu(padded, conv_weight, conv_bias, row_count):
    total = jnp.zeros((row_count, padded.shape[1]), jnp.float32) + conv_bias[None, :]
    for offset in range(conv_weight.shape[1]):
        total = total + conv_weight[:, offset][None, :] * padded[offset : offset + row_count]
    return jax.nn.silu(total)


def head_lanes():
    lanes = jnp.arange(DI, dtype=jnp.int32) // HEAD_DIM
    return (jnp.arange(HEADS, dtype=jnp.int32)[:, None] == lanes[None, :]).astype(jnp.float32)


def spread_heads(by_head):
    return jnp.dot(by_head, head_lanes(), precision=HIGH)


def sum_heads(by_lane):
    return jnp.dot(by_lane, head_lanes().T, precision=HIGH)


def before_states(xbc, dt_raw, edge, conv_weight, conv_bias, dt_bias, a_log):
    row_count = xbc.shape[0]
    activated = conv_silu(jnp.concatenate([edge, xbc], axis=0), conv_weight, conv_bias, row_count)
    xs = activated[:, :DI]
    b_mat = activated[:, DI : DI + STATE]
    c_mat = activated[:, DI + STATE :]
    step = jax.nn.softplus(dt_raw + dt_bias)
    log_decay = step * -jnp.exp(a_log)
    at = jnp.arange(row_count)
    lower = (at[:, None] >= at[None, :]).astype(jnp.float32)
    cumulative = jnp.dot(lower, log_decay, precision=HIGH)
    scaled_x = xs * spread_heads(step)
    tail = jnp.exp(cumulative[-1][None, :] - cumulative)
    fresh = jnp.dot(b_mat.T, scaled_x * spread_heads(tail), precision=HIGH)
    return (xs, scaled_x, b_mat, c_mat, cumulative, fresh)


def post_gate(ssd_out, xs, gate_part, skip_gain, gated_gain):
    skipped = xs * spread_heads(skip_gain[None, :])
    mixed_in = (ssd_out + skipped) * jax.nn.silu(gate_part)
    scale_rms = lax.rsqrt(jnp.mean(mixed_in * mixed_in, axis=-1, keepdims=True) + EPS)
    return mixed_in * scale_rms * gated_gain


def contract_rows(left, right):
    return lax.dot_general(
        left, right, (((0,), (0,)), ((), ())), preferred_element_type=jnp.float32
    )


def contract_cols(left, right):
    return lax.dot_general(
        left, right, (((1,), (1,)), ((), ())), preferred_element_type=jnp.float32
    )


def body(
    inputs,
    norm_gain,
    in_proj,
    conv_weight,
    conv_bias,
    dt_bias,
    a_log,
    skip_gain,
    gated_gain,
    out_proj,
    cotangent,
):
    row_count = inputs.shape[0]
    residual_in = inputs.astype(jnp.float32)
    normed_full, norm_back = jax.vjp(pre_norm, residual_in, norm_gain)
    normed = normed_full.astype(jnp.bfloat16)
    in_whole, out_whole = gather_all(
        [jnp.pad(in_proj, ((0, 0), (0, WIDE - PROJ))), out_proj], collective_id=1
    )
    in_whole = in_whole.reshape(-1, WIDE)
    out_whole = out_whole.reshape(-1, DI)
    projected = jnp.dot(normed, in_whole, preferred_element_type=jnp.float32)
    gate_part = projected[:, :DI]
    xbc = projected[:, DI : DI + XBC]
    dt_raw = projected[:, DI + XBC : PROJ]
    edge = passed_along(xbc[row_count - (CONV - 1) :], "seq", 1)
    primal, mid_back = jax.vjp(
        before_states, xbc, dt_raw, edge, conv_weight, conv_bias, dt_bias, a_log
    )
    xs, scaled_x, b_mat, c_mat, cumulative, s_local = primal
    by_head = cumulative.T
    decay = jnp.exp(cumulative[-1])
    wide_decay = spread_heads(decay[None, :])[0]
    square = (row_count, row_count)
    state_in, local_out = scan_states(
        s_local,
        wide_decay,
        inside_work,
        [scaled_x, b_mat, c_mat, by_head],
        [xs.shape],
        [square],
        False,
        collective_id=2,
    )
    weighted = spread_heads(jnp.exp(cumulative))
    carried_part = jnp.dot(c_mat, state_in, precision=HIGH) * weighted
    ssd_out = local_out + carried_part
    gated_full, post_back = jax.vjp(post_gate, ssd_out, xs, gate_part, skip_gain, gated_gain)
    gated = gated_full.astype(jnp.bfloat16)
    mixed = contract_cols(gated, out_whole)
    layer_out = (residual_in + mixed).astype(jnp.bfloat16)
    gated_cot = jnp.dot(cotangent, out_whole, preferred_element_type=jnp.float32)
    ssd_cot, xs_cot, gate_cot, skip_grad, gated_gain_grad = post_back(gated_cot)
    scaled_cot = ssd_cot * weighted
    local_grad = jnp.dot(c_mat.T, scaled_cot, precision=HIGH)
    later_grad, scaled_x_cot, b_cot, inner_c_cot, by_head_cot = scan_states(
        local_grad,
        wide_decay,
        inside_back,
        [ssd_cot, scaled_x, b_mat, c_mat, by_head],
        [xs.shape, b_mat.shape, c_mat.shape, by_head.shape],
        [square, square],
        True,
        collective_id=3,
    )
    c_cot = lax.dot_general(scaled_cot, state_in, (((1,), (1,)), ((), ())), precision=HIGH)
    cum_cot = sum_heads(ssd_cot * carried_part)
    last_cot = sum_heads(jnp.sum(later_grad * state_in, axis=0, keepdims=True))[0] * decay
    is_last = (jnp.arange(row_count) == row_count - 1)[:, None]
    cum_cot = cum_cot + jnp.where(is_last, last_cot[None, :], 0.0)
    mid_grads = mid_back(
        (xs_cot, scaled_x_cot, b_cot, c_cot + inner_c_cot, cum_cot + by_head_cot.T, later_grad)
    )
    xbc_cot, dt_cot, edge_cot, conv_weight_grad, conv_bias_grad, dt_bias_grad, a_log_grad = (
        mid_grads
    )
    edge_back = passed_along(edge_cot, "seq", -1)
    xbc_cot = xbc_cot + jnp.pad(edge_back, ((row_count - (CONV - 1), 0), (0, 0)))
    projected_cot = jnp.concatenate(
        [gate_cot, xbc_cot, dt_cot, jnp.zeros((row_count, WIDE - PROJ), jnp.float32)], axis=1
    ).astype(jnp.bfloat16)
    in_term = contract_rows(normed, projected_cot).astype(jnp.bfloat16)
    out_term = contract_rows(cotangent, gated).astype(jnp.bfloat16)
    normed_cot = contract_cols(projected_cot, in_whole)
    input_part, norm_gain_grad = norm_back(normed_cot)
    input_grad = cotangent.astype(jnp.float32) + input_part
    small = (
        norm_gain_grad,
        conv_weight_grad.T,
        conv_bias_grad,
        gated_gain_grad,
        dt_bias_grad,
        a_log_grad,
        skip_grad,
    )
    flat = jnp.concatenate([a.reshape(-1) for a in small])
    tile = 8 * LANES
    flat = jnp.pad(flat, (0, -flat.shape[0] % tile))
    in_proj_grad, out_proj_grad, summed = sum_to_owners(
        [in_term, out_term], flat.reshape(-1, LANES), collective_id=4
    )
    summed = summed.reshape(-1)
    parts, at = [], 0
    for a in small:
        parts.append(summed[at : at + a.size].reshape(a.shape))
        at += a.size
    return (
        layer_out,
        input_grad,
        in_proj_grad[:, :PROJ],
        out_proj_grad,
        parts[0],
        parts[1].T,
        parts[2],
        parts[4],
        parts[5],
        parts[6],
        parts[3],
    )


QUAD = 4
CHUNK = 128
TAIL = 16
QCH = DI // QUAD
QHEADS = HEADS // QUAD
PAIRS = QCH // LANES
BC = 2 * STATE
QXBC = QCH + BC
SLAB = QXBC + LANES
PARTS = 3
PART = SLAB // PARTS
GRAD_ROWS = 8
SEMS = 94


def flip(value, bit):
    return value + (1 - 2 * bit_at(value, bit)) * 2**bit


def flip_quad(value, mask):
    for bit in range(2):
        if mask >> bit & 1:
            value = flip(value, bit)
    return value


def dot_nn(left, right):
    return lax.dot_general(
        left, right, (((1,), (0,)), ((), ())), preferred_element_type=jnp.float32
    )


def dot_nt(left, right):
    return lax.dot_general(
        left, right, (((1,), (1,)), ((), ())), preferred_element_type=jnp.float32
    )


def dot_tn(left, right):
    return lax.dot_general(
        left, right, (((0,), (0,)), ((), ())), preferred_element_type=jnp.float32
    )


def in_parts(value, count):
    parts = []
    for _ in range(count):
        part = value.astype(jnp.bfloat16)
        parts.append(part)
        value = value - part.astype(jnp.float32)
    return parts


def lane_tile(i):
    return pl.ds(i * LANES, LANES)


def chunk_rows(c, offset=0, count=CHUNK):
    return pl.ds(pl.multiple_of(c * CHUNK + offset, 8), count)


def column_sum(value):
    return jnp.sum(value, axis=0, keepdims=True)


def block_kernel(
    x_hbm,
    gain_hbm,
    in_hbm,
    taps_hbm,
    bias_hbm,
    dt_bias_hbm,
    a_log_hbm,
    skip_hbm,
    gated_gain_hbm,
    proj_hbm,
    cot_hbm,
    out_ref,
    grad_ref,
    in_grad_ref,
    proj_grad_ref,
    gain_grad_ref,
    taps_grad_ref,
    bias_grad_ref,
    dt_bias_grad_ref,
    a_log_grad_ref,
    skip_grad_ref,
    gated_gain_grad_ref,
    x_ref,
    gain_ref,
    in_ref,
    taps_ref,
    bias_ref,
    dt_bias_ref,
    a_log_ref,
    skip_ref,
    gated_gain_ref,
    proj_ref,
    cot_ref,
    load_sem,
    early_ref,
    late_ref,
    xq,
    cq,
    xtail,
    early_slots,
    late_slots,
    early_w,
    late_w,
    xn,
    proj,
    act,
    act_slope,
    step_s,
    step_slope,
    log_s,
    cum_s,
    sx_s,
    fresh_s,
    state_out,
    state_come,
    state_s,
    weights_s,
    scores_s,
    ssd_s,
    gate_s,
    gc_s,
    m_s,
    sums_s,
    gated_s,
    gate_cot_s,
    y_s,
    z_s,
    back_s,
    later_s,
    cross_s,
    sx_cot_s,
    pre_cot_s,
    early_cot_s,
    late_term,
    early_term,
    mixed_s,
    mixed_come,
    normed_t,
    cot_t,
    early_wt,
    late_wt,
    normed_cot_s,
    normed_out,
    normed_come,
    tail_out,
    tail_come,
    small_s,
    skip_s,
    small_come,
    small_quad,
    *rest,
):
    stream_held = [rest[4 * i : 4 * i + 4] for i in range(1 + PARTS)]
    send_sem, recv_sem = rest[4 + 4 * PARTS :]
    f32, bf16 = jnp.float32, jnp.bfloat16
    dp_at, seq_at = places()
    q, g = seq_at % QUAD, seq_at // QUAD
    core, y_at = dp_at % 2, dp_at // 2
    place = dp_at * 8 + seq_at
    used = [0]
    sent = []

    loads = [
        pltpu.make_async_copy(source, landing, load_sem.at[i])
        for i, (source, landing) in enumerate(
            [
                (in_hbm, in_ref),
                (proj_hbm, proj_ref),
                (x_hbm, x_ref),
                (gain_hbm, gain_ref),
                (taps_hbm, taps_ref),
                (bias_hbm, bias_ref),
                (dt_bias_hbm, dt_bias_ref),
                (a_log_hbm, a_log_ref),
                (skip_hbm, skip_ref),
                (gated_gain_hbm, gated_gain_ref),
                (cot_hbm, cot_ref),
            ]
        )
    ]
    for load in loads:
        load.start()

    barrier = pltpu.get_barrier_semaphore()
    peers = [(dp_at, (seq_at + hop) % 8) for hop in range(1, 8)]
    peers += [(flip(dp_at, 0), seq_at), (flip(dp_at, 1), seq_at)]
    peers += [(flip(dp_at, 1), flip(seq_at, 2))]
    for peer in peers:
        pl.semaphore_signal(barrier, inc=1, device_id=peer, device_id_type=MESH)

    def remote(source, landing, target, own=True):
        at = used[0]
        used[0] += 1
        copy = pltpu.make_async_remote_copy(
            src_ref=source,
            dst_ref=landing,
            send_sem=send_sem.at[at],
            recv_sem=recv_sem.at[at],
            device_id=target,
            device_id_type=MESH,
        )
        if own:
            copy.start()
            sent.append(copy)
        return copy

    half_lanes = [pl.ds(h * SLAB // 2, SLAB // 2) for h in range(2)]

    def share_block(own_block, slots):
        over_z = [
            remote(own_block.at[:, lanes], slots.at[q, :, lanes], in_quad(2))
            for lanes in half_lanes
        ]
        return over_z, remote(own_block, slots.at[q], in_quad(1))

    def pass_block(slots, over_z):
        made = []
        for copy, lanes in zip(over_z, half_lanes):
            copy.wait_recv()
            view = slots.at[flip_quad(q, 2), :, lanes]
            made.append(remote(view, view, in_quad(1)))
        return made

    def send_sums(blocks, landing):
        over_x = [
            remote(blocks.at[flip_quad(q, 3), :, lanes], landing.at[0, :, lanes], in_quad(1))
            for lanes in half_lanes
        ]
        return over_x, remote(blocks.at[flip_quad(q, 1)], landing.at[1], in_quad(1))

    def pass_sums(mine, blocks, landing, over_x):
        made = []
        other = flip_quad(q, 2)
        for copy, lanes in zip(over_x, half_lanes):
            copy.wait_recv()
            blocks[other, :, lanes] = (
                mine[other, :, lanes].astype(f32) + landing[0, :, lanes].astype(f32)
            ).astype(bf16)
            made.append(
                remote(blocks.at[other, :, lanes], landing.at[2, :, lanes], in_quad(2))
            )
        return made

    def in_quad(mask):
        return dp_at, flip_quad(seq_at, mask)

    far = (dp_at, flip(seq_at, 2))
    beside = (flip(dp_at, 1), seq_at)
    twin = (flip(dp_at, 0), seq_at)

    def arrived(copies):
        for copy in copies:
            copy.wait_recv()

    lane = lax.broadcasted_iota(jnp.int32, (1, LANES), 1)
    first_half = lane < HEAD_DIM
    half0 = jnp.where(first_half, 1.0, 0.0)
    half1 = 1.0 - half0
    half0b, half1b = half0.astype(bf16), half1.astype(bf16)
    row_at = lax.broadcasted_iota(jnp.int32, (CHUNK, CHUNK), 0)
    lane_at = lax.broadcasted_iota(jnp.int32, (CHUNK, CHUNK), 1)
    causal = row_at >= lane_at
    lower = jnp.where(causal, 1.0, 0.0).astype(bf16)
    upper = jnp.where(row_at <= lane_at, 1.0, 0.0).astype(bf16)
    lower3 = jnp.concatenate([lower] * 3, axis=1)
    upper3 = jnp.concatenate([upper] * 3, axis=1)

    def spread(by_head, i):
        return jnp.where(first_half, by_head[:, 2 * i : 2 * i + 1], by_head[:, 2 * i + 1 : 2 * i + 2])

    head_picks = []
    for i in range(PAIRS):
        pick = jnp.where(2 * i + row_at // HEAD_DIM == lane_at, 1.0, 0.0).astype(bf16)
        head_picks.append(jnp.concatenate([pick] * 2, axis=0))

    def head_sum(value, i):
        return dot_nn(jnp.concatenate(in_parts(value, 2), axis=1), head_picks[i])

    def flat_row(ref, low, count):
        return ref[pl.ds(low, count)].reshape(1, count)

    def own_channels(i):
        return pl.ds(pl.multiple_of(q * QCH + i * LANES, LANES), LANES)

    def conv_channels(i):
        return own_channels(i) if i < PAIRS else pl.ds(DI + (i - PAIRS) * LANES, LANES)

    def tap(k, i):
        return taps_ref[pl.ds(k, 1), conv_channels(i)]

    def gated_gain(i):
        return gated_gain_ref[own_channels(i)].reshape(1, LANES)

    def own_heads(ref):
        head_at = lax.broadcasted_iota(jnp.int32, (HEADS, LANES), 0)
        to = lax.broadcasted_iota(jnp.int32, (HEADS, LANES), 1)
        pick = jnp.where((head_at == to + q * QHEADS) & (to < QHEADS), 1.0, 0.0)
        value = jnp.broadcast_to(ref[...].reshape(1, HEADS), (8, HEADS))
        return inner_product(value, pick, ((1,), (0,)))[:1]

    def stacked(value):
        return jnp.concatenate([value * half0b, value * half1b], axis=0)

    loads[0].wait()
    loads[1].wait()
    for j in range(QUAD):
        own = pl.ds(j * QCH, QCH)
        early_ref[j, :, pl.ds(0, QCH)] = in_ref[:, pl.ds(DI + j * QCH, QCH)]
        early_ref[j, :, pl.ds(QCH, BC)] = in_ref[:, pl.ds(2 * DI, BC)]
        head_at = lax.broadcasted_iota(jnp.int32, (HEADS, LANES), 0)
        to = lax.broadcasted_iota(jnp.int32, (HEADS, LANES), 1)
        pick = jnp.where((head_at == to + j * QHEADS) & (to < QHEADS), 1.0, 0.0)
        early_ref[j, :, pl.ds(QXBC, LANES)] = dot_nn(
            in_ref[:, pl.ds(DI + XBC, HEADS)], pick.astype(bf16)
        ).astype(bf16)
        late_ref[j, :, pl.ds(0, QCH)] = in_ref[:, own]
        late_ref[j, :, pl.ds(QCH, QCH)] = proj_ref[:, own]

    for load in loads[2:]:
        load.wait()
    pl.semaphore_wait(barrier, len(peers))

    def scatter(shard, slots):
        return [
            remote(shard.at[flip_quad(q, mask)], slots.at[place], in_quad(mask))
            for mask in (1, 2, 3)
        ]

    early_0 = scatter(early_ref, early_slots)
    late_0 = scatter(late_ref, late_slots)
    token_z, token_x = share_block(x_ref, xq)
    tail_sends = [
        remote(x_ref.at[pl.ds(CHUNK - TAIL, TAIL)], xtail, (dp_at, QUAD + i), own=False)
        for i in range(QUAD)
    ]
    at_end = seq_at == QUAD - 1

    @pl.when(at_end)
    def _():
        for copy in tail_sends:
            copy.start()

    early_slots[place] = early_ref[q]
    late_slots[place] = late_ref[q]
    xq[q] = x_ref[...]
    cq[q] = cot_ref[...]

    def cross_far(slots, parts):
        wide = SLAB // parts
        return [
            remote(
                slots.at[pl.ds(dp_at * 8 + g * 4, 4), :, lane_part],
                slots.at[pl.ds(dp_at * 8 + g * 4, 4), :, lane_part],
                far,
            )
            for lane_part in [pl.ds(part * wide, wide) for part in range(parts)]
        ]

    def cross_beside(slots, copies):
        made = []
        for part, copy in enumerate(copies):
            copy.wait_recv()
            wide = SLAB // len(copies)
            view = slots.at[pl.ds(dp_at * 8, 8), :, pl.ds(part * wide, wide)]
            made.append(remote(view, view, beside))
        return made

    def cross_twin(slots, copies):
        made = []
        for part, copy in enumerate(copies):
            copy.wait_recv()
            for up in range(2):
                wide = SLAB // len(copies)
                view = slots.at[pl.ds((2 * up + core) * 8, 8), :, pl.ds(part * wide, wide)]
                made.append(remote(view, view, twin))
        return made

    def flatten(slots, flat, low=0, wide=SLAB):
        lanes = pl.ds(low, wide)

        def one(pair, carry):
            value = slots[pl.ds(2 * pair, 2), :, lanes].astype(f32).reshape(48, wide)
            flat[pl.ds(pl.multiple_of(pair * 48, 16), 48), lanes] = value.astype(bf16)
            return carry

        lax.fori_loop(0, 16, one, 0)

    arrived(early_0)
    early_1 = cross_far(early_slots, PARTS)
    token_pass = pass_block(xq, token_z)
    early_2 = cross_beside(early_slots, early_1)
    arrived(late_0)
    late_1 = cross_far(late_slots, 2)
    cot_z, cot_x = share_block(cot_ref, cq)

    arrived([token_x, *token_pass])

    for i in range(QUAD):

        @pl.when((g == 1) & (q == i))
        def _():
            tail_sends[i].wait_recv()

    @pl.when(g == 0)
    def _():
        xtail[...] = jnp.zeros_like(xtail)

    gain = flat_row(gain_ref, 0, x_ref.shape[1])

    def scaled_rows(value):
        value = value.astype(f32)
        return value * lax.rsqrt(jnp.mean(value * value, axis=-1, keepdims=True) + EPS)

    tail_rows = scaled_rows(xtail[...]) * gain
    xn[pl.ds(0, TAIL), :] = tail_rows.astype(bf16)
    normed_t[:, pl.ds(QUAD * CHUNK, LANES)] = jnp.concatenate(
        [tail_rows, jnp.zeros((LANES - TAIL, tail_rows.shape[1]), f32)], axis=0
    ).T.astype(bf16)
    early_cot_s[pl.ds(QUAD * CHUNK, LANES), :] = jnp.zeros((LANES, SLAB), bf16)

    def norm_block(c, carry):
        value = scaled_rows(xq[c]) * gain
        xn[pl.ds(pl.multiple_of(c * CHUNK + TAIL, 16), CHUNK), :] = value.astype(bf16)
        normed_t[:, pl.ds(pl.multiple_of(c * CHUNK, CHUNK), CHUNK)] = value.T.astype(bf16)
        return carry

    lax.fori_loop(0, QUAD, norm_block, 0)
    early_3 = cross_twin(early_slots, early_2)
    cot_pass = pass_block(cq, cot_z)
    late_2 = cross_beside(late_slots, late_1)
    small_s[...] = jnp.zeros_like(small_s)
    skip_s[...] = jnp.zeros_like(skip_s)
    pre_cot_s[pl.ds(0, TAIL), :] = jnp.zeros((TAIL, QXBC), f32)
    pre_cot_s[pl.ds(TAIL + QUAD * CHUNK, 8), :] = jnp.zeros((8, QXBC), f32)
    for part in range(PARTS):
        cols = pl.ds(part * PART, PART)
        each = len(early_3) // PARTS
        arrived(early_3[part * each : (part + 1) * each])
        flatten(early_slots, early_w, part * PART, PART)
        proj[:, cols] = dot_nn(xn[...], early_w[:, cols])

        def forward_conv(c, carry, part=part):
            rows = chunk_rows(c)
            for i in range(part * PART // LANES, min((part + 1) * PART, QXBC) // LANES):
                lanes = lane_tile(i)
                window = proj[chunk_rows(c, 8, CHUNK + 8), lanes]
                total = bias_ref[conv_channels(i)].reshape(1, LANES)
                for k in range(CONV):
                    total = total + tap(k, i) * pltpu.roll(window, CHUNK + 3 - k, 0)[:CHUNK]
                sig = lax.logistic(total)
                act[rows, lanes] = total * sig
                act_slope[rows, lanes] = sig * (1.0 + total * (1.0 - sig))
            return carry

        lax.fori_loop(0, QUAD, forward_conv, 0)

    rate = -jnp.exp(own_heads(a_log_ref))
    dt_bias = own_heads(dt_bias_ref)
    skips = own_heads(skip_ref)
    skip_wide = [spread(skips, i) for i in range(PAIRS)]
    head_lane = lane < QHEADS

    def forward_states(c, carry):
        rows = chunk_rows(c)
        raw = proj[chunk_rows(c, TAIL), pl.ds(QXBC, LANES)] + dt_bias
        step = jnp.maximum(raw, 0.0) + jnp.log1p(jnp.exp(-jnp.abs(raw)))
        step = jnp.where(head_lane, step, 0.0)
        log_decay = step * rate
        cum = dot_nn(lower3, jnp.concatenate(in_parts(log_decay, 3), axis=0))
        step_s[rows, :] = step
        step_slope[rows, :] = lax.logistic(raw)
        log_s[rows, :] = log_decay
        cum_s[rows, :] = cum
        tail = jnp.exp(cum[CHUNK - 1 :] - cum)
        b_mat = act[rows, pl.ds(QCH, STATE)].astype(bf16)
        for i in range(PAIRS):
            lanes = lane_tile(i)
            sx = act[rows, lanes] * spread(step, i)
            sx_s[rows, lanes] = sx.astype(bf16)
            fresh_s[c, i] = dot_tn(b_mat, (sx * spread(tail, i)).astype(bf16))
        return carry

    lax.fori_loop(0, QUAD, forward_states, 0)

    def chunk_decay(c, i):
        last = cum_s[chunk_rows(c, CHUNK - 8, 8), :][7:]
        return spread(jnp.exp(last), i)

    for i in range(PAIRS):
        total = fresh_s[0, i]
        for c in range(1, QUAD):
            total = chunk_decay(c, i) * total + fresh_s[c, i]
        state_out[i] = total.astype(bf16)
    state_copy = remote(state_out, state_come, far)
    late_3 = cross_twin(late_slots, late_2)

    def forward_local(c, carry):
        rows = chunk_rows(c)
        b_mat = act[rows, pl.ds(QCH, STATE)].astype(bf16)
        c_mat = act[rows, pl.ds(QCH + STATE, STATE)].astype(bf16)
        crossed = dot_nt(c_mat, b_mat)
        cum = cum_s[rows, :]
        cum_t = cum.T
        for i in range(PAIRS):
            lanes = lane_tile(i)
            pair = []
            for head in (2 * i, 2 * i + 1):
                gap = cum[:, head : head + 1] - cum_t[head : head + 1, :]
                pair.append(jnp.exp(jnp.where(causal, gap, -1e30)))
            weights_s[c, i] = jnp.concatenate(pair, axis=1).astype(bf16)
            scores = jnp.concatenate([w * crossed for w in pair], axis=1).astype(bf16)
            scores_s[c, i] = scores
            ssd_s[rows, lanes] = dot_nn(scores, stacked(sx_s[rows, lanes]))
        return carry

    lax.fori_loop(0, QUAD, forward_local, 0)
    gate_w = pl.ds(0, QCH)
    out_w = pl.ds(QCH, QCH)
    arrived(late_3[:2])
    flatten(late_slots, late_w, 0, QCH)
    gate_s[...] = dot_nn(xn[pl.ds(TAIL, QUAD * CHUNK), :], late_w[:, gate_w])
    arrived(late_3[2:])
    flatten(late_slots, late_w, QCH, QCH)
    arrived([cot_x, *cot_pass])

    def cot_block(c, carry):
        gc_s[chunk_rows(c), :] = dot_nn(cq[c], late_w[:, out_w])
        return carry

    lax.fori_loop(0, QUAD, cot_block, 0)
    state_copy.wait_recv()
    for i in range(PAIRS):
        total = jnp.where(g == 1, state_come[i].astype(f32), 0.0)
        for c in range(QUAD):
            state_s[c, i] = total.astype(bf16)
            if c < QUAD - 1:
                total = chunk_decay(c, i) * total + fresh_s[c, i]

    def forward_gate(c, carry):
        rows = chunk_rows(c)
        c_mat = act[rows, pl.ds(QCH + STATE, STATE)].astype(bf16)
        grown = jnp.exp(cum_s[rows, :])
        square, crossed = 0.0, 0.0
        for i in range(PAIRS):
            lanes = lane_tile(i)
            ssd = ssd_s[rows, lanes] + dot_nn(c_mat, state_s[c, i]) * spread(grown, i)
            ssd_s[rows, lanes] = ssd
            gate = gate_s[rows, lanes]
            m = (ssd + act[rows, lanes] * skip_wide[i]) * gate * lax.logistic(gate)
            m_s[rows, lanes] = m
            square = square + m * m
            crossed = crossed + gc_s[rows, lanes] * gated_gain(i) * m
        square = jnp.sum(square, axis=1, keepdims=True)
        crossed = jnp.sum(crossed, axis=1, keepdims=True)
        both = jnp.where(lane == 0, square, jnp.where(lane == 1, crossed, 0.0))
        sums_s[q, :, pl.ds(pl.multiple_of(c * CHUNK, CHUNK), CHUNK)] = (
            both.T[:8]
        )
        return carry

    lax.fori_loop(0, QUAD, forward_gate, 0)
    sums_copies = [remote(sums_s.at[q], sums_s.at[q], in_quad(mask)) for mask in (1, 2, 3)]

    def turn_cot(c, carry):
        cot_t[:, pl.ds(pl.multiple_of(c * CHUNK, CHUNK), CHUNK)] = (
            cq[c].astype(f32).T.astype(bf16)
        )
        return carry

    lax.fori_loop(0, QUAD, turn_cot, 0)

    def turn_weights(c, carry):
        own = pl.ds(pl.multiple_of(c * CHUNK, CHUNK), CHUNK)
        late_wt[:, own] = late_w[own, :].astype(f32).T.astype(bf16)
        early_wt[:, own] = early_w[own, :].astype(f32).T.astype(bf16)
        return carry

    lax.fori_loop(0, x_ref.shape[1] // CHUNK, turn_weights, 0)
    arrived(sums_copies)

    def backward_states(c, carry):
        rows = chunk_rows(c)
        cols = pl.ds(pl.multiple_of(c * CHUNK, CHUNK), CHUNK)
        sums = sums_s[0, :, cols] + sums_s[1, :, cols] + sums_s[2, :, cols] + sums_s[3, :, cols]
        sums = jnp.concatenate([sums] * (CHUNK // 8), axis=0).T
        scale = lax.rsqrt(sums[:, 0:1] * (1.0 / DI) + EPS)
        pull = scale * scale * scale * (sums[:, 1:2] * (1.0 / DI))
        c_mat = act[rows, pl.ds(QCH + STATE, STATE)].astype(bf16)
        grown = jnp.exp(cum_s[rows, :])
        for i in range(PAIRS):
            lanes = lane_tile(i)
            m, gc, gate = m_s[rows, lanes], gc_s[rows, lanes], gate_s[rows, lanes]
            xs = act[rows, lanes]
            mr = m * scale
            gated_s[rows, lanes] = (mr * gated_gain(i)).astype(bf16)
            small_s[5:6, lanes] += column_sum(gc * mr)
            m_cot = scale * (gc * gated_gain(i)) - m * pull
            sig = lax.logistic(gate)
            mixed = ssd_s[rows, lanes] + xs * skip_wide[i]
            gate_cot_s[rows, lanes] = (
                m_cot * mixed * (sig * (1.0 + gate * (1.0 - sig)))
            ).astype(bf16)
            y = m_cot * gate * sig
            y_s[rows, lanes] = y
            skip_s[0:1, lanes] += column_sum(y * xs)
            z = (y * spread(grown, i)).astype(bf16)
            z_s[rows, lanes] = z
            back_s[c, i] = dot_tn(c_mat, z)
        return carry

    lax.fori_loop(0, QUAD, backward_states, 0)
    state_copy.wait_send()
    sent[:] = [copy for copy in sent if copy is not state_copy]
    for i in range(PAIRS):
        total = back_s[QUAD - 1, i]
        for c in range(QUAD - 2, -1, -1):
            total = chunk_decay(c, i) * total + back_s[c, i]
        state_out[i] = total.astype(bf16)
    later_copy = remote(state_out, later_s.at[QUAD], far)

    def term_rows(term, half, value, lanes):
        term[pl.ds(half * 16, 16), :, lanes] = value.reshape(16, 24, value.shape[1]).astype(bf16)

    def late_half(half, carry):
        own = pl.ds(pl.multiple_of(half * QCH, QCH), QCH)
        term_rows(late_term, half, dot_nn(normed_t[own, pl.ds(0, QUAD * CHUNK)], gate_cot_s[...]), gate_w)
        term_rows(late_term, half, dot_nn(cot_t[own, :], gated_s[...]), out_w)
        return carry

    lax.fori_loop(0, 2, late_half, 0)

    streams = [(late_term, pl.ds(0, SLAB))] + [
        (early_term, pl.ds(i * PART, PART)) for i in range(PARTS)
    ]

    def reduce_twin(stream):
        term, lanes = streams[stream]
        return [
            remote(
                term.at[pl.ds((2 * up + 1 - core) * 8, 8), :, lanes],
                stream_held[stream][0].at[pl.ds(8 * up, 8)],
                twin,
            )
            for up in range(2)
        ]

    def reduce_beside(stream, copies):
        arrived(copies)
        term, lanes = streams[stream]
        held = stream_held[stream][0]

        def add(four, carry):
            mine = pl.ds((2 * (four // 2) + core) * 8 + four % 2 * 4, 4)
            own = pl.ds(four * 4, 4)
            held[own] = (term[mine, :, lanes].astype(f32) + held[own].astype(f32)).astype(bf16)
            return carry

        lax.fori_loop(0, 4, add, 0)
        return [remote(held.at[pl.ds((1 - y_at) * 8, 8)], stream_held[stream][1], beside)]

    def reduce_far(stream, copies):
        arrived(copies)
        before, held = stream_held[stream][:2]

        def add(four, carry):
            own = pl.ds(four * 4, 4)
            held[own] = (
                before[pl.ds(y_at * 8 + four * 4, 4)].astype(f32) + held[own].astype(f32)
            ).astype(bf16)
            return carry

        lax.fori_loop(0, 2, add, 0)
        return [remote(held.at[pl.ds((1 - g) * 4, 4)], stream_held[stream][2], far)]

    def reduce_quad(stream, copies):
        arrived(copies)
        before, held, result = stream_held[stream][1:]

        held[...] = (before[pl.ds(g * 4, 4)].astype(f32) + held[...].astype(f32)).astype(bf16)
        made = [
            remote(held.at[flip_quad(q, mask)], result.at[q], in_quad(mask)) for mask in (1, 2, 3)
        ]
        result[q] = held[q]
        return made

    late_r0 = reduce_twin(0)

    for n in range(3):
        cols = pl.ds(n * 256, 256)
        value = dot_nn(gated_s[...], late_wt[out_w, cols]).astype(bf16)
        for c in range(QUAD):
            mixed_s[c, :, cols] = value[c * CHUNK : (c + 1) * CHUNK]

    mixed_x, mixed_own = send_sums(mixed_s, mixed_come)

    def backward_local(c, carry):
        rows = chunk_rows(c)
        total = jnp.zeros((CHUNK, CHUNK), f32)
        for i in range(PAIRS):
            lanes = lane_tile(i)
            y = y_s[rows, lanes].astype(bf16)
            moved = weights_s[c, i].astype(f32) * dot_nt(y, stacked(sx_s[rows, lanes]))
            total = total + moved[:, :CHUNK] + moved[:, CHUNK:]
            both = dot_tn(scores_s[c, i], y)
            sx_cot_s[rows, lanes] = both[:CHUNK] * half0 + both[CHUNK:] * half1
        cross_s[c] = total.astype(bf16)
        return carry

    lax.fori_loop(0, QUAD, backward_local, 0)
    late_r1 = reduce_beside(0, late_r0)
    mixed_z = pass_sums(mixed_s, mixed_s, mixed_come, mixed_x)
    later_copy.wait_recv()
    for i in range(PAIRS):
        total = jnp.where(g == 0, later_s[QUAD, i].astype(f32), 0.0)
        for c in range(QUAD - 1, -1, -1):
            later_s[c, i] = total.astype(bf16)
            if c > 0:
                total = chunk_decay(c, i) * total + back_s[c, i]

    def backward_mix(c, carry):
        rows = chunk_rows(c)
        shifted = chunk_rows(c, TAIL)
        b_mat = act[rows, pl.ds(QCH, STATE)].astype(bf16)
        c_mat = act[rows, pl.ds(QCH + STATE, STATE)].astype(bf16)
        cum, step = cum_s[rows, :], step_s[rows, :]
        tail = jnp.exp(cum[CHUNK - 1 :] - cum)
        decay = jnp.exp(cum[CHUNK - 1 :])
        cross = cross_s[c]
        b_cot = dot_tn(cross, c_mat)
        c_cot = dot_nn(cross, b_mat)
        by_head = jnp.zeros((2 * CHUNK + 8, LANES), f32)
        for i in range(PAIRS):
            lanes = lane_tile(i)
            xs, y = act[rows, lanes], y_s[rows, lanes]
            later, state = later_s[c, i], state_s[c, i]
            wide_step, wide_tail = spread(step, i), spread(tail, i)
            tailed = (xs * wide_step * wide_tail).astype(bf16)
            from_later = dot_nn(b_mat, later) * wide_tail
            b_cot = b_cot + dot_nt(tailed, later)
            c_cot = c_cot + dot_nt(z_s[rows, lanes], state)
            sx = sx_s[rows, lanes].astype(f32)
            sx_cot = sx_cot_s[rows, lanes] + from_later
            last = column_sum(sx * from_later) + column_sum(
                later.astype(f32) * state.astype(f32)
            ) * spread(decay, i)
            by_head = by_head + head_sum(
                jnp.concatenate(
                    [
                        y.astype(bf16).astype(f32) * ssd_s[rows, lanes] - sx * sx_cot,
                        sx_cot * xs,
                        jnp.broadcast_to(last, (8, LANES)),
                    ],
                    axis=0,
                ),
                i,
            )
            pre_cot_s[shifted, lanes] = (
                sx_cot * wide_step + y * skip_wide[i]
            ) * act_slope[rows, lanes]
        pre_cot_s[shifted, pl.ds(QCH, STATE)] = b_cot * act_slope[rows, pl.ds(QCH, STATE)]
        pre_cot_s[shifted, pl.ds(QCH + STATE, STATE)] = (
            c_cot * act_slope[rows, pl.ds(QCH + STATE, STATE)]
        )
        cum_cot, step_cot = by_head[:CHUNK], by_head[CHUNK : 2 * CHUNK]
        last_cot = by_head[2 * CHUNK : 2 * CHUNK + 1]
        log_cot = dot_nn(upper3, jnp.concatenate(in_parts(cum_cot, 3), axis=0)) + last_cot
        dt_cot = (step_cot + log_cot * rate) * step_slope[rows, :]
        small_s[7:8, lane_tile(1)] += column_sum(log_cot * log_s[rows, :])
        small_s[5:6, lane_tile(4)] += column_sum(dt_cot)
        early_cot_s[rows, pl.ds(QXBC, LANES)] = dt_cot.astype(bf16)
        return carry

    lax.fori_loop(0, QUAD, backward_mix, 0)
    late_r2 = reduce_far(0, late_r1)

    for i in range(QXBC // LANES):
        lanes = lane_tile(i)
        edge = pre_cot_s[pl.ds(0, 24), lanes]
        total = tap(CONV - 1, i) * edge[:TAIL]
        for k in range(CONV - 1):
            total = total + tap(k, i) * pltpu.roll(edge, 24 - (3 - k), 0)[:TAIL]
        early_cot_s[pl.ds(QUAD * CHUNK, TAIL), lanes] = total.astype(bf16)

    def backward_conv(c, carry):
        for i in range(QXBC // LANES):
            lanes = lane_tile(i)
            cots = pre_cot_s[chunk_rows(c, TAIL, CHUNK + 8), lanes]
            window = proj[chunk_rows(c, 8, CHUNK + 8), lanes]
            cot = cots[:CHUNK]
            total = tap(CONV - 1, i) * cot
            for k in range(CONV - 1):
                total = total + tap(k, i) * pltpu.roll(cots, CHUNK + 8 - (3 - k), 0)[:CHUNK]
            early_cot_s[chunk_rows(c), lanes] = total.astype(bf16)
            for k in range(CONV):
                small_s[k : k + 1, lanes] += column_sum(
                    cot * pltpu.roll(window, CHUNK + 3 - k, 0)[:CHUNK]
                )
            small_s[4:5, lanes] += column_sum(cot)
        return carry

    lax.fori_loop(0, QUAD, backward_conv, 0)

    heads = jnp.zeros((8, LANES), f32)
    for i in range(PAIRS):
        heads = heads + head_sum(jnp.broadcast_to(skip_s[0:1, lane_tile(i)], (8, LANES)), i)
    small_s[5:6, lane_tile(3)] = heads[:1]

    tail_value = dot_nn(early_cot_s[pl.ds(QUAD * CHUNK, TAIL), :], early_wt[...])
    tail_out[...] = tail_value
    tail_index = used[0]
    used[0] += QUAD

    def tail_copy(i):
        return pltpu.make_async_remote_copy(
            src_ref=tail_out,
            dst_ref=tail_come.at[i],
            send_sem=send_sem.at[tail_index + i],
            recv_sem=recv_sem.at[tail_index + i],
            device_id=(dp_at, QUAD - 1),
            device_id_type=MESH,
        )

    for i in range(QUAD):

        @pl.when((g == 1) & (q == i))
        def _():
            tail_copy(i).start()

    def add_gain(value, rows):
        total = column_sum(value * scaled_rows(rows))
        small_s[6:7, :] += total[:, :QXBC]
        small_s[7:8, lane_tile(0)] += total[:, QXBC:]

    add_gain(tail_value, xtail[...])

    for n in range(3):
        cols = pl.ds(n * 256, 256)
        value = dot_nn(early_cot_s[pl.ds(0, QUAD * CHUNK), :], early_wt[:, cols])
        value = value + dot_nn(gate_cot_s[...], late_wt[gate_w, cols])
        for c in range(QUAD):
            part = value[c * CHUNK : (c + 1) * CHUNK]
            normed_cot_s[c, :, cols] = part
            normed_out[c, :, cols] = part.astype(bf16)

    normed_x, normed_own = send_sums(normed_out, normed_come)
    for c in range(QUAD):
        add_gain(normed_cot_s[c], xq[c])
    small_copy = remote(small_s, small_come.at[0], twin)
    early_r0 = []
    for part in range(PARTS):
        lanes = pl.ds(part * PART, PART)

        def early_half(half, carry, lanes=lanes):
            own = pl.ds(pl.multiple_of(half * QCH, QCH), QCH)
            value = dot_nn(normed_t[own, :], early_cot_s[:, lanes])
            term_rows(early_term, half, value, lanes)
            return carry

        lax.fori_loop(0, 2, early_half, 0)
        early_r0.append(reduce_twin(1 + part))

    early_r1 = [reduce_beside(1 + part, early_r0[part]) for part in range(PARTS)]
    normed_z = pass_sums(normed_cot_s, normed_out, normed_come, normed_x)

    early_r2 = [reduce_far(1, early_r1[0])]
    small_copy.wait_recv()
    small_come[4] = small_s[...] + small_come[0]
    across = (flip(dp_at, 1), flip(seq_at, 2))
    small_copies = [
        remote(small_come.at[4], small_come.at[1 + i], target)
        for i, target in enumerate((beside, far, across))
    ]
    early_r2.append(reduce_far(2, early_r1[1]))
    late_r3 = reduce_quad(0, late_r2)
    early_r2.append(reduce_far(3, early_r1[2]))
    arrived(small_copies)
    small_quad[q] = small_come[4] + small_come[1] + (small_come[2] + small_come[3])
    small_copies = [remote(small_quad.at[q], small_quad.at[q], in_quad(mask)) for mask in (1, 2, 3)]

    arrived([mixed_own, *mixed_z])
    total = x_ref[...].astype(f32) + mixed_s[q].astype(f32)
    total = total + mixed_come[1].astype(f32) + mixed_come[2].astype(f32)
    out_ref[...] = total.astype(bf16)
    early_r3 = [reduce_quad(1 + part, early_r2[part]) for part in range(PARTS)]

    arrived([normed_own, *normed_z])
    value = normed_cot_s[q] + normed_come[1].astype(f32) + normed_come[2].astype(f32)
    normed_cot_s[q] = value

    @pl.when(at_end)
    def _():
        for i in range(QUAD):
            tail_copy(i).wait_recv()
        rows = pl.ds(CHUNK - TAIL, TAIL)
        normed_cot_s[q, rows, :] += tail_come[0] + tail_come[1] + tail_come[2] + tail_come[3]

    cot = normed_cot_s[q] * gain
    rows = x_ref[...].astype(f32)
    scale = lax.rsqrt(jnp.mean(rows * rows, axis=-1, keepdims=True) + EPS)
    pull = scale * scale * scale * jnp.mean(cot * rows, axis=-1, keepdims=True)
    grad_ref[...] = cot_ref[...].astype(f32) + scale * cot - rows * pull

    arrived(small_copies)
    for j in range(QUAD):
        own = pl.ds(j * QCH, QCH)
        taps_grad_ref[:, own] = small_quad[j, 0:CONV, pl.ds(0, QCH)]
        bias_grad_ref[own] = small_quad[j, CONV : CONV + 1, pl.ds(0, QCH)].reshape(QCH)
        gated_gain_grad_ref[own] = small_quad[j, 5:6, pl.ds(0, QCH)].reshape(QCH)
    quads = small_quad[0] + small_quad[1] + small_quad[2] + small_quad[3]
    taps_grad_ref[:, pl.ds(DI, BC)] = quads[:CONV, QCH:QXBC]
    bias_grad_ref[pl.ds(DI, BC)] = quads[CONV : CONV + 1, QCH:QXBC].reshape(BC)
    gain_grad_ref[pl.ds(0, QXBC)] = quads[6:7].reshape(QXBC)
    gain_grad_ref[pl.ds(QXBC, LANES)] = quads[7:8, :LANES].reshape(LANES)

    def in_head_order(parts):
        total = parts[0]
        for j in range(1, QUAD):
            total = total + pltpu.roll(parts[j], j * QHEADS, 1)
        return total[:, :HEADS]

    def small_heads(row, i):
        parts = [small_quad[j, :, lane_tile(i)] for j in range(QUAD)]
        return in_head_order(parts)[row : row + 1].reshape(HEADS)

    skip_grad_ref[...] = small_heads(5, 3)
    dt_bias_grad_ref[...] = small_heads(5, 4)
    a_log_grad_ref[...] = small_heads(7, 1)

    arrived(late_r3)
    for j in range(QUAD):
        own = pl.ds(j * QCH, QCH)
        in_grad_ref[:, own] = stream_held[0][3][j, :, pl.ds(0, QCH)].astype(f32)
        proj_grad_ref[:, own] = stream_held[0][3][j, :, pl.ds(QCH, QCH)].astype(f32)
    for part in range(PARTS):
        arrived(early_r3[part])

    def early_result(j, low):
        return stream_held[1 + low // PART][3][j, :, pl.ds(low % PART, LANES)].astype(f32)

    for j in range(QUAD):
        for i in range(PAIRS):
            in_grad_ref[:, pl.ds(DI + j * QCH + i * LANES, LANES)] = early_result(j, i * LANES)
    for i in range(BC // LANES):
        total = early_result(0, QCH + i * LANES)
        for j in range(1, QUAD):
            total = total + early_result(j, QCH + i * LANES)
        in_grad_ref[:, pl.ds(2 * DI + i * LANES, LANES)] = total
    in_grad_ref[:, pl.ds(DI + XBC, HEADS)] = in_head_order(
        [early_result(j, QXBC) for j in range(QUAD)]
    )

    assert used[0] == SEMS
    for copy in sent:
        copy.wait_send()

    @pl.when(at_end)
    def _():
        for copy in tail_sends:
            copy.wait_send()

    for i in range(QUAD):

        @pl.when((g == 1) & (q == i))
        def _():
            tail_copy(i).wait_send()


def quad_body(
    inputs,
    norm_gain,
    in_proj,
    conv_weight,
    conv_bias,
    dt_bias,
    a_log,
    skip_gain,
    gated_gain,
    out_proj,
    cotangent,
):
    f32, bf16 = jnp.float32, jnp.bfloat16
    rows = in_proj.shape[0]
    tokens = QUAD * CHUNK
    slots = lax.axis_size("dp") * lax.axis_size("seq")
    width = inputs.shape[1]
    vmem = pltpu.VMEM
    held = [
        vmem((count, rows, w), bf16) for w in (SLAB, *[PART] * PARTS) for count in (16, 8, 4, 4)
    ]
    operands = (
        inputs,
        norm_gain,
        in_proj,
        conv_weight.T,
        conv_bias,
        dt_bias,
        a_log,
        skip_gain,
        gated_gain,
        out_proj,
        cotangent,
    )
    scratch = [
        *(vmem(operand.shape, operand.dtype) for operand in operands),
        pltpu.SemaphoreType.DMA((len(operands),)),
        vmem((QUAD, rows, SLAB), bf16),
        vmem((QUAD, rows, SLAB), bf16),
        vmem((QUAD, CHUNK, width), bf16),
        vmem((QUAD, CHUNK, width), bf16),
        vmem((TAIL, width), bf16),
        vmem((slots, rows, SLAB), bf16),
        vmem((slots, rows, SLAB), bf16),
        vmem((width, SLAB), bf16),
        vmem((width, SLAB), bf16),
        vmem((TAIL + tokens, width), bf16),
        vmem((TAIL + tokens, SLAB), f32),
        vmem((tokens, QXBC), f32),
        vmem((tokens, QXBC), f32),
        vmem((tokens, LANES), f32),
        vmem((tokens, LANES), f32),
        vmem((tokens, LANES), f32),
        vmem((tokens, LANES), f32),
        vmem((tokens, QCH), bf16),
        vmem((QUAD, PAIRS, STATE, LANES), f32),
        vmem((PAIRS, STATE, LANES), bf16),
        vmem((PAIRS, STATE, LANES), bf16),
        vmem((QUAD, PAIRS, STATE, LANES), bf16),
        vmem((QUAD, PAIRS, CHUNK, 2 * CHUNK), bf16),
        vmem((QUAD, PAIRS, CHUNK, 2 * CHUNK), bf16),
        vmem((tokens, QCH), f32),
        vmem((tokens, QCH), f32),
        vmem((tokens, QCH), f32),
        vmem((tokens, QCH), f32),
        vmem((QUAD, 8, tokens), f32),
        vmem((tokens, QCH), bf16),
        vmem((tokens, QCH), bf16),
        vmem((tokens, QCH), f32),
        vmem((tokens, QCH), bf16),
        vmem((QUAD, PAIRS, STATE, LANES), f32),
        vmem((QUAD + 1, PAIRS, STATE, LANES), bf16),
        vmem((QUAD, CHUNK, CHUNK), bf16),
        vmem((tokens, QCH), f32),
        vmem((TAIL + tokens + 8, QXBC), f32),
        vmem((tokens + LANES, SLAB), bf16),
        vmem((slots, rows, SLAB), bf16),
        vmem((slots, rows, SLAB), bf16),
        vmem((QUAD, CHUNK, width), bf16),
        vmem((3, CHUNK, width), bf16),
        vmem((width, tokens + LANES), bf16),
        vmem((width, tokens), bf16),
        vmem((SLAB, width), bf16),
        vmem((SLAB, width), bf16),
        vmem((QUAD, CHUNK, width), f32),
        vmem((QUAD, CHUNK, width), bf16),
        vmem((3, CHUNK, width), bf16),
        vmem((TAIL, width), f32),
        vmem((QUAD, TAIL, width), f32),
        vmem((GRAD_ROWS, QXBC), f32),
        vmem((8, QCH), f32),
        vmem((5, GRAD_ROWS, QXBC), f32),
        vmem((QUAD, GRAD_ROWS, QXBC), f32),
        *held,
        pltpu.SemaphoreType.DMA((SEMS,)),
        pltpu.SemaphoreType.DMA((SEMS,)),
    ]
    in_vmem = pl.BlockSpec(memory_space=pltpu.VMEM)
    shapes = [inputs.shape, inputs.shape, in_proj.shape, out_proj.shape]
    shapes += [(width,), (CONV, XBC), (XBC,), (HEADS,), (HEADS,), (HEADS,), (DI,)]
    got = pl.pallas_call(
        block_kernel,
        out_shape=[
            jax.ShapeDtypeStruct(shape, f32 if at else bf16) for at, shape in enumerate(shapes)
        ],
        in_specs=[pl.BlockSpec(memory_space=pl.ANY)] * 11,
        out_specs=[in_vmem] * 11,
        scratch_shapes=scratch,
        compiler_params=pltpu.CompilerParams(
            collective_id=1, has_side_effects=True, vmem_limit_bytes=VMEM_BYTES
        ),
        name="residual_block",
    )(*operands)
    got = pl.pallas_call(
        copy_out_kernel,
        out_shape=[jax.ShapeDtypeStruct(value.shape, value.dtype) for value in got],
        in_specs=[in_vmem] * 11,
        out_specs=[pl.BlockSpec(memory_space=pl.ANY)] * 11,
        scratch_shapes=[pltpu.SemaphoreType.DMA((11,))],
        name="copy_out",
    )(*got)
    return (*got[:5], got[5].T, *got[6:])


def copy_out_kernel(*refs):
    count = len(refs) // 2
    sems = refs[2 * count]
    copies = [
        pltpu.make_async_copy(refs[i], refs[count + i], sems.at[i]) for i in range(count)
    ]
    for copy in copies:
        copy.start()
    for copy in copies:
        copy.wait()


def fits_quads(mesh):
    return mesh.shape["dp"] == 4 and mesh.shape["seq"] == 2 * QUAD


def solution(mesh):
    placed = (
        P(("dp", "seq"), None),
        P(),
        P(("dp", "seq"), None),
        P(),
        P(),
        P(),
        P(),
        P(),
        P(),
        P(("dp", "seq"), None),
        P(("dp", "seq"), None),
    )
    return jax.shard_map(
        quad_body if fits_quads(mesh) else body,
        mesh=mesh,
        in_specs=placed,
        out_specs=(
            P(("dp", "seq"), None),
            P(("dp", "seq"), None),
            P(("dp", "seq"), None),
            P(("dp", "seq"), None),
            P(),
            P(),
            P(),
            P(),
            P(),
            P(),
            P(),
        ),
        check_vma=False,
    )
```

```python
from functools import partial

import jax
import jax.numpy as jnp
from jax import lax
from jax.experimental import pallas as pl
from jax.experimental.pallas import tpu as pltpu
from jax.sharding import PartitionSpec as P

HEADS = 24
HEAD_DIM = 64
STATE = 128
CONV = 4
DI = 1536
XBC = 1792
PROJ = DI + XBC + HEADS
LANES = 128
WIDE = -(-PROJ // LANES) * LANES


EPS = 1e-05
HIGH = lax.Precision.HIGHEST
MESH = pl.DeviceIdType.MESH
VMEM_BYTES = 60 * 1024 * 1024


def bits_of(count):
    return count.bit_length() - 1


def bit_at(place, bit):
    return (place // 2**bit) % 2


def places():
    return lax.axis_index("dp"), lax.axis_index("seq")


def partner(bit, seq_bits):
    dp_at, seq_at = places()
    if bit < seq_bits:
        return dp_at, seq_at + (1 - 2 * bit_at(seq_at, bit)) * 2**bit
    up = bit - seq_bits
    return dp_at + (1 - 2 * bit_at(dp_at, up)) * 2**up, seq_at


def greet(bits, seq_bits):
    barrier = pltpu.get_barrier_semaphore()
    for bit in range(bits):
        pl.semaphore_signal(barrier, inc=1, device_id=partner(bit, seq_bits), device_id_type=MESH)
    pl.semaphore_wait(barrier, bits)


def gather_orders(seq_bits, dp_bits):
    x_count = seq_bits // 2
    x_bits = list(range(x_count))
    z_bits = list(range(x_count, seq_bits))[::-1]
    core = [seq_bits]
    y_bits = [seq_bits + 1 + i for i in range(dp_bits - 1)]
    return (
        z_bits + x_bits + y_bits + core,
        z_bits + y_bits + x_bits + core,
        z_bits[:1] + x_bits + y_bits + z_bits[1:] + core,
        z_bits[:1] + y_bits + x_bits + z_bits[1:] + core,
    )


SHARES = (0.3, 0.3, 0.2, 0.2)


def split_lanes(width, shares):
    tiles = width // LANES
    edges = [round(tiles * sum(shares[:i])) * LANES for i in range(len(shares) + 1)]
    return [(low, high - low) for low, high in zip(edges, edges[1:])]


def gather_kernel(seq_bits, streams, bits, *refs):
    array_count = 1 + max(stream[0] for stream in streams)
    shards, outs = refs[:array_count], refs[array_count : 2 * array_count]
    send_sem, recv_sem, own_sem = refs[2 * array_count :]
    dp_at, seq_at = places()
    place = dp_at * 2**seq_bits + seq_at
    own = [
        pltpu.make_async_copy(shard, out.at[place], own_sem.at[i])
        for i, (shard, out) in enumerate(zip(shards, outs))
    ]
    for copy in own:
        copy.start()
    greet(bits, seq_bits)
    for copy in own:
        copy.wait()

    def landed(stream, stage, sem):
        which, low, width, _ = streams[stream]
        view = outs[which].at[pl.ds(0, 2**stage), :, pl.ds(low, width)]
        pltpu.make_async_copy(view, view, sem.at[stream, stage]).wait()

    for stage in range(bits + 1):
        for stream, (which, low, width, order) in enumerate(streams):
            if stage > 0:
                landed(stream, stage - 1, recv_sem)
            if stage == bits:
                continue
            free = order[:stage]
            run = 0
            while run in free:
                run += 1
            base = place
            for bit in free:
                base = base - bit_at(place, bit) * 2**bit
            upper = [bit for bit in free if bit > run]
            for combo in range(2 ** len(upper)):
                start = base + sum(2**bit for i, bit in enumerate(upper) if combo >> i & 1)
                view = outs[which].at[pl.ds(start, 2**run), :, pl.ds(low, width)]
                pltpu.make_async_remote_copy(
                    src_ref=view,
                    dst_ref=view,
                    send_sem=send_sem.at[stream, stage],
                    recv_sem=recv_sem.at[stream, stage],
                    device_id=partner(order[stage], seq_bits),
                    device_id_type=MESH,
                ).start()
    for stage in range(bits):
        for stream in range(len(streams)):
            landed(stream, stage, send_sem)


def gather_all(shards, collective_id):
    seq_bits, dp_bits = bits_of(lax.axis_size("seq")), bits_of(lax.axis_size("dp"))
    bits = seq_bits + dp_bits
    orders = gather_orders(seq_bits, dp_bits)
    streams = [
        (which, low, width, order)
        for which, shard in enumerate(shards)
        for (low, width), order in zip(split_lanes(shard.shape[1], SHARES), orders)
    ]
    return pl.pallas_call(
        partial(gather_kernel, seq_bits, streams, bits),
        out_shape=[jax.ShapeDtypeStruct((2**bits, *a.shape), a.dtype) for a in shards],
        in_specs=[pl.BlockSpec(memory_space=pltpu.VMEM)] * len(shards),
        out_specs=[pl.BlockSpec(memory_space=pl.ANY)] * len(shards),
        scratch_shapes=[
            pltpu.SemaphoreType.DMA((len(streams), bits)),
            pltpu.SemaphoreType.DMA((len(streams), bits)),
            pltpu.SemaphoreType.DMA((len(shards),)),
        ],
        compiler_params=pltpu.CompilerParams(
            collective_id=collective_id, has_side_effects=True, vmem_limit_bytes=VMEM_BYTES
        ),
        name="gather_rows",
    )(*shards)


def sum_kernel(seq_bits, streams, bits, array_count, *refs):
    terms, vector = refs[:array_count], refs[array_count]
    outs, vector_out = refs[array_count + 1 : 2 * array_count + 1], refs[2 * array_count + 1]
    held = refs[2 * array_count + 2 : 2 * array_count + 2 + len(streams) * bits]
    rest = refs[2 * array_count + 2 + len(streams) * bits :]
    vector_in, vector_sum, send_sem, recv_sem, vector_send, vector_recv = rest
    dp_at, seq_at = places()
    place = dp_at * 2**seq_bits + seq_at
    greet(bits, seq_bits)

    def source(stream, stage):
        which, low, width, _ = streams[stream]
        if stage == 0:
            return terms[which], pl.ds(low, width)
        return held[stream * bits + stage - 1], pl.ds(0, width)

    def position(stream, stage):
        order = streams[stream][3]
        remaining = sorted(order[stage:])
        return remaining.index(order[stage]), bit_at(place, order[stage])

    def landed(stream, stage, sem):
        view = held[stream * bits + stage]
        pltpu.make_async_copy(view, view, sem.at[stream, stage]).wait()

    def vector_copy(stage):
        return pltpu.make_async_remote_copy(
            src_ref=vector if stage == 0 else vector_sum.at[stage - 1],
            dst_ref=vector_in.at[stage],
            send_sem=vector_send.at[stage],
            recv_sem=vector_recv.at[stage],
            device_id=partner(stage, seq_bits),
            device_id_type=MESH,
        )

    for stage in range(bits + 1):
        if stage > 0:
            vector_copy(stage - 1).wait_recv()
            before = vector[...] if stage == 1 else vector_sum[stage - 2]
            total = before + vector_in[stage - 1]
            if stage < bits:
                vector_sum[stage - 1] = total
            else:
                vector_out[...] = total
        if stage < bits:
            vector_copy(stage).start()
        for stream, (which, low, width, order) in enumerate(streams):
            if stage > 0:
                landed(stream, stage - 1, recv_sem)
                spot, mine = position(stream, stage - 1)
                kept, lanes = source(stream, stage - 1)
                came = held[stream * bits + stage - 1]
                if stage == bits:
                    outs[which][:, pl.ds(low, width)] = kept[mine, :, lanes].astype(
                        jnp.float32
                    ) + came[0].astype(jnp.float32)
                    continue

                def add_one(block, carry, spot=spot, mine=mine, kept=kept, lanes=lanes, came=came):
                    from_block = (block // 2**spot) * 2 ** (spot + 1) + mine * 2**spot
                    from_block = from_block + block % 2**spot
                    added = kept[from_block, :, lanes].astype(jnp.float32) + came[block].astype(
                        jnp.float32
                    )
                    came[block] = added.astype(came.dtype)
                    return carry

                lax.fori_loop(0, 2 ** (bits - stage), add_one, 0)
            spot, mine = position(stream, stage)
            sent, lanes = source(stream, stage)
            for high in range(2 ** (bits - stage - 1 - spot)):
                start = high * 2 ** (spot + 1) + (1 - mine) * 2**spot
                pltpu.make_async_remote_copy(
                    src_ref=sent.at[pl.ds(start, 2**spot), :, lanes],
                    dst_ref=held[stream * bits + stage].at[pl.ds(high * 2**spot, 2**spot)],
                    send_sem=send_sem.at[stream, stage],
                    recv_sem=recv_sem.at[stream, stage],
                    device_id=partner(order[stage], seq_bits),
                    device_id_type=MESH,
                ).start()
    for stage in range(bits):
        vector_copy(stage).wait_send()
        for stream in range(len(streams)):
            landed(stream, stage, send_sem)


def sum_to_owners(terms, vector, collective_id):
    seq_bits, dp_bits = bits_of(lax.axis_size("seq")), bits_of(lax.axis_size("dp"))
    bits = seq_bits + dp_bits
    orders = [order[::-1] for order in gather_orders(seq_bits, dp_bits)]
    terms = [term.reshape(2**bits, -1, term.shape[1]) for term in terms]
    streams = [
        (which, low, width, order)
        for which, term in enumerate(terms)
        for (low, width), order in zip(split_lanes(term.shape[2], SHARES), orders)
    ]
    rows = terms[0].shape[1]
    in_vmem = pl.BlockSpec(memory_space=pltpu.VMEM)
    held = [
        pltpu.VMEM((2 ** (bits - 1 - stage), rows, width), jnp.bfloat16)
        for _, _, width, _ in streams
        for stage in range(bits)
    ]
    return pl.pallas_call(
        partial(sum_kernel, seq_bits, streams, bits, len(terms)),
        out_shape=[jax.ShapeDtypeStruct(a.shape[1:], jnp.float32) for a in terms]
        + [jax.ShapeDtypeStruct(vector.shape, vector.dtype)],
        in_specs=[in_vmem] * (len(terms) + 1),
        out_specs=[in_vmem] * (len(terms) + 1),
        scratch_shapes=held
        + [
            pltpu.VMEM((bits, *vector.shape), jnp.float32),
            pltpu.VMEM((bits, *vector.shape), jnp.float32),
            pltpu.SemaphoreType.DMA((len(streams), bits)),
            pltpu.SemaphoreType.DMA((len(streams), bits)),
            pltpu.SemaphoreType.DMA((bits,)),
            pltpu.SemaphoreType.DMA((bits,)),
        ],
        compiler_params=pltpu.CompilerParams(
            collective_id=collective_id, has_side_effects=True, vmem_limit_bytes=VMEM_BYTES
        ),
        name="sum_rows",
    )(*terms, vector)


GROUP = 4
GROUP_LANES = GROUP * HEAD_DIM


def inner_product(left, right, dims):
    return lax.dot_general(
        left, right, (dims, ((), ())), precision=HIGH, preferred_element_type=jnp.float32
    )


def group_lanes(group):
    return pl.ds(pl.multiple_of(group * GROUP_LANES, GROUP_LANES), GROUP_LANES)


def head_weights(cumulative, head):
    row = cumulative[pl.ds(head, 1), :]
    count = row.shape[1]
    spread = jnp.broadcast_to(row, (count, count))
    later = lax.broadcasted_iota(jnp.int32, (count, count), 0)
    earlier = lax.broadcasted_iota(jnp.int32, (count, count), 1)
    return jnp.exp(jnp.where(later >= earlier, spread.T - spread, -jnp.inf))


def inside_work(first, last, scaled_x, b_mat, c_mat, cumulative, output, crossed):
    if first == 0:
        crossed[...] = inner_product(c_mat[...], b_mat[...], ((1,), (1,)))

    def one(group, carry):
        values = scaled_x[:, group_lanes(group)]
        parts = []
        for i in range(GROUP):
            scores = head_weights(cumulative, group * GROUP + i) * crossed[...]
            head = values[:, i * HEAD_DIM : (i + 1) * HEAD_DIM]
            parts.append(inner_product(scores, head, ((1,), (0,))))
        output[:, group_lanes(group)] = jnp.concatenate(parts, axis=1)
        return carry

    lax.fori_loop(first, last, one, 0)


def inside_back(
    first,
    last,
    output_cot,
    scaled_x,
    b_mat,
    c_mat,
    cumulative,
    scaled_cot,
    b_cot,
    c_cot,
    cumulative_cot,
    crossed,
    crossed_cot,
):
    if first == 0:
        crossed[...] = inner_product(c_mat[...], b_mat[...], ((1,), (1,)))
        crossed_cot[...] = jnp.zeros_like(crossed_cot)

    def one(group, carry):
        values = scaled_x[:, group_lanes(group)]
        cots = output_cot[:, group_lanes(group)]
        parts = []
        total = crossed_cot[...]
        for i in range(GROUP):
            weights = head_weights(cumulative, group * GROUP + i)
            scores = weights * crossed[...]
            head = values[:, i * HEAD_DIM : (i + 1) * HEAD_DIM]
            cot = cots[:, i * HEAD_DIM : (i + 1) * HEAD_DIM]
            weighted = weights * inner_product(cot, head, ((1,), (1,)))
            total = total + weighted
            parts.append(inner_product(scores, cot, ((0,), (0,))))
            moved = weighted * crossed[...]
            cumulative_cot[pl.ds(group * GROUP + i, 1), :] = jnp.sum(
                moved.T, axis=0, keepdims=True
            ) - jnp.sum(moved, axis=0, keepdims=True)
        crossed_cot[...] = total
        scaled_cot[:, group_lanes(group)] = jnp.concatenate(parts, axis=1)
        return carry

    lax.fori_loop(first, last, one, 0)
    if last == HEADS // GROUP:
        b_cot[...] = inner_product(crossed_cot[...], c_mat[...], ((0,), (0,)))
        c_cot[...] = inner_product(crossed_cot[...], b_mat[...], ((1,), (0,)))


def scan_kernel(count, reverse, work, inputs, outputs, *refs):
    state, decay = refs[:2]
    given = refs[2 : 2 + inputs]
    out = refs[2 + inputs]
    made = refs[3 + inputs : 3 + inputs + outputs]
    came, came_decay, ready = refs[3 + inputs + outputs : 6 + inputs + outputs]
    sems = refs[6 + inputs + outputs : 12 + inputs + outputs]
    held = refs[12 + inputs + outputs :]
    out_send, out_recv, decay_send, decay_recv, back_send, back_recv = sems
    dp_at, seq_at = places()
    barrier = pltpu.get_barrier_semaphore()
    peers = [(seq_at + hop) % count for hop in range(1, count)]
    for peer in peers:
        pl.semaphore_signal(barrier, inc=1, device_id=(dp_at, peer), device_id_type=MESH)
    pl.semaphore_wait(barrier, count - 1)

    def copy(hop, which):
        target = (seq_at + hop) % count
        source, landing, send_sem, recv_sem = (
            (state.at[target], came.at[seq_at], out_send, out_recv),
            (decay, came_decay.at[seq_at], decay_send, decay_recv),
            (ready.at[target], out.at[seq_at], back_send, back_recv),
        )[which]
        return pltpu.make_async_remote_copy(
            src_ref=source,
            dst_ref=landing,
            send_sem=send_sem.at[hop],
            recv_sem=recv_sem.at[hop],
            device_id=(dp_at, target),
            device_id_type=MESH,
        )

    for hop in range(1, count):
        copy(hop, 0).start()
        copy(hop, 1).start()
    came[seq_at] = state[seq_at]
    came_decay[seq_at] = decay[...]
    groups = HEADS // GROUP
    work(0, groups // 2, *given, *made, *held)
    for hop in range(1, count):
        copy(hop, 0).wait_recv()
        copy(hop, 1).wait_recv()
    total = jnp.zeros(state.shape[1:], jnp.float32)
    for place in range(count)[:: -1 if reverse else 1]:
        ready[place] = total.astype(ready.dtype)
        total = came_decay[place] * total + came[place].astype(jnp.float32)
    for hop in range(1, count):
        copy(hop, 2).start()
    out[seq_at] = ready[seq_at]
    work(groups // 2, groups, *given, *made, *held)
    for hop in range(1, count):
        copy(hop, 2).wait_recv()
    for hop in range(1, count):
        for which in range(3):
            copy(hop, which).wait_send()


def scan_states(state, decay, work, given, made, held, reverse, collective_id):
    count = lax.axis_size("seq")
    state = state.astype(jnp.bfloat16).reshape(count, STATE // count, DI)
    in_vmem = pl.BlockSpec(memory_space=pltpu.VMEM)
    got = pl.pallas_call(
        partial(scan_kernel, count, reverse, work, len(given), len(made)),
        out_shape=[jax.ShapeDtypeStruct(state.shape, state.dtype)]
        + [jax.ShapeDtypeStruct(shape, jnp.float32) for shape in made],
        in_specs=[in_vmem] * (2 + len(given)),
        out_specs=[in_vmem] * (1 + len(made)),
        scratch_shapes=[
            pltpu.VMEM(state.shape, state.dtype),
            pltpu.VMEM((count, 1, DI), jnp.float32),
            pltpu.VMEM(state.shape, state.dtype),
        ]
        + [pltpu.SemaphoreType.DMA((count,))] * 6
        + [pltpu.VMEM(shape, jnp.float32) for shape in held],
        compiler_params=pltpu.CompilerParams(
            collective_id=collective_id, has_side_effects=True, vmem_limit_bytes=VMEM_BYTES
        ),
        name="scan_back" if reverse else "scan_states",
    )(state, decay[None, :], *given)
    return got[0].reshape(STATE, DI).astype(jnp.float32), *got[1:]


def passed_along(value, axis, steps):
    count = lax.axis_size(axis)
    first, last = (max(0, -steps), min(count, count - steps))
    return lax.ppermute(value, axis, [(source, source + steps) for source in range(first, last)])


def pre_norm(residual_in, norm_gain):
    scale_rms = lax.rsqrt(jnp.mean(residual_in * residual_in, axis=-1, keepdims=True) + EPS)
    return residual_in * scale_rms * norm_gain


def conv_silu(padded, conv_weight, conv_bias, row_count):
    total = jnp.zeros((row_count, padded.shape[1]), jnp.float32) + conv_bias[None, :]
    for offset in range(conv_weight.shape[1]):
        total = total + conv_weight[:, offset][None, :] * padded[offset : offset + row_count]
    return jax.nn.silu(total)


def head_lanes():
    lanes = jnp.arange(DI, dtype=jnp.int32) // HEAD_DIM
    return (jnp.arange(HEADS, dtype=jnp.int32)[:, None] == lanes[None, :]).astype(jnp.float32)


def spread_heads(by_head):
    return jnp.dot(by_head, head_lanes(), precision=HIGH)


def sum_heads(by_lane):
    return jnp.dot(by_lane, head_lanes().T, precision=HIGH)


def before_states(xbc, dt_raw, edge, conv_weight, conv_bias, dt_bias, a_log):
    row_count = xbc.shape[0]
    activated = conv_silu(jnp.concatenate([edge, xbc], axis=0), conv_weight, conv_bias, row_count)
    xs = activated[:, :DI]
    b_mat = activated[:, DI : DI + STATE]
    c_mat = activated[:, DI + STATE :]
    step = jax.nn.softplus(dt_raw + dt_bias)
    log_decay = step * -jnp.exp(a_log)
    at = jnp.arange(row_count)
    lower = (at[:, None] >= at[None, :]).astype(jnp.float32)
    cumulative = jnp.dot(lower, log_decay, precision=HIGH)
    scaled_x = xs * spread_heads(step)
    tail = jnp.exp(cumulative[-1][None, :] - cumulative)
    fresh = jnp.dot(b_mat.T, scaled_x * spread_heads(tail), precision=HIGH)
    return (xs, scaled_x, b_mat, c_mat, cumulative, fresh)


def post_gate(ssd_out, xs, gate_part, skip_gain, gated_gain):
    skipped = xs * spread_heads(skip_gain[None, :])
    mixed_in = (ssd_out + skipped) * jax.nn.silu(gate_part)
    scale_rms = lax.rsqrt(jnp.mean(mixed_in * mixed_in, axis=-1, keepdims=True) + EPS)
    return mixed_in * scale_rms * gated_gain


def contract_rows(left, right):
    return lax.dot_general(
        left, right, (((0,), (0,)), ((), ())), preferred_element_type=jnp.float32
    )


def contract_cols(left, right):
    return lax.dot_general(
        left, right, (((1,), (1,)), ((), ())), preferred_element_type=jnp.float32
    )


def body(
    inputs,
    norm_gain,
    in_proj,
    conv_weight,
    conv_bias,
    dt_bias,
    a_log,
    skip_gain,
    gated_gain,
    out_proj,
    cotangent,
):
    row_count = inputs.shape[0]
    residual_in = inputs.astype(jnp.float32)
    normed_full, norm_back = jax.vjp(pre_norm, residual_in, norm_gain)
    normed = normed_full.astype(jnp.bfloat16)
    in_whole, out_whole = gather_all(
        [jnp.pad(in_proj, ((0, 0), (0, WIDE - PROJ))), out_proj], collective_id=1
    )
    in_whole = in_whole.reshape(-1, WIDE)
    out_whole = out_whole.reshape(-1, DI)
    projected = jnp.dot(normed, in_whole, preferred_element_type=jnp.float32)
    gate_part = projected[:, :DI]
    xbc = projected[:, DI : DI + XBC]
    dt_raw = projected[:, DI + XBC : PROJ]
    edge = passed_along(xbc[row_count - (CONV - 1) :], "seq", 1)
    primal, mid_back = jax.vjp(
        before_states, xbc, dt_raw, edge, conv_weight, conv_bias, dt_bias, a_log
    )
    xs, scaled_x, b_mat, c_mat, cumulative, s_local = primal
    by_head = cumulative.T
    decay = jnp.exp(cumulative[-1])
    wide_decay = spread_heads(decay[None, :])[0]
    square = (row_count, row_count)
    state_in, local_out = scan_states(
        s_local,
        wide_decay,
        inside_work,
        [scaled_x, b_mat, c_mat, by_head],
        [xs.shape],
        [square],
        False,
        collective_id=2,
    )
    weighted = spread_heads(jnp.exp(cumulative))
    carried_part = jnp.dot(c_mat, state_in, precision=HIGH) * weighted
    ssd_out = local_out + carried_part
    gated_full, post_back = jax.vjp(post_gate, ssd_out, xs, gate_part, skip_gain, gated_gain)
    gated = gated_full.astype(jnp.bfloat16)
    mixed = contract_cols(gated, out_whole)
    layer_out = (residual_in + mixed).astype(jnp.bfloat16)
    gated_cot = jnp.dot(cotangent, out_whole, preferred_element_type=jnp.float32)
    ssd_cot, xs_cot, gate_cot, skip_grad, gated_gain_grad = post_back(gated_cot)
    scaled_cot = ssd_cot * weighted
    local_grad = jnp.dot(c_mat.T, scaled_cot, precision=HIGH)
    later_grad, scaled_x_cot, b_cot, inner_c_cot, by_head_cot = scan_states(
        local_grad,
        wide_decay,
        inside_back,
        [ssd_cot, scaled_x, b_mat, c_mat, by_head],
        [xs.shape, b_mat.shape, c_mat.shape, by_head.shape],
        [square, square],
        True,
        collective_id=3,
    )
    c_cot = lax.dot_general(scaled_cot, state_in, (((1,), (1,)), ((), ())), precision=HIGH)
    cum_cot = sum_heads(ssd_cot * carried_part)
    last_cot = sum_heads(jnp.sum(later_grad * state_in, axis=0, keepdims=True))[0] * decay
    is_last = (jnp.arange(row_count) == row_count - 1)[:, None]
    cum_cot = cum_cot + jnp.where(is_last, last_cot[None, :], 0.0)
    mid_grads = mid_back(
        (xs_cot, scaled_x_cot, b_cot, c_cot + inner_c_cot, cum_cot + by_head_cot.T, later_grad)
    )
    xbc_cot, dt_cot, edge_cot, conv_weight_grad, conv_bias_grad, dt_bias_grad, a_log_grad = (
        mid_grads
    )
    edge_back = passed_along(edge_cot, "seq", -1)
    xbc_cot = xbc_cot + jnp.pad(edge_back, ((row_count - (CONV - 1), 0), (0, 0)))
    projected_cot = jnp.concatenate(
        [gate_cot, xbc_cot, dt_cot, jnp.zeros((row_count, WIDE - PROJ), jnp.float32)], axis=1
    ).astype(jnp.bfloat16)
    in_term = contract_rows(normed, projected_cot).astype(jnp.bfloat16)
    out_term = contract_rows(cotangent, gated).astype(jnp.bfloat16)
    normed_cot = contract_cols(projected_cot, in_whole)
    input_part, norm_gain_grad = norm_back(normed_cot)
    input_grad = cotangent.astype(jnp.float32) + input_part
    small = (
        norm_gain_grad,
        conv_weight_grad.T,
        conv_bias_grad,
        gated_gain_grad,
        dt_bias_grad,
        a_log_grad,
        skip_grad,
    )
    flat = jnp.concatenate([a.reshape(-1) for a in small])
    tile = 8 * LANES
    flat = jnp.pad(flat, (0, -flat.shape[0] % tile))
    in_proj_grad, out_proj_grad, summed = sum_to_owners(
        [in_term, out_term], flat.reshape(-1, LANES), collective_id=4
    )
    summed = summed.reshape(-1)
    parts, at = [], 0
    for a in small:
        parts.append(summed[at : at + a.size].reshape(a.shape))
        at += a.size
    return (
        layer_out,
        input_grad,
        in_proj_grad[:, :PROJ],
        out_proj_grad,
        parts[0],
        parts[1].T,
        parts[2],
        parts[4],
        parts[5],
        parts[6],
        parts[3],
    )


QUAD = 4
CHUNK = 128
TAIL = 16
QCH = DI // QUAD
QHEADS = HEADS // QUAD
PAIRS = QCH // LANES
BC = 2 * STATE
QXBC = QCH + BC
SLAB = QXBC + LANES
PARTS = 3
PART = SLAB // PARTS
GRAD_ROWS = 8
SEMS = 94


def flip(value, bit):
    return value + (1 - 2 * bit_at(value, bit)) * 2**bit


def flip_quad(value, mask):
    for bit in range(2):
        if mask >> bit & 1:
            value = flip(value, bit)
    return value


def dot_nn(left, right):
    return lax.dot_general(
        left, right, (((1,), (0,)), ((), ())), preferred_element_type=jnp.float32
    )


def dot_nt(left, right):
    return lax.dot_general(
        left, right, (((1,), (1,)), ((), ())), preferred_element_type=jnp.float32
    )


def dot_tn(left, right):
    return lax.dot_general(
        left, right, (((0,), (0,)), ((), ())), preferred_element_type=jnp.float32
    )


def in_parts(value, count):
    parts = []
    for _ in range(count):
        part = value.astype(jnp.bfloat16)
        parts.append(part)
        value = value - part.astype(jnp.float32)
    return parts


def lane_tile(i):
    return pl.ds(i * LANES, LANES)


def chunk_rows(c, offset=0, count=CHUNK):
    return pl.ds(pl.multiple_of(c * CHUNK + offset, 8), count)


def column_sum(value):
    return jnp.sum(value, axis=0, keepdims=True)


def block_kernel(
    x_hbm,
    gain_hbm,
    in_hbm,
    taps_hbm,
    bias_hbm,
    dt_bias_hbm,
    a_log_hbm,
    skip_hbm,
    gated_gain_hbm,
    proj_hbm,
    cot_hbm,
    out_to,
    grad_to,
    in_grad_to,
    proj_grad_to,
    gain_grad_to,
    taps_grad_to,
    bias_grad_to,
    dt_bias_grad_to,
    a_log_grad_to,
    skip_grad_to,
    gated_gain_grad_to,
    out_ref,
    grad_ref,
    in_grad_ref,
    proj_grad_ref,
    gain_grad_ref,
    taps_grad_ref,
    bias_grad_ref,
    dt_bias_grad_ref,
    a_log_grad_ref,
    skip_grad_ref,
    gated_gain_grad_ref,
    store_sem,
    x_ref,
    gain_ref,
    in_ref,
    taps_ref,
    bias_ref,
    dt_bias_ref,
    a_log_ref,
    skip_ref,
    gated_gain_ref,
    proj_ref,
    cot_ref,
    load_sem,
    early_ref,
    late_ref,
    xq,
    cq,
    xtail,
    early_slots,
    late_slots,
    early_w,
    late_w,
    xn,
    proj,
    act,
    act_slope,
    step_s,
    step_slope,
    log_s,
    cum_s,
    sx_s,
    fresh_s,
    state_out,
    state_come,
    state_s,
    weights_s,
    scores_s,
    ssd_s,
    gate_s,
    gc_s,
    m_s,
    sums_s,
    gated_s,
    gate_cot_s,
    y_s,
    z_s,
    back_s,
    later_s,
    cross_s,
    sx_cot_s,
    pre_cot_s,
    early_cot_s,
    late_term,
    early_term,
    mixed_s,
    mixed_come,
    normed_t,
    cot_t,
    early_wt,
    late_wt,
    normed_cot_s,
    normed_out,
    normed_come,
    tail_out,
    tail_come,
    small_s,
    skip_s,
    small_come,
    small_quad,
    *rest,
):
    stream_held = [rest[4 * i : 4 * i + 4] for i in range(1 + PARTS)]
    send_sem, recv_sem = rest[4 + 4 * PARTS :]
    f32, bf16 = jnp.float32, jnp.bfloat16
    dp_at, seq_at = places()
    q, g = seq_at % QUAD, seq_at // QUAD
    core, y_at = dp_at % 2, dp_at // 2
    place = dp_at * 8 + seq_at
    used = [0]
    sent = []

    loads = [
        pltpu.make_async_copy(source, landing, load_sem.at[i])
        for i, (source, landing) in enumerate(
            [
                (in_hbm, in_ref),
                (proj_hbm, proj_ref),
                (x_hbm, x_ref),
                (gain_hbm, gain_ref),
                (taps_hbm, taps_ref),
                (bias_hbm, bias_ref),
                (dt_bias_hbm, dt_bias_ref),
                (a_log_hbm, a_log_ref),
                (skip_hbm, skip_ref),
                (gated_gain_hbm, gated_gain_ref),
                (cot_hbm, cot_ref),
            ]
        )
    ]
    for load in loads:
        load.start()

    barrier = pltpu.get_barrier_semaphore()
    peers = [(dp_at, (seq_at + hop) % 8) for hop in range(1, 8)]
    peers += [(flip(dp_at, 0), seq_at), (flip(dp_at, 1), seq_at)]
    peers += [(flip(dp_at, 1), flip(seq_at, 2))]
    for peer in peers:
        pl.semaphore_signal(barrier, inc=1, device_id=peer, device_id_type=MESH)

    def remote(source, landing, target, own=True):
        at = used[0]
        used[0] += 1
        copy = pltpu.make_async_remote_copy(
            src_ref=source,
            dst_ref=landing,
            send_sem=send_sem.at[at],
            recv_sem=recv_sem.at[at],
            device_id=target,
            device_id_type=MESH,
        )
        if own:
            copy.start()
            sent.append(copy)
        return copy

    half_lanes = [pl.ds(h * SLAB // 2, SLAB // 2) for h in range(2)]

    def share_block(own_block, slots):
        over_z = [
            remote(own_block.at[:, lanes], slots.at[q, :, lanes], in_quad(2))
            for lanes in half_lanes
        ]
        return over_z, remote(own_block, slots.at[q], in_quad(1))

    def pass_block(slots, over_z):
        made = []
        for copy, lanes in zip(over_z, half_lanes):
            copy.wait_recv()
            view = slots.at[flip_quad(q, 2), :, lanes]
            made.append(remote(view, view, in_quad(1)))
        return made

    def send_sums(blocks, landing):
        over_x = [
            remote(blocks.at[flip_quad(q, 3), :, lanes], landing.at[0, :, lanes], in_quad(1))
            for lanes in half_lanes
        ]
        return over_x, remote(blocks.at[flip_quad(q, 1)], landing.at[1], in_quad(1))

    def pass_sums(mine, blocks, landing, over_x):
        made = []
        other = flip_quad(q, 2)
        for copy, lanes in zip(over_x, half_lanes):
            copy.wait_recv()
            blocks[other, :, lanes] = (
                mine[other, :, lanes].astype(f32) + landing[0, :, lanes].astype(f32)
            ).astype(bf16)
            made.append(
                remote(blocks.at[other, :, lanes], landing.at[2, :, lanes], in_quad(2))
            )
        return made

    def in_quad(mask):
        return dp_at, flip_quad(seq_at, mask)

    far = (dp_at, flip(seq_at, 2))
    beside = (flip(dp_at, 1), seq_at)
    twin = (flip(dp_at, 0), seq_at)

    def arrived(copies):
        for copy in copies:
            copy.wait_recv()

    lane = lax.broadcasted_iota(jnp.int32, (1, LANES), 1)
    first_half = lane < HEAD_DIM
    half0 = jnp.where(first_half, 1.0, 0.0)
    half1 = 1.0 - half0
    half0b, half1b = half0.astype(bf16), half1.astype(bf16)
    row_at = lax.broadcasted_iota(jnp.int32, (CHUNK, CHUNK), 0)
    lane_at = lax.broadcasted_iota(jnp.int32, (CHUNK, CHUNK), 1)
    causal = row_at >= lane_at
    lower = jnp.where(causal, 1.0, 0.0).astype(bf16)
    upper = jnp.where(row_at <= lane_at, 1.0, 0.0).astype(bf16)
    lower3 = jnp.concatenate([lower] * 3, axis=1)
    upper3 = jnp.concatenate([upper] * 3, axis=1)

    def spread(by_head, i):
        return jnp.where(first_half, by_head[:, 2 * i : 2 * i + 1], by_head[:, 2 * i + 1 : 2 * i + 2])

    head_picks = []
    for i in range(PAIRS):
        pick = jnp.where(2 * i + row_at // HEAD_DIM == lane_at, 1.0, 0.0).astype(bf16)
        head_picks.append(jnp.concatenate([pick] * 2, axis=0))

    def head_sum(value, i):
        return dot_nn(jnp.concatenate(in_parts(value, 2), axis=1), head_picks[i])

    def flat_row(ref, low, count):
        return ref[pl.ds(low, count)].reshape(1, count)

    def own_channels(i):
        return pl.ds(pl.multiple_of(q * QCH + i * LANES, LANES), LANES)

    def conv_channels(i):
        return own_channels(i) if i < PAIRS else pl.ds(DI + (i - PAIRS) * LANES, LANES)

    def tap(k, i):
        return taps_ref[pl.ds(k, 1), conv_channels(i)]

    def gated_gain(i):
        return gated_gain_ref[own_channels(i)].reshape(1, LANES)

    stores = []

    def store(source, landing):
        copy = pltpu.make_async_copy(source, landing, store_sem.at[len(stores)])
        copy.start()
        stores.append(copy)

    def own_heads(ref):
        head_at = lax.broadcasted_iota(jnp.int32, (HEADS, LANES), 0)
        to = lax.broadcasted_iota(jnp.int32, (HEADS, LANES), 1)
        pick = jnp.where((head_at == to + q * QHEADS) & (to < QHEADS), 1.0, 0.0)
        value = jnp.broadcast_to(ref[...].reshape(1, HEADS), (8, HEADS))
        return inner_product(value, pick, ((1,), (0,)))[:1]

    def stacked(value):
        return jnp.concatenate([value * half0b, value * half1b], axis=0)

    loads[0].wait()
    loads[1].wait()
    for j in range(QUAD):
        own = pl.ds(j * QCH, QCH)
        early_ref[j, :, pl.ds(0, QCH)] = in_ref[:, pl.ds(DI + j * QCH, QCH)]
        early_ref[j, :, pl.ds(QCH, BC)] = in_ref[:, pl.ds(2 * DI, BC)]
        head_at = lax.broadcasted_iota(jnp.int32, (HEADS, LANES), 0)
        to = lax.broadcasted_iota(jnp.int32, (HEADS, LANES), 1)
        pick = jnp.where((head_at == to + j * QHEADS) & (to < QHEADS), 1.0, 0.0)
        early_ref[j, :, pl.ds(QXBC, LANES)] = dot_nn(
            in_ref[:, pl.ds(DI + XBC, HEADS)], pick.astype(bf16)
        ).astype(bf16)
        late_ref[j, :, pl.ds(0, QCH)] = in_ref[:, own]
        late_ref[j, :, pl.ds(QCH, QCH)] = proj_ref[:, own]

    for load in loads[2:]:
        load.wait()
    pl.semaphore_wait(barrier, len(peers))

    def scatter(shard, slots):
        return [
            remote(shard.at[flip_quad(q, mask)], slots.at[place], in_quad(mask))
            for mask in (1, 2, 3)
        ]

    early_0 = scatter(early_ref, early_slots)
    late_0 = scatter(late_ref, late_slots)
    token_z, token_x = share_block(x_ref, xq)
    tail_sends = [
        remote(x_ref.at[pl.ds(CHUNK - TAIL, TAIL)], xtail, (dp_at, QUAD + i), own=False)
        for i in range(QUAD)
    ]
    at_end = seq_at == QUAD - 1

    @pl.when(at_end)
    def _():
        for copy in tail_sends:
            copy.start()

    early_slots[place] = early_ref[q]
    late_slots[place] = late_ref[q]
    xq[q] = x_ref[...]
    cq[q] = cot_ref[...]

    def cross_far(slots, parts):
        wide = SLAB // parts
        return [
            remote(
                slots.at[pl.ds(dp_at * 8 + g * 4, 4), :, lane_part],
                slots.at[pl.ds(dp_at * 8 + g * 4, 4), :, lane_part],
                far,
            )
            for lane_part in [pl.ds(part * wide, wide) for part in range(parts)]
        ]

    def cross_beside(slots, copies):
        made = []
        for part, copy in enumerate(copies):
            copy.wait_recv()
            wide = SLAB // len(copies)
            view = slots.at[pl.ds(dp_at * 8, 8), :, pl.ds(part * wide, wide)]
            made.append(remote(view, view, beside))
        return made

    def cross_twin(slots, copies):
        made = []
        for part, copy in enumerate(copies):
            copy.wait_recv()
            for up in range(2):
                wide = SLAB // len(copies)
                view = slots.at[pl.ds((2 * up + core) * 8, 8), :, pl.ds(part * wide, wide)]
                made.append(remote(view, view, twin))
        return made

    def flatten(slots, flat, low=0, wide=SLAB):
        lanes = pl.ds(low, wide)

        def one(pair, carry):
            value = slots[pl.ds(2 * pair, 2), :, lanes].astype(f32).reshape(48, wide)
            flat[pl.ds(pl.multiple_of(pair * 48, 16), 48), lanes] = value.astype(bf16)
            return carry

        lax.fori_loop(0, 16, one, 0)

    arrived(early_0)
    early_1 = cross_far(early_slots, PARTS)
    token_pass = pass_block(xq, token_z)
    early_2 = cross_beside(early_slots, early_1)
    arrived(late_0)
    late_1 = cross_far(late_slots, 2)
    cot_z, cot_x = share_block(cot_ref, cq)

    arrived([token_x, *token_pass])

    for i in range(QUAD):

        @pl.when((g == 1) & (q == i))
        def _():
            tail_sends[i].wait_recv()

    @pl.when(g == 0)
    def _():
        xtail[...] = jnp.zeros_like(xtail)

    gain = flat_row(gain_ref, 0, x_ref.shape[1])

    def scaled_rows(value):
        value = value.astype(f32)
        return value * lax.rsqrt(jnp.mean(value * value, axis=-1, keepdims=True) + EPS)

    tail_rows = scaled_rows(xtail[...]) * gain
    xn[pl.ds(0, TAIL), :] = tail_rows.astype(bf16)
    normed_t[:, pl.ds(QUAD * CHUNK, LANES)] = jnp.concatenate(
        [tail_rows, jnp.zeros((LANES - TAIL, tail_rows.shape[1]), f32)], axis=0
    ).T.astype(bf16)
    early_cot_s[pl.ds(QUAD * CHUNK, LANES), :] = jnp.zeros((LANES, SLAB), bf16)

    def norm_block(c, carry):
        value = scaled_rows(xq[c]) * gain
        xn[pl.ds(pl.multiple_of(c * CHUNK + TAIL, 16), CHUNK), :] = value.astype(bf16)
        normed_t[:, pl.ds(pl.multiple_of(c * CHUNK, CHUNK), CHUNK)] = value.T.astype(bf16)
        return carry

    lax.fori_loop(0, QUAD, norm_block, 0)
    early_3 = cross_twin(early_slots, early_2)
    cot_pass = pass_block(cq, cot_z)
    late_2 = cross_beside(late_slots, late_1)
    small_s[...] = jnp.zeros_like(small_s)
    skip_s[...] = jnp.zeros_like(skip_s)
    pre_cot_s[pl.ds(0, TAIL), :] = jnp.zeros((TAIL, QXBC), f32)
    pre_cot_s[pl.ds(TAIL + QUAD * CHUNK, 8), :] = jnp.zeros((8, QXBC), f32)
    for part in range(PARTS):
        cols = pl.ds(part * PART, PART)
        each = len(early_3) // PARTS
        arrived(early_3[part * each : (part + 1) * each])
        flatten(early_slots, early_w, part * PART, PART)
        proj[:, cols] = dot_nn(xn[...], early_w[:, cols])

        def forward_conv(c, carry, part=part):
            rows = chunk_rows(c)
            for i in range(part * PART // LANES, min((part + 1) * PART, QXBC) // LANES):
                lanes = lane_tile(i)
                window = proj[chunk_rows(c, 8, CHUNK + 8), lanes]
                total = bias_ref[conv_channels(i)].reshape(1, LANES)
                for k in range(CONV):
                    total = total + tap(k, i) * pltpu.roll(window, CHUNK + 3 - k, 0)[:CHUNK]
                sig = lax.logistic(total)
                act[rows, lanes] = total * sig
                act_slope[rows, lanes] = sig * (1.0 + total * (1.0 - sig))
            return carry

        lax.fori_loop(0, QUAD, forward_conv, 0)

    rate = -jnp.exp(own_heads(a_log_ref))
    dt_bias = own_heads(dt_bias_ref)
    skips = own_heads(skip_ref)
    skip_wide = [spread(skips, i) for i in range(PAIRS)]
    head_lane = lane < QHEADS

    def forward_states(c, carry):
        rows = chunk_rows(c)
        raw = proj[chunk_rows(c, TAIL), pl.ds(QXBC, LANES)] + dt_bias
        step = jnp.maximum(raw, 0.0) + jnp.log1p(jnp.exp(-jnp.abs(raw)))
        step = jnp.where(head_lane, step, 0.0)
        log_decay = step * rate
        cum = dot_nn(lower3, jnp.concatenate(in_parts(log_decay, 3), axis=0))
        step_s[rows, :] = step
        step_slope[rows, :] = lax.logistic(raw)
        log_s[rows, :] = log_decay
        cum_s[rows, :] = cum
        tail = jnp.exp(cum[CHUNK - 1 :] - cum)
        b_mat = act[rows, pl.ds(QCH, STATE)].astype(bf16)
        for i in range(PAIRS):
            lanes = lane_tile(i)
            sx = act[rows, lanes] * spread(step, i)
            sx_s[rows, lanes] = sx.astype(bf16)
            fresh_s[c, i] = dot_tn(b_mat, (sx * spread(tail, i)).astype(bf16))
        return carry

    lax.fori_loop(0, QUAD, forward_states, 0)

    def chunk_decay(c, i):
        last = cum_s[chunk_rows(c, CHUNK - 8, 8), :][7:]
        return spread(jnp.exp(last), i)

    for i in range(PAIRS):
        total = fresh_s[0, i]
        for c in range(1, QUAD):
            total = chunk_decay(c, i) * total + fresh_s[c, i]
        state_out[i] = total.astype(bf16)
    state_copy = remote(state_out, state_come, far)
    late_3 = cross_twin(late_slots, late_2)

    def forward_local(c, carry):
        rows = chunk_rows(c)
        b_mat = act[rows, pl.ds(QCH, STATE)].astype(bf16)
        c_mat = act[rows, pl.ds(QCH + STATE, STATE)].astype(bf16)
        crossed = dot_nt(c_mat, b_mat)
        cum = cum_s[rows, :]
        cum_t = cum.T
        for i in range(PAIRS):
            lanes = lane_tile(i)
            pair = []
            for head in (2 * i, 2 * i + 1):
                gap = cum[:, head : head + 1] - cum_t[head : head + 1, :]
                pair.append(jnp.exp(jnp.where(causal, gap, -1e30)))
            weights_s[c, i] = jnp.concatenate(pair, axis=1).astype(bf16)
            scores = jnp.concatenate([w * crossed for w in pair], axis=1).astype(bf16)
            scores_s[c, i] = scores
            ssd_s[rows, lanes] = dot_nn(scores, stacked(sx_s[rows, lanes]))
        return carry

    lax.fori_loop(0, QUAD, forward_local, 0)
    gate_w = pl.ds(0, QCH)
    out_w = pl.ds(QCH, QCH)
    arrived(late_3[:2])
    flatten(late_slots, late_w, 0, QCH)
    gate_s[...] = dot_nn(xn[pl.ds(TAIL, QUAD * CHUNK), :], late_w[:, gate_w])
    arrived(late_3[2:])
    flatten(late_slots, late_w, QCH, QCH)
    arrived([cot_x, *cot_pass])

    def cot_block(c, carry):
        gc_s[chunk_rows(c), :] = dot_nn(cq[c], late_w[:, out_w])
        return carry

    lax.fori_loop(0, QUAD, cot_block, 0)
    state_copy.wait_recv()
    for i in range(PAIRS):
        total = jnp.where(g == 1, state_come[i].astype(f32), 0.0)
        for c in range(QUAD):
            state_s[c, i] = total.astype(bf16)
            if c < QUAD - 1:
                total = chunk_decay(c, i) * total + fresh_s[c, i]

    def forward_gate(c, carry):
        rows = chunk_rows(c)
        c_mat = act[rows, pl.ds(QCH + STATE, STATE)].astype(bf16)
        grown = jnp.exp(cum_s[rows, :])
        square, crossed = 0.0, 0.0
        for i in range(PAIRS):
            lanes = lane_tile(i)
            ssd = ssd_s[rows, lanes] + dot_nn(c_mat, state_s[c, i]) * spread(grown, i)
            ssd_s[rows, lanes] = ssd
            gate = gate_s[rows, lanes]
            m = (ssd + act[rows, lanes] * skip_wide[i]) * gate * lax.logistic(gate)
            m_s[rows, lanes] = m
            square = square + m * m
            crossed = crossed + gc_s[rows, lanes] * gated_gain(i) * m
        square = jnp.sum(square, axis=1, keepdims=True)
        crossed = jnp.sum(crossed, axis=1, keepdims=True)
        both = jnp.where(lane == 0, square, jnp.where(lane == 1, crossed, 0.0))
        sums_s[q, :, pl.ds(pl.multiple_of(c * CHUNK, CHUNK), CHUNK)] = (
            both.T[:8]
        )
        return carry

    lax.fori_loop(0, QUAD, forward_gate, 0)
    sums_copies = [remote(sums_s.at[q], sums_s.at[q], in_quad(mask)) for mask in (1, 2, 3)]

    def turn_cot(c, carry):
        cot_t[:, pl.ds(pl.multiple_of(c * CHUNK, CHUNK), CHUNK)] = (
            cq[c].astype(f32).T.astype(bf16)
        )
        return carry

    lax.fori_loop(0, QUAD, turn_cot, 0)

    def turn_weights(c, carry):
        own = pl.ds(pl.multiple_of(c * CHUNK, CHUNK), CHUNK)
        late_wt[:, own] = late_w[own, :].astype(f32).T.astype(bf16)
        early_wt[:, own] = early_w[own, :].astype(f32).T.astype(bf16)
        return carry

    lax.fori_loop(0, x_ref.shape[1] // CHUNK, turn_weights, 0)
    arrived(sums_copies)

    def backward_states(c, carry):
        rows = chunk_rows(c)
        cols = pl.ds(pl.multiple_of(c * CHUNK, CHUNK), CHUNK)
        sums = sums_s[0, :, cols] + sums_s[1, :, cols] + sums_s[2, :, cols] + sums_s[3, :, cols]
        sums = jnp.concatenate([sums] * (CHUNK // 8), axis=0).T
        scale = lax.rsqrt(sums[:, 0:1] * (1.0 / DI) + EPS)
        pull = scale * scale * scale * (sums[:, 1:2] * (1.0 / DI))
        c_mat = act[rows, pl.ds(QCH + STATE, STATE)].astype(bf16)
        grown = jnp.exp(cum_s[rows, :])
        for i in range(PAIRS):
            lanes = lane_tile(i)
            m, gc, gate = m_s[rows, lanes], gc_s[rows, lanes], gate_s[rows, lanes]
            xs = act[rows, lanes]
            mr = m * scale
            gated_s[rows, lanes] = (mr * gated_gain(i)).astype(bf16)
            small_s[5:6, lanes] += column_sum(gc * mr)
            m_cot = scale * (gc * gated_gain(i)) - m * pull
            sig = lax.logistic(gate)
            mixed = ssd_s[rows, lanes] + xs * skip_wide[i]
            gate_cot_s[rows, lanes] = (
                m_cot * mixed * (sig * (1.0 + gate * (1.0 - sig)))
            ).astype(bf16)
            y = m_cot * gate * sig
            y_s[rows, lanes] = y
            skip_s[0:1, lanes] += column_sum(y * xs)
            z = (y * spread(grown, i)).astype(bf16)
            z_s[rows, lanes] = z
            back_s[c, i] = dot_tn(c_mat, z)
        return carry

    lax.fori_loop(0, QUAD, backward_states, 0)
    state_copy.wait_send()
    sent[:] = [copy for copy in sent if copy is not state_copy]
    for i in range(PAIRS):
        total = back_s[QUAD - 1, i]
        for c in range(QUAD - 2, -1, -1):
            total = chunk_decay(c, i) * total + back_s[c, i]
        state_out[i] = total.astype(bf16)
    later_copy = remote(state_out, later_s.at[QUAD], far)

    def term_rows(term, half, value, lanes):
        term[pl.ds(half * 16, 16), :, lanes] = value.reshape(16, 24, value.shape[1]).astype(bf16)

    def late_half(half, carry):
        own = pl.ds(pl.multiple_of(half * QCH, QCH), QCH)
        term_rows(late_term, half, dot_nn(normed_t[own, pl.ds(0, QUAD * CHUNK)], gate_cot_s[...]), gate_w)
        term_rows(late_term, half, dot_nn(cot_t[own, :], gated_s[...]), out_w)
        return carry

    lax.fori_loop(0, 2, late_half, 0)

    streams = [(late_term, pl.ds(0, SLAB))] + [
        (early_term, pl.ds(i * PART, PART)) for i in range(PARTS)
    ]

    def reduce_twin(stream):
        term, lanes = streams[stream]
        return [
            remote(
                term.at[pl.ds((2 * up + 1 - core) * 8, 8), :, lanes],
                stream_held[stream][0].at[pl.ds(8 * up, 8)],
                twin,
            )
            for up in range(2)
        ]

    def reduce_beside(stream, copies):
        arrived(copies)
        term, lanes = streams[stream]
        held = stream_held[stream][0]

        def add(four, carry):
            mine = pl.ds((2 * (four // 2) + core) * 8 + four % 2 * 4, 4)
            own = pl.ds(four * 4, 4)
            held[own] = (term[mine, :, lanes].astype(f32) + held[own].astype(f32)).astype(bf16)
            return carry

        lax.fori_loop(0, 4, add, 0)
        return [remote(held.at[pl.ds((1 - y_at) * 8, 8)], stream_held[stream][1], beside)]

    def reduce_far(stream, copies):
        arrived(copies)
        before, held = stream_held[stream][:2]

        def add(four, carry):
            own = pl.ds(four * 4, 4)
            held[own] = (
                before[pl.ds(y_at * 8 + four * 4, 4)].astype(f32) + held[own].astype(f32)
            ).astype(bf16)
            return carry

        lax.fori_loop(0, 2, add, 0)
        return [remote(held.at[pl.ds((1 - g) * 4, 4)], stream_held[stream][2], far)]

    def reduce_quad(stream, copies):
        arrived(copies)
        before, held, result = stream_held[stream][1:]

        held[...] = (before[pl.ds(g * 4, 4)].astype(f32) + held[...].astype(f32)).astype(bf16)
        made = [
            remote(held.at[flip_quad(q, mask)], result.at[q], in_quad(mask)) for mask in (1, 2, 3)
        ]
        result[q] = held[q]
        return made

    late_r0 = reduce_twin(0)

    for n in range(3):
        cols = pl.ds(n * 256, 256)
        value = dot_nn(gated_s[...], late_wt[out_w, cols]).astype(bf16)
        for c in range(QUAD):
            mixed_s[c, :, cols] = value[c * CHUNK : (c + 1) * CHUNK]

    mixed_x, mixed_own = send_sums(mixed_s, mixed_come)

    def backward_local(c, carry):
        rows = chunk_rows(c)
        total = jnp.zeros((CHUNK, CHUNK), f32)
        for i in range(PAIRS):
            lanes = lane_tile(i)
            y = y_s[rows, lanes].astype(bf16)
            moved = weights_s[c, i].astype(f32) * dot_nt(y, stacked(sx_s[rows, lanes]))
            total = total + moved[:, :CHUNK] + moved[:, CHUNK:]
            both = dot_tn(scores_s[c, i], y)
            sx_cot_s[rows, lanes] = both[:CHUNK] * half0 + both[CHUNK:] * half1
        cross_s[c] = total.astype(bf16)
        return carry

    lax.fori_loop(0, QUAD, backward_local, 0)
    late_r1 = reduce_beside(0, late_r0)
    mixed_z = pass_sums(mixed_s, mixed_s, mixed_come, mixed_x)
    later_copy.wait_recv()
    for i in range(PAIRS):
        total = jnp.where(g == 0, later_s[QUAD, i].astype(f32), 0.0)
        for c in range(QUAD - 1, -1, -1):
            later_s[c, i] = total.astype(bf16)
            if c > 0:
                total = chunk_decay(c, i) * total + back_s[c, i]

    def backward_mix(c, carry):
        rows = chunk_rows(c)
        shifted = chunk_rows(c, TAIL)
        b_mat = act[rows, pl.ds(QCH, STATE)].astype(bf16)
        c_mat = act[rows, pl.ds(QCH + STATE, STATE)].astype(bf16)
        cum, step = cum_s[rows, :], step_s[rows, :]
        tail = jnp.exp(cum[CHUNK - 1 :] - cum)
        decay = jnp.exp(cum[CHUNK - 1 :])
        cross = cross_s[c]
        b_cot = dot_tn(cross, c_mat)
        c_cot = dot_nn(cross, b_mat)
        by_head = jnp.zeros((2 * CHUNK + 8, LANES), f32)
        for i in range(PAIRS):
            lanes = lane_tile(i)
            xs, y = act[rows, lanes], y_s[rows, lanes]
            later, state = later_s[c, i], state_s[c, i]
            wide_step, wide_tail = spread(step, i), spread(tail, i)
            tailed = (xs * wide_step * wide_tail).astype(bf16)
            from_later = dot_nn(b_mat, later) * wide_tail
            b_cot = b_cot + dot_nt(tailed, later)
            c_cot = c_cot + dot_nt(z_s[rows, lanes], state)
            sx = sx_s[rows, lanes].astype(f32)
            sx_cot = sx_cot_s[rows, lanes] + from_later
            last = column_sum(sx * from_later) + column_sum(
                later.astype(f32) * state.astype(f32)
            ) * spread(decay, i)
            by_head = by_head + head_sum(
                jnp.concatenate(
                    [
                        y.astype(bf16).astype(f32) * ssd_s[rows, lanes] - sx * sx_cot,
                        sx_cot * xs,
                        jnp.broadcast_to(last, (8, LANES)),
                    ],
                    axis=0,
                ),
                i,
            )
            pre_cot_s[shifted, lanes] = (
                sx_cot * wide_step + y * skip_wide[i]
            ) * act_slope[rows, lanes]
        pre_cot_s[shifted, pl.ds(QCH, STATE)] = b_cot * act_slope[rows, pl.ds(QCH, STATE)]
        pre_cot_s[shifted, pl.ds(QCH + STATE, STATE)] = (
            c_cot * act_slope[rows, pl.ds(QCH + STATE, STATE)]
        )
        cum_cot, step_cot = by_head[:CHUNK], by_head[CHUNK : 2 * CHUNK]
        last_cot = by_head[2 * CHUNK : 2 * CHUNK + 1]
        log_cot = dot_nn(upper3, jnp.concatenate(in_parts(cum_cot, 3), axis=0)) + last_cot
        dt_cot = (step_cot + log_cot * rate) * step_slope[rows, :]
        small_s[7:8, lane_tile(1)] += column_sum(log_cot * log_s[rows, :])
        small_s[5:6, lane_tile(4)] += column_sum(dt_cot)
        early_cot_s[rows, pl.ds(QXBC, LANES)] = dt_cot.astype(bf16)
        return carry

    lax.fori_loop(0, QUAD, backward_mix, 0)
    late_r2 = reduce_far(0, late_r1)

    for i in range(QXBC // LANES):
        lanes = lane_tile(i)
        edge = pre_cot_s[pl.ds(0, 24), lanes]
        total = tap(CONV - 1, i) * edge[:TAIL]
        for k in range(CONV - 1):
            total = total + tap(k, i) * pltpu.roll(edge, 24 - (3 - k), 0)[:TAIL]
        early_cot_s[pl.ds(QUAD * CHUNK, TAIL), lanes] = total.astype(bf16)

    def backward_conv(c, carry):
        for i in range(QXBC // LANES):
            lanes = lane_tile(i)
            cots = pre_cot_s[chunk_rows(c, TAIL, CHUNK + 8), lanes]
            window = proj[chunk_rows(c, 8, CHUNK + 8), lanes]
            cot = cots[:CHUNK]
            total = tap(CONV - 1, i) * cot
            for k in range(CONV - 1):
                total = total + tap(k, i) * pltpu.roll(cots, CHUNK + 8 - (3 - k), 0)[:CHUNK]
            early_cot_s[chunk_rows(c), lanes] = total.astype(bf16)
            for k in range(CONV):
                small_s[k : k + 1, lanes] += column_sum(
                    cot * pltpu.roll(window, CHUNK + 3 - k, 0)[:CHUNK]
                )
            small_s[4:5, lanes] += column_sum(cot)
        return carry

    lax.fori_loop(0, QUAD, backward_conv, 0)

    heads = jnp.zeros((8, LANES), f32)
    for i in range(PAIRS):
        heads = heads + head_sum(jnp.broadcast_to(skip_s[0:1, lane_tile(i)], (8, LANES)), i)
    small_s[5:6, lane_tile(3)] = heads[:1]

    tail_value = dot_nn(early_cot_s[pl.ds(QUAD * CHUNK, TAIL), :], early_wt[...])
    tail_out[...] = tail_value
    tail_index = used[0]
    used[0] += QUAD

    def tail_copy(i):
        return pltpu.make_async_remote_copy(
            src_ref=tail_out,
            dst_ref=tail_come.at[i],
            send_sem=send_sem.at[tail_index + i],
            recv_sem=recv_sem.at[tail_index + i],
            device_id=(dp_at, QUAD - 1),
            device_id_type=MESH,
        )

    for i in range(QUAD):

        @pl.when((g == 1) & (q == i))
        def _():
            tail_copy(i).start()

    def add_gain(value, rows):
        total = column_sum(value * scaled_rows(rows))
        small_s[6:7, :] += total[:, :QXBC]
        small_s[7:8, lane_tile(0)] += total[:, QXBC:]

    add_gain(tail_value, xtail[...])

    for n in range(3):
        cols = pl.ds(n * 256, 256)
        value = dot_nn(early_cot_s[pl.ds(0, QUAD * CHUNK), :], early_wt[:, cols])
        value = value + dot_nn(gate_cot_s[...], late_wt[gate_w, cols])
        for c in range(QUAD):
            part = value[c * CHUNK : (c + 1) * CHUNK]
            normed_cot_s[c, :, cols] = part
            normed_out[c, :, cols] = part.astype(bf16)

    normed_x, normed_own = send_sums(normed_out, normed_come)
    for c in range(QUAD):
        add_gain(normed_cot_s[c], xq[c])
    small_copy = remote(small_s, small_come.at[0], twin)
    early_r0 = []
    for part in range(PARTS):
        lanes = pl.ds(part * PART, PART)

        def early_half(half, carry, lanes=lanes):
            own = pl.ds(pl.multiple_of(half * QCH, QCH), QCH)
            value = dot_nn(normed_t[own, :], early_cot_s[:, lanes])
            term_rows(early_term, half, value, lanes)
            return carry

        lax.fori_loop(0, 2, early_half, 0)
        early_r0.append(reduce_twin(1 + part))

    small_copy.wait_recv()
    small_come[4] = small_s[...] + small_come[0]
    across = (flip(dp_at, 1), flip(seq_at, 2))
    small_copies = [
        remote(small_come.at[4], small_come.at[1 + i], target)
        for i, target in enumerate((beside, far, across))
    ]
    early_r1 = [reduce_beside(1 + part, early_r0[part]) for part in range(PARTS)]
    normed_z = pass_sums(normed_cot_s, normed_out, normed_come, normed_x)

    early_r2 = [reduce_far(1, early_r1[0])]
    early_r2.append(reduce_far(2, early_r1[1]))
    late_r3 = reduce_quad(0, late_r2)
    early_r2.append(reduce_far(3, early_r1[2]))
    arrived(small_copies)
    small_quad[q] = small_come[4] + small_come[1] + (small_come[2] + small_come[3])
    small_copies = [remote(small_quad.at[q], small_quad.at[q], in_quad(mask)) for mask in (1, 2, 3)]

    arrived([mixed_own, *mixed_z])
    total = x_ref[...].astype(f32) + mixed_s[q].astype(f32)
    total = total + mixed_come[1].astype(f32) + mixed_come[2].astype(f32)
    out_ref[...] = total.astype(bf16)
    store(out_ref, out_to)
    early_r3 = [reduce_quad(1 + part, early_r2[part]) for part in range(PARTS)]

    arrived([normed_own, *normed_z])
    value = normed_cot_s[q] + normed_come[1].astype(f32) + normed_come[2].astype(f32)
    normed_cot_s[q] = value

    @pl.when(at_end)
    def _():
        for i in range(QUAD):
            tail_copy(i).wait_recv()
        rows = pl.ds(CHUNK - TAIL, TAIL)
        normed_cot_s[q, rows, :] += tail_come[0] + tail_come[1] + tail_come[2] + tail_come[3]

    cot = normed_cot_s[q] * gain
    rows = x_ref[...].astype(f32)
    scale = lax.rsqrt(jnp.mean(rows * rows, axis=-1, keepdims=True) + EPS)
    pull = scale * scale * scale * jnp.mean(cot * rows, axis=-1, keepdims=True)
    grad_ref[...] = cot_ref[...].astype(f32) + scale * cot - rows * pull
    store(grad_ref, grad_to)

    arrived(small_copies)
    for j in range(QUAD):
        own = pl.ds(j * QCH, QCH)
        taps_grad_ref[:, own] = small_quad[j, 0:CONV, pl.ds(0, QCH)]
        bias_grad_ref[own] = small_quad[j, CONV : CONV + 1, pl.ds(0, QCH)].reshape(QCH)
        gated_gain_grad_ref[own] = small_quad[j, 5:6, pl.ds(0, QCH)].reshape(QCH)
    quads = small_quad[0] + small_quad[1] + small_quad[2] + small_quad[3]
    taps_grad_ref[:, pl.ds(DI, BC)] = quads[:CONV, QCH:QXBC]
    bias_grad_ref[pl.ds(DI, BC)] = quads[CONV : CONV + 1, QCH:QXBC].reshape(BC)
    gain_grad_ref[pl.ds(0, QXBC)] = quads[6:7].reshape(QXBC)
    gain_grad_ref[pl.ds(QXBC, LANES)] = quads[7:8, :LANES].reshape(LANES)

    def in_head_order(parts):
        total = parts[0]
        for j in range(1, QUAD):
            total = total + pltpu.roll(parts[j], j * QHEADS, 1)
        return total[:, :HEADS]

    def small_heads(row, i):
        parts = [small_quad[j, :, lane_tile(i)] for j in range(QUAD)]
        return in_head_order(parts)[row : row + 1].reshape(HEADS)

    skip_grad_ref[...] = small_heads(5, 3)
    dt_bias_grad_ref[...] = small_heads(5, 4)
    a_log_grad_ref[...] = small_heads(7, 1)
    store(gain_grad_ref, gain_grad_to)
    store(taps_grad_ref, taps_grad_to)
    store(bias_grad_ref, bias_grad_to)
    store(dt_bias_grad_ref, dt_bias_grad_to)
    store(a_log_grad_ref, a_log_grad_to)
    store(skip_grad_ref, skip_grad_to)
    store(gated_gain_grad_ref, gated_gain_grad_to)

    arrived(late_r3)
    for j in range(QUAD):
        own = pl.ds(j * QCH, QCH)
        in_grad_ref[:, own] = stream_held[0][3][j, :, pl.ds(0, QCH)].astype(f32)
        proj_grad_ref[:, own] = stream_held[0][3][j, :, pl.ds(QCH, QCH)].astype(f32)
    store(proj_grad_ref, proj_grad_to)
    for part in range(PARTS):
        arrived(early_r3[part])

    def early_result(j, low):
        return stream_held[1 + low // PART][3][j, :, pl.ds(low % PART, LANES)].astype(f32)

    for j in range(QUAD):
        for i in range(PAIRS):
            in_grad_ref[:, pl.ds(DI + j * QCH + i * LANES, LANES)] = early_result(j, i * LANES)
    for i in range(BC // LANES):
        total = early_result(0, QCH + i * LANES)
        for j in range(1, QUAD):
            total = total + early_result(j, QCH + i * LANES)
        in_grad_ref[:, pl.ds(2 * DI + i * LANES, LANES)] = total
    in_grad_ref[:, pl.ds(DI + XBC, HEADS)] = in_head_order(
        [early_result(j, QXBC) for j in range(QUAD)]
    )

    store(in_grad_ref, in_grad_to)
    assert used[0] == SEMS
    for copy in sent:
        copy.wait_send()

    @pl.when(at_end)
    def _():
        for copy in tail_sends:
            copy.wait_send()

    for i in range(QUAD):

        @pl.when((g == 1) & (q == i))
        def _():
            tail_copy(i).wait_send()

    for copy in stores:
        copy.wait()


def quad_body(
    inputs,
    norm_gain,
    in_proj,
    conv_weight,
    conv_bias,
    dt_bias,
    a_log,
    skip_gain,
    gated_gain,
    out_proj,
    cotangent,
):
    f32, bf16 = jnp.float32, jnp.bfloat16
    rows = in_proj.shape[0]
    tokens = QUAD * CHUNK
    slots = lax.axis_size("dp") * lax.axis_size("seq")
    width = inputs.shape[1]
    vmem = pltpu.VMEM
    held = [
        vmem((count, rows, w), bf16) for w in (SLAB, *[PART] * PARTS) for count in (16, 8, 4, 4)
    ]
    shapes = [inputs.shape, inputs.shape, in_proj.shape, out_proj.shape]
    shapes += [(width,), (CONV, XBC), (XBC,), (HEADS,), (HEADS,), (HEADS,), (DI,)]
    operands = (
        inputs,
        norm_gain,
        in_proj,
        conv_weight.T,
        conv_bias,
        dt_bias,
        a_log,
        skip_gain,
        gated_gain,
        out_proj,
        cotangent,
    )
    scratch = [
        *(vmem(shape, f32 if at else bf16) for at, shape in enumerate(shapes)),
        pltpu.SemaphoreType.DMA((len(shapes),)),
        *(vmem(operand.shape, operand.dtype) for operand in operands),
        pltpu.SemaphoreType.DMA((len(operands),)),
        vmem((QUAD, rows, SLAB), bf16),
        vmem((QUAD, rows, SLAB), bf16),
        vmem((QUAD, CHUNK, width), bf16),
        vmem((QUAD, CHUNK, width), bf16),
        vmem((TAIL, width), bf16),
        vmem((slots, rows, SLAB), bf16),
        vmem((slots, rows, SLAB), bf16),
        vmem((width, SLAB), bf16),
        vmem((width, SLAB), bf16),
        vmem((TAIL + tokens, width), bf16),
        vmem((TAIL + tokens, SLAB), f32),
        vmem((tokens, QXBC), f32),
        vmem((tokens, QXBC), f32),
        vmem((tokens, LANES), f32),
        vmem((tokens, LANES), f32),
        vmem((tokens, LANES), f32),
        vmem((tokens, LANES), f32),
        vmem((tokens, QCH), bf16),
        vmem((QUAD, PAIRS, STATE, LANES), f32),
        vmem((PAIRS, STATE, LANES), bf16),
        vmem((PAIRS, STATE, LANES), bf16),
        vmem((QUAD, PAIRS, STATE, LANES), bf16),
        vmem((QUAD, PAIRS, CHUNK, 2 * CHUNK), bf16),
        vmem((QUAD, PAIRS, CHUNK, 2 * CHUNK), bf16),
        vmem((tokens, QCH), f32),
        vmem((tokens, QCH), f32),
        vmem((tokens, QCH), f32),
        vmem((tokens, QCH), f32),
        vmem((QUAD, 8, tokens), f32),
        vmem((tokens, QCH), bf16),
        vmem((tokens, QCH), bf16),
        vmem((tokens, QCH), f32),
        vmem((tokens, QCH), bf16),
        vmem((QUAD, PAIRS, STATE, LANES), f32),
        vmem((QUAD + 1, PAIRS, STATE, LANES), bf16),
        vmem((QUAD, CHUNK, CHUNK), bf16),
        vmem((tokens, QCH), f32),
        vmem((TAIL + tokens + 8, QXBC), f32),
        vmem((tokens + LANES, SLAB), bf16),
        vmem((slots, rows, SLAB), bf16),
        vmem((slots, rows, SLAB), bf16),
        vmem((QUAD, CHUNK, width), bf16),
        vmem((3, CHUNK, width), bf16),
        vmem((width, tokens + LANES), bf16),
        vmem((width, tokens), bf16),
        vmem((SLAB, width), bf16),
        vmem((SLAB, width), bf16),
        vmem((QUAD, CHUNK, width), f32),
        vmem((QUAD, CHUNK, width), bf16),
        vmem((3, CHUNK, width), bf16),
        vmem((TAIL, width), f32),
        vmem((QUAD, TAIL, width), f32),
        vmem((GRAD_ROWS, QXBC), f32),
        vmem((8, QCH), f32),
        vmem((5, GRAD_ROWS, QXBC), f32),
        vmem((QUAD, GRAD_ROWS, QXBC), f32),
        *held,
        pltpu.SemaphoreType.DMA((SEMS,)),
        pltpu.SemaphoreType.DMA((SEMS,)),
    ]
    in_vmem = pl.BlockSpec(memory_space=pltpu.VMEM)
    got = pl.pallas_call(
        block_kernel,
        out_shape=[
            jax.ShapeDtypeStruct(shape, f32 if at else bf16) for at, shape in enumerate(shapes)
        ],
        in_specs=[pl.BlockSpec(memory_space=pl.ANY)] * 11,
        out_specs=[pl.BlockSpec(memory_space=pl.ANY)] * 11,
        scratch_shapes=scratch,
        compiler_params=pltpu.CompilerParams(
            collective_id=1, has_side_effects=True, vmem_limit_bytes=VMEM_BYTES
        ),
        name="residual_block",
    )(*operands)
    got = pl.pallas_call(
        copy_out_kernel,
        out_shape=[jax.ShapeDtypeStruct(value.shape, value.dtype) for value in got],
        in_specs=[pl.BlockSpec(memory_space=pl.ANY)] * 11,
        out_specs=[pl.BlockSpec(memory_space=pl.ANY)] * 11,
        scratch_shapes=[vmem(value.shape, value.dtype) for value in got]
        + [pltpu.SemaphoreType.DMA((11,))] * 2,
        name="copy_out",
    )(*got)
    return (*got[:5], got[5].T, *got[6:])


def copy_out_kernel(*refs):
    count = (len(refs) - 2) // 3
    sources, landings, held = refs[:count], refs[count : 2 * count], refs[2 * count : 3 * count]
    load_sem, store_sem = refs[3 * count :]
    loads = [pltpu.make_async_copy(sources[i], held[i], load_sem.at[i]) for i in range(count)]
    stores = [pltpu.make_async_copy(held[i], landings[i], store_sem.at[i]) for i in range(count)]
    for load in loads:
        load.start()
    for load, store in zip(loads, stores):
        load.wait()
        store.start()
    for store in stores:
        store.wait()


def fits_quads(mesh):
    return mesh.shape["dp"] == 4 and mesh.shape["seq"] == 2 * QUAD


def solution(mesh):
    placed = (
        P(("dp", "seq"), None),
        P(),
        P(("dp", "seq"), None),
        P(),
        P(),
        P(),
        P(),
        P(),
        P(),
        P(("dp", "seq"), None),
        P(("dp", "seq"), None),
    )
    return jax.shard_map(
        quad_body if fits_quads(mesh) else body,
        mesh=mesh,
        in_specs=placed,
        out_specs=(
            P(("dp", "seq"), None),
            P(("dp", "seq"), None),
            P(("dp", "seq"), None),
            P(("dp", "seq"), None),
            P(),
            P(),
            P(),
            P(),
            P(),
            P(),
            P(),
        ),
        check_vma=False,
    )
```

```python
from functools import partial

import jax
import jax.numpy as jnp
from jax import lax
from jax.experimental import pallas as pl
from jax.experimental.pallas import tpu as pltpu
from jax.sharding import PartitionSpec as P

HEADS = 24
HEAD_DIM = 64
STATE = 128
CONV = 4
DI = 1536
XBC = 1792
PROJ = DI + XBC + HEADS
LANES = 128
WIDE = -(-PROJ // LANES) * LANES


EPS = 1e-05
HIGH = lax.Precision.HIGHEST
MESH = pl.DeviceIdType.MESH
VMEM_BYTES = 60 * 1024 * 1024


def bits_of(count):
    return count.bit_length() - 1


def bit_at(place, bit):
    return (place // 2**bit) % 2


def places():
    return lax.axis_index("dp"), lax.axis_index("seq")


def partner(bit, seq_bits):
    dp_at, seq_at = places()
    if bit < seq_bits:
        return dp_at, seq_at + (1 - 2 * bit_at(seq_at, bit)) * 2**bit
    up = bit - seq_bits
    return dp_at + (1 - 2 * bit_at(dp_at, up)) * 2**up, seq_at


def greet(bits, seq_bits):
    barrier = pltpu.get_barrier_semaphore()
    for bit in range(bits):
        pl.semaphore_signal(barrier, inc=1, device_id=partner(bit, seq_bits), device_id_type=MESH)
    pl.semaphore_wait(barrier, bits)


def gather_orders(seq_bits, dp_bits):
    x_count = seq_bits // 2
    x_bits = list(range(x_count))
    z_bits = list(range(x_count, seq_bits))[::-1]
    core = [seq_bits]
    y_bits = [seq_bits + 1 + i for i in range(dp_bits - 1)]
    return (
        z_bits + x_bits + y_bits + core,
        z_bits + y_bits + x_bits + core,
        z_bits[:1] + x_bits + y_bits + z_bits[1:] + core,
        z_bits[:1] + y_bits + x_bits + z_bits[1:] + core,
    )


SHARES = (0.3, 0.3, 0.2, 0.2)


def split_lanes(width, shares):
    tiles = width // LANES
    edges = [round(tiles * sum(shares[:i])) * LANES for i in range(len(shares) + 1)]
    return [(low, high - low) for low, high in zip(edges, edges[1:])]


def gather_kernel(seq_bits, streams, bits, *refs):
    array_count = 1 + max(stream[0] for stream in streams)
    shards, outs = refs[:array_count], refs[array_count : 2 * array_count]
    send_sem, recv_sem, own_sem = refs[2 * array_count :]
    dp_at, seq_at = places()
    place = dp_at * 2**seq_bits + seq_at
    own = [
        pltpu.make_async_copy(shard, out.at[place], own_sem.at[i])
        for i, (shard, out) in enumerate(zip(shards, outs))
    ]
    for copy in own:
        copy.start()
    greet(bits, seq_bits)
    for copy in own:
        copy.wait()

    def landed(stream, stage, sem):
        which, low, width, _ = streams[stream]
        view = outs[which].at[pl.ds(0, 2**stage), :, pl.ds(low, width)]
        pltpu.make_async_copy(view, view, sem.at[stream, stage]).wait()

    for stage in range(bits + 1):
        for stream, (which, low, width, order) in enumerate(streams):
            if stage > 0:
                landed(stream, stage - 1, recv_sem)
            if stage == bits:
                continue
            free = order[:stage]
            run = 0
            while run in free:
                run += 1
            base = place
            for bit in free:
                base = base - bit_at(place, bit) * 2**bit
            upper = [bit for bit in free if bit > run]
            for combo in range(2 ** len(upper)):
                start = base + sum(2**bit for i, bit in enumerate(upper) if combo >> i & 1)
                view = outs[which].at[pl.ds(start, 2**run), :, pl.ds(low, width)]
                pltpu.make_async_remote_copy(
                    src_ref=view,
                    dst_ref=view,
                    send_sem=send_sem.at[stream, stage],
                    recv_sem=recv_sem.at[stream, stage],
                    device_id=partner(order[stage], seq_bits),
                    device_id_type=MESH,
                ).start()
    for stage in range(bits):
        for stream in range(len(streams)):
            landed(stream, stage, send_sem)


def gather_all(shards, collective_id):
    seq_bits, dp_bits = bits_of(lax.axis_size("seq")), bits_of(lax.axis_size("dp"))
    bits = seq_bits + dp_bits
    orders = gather_orders(seq_bits, dp_bits)
    streams = [
        (which, low, width, order)
        for which, shard in enumerate(shards)
        for (low, width), order in zip(split_lanes(shard.shape[1], SHARES), orders)
    ]
    return pl.pallas_call(
        partial(gather_kernel, seq_bits, streams, bits),
        out_shape=[jax.ShapeDtypeStruct((2**bits, *a.shape), a.dtype) for a in shards],
        in_specs=[pl.BlockSpec(memory_space=pltpu.VMEM)] * len(shards),
        out_specs=[pl.BlockSpec(memory_space=pl.ANY)] * len(shards),
        scratch_shapes=[
            pltpu.SemaphoreType.DMA((len(streams), bits)),
            pltpu.SemaphoreType.DMA((len(streams), bits)),
            pltpu.SemaphoreType.DMA((len(shards),)),
        ],
        compiler_params=pltpu.CompilerParams(
            collective_id=collective_id, has_side_effects=True, vmem_limit_bytes=VMEM_BYTES
        ),
        name="gather_rows",
    )(*shards)


def sum_kernel(seq_bits, streams, bits, array_count, *refs):
    terms, vector = refs[:array_count], refs[array_count]
    outs, vector_out = refs[array_count + 1 : 2 * array_count + 1], refs[2 * array_count + 1]
    held = refs[2 * array_count + 2 : 2 * array_count + 2 + len(streams) * bits]
    rest = refs[2 * array_count + 2 + len(streams) * bits :]
    vector_in, vector_sum, send_sem, recv_sem, vector_send, vector_recv = rest
    dp_at, seq_at = places()
    place = dp_at * 2**seq_bits + seq_at
    greet(bits, seq_bits)

    def source(stream, stage):
        which, low, width, _ = streams[stream]
        if stage == 0:
            return terms[which], pl.ds(low, width)
        return held[stream * bits + stage - 1], pl.ds(0, width)

    def position(stream, stage):
        order = streams[stream][3]
        remaining = sorted(order[stage:])
        return remaining.index(order[stage]), bit_at(place, order[stage])

    def landed(stream, stage, sem):
        view = held[stream * bits + stage]
        pltpu.make_async_copy(view, view, sem.at[stream, stage]).wait()

    def vector_copy(stage):
        return pltpu.make_async_remote_copy(
            src_ref=vector if stage == 0 else vector_sum.at[stage - 1],
            dst_ref=vector_in.at[stage],
            send_sem=vector_send.at[stage],
            recv_sem=vector_recv.at[stage],
            device_id=partner(stage, seq_bits),
            device_id_type=MESH,
        )

    for stage in range(bits + 1):
        if stage > 0:
            vector_copy(stage - 1).wait_recv()
            before = vector[...] if stage == 1 else vector_sum[stage - 2]
            total = before + vector_in[stage - 1]
            if stage < bits:
                vector_sum[stage - 1] = total
            else:
                vector_out[...] = total
        if stage < bits:
            vector_copy(stage).start()
        for stream, (which, low, width, order) in enumerate(streams):
            if stage > 0:
                landed(stream, stage - 1, recv_sem)
                spot, mine = position(stream, stage - 1)
                kept, lanes = source(stream, stage - 1)
                came = held[stream * bits + stage - 1]
                if stage == bits:
                    outs[which][:, pl.ds(low, width)] = kept[mine, :, lanes].astype(
                        jnp.float32
                    ) + came[0].astype(jnp.float32)
                    continue

                def add_one(block, carry, spot=spot, mine=mine, kept=kept, lanes=lanes, came=came):
                    from_block = (block // 2**spot) * 2 ** (spot + 1) + mine * 2**spot
                    from_block = from_block + block % 2**spot
                    added = kept[from_block, :, lanes].astype(jnp.float32) + came[block].astype(
                        jnp.float32
                    )
                    came[block] = added.astype(came.dtype)
                    return carry

                lax.fori_loop(0, 2 ** (bits - stage), add_one, 0)
            spot, mine = position(stream, stage)
            sent, lanes = source(stream, stage)
            for high in range(2 ** (bits - stage - 1 - spot)):
                start = high * 2 ** (spot + 1) + (1 - mine) * 2**spot
                pltpu.make_async_remote_copy(
                    src_ref=sent.at[pl.ds(start, 2**spot), :, lanes],
                    dst_ref=held[stream * bits + stage].at[pl.ds(high * 2**spot, 2**spot)],
                    send_sem=send_sem.at[stream, stage],
                    recv_sem=recv_sem.at[stream, stage],
                    device_id=partner(order[stage], seq_bits),
                    device_id_type=MESH,
                ).start()
    for stage in range(bits):
        vector_copy(stage).wait_send()
        for stream in range(len(streams)):
            landed(stream, stage, send_sem)


def sum_to_owners(terms, vector, collective_id):
    seq_bits, dp_bits = bits_of(lax.axis_size("seq")), bits_of(lax.axis_size("dp"))
    bits = seq_bits + dp_bits
    orders = [order[::-1] for order in gather_orders(seq_bits, dp_bits)]
    terms = [term.reshape(2**bits, -1, term.shape[1]) for term in terms]
    streams = [
        (which, low, width, order)
        for which, term in enumerate(terms)
        for (low, width), order in zip(split_lanes(term.shape[2], SHARES), orders)
    ]
    rows = terms[0].shape[1]
    in_vmem = pl.BlockSpec(memory_space=pltpu.VMEM)
    held = [
        pltpu.VMEM((2 ** (bits - 1 - stage), rows, width), jnp.bfloat16)
        for _, _, width, _ in streams
        for stage in range(bits)
    ]
    return pl.pallas_call(
        partial(sum_kernel, seq_bits, streams, bits, len(terms)),
        out_shape=[jax.ShapeDtypeStruct(a.shape[1:], jnp.float32) for a in terms]
        + [jax.ShapeDtypeStruct(vector.shape, vector.dtype)],
        in_specs=[in_vmem] * (len(terms) + 1),
        out_specs=[in_vmem] * (len(terms) + 1),
        scratch_shapes=held
        + [
            pltpu.VMEM((bits, *vector.shape), jnp.float32),
            pltpu.VMEM((bits, *vector.shape), jnp.float32),
            pltpu.SemaphoreType.DMA((len(streams), bits)),
            pltpu.SemaphoreType.DMA((len(streams), bits)),
            pltpu.SemaphoreType.DMA((bits,)),
            pltpu.SemaphoreType.DMA((bits,)),
        ],
        compiler_params=pltpu.CompilerParams(
            collective_id=collective_id, has_side_effects=True, vmem_limit_bytes=VMEM_BYTES
        ),
        name="sum_rows",
    )(*terms, vector)


GROUP = 4
GROUP_LANES = GROUP * HEAD_DIM


def inner_product(left, right, dims):
    return lax.dot_general(
        left, right, (dims, ((), ())), precision=HIGH, preferred_element_type=jnp.float32
    )


def group_lanes(group):
    return pl.ds(pl.multiple_of(group * GROUP_LANES, GROUP_LANES), GROUP_LANES)


def head_weights(cumulative, head):
    row = cumulative[pl.ds(head, 1), :]
    count = row.shape[1]
    spread = jnp.broadcast_to(row, (count, count))
    later = lax.broadcasted_iota(jnp.int32, (count, count), 0)
    earlier = lax.broadcasted_iota(jnp.int32, (count, count), 1)
    return jnp.exp(jnp.where(later >= earlier, spread.T - spread, -jnp.inf))


def inside_work(first, last, scaled_x, b_mat, c_mat, cumulative, output, crossed):
    if first == 0:
        crossed[...] = inner_product(c_mat[...], b_mat[...], ((1,), (1,)))

    def one(group, carry):
        values = scaled_x[:, group_lanes(group)]
        parts = []
        for i in range(GROUP):
            scores = head_weights(cumulative, group * GROUP + i) * crossed[...]
            head = values[:, i * HEAD_DIM : (i + 1) * HEAD_DIM]
            parts.append(inner_product(scores, head, ((1,), (0,))))
        output[:, group_lanes(group)] = jnp.concatenate(parts, axis=1)
        return carry

    lax.fori_loop(first, last, one, 0)


def inside_back(
    first,
    last,
    output_cot,
    scaled_x,
    b_mat,
    c_mat,
    cumulative,
    scaled_cot,
    b_cot,
    c_cot,
    cumulative_cot,
    crossed,
    crossed_cot,
):
    if first == 0:
        crossed[...] = inner_product(c_mat[...], b_mat[...], ((1,), (1,)))
        crossed_cot[...] = jnp.zeros_like(crossed_cot)

    def one(group, carry):
        values = scaled_x[:, group_lanes(group)]
        cots = output_cot[:, group_lanes(group)]
        parts = []
        total = crossed_cot[...]
        for i in range(GROUP):
            weights = head_weights(cumulative, group * GROUP + i)
            scores = weights * crossed[...]
            head = values[:, i * HEAD_DIM : (i + 1) * HEAD_DIM]
            cot = cots[:, i * HEAD_DIM : (i + 1) * HEAD_DIM]
            weighted = weights * inner_product(cot, head, ((1,), (1,)))
            total = total + weighted
            parts.append(inner_product(scores, cot, ((0,), (0,))))
            moved = weighted * crossed[...]
            cumulative_cot[pl.ds(group * GROUP + i, 1), :] = jnp.sum(
                moved.T, axis=0, keepdims=True
            ) - jnp.sum(moved, axis=0, keepdims=True)
        crossed_cot[...] = total
        scaled_cot[:, group_lanes(group)] = jnp.concatenate(parts, axis=1)
        return carry

    lax.fori_loop(first, last, one, 0)
    if last == HEADS // GROUP:
        b_cot[...] = inner_product(crossed_cot[...], c_mat[...], ((0,), (0,)))
        c_cot[...] = inner_product(crossed_cot[...], b_mat[...], ((1,), (0,)))


def scan_kernel(count, reverse, work, inputs, outputs, *refs):
    state, decay = refs[:2]
    given = refs[2 : 2 + inputs]
    out = refs[2 + inputs]
    made = refs[3 + inputs : 3 + inputs + outputs]
    came, came_decay, ready = refs[3 + inputs + outputs : 6 + inputs + outputs]
    sems = refs[6 + inputs + outputs : 12 + inputs + outputs]
    held = refs[12 + inputs + outputs :]
    out_send, out_recv, decay_send, decay_recv, back_send, back_recv = sems
    dp_at, seq_at = places()
    barrier = pltpu.get_barrier_semaphore()
    peers = [(seq_at + hop) % count for hop in range(1, count)]
    for peer in peers:
        pl.semaphore_signal(barrier, inc=1, device_id=(dp_at, peer), device_id_type=MESH)
    pl.semaphore_wait(barrier, count - 1)

    def copy(hop, which):
        target = (seq_at + hop) % count
        source, landing, send_sem, recv_sem = (
            (state.at[target], came.at[seq_at], out_send, out_recv),
            (decay, came_decay.at[seq_at], decay_send, decay_recv),
            (ready.at[target], out.at[seq_at], back_send, back_recv),
        )[which]
        return pltpu.make_async_remote_copy(
            src_ref=source,
            dst_ref=landing,
            send_sem=send_sem.at[hop],
            recv_sem=recv_sem.at[hop],
            device_id=(dp_at, target),
            device_id_type=MESH,
        )

    for hop in range(1, count):
        copy(hop, 0).start()
        copy(hop, 1).start()
    came[seq_at] = state[seq_at]
    came_decay[seq_at] = decay[...]
    groups = HEADS // GROUP
    work(0, groups // 2, *given, *made, *held)
    for hop in range(1, count):
        copy(hop, 0).wait_recv()
        copy(hop, 1).wait_recv()
    total = jnp.zeros(state.shape[1:], jnp.float32)
    for place in range(count)[:: -1 if reverse else 1]:
        ready[place] = total.astype(ready.dtype)
        total = came_decay[place] * total + came[place].astype(jnp.float32)
    for hop in range(1, count):
        copy(hop, 2).start()
    out[seq_at] = ready[seq_at]
    work(groups // 2, groups, *given, *made, *held)
    for hop in range(1, count):
        copy(hop, 2).wait_recv()
    for hop in range(1, count):
        for which in range(3):
            copy(hop, which).wait_send()


def scan_states(state, decay, work, given, made, held, reverse, collective_id):
    count = lax.axis_size("seq")
    state = state.astype(jnp.bfloat16).reshape(count, STATE // count, DI)
    in_vmem = pl.BlockSpec(memory_space=pltpu.VMEM)
    got = pl.pallas_call(
        partial(scan_kernel, count, reverse, work, len(given), len(made)),
        out_shape=[jax.ShapeDtypeStruct(state.shape, state.dtype)]
        + [jax.ShapeDtypeStruct(shape, jnp.float32) for shape in made],
        in_specs=[in_vmem] * (2 + len(given)),
        out_specs=[in_vmem] * (1 + len(made)),
        scratch_shapes=[
            pltpu.VMEM(state.shape, state.dtype),
            pltpu.VMEM((count, 1, DI), jnp.float32),
            pltpu.VMEM(state.shape, state.dtype),
        ]
        + [pltpu.SemaphoreType.DMA((count,))] * 6
        + [pltpu.VMEM(shape, jnp.float32) for shape in held],
        compiler_params=pltpu.CompilerParams(
            collective_id=collective_id, has_side_effects=True, vmem_limit_bytes=VMEM_BYTES
        ),
        name="scan_back" if reverse else "scan_states",
    )(state, decay[None, :], *given)
    return got[0].reshape(STATE, DI).astype(jnp.float32), *got[1:]


def passed_along(value, axis, steps):
    count = lax.axis_size(axis)
    first, last = (max(0, -steps), min(count, count - steps))
    return lax.ppermute(value, axis, [(source, source + steps) for source in range(first, last)])


def pre_norm(residual_in, norm_gain):
    scale_rms = lax.rsqrt(jnp.mean(residual_in * residual_in, axis=-1, keepdims=True) + EPS)
    return residual_in * scale_rms * norm_gain


def conv_silu(padded, conv_weight, conv_bias, row_count):
    total = jnp.zeros((row_count, padded.shape[1]), jnp.float32) + conv_bias[None, :]
    for offset in range(conv_weight.shape[1]):
        total = total + conv_weight[:, offset][None, :] * padded[offset : offset + row_count]
    return jax.nn.silu(total)


def head_lanes():
    lanes = jnp.arange(DI, dtype=jnp.int32) // HEAD_DIM
    return (jnp.arange(HEADS, dtype=jnp.int32)[:, None] == lanes[None, :]).astype(jnp.float32)


def spread_heads(by_head):
    return jnp.dot(by_head, head_lanes(), precision=HIGH)


def sum_heads(by_lane):
    return jnp.dot(by_lane, head_lanes().T, precision=HIGH)


def before_states(xbc, dt_raw, edge, conv_weight, conv_bias, dt_bias, a_log):
    row_count = xbc.shape[0]
    activated = conv_silu(jnp.concatenate([edge, xbc], axis=0), conv_weight, conv_bias, row_count)
    xs = activated[:, :DI]
    b_mat = activated[:, DI : DI + STATE]
    c_mat = activated[:, DI + STATE :]
    step = jax.nn.softplus(dt_raw + dt_bias)
    log_decay = step * -jnp.exp(a_log)
    at = jnp.arange(row_count)
    lower = (at[:, None] >= at[None, :]).astype(jnp.float32)
    cumulative = jnp.dot(lower, log_decay, precision=HIGH)
    scaled_x = xs * spread_heads(step)
    tail = jnp.exp(cumulative[-1][None, :] - cumulative)
    fresh = jnp.dot(b_mat.T, scaled_x * spread_heads(tail), precision=HIGH)
    return (xs, scaled_x, b_mat, c_mat, cumulative, fresh)


def post_gate(ssd_out, xs, gate_part, skip_gain, gated_gain):
    skipped = xs * spread_heads(skip_gain[None, :])
    mixed_in = (ssd_out + skipped) * jax.nn.silu(gate_part)
    scale_rms = lax.rsqrt(jnp.mean(mixed_in * mixed_in, axis=-1, keepdims=True) + EPS)
    return mixed_in * scale_rms * gated_gain


def contract_rows(left, right):
    return lax.dot_general(
        left, right, (((0,), (0,)), ((), ())), preferred_element_type=jnp.float32
    )


def contract_cols(left, right):
    return lax.dot_general(
        left, right, (((1,), (1,)), ((), ())), preferred_element_type=jnp.float32
    )


def body(
    inputs,
    norm_gain,
    in_proj,
    conv_weight,
    conv_bias,
    dt_bias,
    a_log,
    skip_gain,
    gated_gain,
    out_proj,
    cotangent,
):
    row_count = inputs.shape[0]
    residual_in = inputs.astype(jnp.float32)
    normed_full, norm_back = jax.vjp(pre_norm, residual_in, norm_gain)
    normed = normed_full.astype(jnp.bfloat16)
    in_whole, out_whole = gather_all(
        [jnp.pad(in_proj, ((0, 0), (0, WIDE - PROJ))), out_proj], collective_id=1
    )
    in_whole = in_whole.reshape(-1, WIDE)
    out_whole = out_whole.reshape(-1, DI)
    projected = jnp.dot(normed, in_whole, preferred_element_type=jnp.float32)
    gate_part = projected[:, :DI]
    xbc = projected[:, DI : DI + XBC]
    dt_raw = projected[:, DI + XBC : PROJ]
    edge = passed_along(xbc[row_count - (CONV - 1) :], "seq", 1)
    primal, mid_back = jax.vjp(
        before_states, xbc, dt_raw, edge, conv_weight, conv_bias, dt_bias, a_log
    )
    xs, scaled_x, b_mat, c_mat, cumulative, s_local = primal
    by_head = cumulative.T
    decay = jnp.exp(cumulative[-1])
    wide_decay = spread_heads(decay[None, :])[0]
    square = (row_count, row_count)
    state_in, local_out = scan_states(
        s_local,
        wide_decay,
        inside_work,
        [scaled_x, b_mat, c_mat, by_head],
        [xs.shape],
        [square],
        False,
        collective_id=2,
    )
    weighted = spread_heads(jnp.exp(cumulative))
    carried_part = jnp.dot(c_mat, state_in, precision=HIGH) * weighted
    ssd_out = local_out + carried_part
    gated_full, post_back = jax.vjp(post_gate, ssd_out, xs, gate_part, skip_gain, gated_gain)
    gated = gated_full.astype(jnp.bfloat16)
    mixed = contract_cols(gated, out_whole)
    layer_out = (residual_in + mixed).astype(jnp.bfloat16)
    gated_cot = jnp.dot(cotangent, out_whole, preferred_element_type=jnp.float32)
    ssd_cot, xs_cot, gate_cot, skip_grad, gated_gain_grad = post_back(gated_cot)
    scaled_cot = ssd_cot * weighted
    local_grad = jnp.dot(c_mat.T, scaled_cot, precision=HIGH)
    later_grad, scaled_x_cot, b_cot, inner_c_cot, by_head_cot = scan_states(
        local_grad,
        wide_decay,
        inside_back,
        [ssd_cot, scaled_x, b_mat, c_mat, by_head],
        [xs.shape, b_mat.shape, c_mat.shape, by_head.shape],
        [square, square],
        True,
        collective_id=3,
    )
    c_cot = lax.dot_general(scaled_cot, state_in, (((1,), (1,)), ((), ())), precision=HIGH)
    cum_cot = sum_heads(ssd_cot * carried_part)
    last_cot = sum_heads(jnp.sum(later_grad * state_in, axis=0, keepdims=True))[0] * decay
    is_last = (jnp.arange(row_count) == row_count - 1)[:, None]
    cum_cot = cum_cot + jnp.where(is_last, last_cot[None, :], 0.0)
    mid_grads = mid_back(
        (xs_cot, scaled_x_cot, b_cot, c_cot + inner_c_cot, cum_cot + by_head_cot.T, later_grad)
    )
    xbc_cot, dt_cot, edge_cot, conv_weight_grad, conv_bias_grad, dt_bias_grad, a_log_grad = (
        mid_grads
    )
    edge_back = passed_along(edge_cot, "seq", -1)
    xbc_cot = xbc_cot + jnp.pad(edge_back, ((row_count - (CONV - 1), 0), (0, 0)))
    projected_cot = jnp.concatenate(
        [gate_cot, xbc_cot, dt_cot, jnp.zeros((row_count, WIDE - PROJ), jnp.float32)], axis=1
    ).astype(jnp.bfloat16)
    in_term = contract_rows(normed, projected_cot).astype(jnp.bfloat16)
    out_term = contract_rows(cotangent, gated).astype(jnp.bfloat16)
    normed_cot = contract_cols(projected_cot, in_whole)
    input_part, norm_gain_grad = norm_back(normed_cot)
    input_grad = cotangent.astype(jnp.float32) + input_part
    small = (
        norm_gain_grad,
        conv_weight_grad.T,
        conv_bias_grad,
        gated_gain_grad,
        dt_bias_grad,
        a_log_grad,
        skip_grad,
    )
    flat = jnp.concatenate([a.reshape(-1) for a in small])
    tile = 8 * LANES
    flat = jnp.pad(flat, (0, -flat.shape[0] % tile))
    in_proj_grad, out_proj_grad, summed = sum_to_owners(
        [in_term, out_term], flat.reshape(-1, LANES), collective_id=4
    )
    summed = summed.reshape(-1)
    parts, at = [], 0
    for a in small:
        parts.append(summed[at : at + a.size].reshape(a.shape))
        at += a.size
    return (
        layer_out,
        input_grad,
        in_proj_grad[:, :PROJ],
        out_proj_grad,
        parts[0],
        parts[1].T,
        parts[2],
        parts[4],
        parts[5],
        parts[6],
        parts[3],
    )


QUAD = 4
CHUNK = 128
TAIL = 16
QCH = DI // QUAD
QHEADS = HEADS // QUAD
PAIRS = QCH // LANES
BC = 2 * STATE
QXBC = QCH + BC
SLAB = QXBC + LANES
PARTS = 3
PART = SLAB // PARTS
GRAD_ROWS = 8
SEMS = 94


def flip(value, bit):
    return value + (1 - 2 * bit_at(value, bit)) * 2**bit


def flip_quad(value, mask):
    for bit in range(2):
        if mask >> bit & 1:
            value = flip(value, bit)
    return value


def dot_nn(left, right):
    return lax.dot_general(
        left, right, (((1,), (0,)), ((), ())), preferred_element_type=jnp.float32
    )


def dot_nt(left, right):
    return lax.dot_general(
        left, right, (((1,), (1,)), ((), ())), preferred_element_type=jnp.float32
    )


def dot_tn(left, right):
    return lax.dot_general(
        left, right, (((0,), (0,)), ((), ())), preferred_element_type=jnp.float32
    )


def in_parts(value, count):
    parts = []
    for _ in range(count):
        part = value.astype(jnp.bfloat16)
        parts.append(part)
        value = value - part.astype(jnp.float32)
    return parts


def lane_tile(i):
    return pl.ds(i * LANES, LANES)


def chunk_rows(c, offset=0, count=CHUNK):
    return pl.ds(pl.multiple_of(c * CHUNK + offset, 8), count)


def column_sum(value):
    return jnp.sum(value, axis=0, keepdims=True)


def block_kernel(
    x_hbm,
    gain_hbm,
    in_hbm,
    taps_hbm,
    bias_hbm,
    dt_bias_hbm,
    a_log_hbm,
    skip_hbm,
    gated_gain_hbm,
    proj_hbm,
    cot_hbm,
    out_to,
    grad_to,
    in_grad_to,
    proj_grad_to,
    gain_grad_to,
    taps_grad_to,
    bias_grad_to,
    dt_bias_grad_to,
    a_log_grad_to,
    skip_grad_to,
    gated_gain_grad_to,
    out_ref,
    grad_ref,
    in_grad_ref,
    proj_grad_ref,
    gain_grad_ref,
    taps_grad_ref,
    bias_grad_ref,
    dt_bias_grad_ref,
    a_log_grad_ref,
    skip_grad_ref,
    gated_gain_grad_ref,
    store_sem,
    x_ref,
    gain_ref,
    in_ref,
    taps_ref,
    bias_ref,
    dt_bias_ref,
    a_log_ref,
    skip_ref,
    gated_gain_ref,
    proj_ref,
    cot_ref,
    load_sem,
    early_ref,
    late_ref,
    xq,
    cq,
    xtail,
    early_slots,
    late_slots,
    early_w,
    late_w,
    xn,
    proj,
    act,
    act_slope,
    step_s,
    step_slope,
    log_s,
    cum_s,
    sx_s,
    fresh_s,
    state_out,
    state_come,
    state_s,
    weights_s,
    scores_s,
    ssd_s,
    gate_s,
    gc_s,
    m_s,
    sums_s,
    gated_s,
    gate_cot_s,
    y_s,
    z_s,
    back_s,
    later_s,
    cross_s,
    sx_cot_s,
    pre_cot_s,
    early_cot_s,
    late_term,
    early_term,
    mixed_s,
    mixed_come,
    normed_t,
    cot_t,
    early_wt,
    late_wt,
    normed_cot_s,
    normed_out,
    normed_come,
    tail_out,
    tail_come,
    small_s,
    skip_s,
    small_come,
    small_quad,
    *rest,
):
    stream_held = [rest[4 * i : 4 * i + 4] for i in range(1 + PARTS)]
    send_sem, recv_sem = rest[4 + 4 * PARTS :]
    f32, bf16 = jnp.float32, jnp.bfloat16
    dp_at, seq_at = places()
    q, g = seq_at % QUAD, seq_at // QUAD
    core, y_at = dp_at % 2, dp_at // 2
    place = dp_at * 8 + seq_at
    used = [0]
    sent = []

    loads = [
        pltpu.make_async_copy(source, landing, load_sem.at[i])
        for i, (source, landing) in enumerate(
            [
                (in_hbm, in_ref),
                (proj_hbm, proj_ref),
                (x_hbm, x_ref),
                (gain_hbm, gain_ref),
                (taps_hbm, taps_ref),
                (bias_hbm, bias_ref),
                (dt_bias_hbm, dt_bias_ref),
                (a_log_hbm, a_log_ref),
                (skip_hbm, skip_ref),
                (gated_gain_hbm, gated_gain_ref),
                (cot_hbm, cot_ref),
            ]
        )
    ]
    for load in loads:
        load.start()

    barrier = pltpu.get_barrier_semaphore()
    peers = [(dp_at, (seq_at + hop) % 8) for hop in range(1, 8)]
    peers += [(flip(dp_at, 0), seq_at), (flip(dp_at, 1), seq_at)]
    peers += [(flip(dp_at, 1), flip(seq_at, 2))]
    for peer in peers:
        pl.semaphore_signal(barrier, inc=1, device_id=peer, device_id_type=MESH)

    def remote(source, landing, target, own=True):
        at = used[0]
        used[0] += 1
        copy = pltpu.make_async_remote_copy(
            src_ref=source,
            dst_ref=landing,
            send_sem=send_sem.at[at],
            recv_sem=recv_sem.at[at],
            device_id=target,
            device_id_type=MESH,
        )
        if own:
            copy.start()
            sent.append(copy)
        return copy

    half_lanes = [pl.ds(h * SLAB // 2, SLAB // 2) for h in range(2)]

    def share_block(own_block, slots):
        over_z = [
            remote(own_block.at[:, lanes], slots.at[q, :, lanes], in_quad(2))
            for lanes in half_lanes
        ]
        return over_z, remote(own_block, slots.at[q], in_quad(1))

    def pass_block(slots, over_z):
        made = []
        for copy, lanes in zip(over_z, half_lanes):
            copy.wait_recv()
            view = slots.at[flip_quad(q, 2), :, lanes]
            made.append(remote(view, view, in_quad(1)))
        return made

    def send_sums(blocks, landing):
        over_x = [
            remote(blocks.at[flip_quad(q, 3), :, lanes], landing.at[0, :, lanes], in_quad(1))
            for lanes in half_lanes
        ]
        return over_x, remote(blocks.at[flip_quad(q, 1)], landing.at[1], in_quad(1))

    def pass_sums(mine, blocks, landing, over_x):
        made = []
        other = flip_quad(q, 2)
        for copy, lanes in zip(over_x, half_lanes):
            copy.wait_recv()
            blocks[other, :, lanes] = (
                mine[other, :, lanes].astype(f32) + landing[0, :, lanes].astype(f32)
            ).astype(bf16)
            made.append(
                remote(blocks.at[other, :, lanes], landing.at[2, :, lanes], in_quad(2))
            )
        return made

    def in_quad(mask):
        return dp_at, flip_quad(seq_at, mask)

    far = (dp_at, flip(seq_at, 2))
    beside = (flip(dp_at, 1), seq_at)
    twin = (flip(dp_at, 0), seq_at)

    def arrived(copies):
        for copy in copies:
            copy.wait_recv()

    lane = lax.broadcasted_iota(jnp.int32, (1, LANES), 1)
    first_half = lane < HEAD_DIM
    half0 = jnp.where(first_half, 1.0, 0.0)
    half1 = 1.0 - half0
    half0b, half1b = half0.astype(bf16), half1.astype(bf16)
    row_at = lax.broadcasted_iota(jnp.int32, (CHUNK, CHUNK), 0)
    lane_at = lax.broadcasted_iota(jnp.int32, (CHUNK, CHUNK), 1)
    causal = row_at >= lane_at
    lower = jnp.where(causal, 1.0, 0.0).astype(bf16)
    upper = jnp.where(row_at <= lane_at, 1.0, 0.0).astype(bf16)
    lower3 = jnp.concatenate([lower] * 3, axis=1)
    upper3 = jnp.concatenate([upper] * 3, axis=1)

    def spread(by_head, i):
        return jnp.where(first_half, by_head[:, 2 * i : 2 * i + 1], by_head[:, 2 * i + 1 : 2 * i + 2])

    head_picks = []
    for i in range(PAIRS):
        pick = jnp.where(2 * i + row_at // HEAD_DIM == lane_at, 1.0, 0.0).astype(bf16)
        head_picks.append(jnp.concatenate([pick] * 2, axis=0))

    def head_sum(value, i):
        return dot_nn(jnp.concatenate(in_parts(value, 2), axis=1), head_picks[i])

    def flat_row(ref, low, count):
        return ref[pl.ds(low, count)].reshape(1, count)

    def own_channels(i):
        return pl.ds(pl.multiple_of(q * QCH + i * LANES, LANES), LANES)

    def conv_channels(i):
        return own_channels(i) if i < PAIRS else pl.ds(DI + (i - PAIRS) * LANES, LANES)

    def tap(k, i):
        return taps_ref[pl.ds(k, 1), conv_channels(i)]

    def gated_gain(i):
        return gated_gain_ref[own_channels(i)].reshape(1, LANES)

    stores = []

    def store(source, landing):
        copy = pltpu.make_async_copy(source, landing, store_sem.at[len(stores)])
        copy.start()
        stores.append(copy)

    def own_heads(ref):
        head_at = lax.broadcasted_iota(jnp.int32, (HEADS, LANES), 0)
        to = lax.broadcasted_iota(jnp.int32, (HEADS, LANES), 1)
        pick = jnp.where((head_at == to + q * QHEADS) & (to < QHEADS), 1.0, 0.0)
        value = jnp.broadcast_to(ref[...].reshape(1, HEADS), (8, HEADS))
        return inner_product(value, pick, ((1,), (0,)))[:1]

    def stacked(value):
        return jnp.concatenate([value * half0b, value * half1b], axis=0)

    loads[0].wait()
    loads[1].wait()
    for j in range(QUAD):
        own = pl.ds(j * QCH, QCH)
        early_ref[j, :, pl.ds(0, QCH)] = in_ref[:, pl.ds(DI + j * QCH, QCH)]
        early_ref[j, :, pl.ds(QCH, BC)] = in_ref[:, pl.ds(2 * DI, BC)]
        head_at = lax.broadcasted_iota(jnp.int32, (HEADS, LANES), 0)
        to = lax.broadcasted_iota(jnp.int32, (HEADS, LANES), 1)
        pick = jnp.where((head_at == to + j * QHEADS) & (to < QHEADS), 1.0, 0.0)
        early_ref[j, :, pl.ds(QXBC, LANES)] = dot_nn(
            in_ref[:, pl.ds(DI + XBC, HEADS)], pick.astype(bf16)
        ).astype(bf16)
        late_ref[j, :, pl.ds(0, QCH)] = in_ref[:, own]
        late_ref[j, :, pl.ds(QCH, QCH)] = proj_ref[:, own]

    for load in loads[2:]:
        load.wait()
    pl.semaphore_wait(barrier, len(peers))

    def scatter(shard, slots):
        return [
            remote(shard.at[flip_quad(q, mask)], slots.at[place], in_quad(mask))
            for mask in (1, 2, 3)
        ]

    early_0 = scatter(early_ref, early_slots)
    late_0 = scatter(late_ref, late_slots)
    token_z, token_x = share_block(x_ref, xq)
    tail_sends = [
        remote(x_ref.at[pl.ds(CHUNK - TAIL, TAIL)], xtail, (dp_at, QUAD + i), own=False)
        for i in range(QUAD)
    ]
    at_end = seq_at == QUAD - 1

    @pl.when(at_end)
    def _():
        for copy in tail_sends:
            copy.start()

    early_slots[place] = early_ref[q]
    late_slots[place] = late_ref[q]
    xq[q] = x_ref[...]
    cq[q] = cot_ref[...]

    def cross_far(slots, parts):
        wide = SLAB // parts
        return [
            remote(
                slots.at[pl.ds(dp_at * 8 + g * 4, 4), :, lane_part],
                slots.at[pl.ds(dp_at * 8 + g * 4, 4), :, lane_part],
                far,
            )
            for lane_part in [pl.ds(part * wide, wide) for part in range(parts)]
        ]

    def cross_beside(slots, copies):
        made = []
        for part, copy in enumerate(copies):
            copy.wait_recv()
            wide = SLAB // len(copies)
            view = slots.at[pl.ds(dp_at * 8, 8), :, pl.ds(part * wide, wide)]
            made.append(remote(view, view, beside))
        return made

    def cross_twin(slots, copies):
        made = []
        for part, copy in enumerate(copies):
            copy.wait_recv()
            for up in range(2):
                wide = SLAB // len(copies)
                view = slots.at[pl.ds((2 * up + core) * 8, 8), :, pl.ds(part * wide, wide)]
                made.append(remote(view, view, twin))
        return made

    def flatten(slots, flat, low=0, wide=SLAB):
        lanes = pl.ds(low, wide)

        def one(pair, carry):
            value = slots[pl.ds(2 * pair, 2), :, lanes].astype(f32).reshape(48, wide)
            flat[pl.ds(pl.multiple_of(pair * 48, 16), 48), lanes] = value.astype(bf16)
            return carry

        lax.fori_loop(0, 16, one, 0)

    arrived(early_0)
    early_1 = cross_far(early_slots, PARTS)
    token_pass = pass_block(xq, token_z)
    early_2 = cross_beside(early_slots, early_1)
    arrived(late_0)
    late_1 = cross_far(late_slots, 2)
    cot_z, cot_x = share_block(cot_ref, cq)

    arrived([token_x, *token_pass])

    for i in range(QUAD):

        @pl.when((g == 1) & (q == i))
        def _():
            tail_sends[i].wait_recv()

    @pl.when(g == 0)
    def _():
        xtail[...] = jnp.zeros_like(xtail)

    gain = flat_row(gain_ref, 0, x_ref.shape[1])

    def scaled_rows(value):
        value = value.astype(f32)
        return value * lax.rsqrt(jnp.mean(value * value, axis=-1, keepdims=True) + EPS)

    tail_rows = scaled_rows(xtail[...]) * gain
    xn[pl.ds(0, TAIL), :] = tail_rows.astype(bf16)
    normed_t[:, pl.ds(QUAD * CHUNK, LANES)] = jnp.concatenate(
        [tail_rows, jnp.zeros((LANES - TAIL, tail_rows.shape[1]), f32)], axis=0
    ).T.astype(bf16)
    early_cot_s[pl.ds(QUAD * CHUNK, LANES), :] = jnp.zeros((LANES, SLAB), bf16)

    def norm_block(c, carry):
        value = scaled_rows(xq[c]) * gain
        xn[pl.ds(pl.multiple_of(c * CHUNK + TAIL, 16), CHUNK), :] = value.astype(bf16)
        normed_t[:, pl.ds(pl.multiple_of(c * CHUNK, CHUNK), CHUNK)] = value.T.astype(bf16)
        return carry

    lax.fori_loop(0, QUAD, norm_block, 0)
    early_3 = cross_twin(early_slots, early_2)
    cot_pass = pass_block(cq, cot_z)
    late_2 = cross_beside(late_slots, late_1)
    small_s[...] = jnp.zeros_like(small_s)
    skip_s[...] = jnp.zeros_like(skip_s)
    pre_cot_s[pl.ds(0, TAIL), :] = jnp.zeros((TAIL, QXBC), f32)
    pre_cot_s[pl.ds(TAIL + QUAD * CHUNK, 8), :] = jnp.zeros((8, QXBC), f32)
    for part in range(PARTS):
        cols = pl.ds(part * PART, PART)
        each = len(early_3) // PARTS
        arrived(early_3[part * each : (part + 1) * each])
        flatten(early_slots, early_w, part * PART, PART)
        proj[:, cols] = dot_nn(xn[...], early_w[:, cols])

        def forward_conv(c, carry, part=part):
            rows = chunk_rows(c)
            for i in range(part * PART // LANES, min((part + 1) * PART, QXBC) // LANES):
                lanes = lane_tile(i)
                window = proj[chunk_rows(c, 8, CHUNK + 8), lanes]
                total = bias_ref[conv_channels(i)].reshape(1, LANES)
                for k in range(CONV):
                    total = total + tap(k, i) * pltpu.roll(window, CHUNK + 3 - k, 0)[:CHUNK]
                sig = lax.logistic(total)
                act[rows, lanes] = total * sig
                act_slope[rows, lanes] = sig * (1.0 + total * (1.0 - sig))
            return carry

        lax.fori_loop(0, QUAD, forward_conv, 0)

    rate = -jnp.exp(own_heads(a_log_ref))
    dt_bias = own_heads(dt_bias_ref)
    skips = own_heads(skip_ref)
    skip_wide = [spread(skips, i) for i in range(PAIRS)]
    head_lane = lane < QHEADS

    def forward_states(c, carry):
        rows = chunk_rows(c)
        raw = proj[chunk_rows(c, TAIL), pl.ds(QXBC, LANES)] + dt_bias
        step = jnp.maximum(raw, 0.0) + jnp.log1p(jnp.exp(-jnp.abs(raw)))
        step = jnp.where(head_lane, step, 0.0)
        log_decay = step * rate
        cum = dot_nn(lower3, jnp.concatenate(in_parts(log_decay, 3), axis=0))
        step_s[rows, :] = step
        step_slope[rows, :] = lax.logistic(raw)
        log_s[rows, :] = log_decay
        cum_s[rows, :] = cum
        tail = jnp.exp(cum[CHUNK - 1 :] - cum)
        b_mat = act[rows, pl.ds(QCH, STATE)].astype(bf16)
        for i in range(PAIRS):
            lanes = lane_tile(i)
            sx = act[rows, lanes] * spread(step, i)
            sx_s[rows, lanes] = sx.astype(bf16)
            fresh_s[c, i] = dot_tn(b_mat, (sx * spread(tail, i)).astype(bf16))
        return carry

    lax.fori_loop(0, QUAD, forward_states, 0)

    def chunk_decay(c, i):
        last = cum_s[chunk_rows(c, CHUNK - 8, 8), :][7:]
        return spread(jnp.exp(last), i)

    for i in range(PAIRS):
        total = fresh_s[0, i]
        for c in range(1, QUAD):
            total = chunk_decay(c, i) * total + fresh_s[c, i]
        state_out[i] = total.astype(bf16)
    state_copy = remote(state_out, state_come, far)
    late_3 = cross_twin(late_slots, late_2)

    def forward_local(c, carry):
        rows = chunk_rows(c)
        b_mat = act[rows, pl.ds(QCH, STATE)].astype(bf16)
        c_mat = act[rows, pl.ds(QCH + STATE, STATE)].astype(bf16)
        crossed = dot_nt(c_mat, b_mat)
        cum = cum_s[rows, :]
        cum_t = cum.T
        for i in range(PAIRS):
            lanes = lane_tile(i)
            pair = []
            for head in (2 * i, 2 * i + 1):
                gap = cum[:, head : head + 1] - cum_t[head : head + 1, :]
                pair.append(jnp.exp(jnp.where(causal, gap, -1e30)))
            weights_s[c, i] = jnp.concatenate(pair, axis=1).astype(bf16)
            scores = jnp.concatenate([w * crossed for w in pair], axis=1).astype(bf16)
            scores_s[c, i] = scores
            ssd_s[rows, lanes] = dot_nn(scores, stacked(sx_s[rows, lanes]))
        return carry

    lax.fori_loop(0, QUAD, forward_local, 0)
    gate_w = pl.ds(0, QCH)
    out_w = pl.ds(QCH, QCH)
    def turn_early(c, carry):
        own = pl.ds(pl.multiple_of(c * CHUNK, CHUNK), CHUNK)
        early_wt[:, own] = early_w[own, :].astype(f32).T.astype(bf16)
        return carry

    lax.fori_loop(0, x_ref.shape[1] // CHUNK, turn_early, 0)
    arrived(late_3[:2])
    flatten(late_slots, late_w, 0, QCH)
    gate_s[...] = dot_nn(xn[pl.ds(TAIL, QUAD * CHUNK), :], late_w[:, gate_w])
    arrived(late_3[2:])
    flatten(late_slots, late_w, QCH, QCH)
    arrived([cot_x, *cot_pass])

    def cot_block(c, carry):
        gc_s[chunk_rows(c), :] = dot_nn(cq[c], late_w[:, out_w])
        return carry

    lax.fori_loop(0, QUAD, cot_block, 0)
    state_copy.wait_recv()
    for i in range(PAIRS):
        total = jnp.where(g == 1, state_come[i].astype(f32), 0.0)
        for c in range(QUAD):
            state_s[c, i] = total.astype(bf16)
            if c < QUAD - 1:
                total = chunk_decay(c, i) * total + fresh_s[c, i]

    def forward_gate(c, carry):
        rows = chunk_rows(c)
        c_mat = act[rows, pl.ds(QCH + STATE, STATE)].astype(bf16)
        grown = jnp.exp(cum_s[rows, :])
        square, crossed = 0.0, 0.0
        for i in range(PAIRS):
            lanes = lane_tile(i)
            ssd = ssd_s[rows, lanes] + dot_nn(c_mat, state_s[c, i]) * spread(grown, i)
            ssd_s[rows, lanes] = ssd
            gate = gate_s[rows, lanes]
            m = (ssd + act[rows, lanes] * skip_wide[i]) * gate * lax.logistic(gate)
            m_s[rows, lanes] = m
            square = square + m * m
            crossed = crossed + gc_s[rows, lanes] * gated_gain(i) * m
        square = jnp.sum(square, axis=1, keepdims=True)
        crossed = jnp.sum(crossed, axis=1, keepdims=True)
        both = jnp.where(lane == 0, square, jnp.where(lane == 1, crossed, 0.0))
        sums_s[q, :, pl.ds(pl.multiple_of(c * CHUNK, CHUNK), CHUNK)] = (
            both.T[:8]
        )
        return carry

    lax.fori_loop(0, QUAD, forward_gate, 0)
    sums_copies = [remote(sums_s.at[q], sums_s.at[q], in_quad(mask)) for mask in (1, 2, 3)]

    def turn_cot(c, carry):
        cot_t[:, pl.ds(pl.multiple_of(c * CHUNK, CHUNK), CHUNK)] = (
            cq[c].astype(f32).T.astype(bf16)
        )
        return carry

    lax.fori_loop(0, QUAD, turn_cot, 0)

    def turn_weights(c, carry):
        own = pl.ds(pl.multiple_of(c * CHUNK, CHUNK), CHUNK)
        late_wt[:, own] = late_w[own, :].astype(f32).T.astype(bf16)
        return carry

    lax.fori_loop(0, x_ref.shape[1] // CHUNK, turn_weights, 0)
    arrived(sums_copies)

    def backward_states(c, carry):
        rows = chunk_rows(c)
        cols = pl.ds(pl.multiple_of(c * CHUNK, CHUNK), CHUNK)
        sums = sums_s[0, :, cols] + sums_s[1, :, cols] + sums_s[2, :, cols] + sums_s[3, :, cols]
        sums = jnp.concatenate([sums] * (CHUNK // 8), axis=0).T
        scale = lax.rsqrt(sums[:, 0:1] * (1.0 / DI) + EPS)
        pull = scale * scale * scale * (sums[:, 1:2] * (1.0 / DI))
        c_mat = act[rows, pl.ds(QCH + STATE, STATE)].astype(bf16)
        grown = jnp.exp(cum_s[rows, :])
        for i in range(PAIRS):
            lanes = lane_tile(i)
            m, gc, gate = m_s[rows, lanes], gc_s[rows, lanes], gate_s[rows, lanes]
            xs = act[rows, lanes]
            mr = m * scale
            gated_s[rows, lanes] = (mr * gated_gain(i)).astype(bf16)
            small_s[5:6, lanes] += column_sum(gc * mr)
            m_cot = scale * (gc * gated_gain(i)) - m * pull
            sig = lax.logistic(gate)
            mixed = ssd_s[rows, lanes] + xs * skip_wide[i]
            gate_cot_s[rows, lanes] = (
                m_cot * mixed * (sig * (1.0 + gate * (1.0 - sig)))
            ).astype(bf16)
            y = m_cot * gate * sig
            y_s[rows, lanes] = y
            skip_s[0:1, lanes] += column_sum(y * xs)
            z = (y * spread(grown, i)).astype(bf16)
            z_s[rows, lanes] = z
            back_s[c, i] = dot_tn(c_mat, z)
        return carry

    lax.fori_loop(0, QUAD, backward_states, 0)
    state_copy.wait_send()
    sent[:] = [copy for copy in sent if copy is not state_copy]
    for i in range(PAIRS):
        total = back_s[QUAD - 1, i]
        for c in range(QUAD - 2, -1, -1):
            total = chunk_decay(c, i) * total + back_s[c, i]
        state_out[i] = total.astype(bf16)
    later_copy = remote(state_out, later_s.at[QUAD], far)

    def term_rows(term, half, value, lanes):
        term[pl.ds(half * 16, 16), :, lanes] = value.reshape(16, 24, value.shape[1]).astype(bf16)

    def late_half(half, carry):
        own = pl.ds(pl.multiple_of(half * QCH, QCH), QCH)
        term_rows(late_term, half, dot_nn(normed_t[own, pl.ds(0, QUAD * CHUNK)], gate_cot_s[...]), gate_w)
        term_rows(late_term, half, dot_nn(cot_t[own, :], gated_s[...]), out_w)
        return carry

    lax.fori_loop(0, 2, late_half, 0)

    streams = [(late_term, pl.ds(0, SLAB))] + [
        (early_term, pl.ds(i * PART, PART)) for i in range(PARTS)
    ]

    def reduce_twin(stream):
        term, lanes = streams[stream]
        return [
            remote(
                term.at[pl.ds((2 * up + 1 - core) * 8, 8), :, lanes],
                stream_held[stream][0].at[pl.ds(8 * up, 8)],
                twin,
            )
            for up in range(2)
        ]

    def reduce_beside(stream, copies):
        arrived(copies)
        term, lanes = streams[stream]
        held = stream_held[stream][0]

        def add(four, carry):
            mine = pl.ds((2 * (four // 2) + core) * 8 + four % 2 * 4, 4)
            own = pl.ds(four * 4, 4)
            held[own] = (term[mine, :, lanes].astype(f32) + held[own].astype(f32)).astype(bf16)
            return carry

        lax.fori_loop(0, 4, add, 0)
        return [remote(held.at[pl.ds((1 - y_at) * 8, 8)], stream_held[stream][1], beside)]

    def reduce_far(stream, copies):
        arrived(copies)
        before, held = stream_held[stream][:2]

        def add(four, carry):
            own = pl.ds(four * 4, 4)
            held[own] = (
                before[pl.ds(y_at * 8 + four * 4, 4)].astype(f32) + held[own].astype(f32)
            ).astype(bf16)
            return carry

        lax.fori_loop(0, 2, add, 0)
        return [remote(held.at[pl.ds((1 - g) * 4, 4)], stream_held[stream][2], far)]

    def reduce_quad(stream, copies):
        arrived(copies)
        before, held, result = stream_held[stream][1:]

        held[...] = (before[pl.ds(g * 4, 4)].astype(f32) + held[...].astype(f32)).astype(bf16)
        made = [
            remote(held.at[flip_quad(q, mask)], result.at[q], in_quad(mask)) for mask in (1, 2, 3)
        ]
        result[q] = held[q]
        return made

    late_r0 = reduce_twin(0)

    for n in range(3):
        cols = pl.ds(n * 256, 256)
        value = dot_nn(gated_s[...], late_wt[out_w, cols]).astype(bf16)
        for c in range(QUAD):
            mixed_s[c, :, cols] = value[c * CHUNK : (c + 1) * CHUNK]

    mixed_x, mixed_own = send_sums(mixed_s, mixed_come)

    def backward_local(c, carry):
        rows = chunk_rows(c)
        total = jnp.zeros((CHUNK, CHUNK), f32)
        for i in range(PAIRS):
            lanes = lane_tile(i)
            y = y_s[rows, lanes].astype(bf16)
            moved = weights_s[c, i].astype(f32) * dot_nt(y, stacked(sx_s[rows, lanes]))
            total = total + moved[:, :CHUNK] + moved[:, CHUNK:]
            both = dot_tn(scores_s[c, i], y)
            sx_cot_s[rows, lanes] = both[:CHUNK] * half0 + both[CHUNK:] * half1
        cross_s[c] = total.astype(bf16)
        return carry

    lax.fori_loop(0, QUAD, backward_local, 0)
    late_r1 = reduce_beside(0, late_r0)
    mixed_z = pass_sums(mixed_s, mixed_s, mixed_come, mixed_x)
    later_copy.wait_recv()
    for i in range(PAIRS):
        total = jnp.where(g == 0, later_s[QUAD, i].astype(f32), 0.0)
        for c in range(QUAD - 1, -1, -1):
            later_s[c, i] = total.astype(bf16)
            if c > 0:
                total = chunk_decay(c, i) * total + back_s[c, i]

    def backward_mix(c, carry):
        rows = chunk_rows(c)
        shifted = chunk_rows(c, TAIL)
        b_mat = act[rows, pl.ds(QCH, STATE)].astype(bf16)
        c_mat = act[rows, pl.ds(QCH + STATE, STATE)].astype(bf16)
        cum, step = cum_s[rows, :], step_s[rows, :]
        tail = jnp.exp(cum[CHUNK - 1 :] - cum)
        decay = jnp.exp(cum[CHUNK - 1 :])
        cross = cross_s[c]
        b_cot = dot_tn(cross, c_mat)
        c_cot = dot_nn(cross, b_mat)
        by_head = jnp.zeros((2 * CHUNK + 8, LANES), f32)
        for i in range(PAIRS):
            lanes = lane_tile(i)
            xs, y = act[rows, lanes], y_s[rows, lanes]
            later, state = later_s[c, i], state_s[c, i]
            wide_step, wide_tail = spread(step, i), spread(tail, i)
            tailed = (xs * wide_step * wide_tail).astype(bf16)
            from_later = dot_nn(b_mat, later) * wide_tail
            b_cot = b_cot + dot_nt(tailed, later)
            c_cot = c_cot + dot_nt(z_s[rows, lanes], state)
            sx = sx_s[rows, lanes].astype(f32)
            sx_cot = sx_cot_s[rows, lanes] + from_later
            last = column_sum(sx * from_later) + column_sum(
                later.astype(f32) * state.astype(f32)
            ) * spread(decay, i)
            by_head = by_head + head_sum(
                jnp.concatenate(
                    [
                        y.astype(bf16).astype(f32) * ssd_s[rows, lanes] - sx * sx_cot,
                        sx_cot * xs,
                        jnp.broadcast_to(last, (8, LANES)),
                    ],
                    axis=0,
                ),
                i,
            )
            pre_cot_s[shifted, lanes] = (
                sx_cot * wide_step + y * skip_wide[i]
            ) * act_slope[rows, lanes]
        pre_cot_s[shifted, pl.ds(QCH, STATE)] = b_cot * act_slope[rows, pl.ds(QCH, STATE)]
        pre_cot_s[shifted, pl.ds(QCH + STATE, STATE)] = (
            c_cot * act_slope[rows, pl.ds(QCH + STATE, STATE)]
        )
        cum_cot, step_cot = by_head[:CHUNK], by_head[CHUNK : 2 * CHUNK]
        last_cot = by_head[2 * CHUNK : 2 * CHUNK + 1]
        log_cot = dot_nn(upper3, jnp.concatenate(in_parts(cum_cot, 3), axis=0)) + last_cot
        dt_cot = (step_cot + log_cot * rate) * step_slope[rows, :]
        small_s[7:8, lane_tile(1)] += column_sum(log_cot * log_s[rows, :])
        small_s[5:6, lane_tile(4)] += column_sum(dt_cot)
        early_cot_s[rows, pl.ds(QXBC, LANES)] = dt_cot.astype(bf16)
        return carry

    lax.fori_loop(0, QUAD, backward_mix, 0)
    late_r2 = reduce_far(0, late_r1)

    for i in range(QXBC // LANES):
        lanes = lane_tile(i)
        edge = pre_cot_s[pl.ds(0, 24), lanes]
        total = tap(CONV - 1, i) * edge[:TAIL]
        for k in range(CONV - 1):
            total = total + tap(k, i) * pltpu.roll(edge, 24 - (3 - k), 0)[:TAIL]
        early_cot_s[pl.ds(QUAD * CHUNK, TAIL), lanes] = total.astype(bf16)

    def backward_conv(c, carry):
        for i in range(QXBC // LANES):
            lanes = lane_tile(i)
            cots = pre_cot_s[chunk_rows(c, TAIL, CHUNK + 8), lanes]
            window = proj[chunk_rows(c, 8, CHUNK + 8), lanes]
            cot = cots[:CHUNK]
            total = tap(CONV - 1, i) * cot
            for k in range(CONV - 1):
                total = total + tap(k, i) * pltpu.roll(cots, CHUNK + 8 - (3 - k), 0)[:CHUNK]
            early_cot_s[chunk_rows(c), lanes] = total.astype(bf16)
            for k in range(CONV):
                small_s[k : k + 1, lanes] += column_sum(
                    cot * pltpu.roll(window, CHUNK + 3 - k, 0)[:CHUNK]
                )
            small_s[4:5, lanes] += column_sum(cot)
        return carry

    lax.fori_loop(0, QUAD, backward_conv, 0)

    heads = jnp.zeros((8, LANES), f32)
    for i in range(PAIRS):
        heads = heads + head_sum(jnp.broadcast_to(skip_s[0:1, lane_tile(i)], (8, LANES)), i)
    small_s[5:6, lane_tile(3)] = heads[:1]

    tail_value = dot_nn(early_cot_s[pl.ds(QUAD * CHUNK, TAIL), :], early_wt[...])
    tail_out[...] = tail_value
    tail_index = used[0]
    used[0] += QUAD

    def tail_copy(i):
        return pltpu.make_async_remote_copy(
            src_ref=tail_out,
            dst_ref=tail_come.at[i],
            send_sem=send_sem.at[tail_index + i],
            recv_sem=recv_sem.at[tail_index + i],
            device_id=(dp_at, QUAD - 1),
            device_id_type=MESH,
        )

    for i in range(QUAD):

        @pl.when((g == 1) & (q == i))
        def _():
            tail_copy(i).start()

    def add_gain(value, rows):
        total = column_sum(value * scaled_rows(rows))
        small_s[6:7, :] += total[:, :QXBC]
        small_s[7:8, lane_tile(0)] += total[:, QXBC:]

    add_gain(tail_value, xtail[...])

    for n in range(3):
        cols = pl.ds(n * 256, 256)
        value = dot_nn(early_cot_s[pl.ds(0, QUAD * CHUNK), :], early_wt[:, cols])
        value = value + dot_nn(gate_cot_s[...], late_wt[gate_w, cols])
        for c in range(QUAD):
            part = value[c * CHUNK : (c + 1) * CHUNK]
            normed_cot_s[c, :, cols] = part
            normed_out[c, :, cols] = part.astype(bf16)

    normed_x, normed_own = send_sums(normed_out, normed_come)
    for c in range(QUAD):
        add_gain(normed_cot_s[c], xq[c])
    small_copy = remote(small_s, small_come.at[0], twin)
    early_r0 = []
    for part in range(PARTS):
        lanes = pl.ds(part * PART, PART)

        def early_half(half, carry, lanes=lanes):
            own = pl.ds(pl.multiple_of(half * QCH, QCH), QCH)
            value = dot_nn(normed_t[own, :], early_cot_s[:, lanes])
            term_rows(early_term, half, value, lanes)
            return carry

        lax.fori_loop(0, 2, early_half, 0)
        early_r0.append(reduce_twin(1 + part))

    small_copy.wait_recv()
    small_come[4] = small_s[...] + small_come[0]
    across = (flip(dp_at, 1), flip(seq_at, 2))
    small_copies = [
        remote(small_come.at[4], small_come.at[1 + i], target)
        for i, target in enumerate((beside, far, across))
    ]
    early_r1 = [reduce_beside(1 + part, early_r0[part]) for part in range(PARTS)]
    normed_z = pass_sums(normed_cot_s, normed_out, normed_come, normed_x)

    early_r2 = [reduce_far(1, early_r1[0])]
    early_r2.append(reduce_far(2, early_r1[1]))
    late_r3 = reduce_quad(0, late_r2)
    early_r2.append(reduce_far(3, early_r1[2]))
    arrived(small_copies)
    small_quad[q] = small_come[4] + small_come[1] + (small_come[2] + small_come[3])
    small_copies = [remote(small_quad.at[q], small_quad.at[q], in_quad(mask)) for mask in (1, 2, 3)]

    arrived([mixed_own, *mixed_z])
    total = x_ref[...].astype(f32) + mixed_s[q].astype(f32)
    total = total + mixed_come[1].astype(f32) + mixed_come[2].astype(f32)
    out_ref[...] = total.astype(bf16)
    store(out_ref, out_to)
    early_r3 = [reduce_quad(1 + part, early_r2[part]) for part in range(PARTS)]

    arrived([normed_own, *normed_z])
    value = normed_cot_s[q] + normed_come[1].astype(f32) + normed_come[2].astype(f32)
    normed_cot_s[q] = value

    @pl.when(at_end)
    def _():
        for i in range(QUAD):
            tail_copy(i).wait_recv()
        rows = pl.ds(CHUNK - TAIL, TAIL)
        normed_cot_s[q, rows, :] += tail_come[0] + tail_come[1] + tail_come[2] + tail_come[3]

    cot = normed_cot_s[q] * gain
    rows = x_ref[...].astype(f32)
    scale = lax.rsqrt(jnp.mean(rows * rows, axis=-1, keepdims=True) + EPS)
    pull = scale * scale * scale * jnp.mean(cot * rows, axis=-1, keepdims=True)
    grad_ref[...] = cot_ref[...].astype(f32) + scale * cot - rows * pull
    store(grad_ref, grad_to)

    arrived(small_copies)
    for j in range(QUAD):
        own = pl.ds(j * QCH, QCH)
        taps_grad_ref[:, own] = small_quad[j, 0:CONV, pl.ds(0, QCH)]
        bias_grad_ref[own] = small_quad[j, CONV : CONV + 1, pl.ds(0, QCH)].reshape(QCH)
        gated_gain_grad_ref[own] = small_quad[j, 5:6, pl.ds(0, QCH)].reshape(QCH)
    quads = small_quad[0] + small_quad[1] + small_quad[2] + small_quad[3]
    taps_grad_ref[:, pl.ds(DI, BC)] = quads[:CONV, QCH:QXBC]
    bias_grad_ref[pl.ds(DI, BC)] = quads[CONV : CONV + 1, QCH:QXBC].reshape(BC)
    gain_grad_ref[pl.ds(0, QXBC)] = quads[6:7].reshape(QXBC)
    gain_grad_ref[pl.ds(QXBC, LANES)] = quads[7:8, :LANES].reshape(LANES)

    def in_head_order(parts):
        total = parts[0]
        for j in range(1, QUAD):
            total = total + pltpu.roll(parts[j], j * QHEADS, 1)
        return total[:, :HEADS]

    def small_heads(row, i):
        parts = [small_quad[j, :, lane_tile(i)] for j in range(QUAD)]
        return in_head_order(parts)[row : row + 1].reshape(HEADS)

    skip_grad_ref[...] = small_heads(5, 3)
    dt_bias_grad_ref[...] = small_heads(5, 4)
    a_log_grad_ref[...] = small_heads(7, 1)
    store(gain_grad_ref, gain_grad_to)
    store(taps_grad_ref, taps_grad_to)
    store(bias_grad_ref, bias_grad_to)
    store(dt_bias_grad_ref, dt_bias_grad_to)
    store(a_log_grad_ref, a_log_grad_to)
    store(skip_grad_ref, skip_grad_to)
    store(gated_gain_grad_ref, gated_gain_grad_to)

    arrived(late_r3)
    for j in range(QUAD):
        own = pl.ds(j * QCH, QCH)
        in_grad_ref[:, own] = stream_held[0][3][j, :, pl.ds(0, QCH)].astype(f32)
        proj_grad_ref[:, own] = stream_held[0][3][j, :, pl.ds(QCH, QCH)].astype(f32)
    store(proj_grad_ref, proj_grad_to)
    for part in range(PARTS):
        arrived(early_r3[part])

    def early_result(j, low):
        return stream_held[1 + low // PART][3][j, :, pl.ds(low % PART, LANES)].astype(f32)

    for j in range(QUAD):
        for i in range(PAIRS):
            in_grad_ref[:, pl.ds(DI + j * QCH + i * LANES, LANES)] = early_result(j, i * LANES)
    for i in range(BC // LANES):
        total = early_result(0, QCH + i * LANES)
        for j in range(1, QUAD):
            total = total + early_result(j, QCH + i * LANES)
        in_grad_ref[:, pl.ds(2 * DI + i * LANES, LANES)] = total
    in_grad_ref[:, pl.ds(DI + XBC, HEADS)] = in_head_order(
        [early_result(j, QXBC) for j in range(QUAD)]
    )

    store(in_grad_ref, in_grad_to)
    assert used[0] == SEMS
    for copy in sent:
        copy.wait_send()

    @pl.when(at_end)
    def _():
        for copy in tail_sends:
            copy.wait_send()

    for i in range(QUAD):

        @pl.when((g == 1) & (q == i))
        def _():
            tail_copy(i).wait_send()

    for copy in stores:
        copy.wait()


def quad_body(
    inputs,
    norm_gain,
    in_proj,
    conv_weight,
    conv_bias,
    dt_bias,
    a_log,
    skip_gain,
    gated_gain,
    out_proj,
    cotangent,
):
    f32, bf16 = jnp.float32, jnp.bfloat16
    rows = in_proj.shape[0]
    tokens = QUAD * CHUNK
    slots = lax.axis_size("dp") * lax.axis_size("seq")
    width = inputs.shape[1]
    vmem = pltpu.VMEM
    held = [
        vmem((count, rows, w), bf16) for w in (SLAB, *[PART] * PARTS) for count in (16, 8, 4, 4)
    ]
    shapes = [inputs.shape, inputs.shape, in_proj.shape, out_proj.shape]
    shapes += [(width,), (CONV, XBC), (XBC,), (HEADS,), (HEADS,), (HEADS,), (DI,)]
    operands = (
        inputs,
        norm_gain,
        in_proj,
        conv_weight.T,
        conv_bias,
        dt_bias,
        a_log,
        skip_gain,
        gated_gain,
        out_proj,
        cotangent,
    )
    scratch = [
        *(vmem(shape, f32 if at else bf16) for at, shape in enumerate(shapes)),
        pltpu.SemaphoreType.DMA((len(shapes),)),
        *(vmem(operand.shape, operand.dtype) for operand in operands),
        pltpu.SemaphoreType.DMA((len(operands),)),
        vmem((QUAD, rows, SLAB), bf16),
        vmem((QUAD, rows, SLAB), bf16),
        vmem((QUAD, CHUNK, width), bf16),
        vmem((QUAD, CHUNK, width), bf16),
        vmem((TAIL, width), bf16),
        vmem((slots, rows, SLAB), bf16),
        vmem((slots, rows, SLAB), bf16),
        vmem((width, SLAB), bf16),
        vmem((width, SLAB), bf16),
        vmem((TAIL + tokens, width), bf16),
        vmem((TAIL + tokens, SLAB), f32),
        vmem((tokens, QXBC), f32),
        vmem((tokens, QXBC), f32),
        vmem((tokens, LANES), f32),
        vmem((tokens, LANES), f32),
        vmem((tokens, LANES), f32),
        vmem((tokens, LANES), f32),
        vmem((tokens, QCH), bf16),
        vmem((QUAD, PAIRS, STATE, LANES), f32),
        vmem((PAIRS, STATE, LANES), bf16),
        vmem((PAIRS, STATE, LANES), bf16),
        vmem((QUAD, PAIRS, STATE, LANES), bf16),
        vmem((QUAD, PAIRS, CHUNK, 2 * CHUNK), bf16),
        vmem((QUAD, PAIRS, CHUNK, 2 * CHUNK), bf16),
        vmem((tokens, QCH), f32),
        vmem((tokens, QCH), f32),
        vmem((tokens, QCH), f32),
        vmem((tokens, QCH), f32),
        vmem((QUAD, 8, tokens), f32),
        vmem((tokens, QCH), bf16),
        vmem((tokens, QCH), bf16),
        vmem((tokens, QCH), f32),
        vmem((tokens, QCH), bf16),
        vmem((QUAD, PAIRS, STATE, LANES), f32),
        vmem((QUAD + 1, PAIRS, STATE, LANES), bf16),
        vmem((QUAD, CHUNK, CHUNK), bf16),
        vmem((tokens, QCH), f32),
        vmem((TAIL + tokens + 8, QXBC), f32),
        vmem((tokens + LANES, SLAB), bf16),
        vmem((slots, rows, SLAB), bf16),
        vmem((slots, rows, SLAB), bf16),
        vmem((QUAD, CHUNK, width), bf16),
        vmem((3, CHUNK, width), bf16),
        vmem((width, tokens + LANES), bf16),
        vmem((width, tokens), bf16),
        vmem((SLAB, width), bf16),
        vmem((SLAB, width), bf16),
        vmem((QUAD, CHUNK, width), f32),
        vmem((QUAD, CHUNK, width), bf16),
        vmem((3, CHUNK, width), bf16),
        vmem((TAIL, width), f32),
        vmem((QUAD, TAIL, width), f32),
        vmem((GRAD_ROWS, QXBC), f32),
        vmem((8, QCH), f32),
        vmem((5, GRAD_ROWS, QXBC), f32),
        vmem((QUAD, GRAD_ROWS, QXBC), f32),
        *held,
        pltpu.SemaphoreType.DMA((SEMS,)),
        pltpu.SemaphoreType.DMA((SEMS,)),
    ]
    in_vmem = pl.BlockSpec(memory_space=pltpu.VMEM)
    got = pl.pallas_call(
        block_kernel,
        out_shape=[
            jax.ShapeDtypeStruct(shape, f32 if at else bf16) for at, shape in enumerate(shapes)
        ],
        in_specs=[pl.BlockSpec(memory_space=pl.ANY)] * 11,
        out_specs=[pl.BlockSpec(memory_space=pl.ANY)] * 11,
        scratch_shapes=scratch,
        compiler_params=pltpu.CompilerParams(
            collective_id=1, has_side_effects=True, vmem_limit_bytes=VMEM_BYTES
        ),
        name="residual_block",
    )(*operands)
    got = pl.pallas_call(
        copy_out_kernel,
        out_shape=[jax.ShapeDtypeStruct(value.shape, value.dtype) for value in got],
        in_specs=[pl.BlockSpec(memory_space=pl.ANY)] * 11,
        out_specs=[pl.BlockSpec(memory_space=pl.ANY)] * 11,
        scratch_shapes=[vmem(value.shape, value.dtype) for value in got]
        + [pltpu.SemaphoreType.DMA((11,))] * 2,
        name="copy_out",
    )(*got)
    return (*got[:5], got[5].T, *got[6:])


def copy_out_kernel(*refs):
    count = (len(refs) - 2) // 3
    sources, landings, held = refs[:count], refs[count : 2 * count], refs[2 * count : 3 * count]
    load_sem, store_sem = refs[3 * count :]
    loads = [pltpu.make_async_copy(sources[i], held[i], load_sem.at[i]) for i in range(count)]
    stores = [pltpu.make_async_copy(held[i], landings[i], store_sem.at[i]) for i in range(count)]
    for load in loads:
        load.start()
    for load, store in zip(loads, stores):
        load.wait()
        store.start()
    for store in stores:
        store.wait()


def fits_quads(mesh):
    return mesh.shape["dp"] == 4 and mesh.shape["seq"] == 2 * QUAD


def solution(mesh):
    placed = (
        P(("dp", "seq"), None),
        P(),
        P(("dp", "seq"), None),
        P(),
        P(),
        P(),
        P(),
        P(),
        P(),
        P(("dp", "seq"), None),
        P(("dp", "seq"), None),
    )
    return jax.shard_map(
        quad_body if fits_quads(mesh) else body,
        mesh=mesh,
        in_specs=placed,
        out_specs=(
            P(("dp", "seq"), None),
            P(("dp", "seq"), None),
            P(("dp", "seq"), None),
            P(("dp", "seq"), None),
            P(),
            P(),
            P(),
            P(),
            P(),
            P(),
            P(),
        ),
        check_vma=False,
    )
```
